32 devices in a mesh: expert: 8 (over z, x), tensor: 4 (over y, core).
Axes of the slice: x: 2, y: 2, z: 4, core: 2. Of those that a mesh axis runs over, the one named last changes fastest.
Arguments:
- tokens: bfloat16 [8192, 2048], P(('expert', 'tensor')), may hold values from -6 to 6
- cotangent: bfloat16 [8192, 2048], P(('expert', 'tensor')), may hold values from -6 to 6
- routes: int32 [8192, 8], P(('expert', 'tensor')), may hold values from 0 to 15, all different within a row; in each aligned block of 256 rows (0 to 255, 256 to 511, ...) at most 170 rows name the same one
- norm_in: float32 [2048], replicated, may hold values from 0.5 to 1.5
- query_w: bfloat16 [2048, 2048], P(None, 'tensor'), may hold values from -0.125 to 0.125
- key_w: bfloat16 [2048, 2048], P(None, 'tensor'), may hold values from -0.125 to 0.125
- value_w: bfloat16 [2048, 2048], P(None, 'tensor'), may hold values from -0.125 to 0.125
- out_w: bfloat16 [2048, 2048], P('tensor'), may hold values from -1 to 1
- query_gain: float32 [128], replicated, may hold values from 0.1 to 1.9
- key_gain: float32 [128], replicated, may hold values from 0.1 to 1.9
- norm_mid: float32 [2048], replicated, may hold values from 0.5 to 1.5
- router_w: float32 [2048, 16], replicated, may hold values from -0.0625 to 0.0625
- gate_w: bfloat16 [16, 2048, 1024], P('expert'), may hold values from -0.125 to 0.125
- up_w: bfloat16 [16, 2048, 1024], P('expert'), may hold values from -0.125 to 0.125
- down_w: bfloat16 [16, 1024, 2048], P('expert'), may hold values from -0.875 to 0.875
Outputs:
- output: bfloat16 [8192, 2048], P(('expert', 'tensor'))
- input_grad: float32 [8192, 2048], P(('expert', 'tensor'))
- norm_in_grad: float32 [2048], replicated
- query_w_grad: float32 [2048, 2048], P('expert', 'tensor')
- key_w_grad: float32 [2048, 2048], P('expert', 'tensor')
- value_w_grad: float32 [2048, 2048], P('expert', 'tensor')
- out_w_grad: float32 [2048, 2048], P('tensor', 'expert')
- query_gain_grad: float32 [128], replicated
- key_gain_grad: float32 [128], replicated
- norm_mid_grad: float32 [2048], replicated
- router_w_grad: float32 [2048, 16], replicated
- gate_w_grad: float32 [16, 2048, 1024], P('expert', None, 'tensor')
- up_w_grad: float32 [16, 2048, 1024], P('expert', None, 'tensor')
- down_w_grad: float32 [16, 1024, 2048], P('expert', 'tensor')
The draws below stay inside these ranges and needn't reach their ends.
Inputs may be any that keep to these rules, and one draw needn't show every extreme that they name: `routes`: each row names 8 different experts. Among the 256 rows of one device (aligned blocks), no expert is named by more than 170 rows, and in some block one expert is named by exactly 170.
All inputs are finite; a program needn't handle non-finite values.
Results may differ from the reference program's by a relative error of at most 0.02.
Values may be sent and summed in bfloat16 or wider, within the bound.
A program may use at most 320 MiB of HBM per device.

```python
import math
from functools import partial
import jax
import jax.numpy as jnp
import numpy as np
from jax import lax

D = 2048
HEADS = 16
HDIM = 128
FF = 1024
TOP = 8
SEQ_LEN = 1024
ROWS = 256
TOKENS = 8192
EXPERTS = 16
CAP = 170
N_EXPERT = 8


def levels(rng, dims, split, smallest, largest):
    def one(dim, shards_of):
        draws = jax.random.uniform(jax.random.fold_in(jax.random.fold_in(rng, 6), dim), (shards_of,), jnp.float32, smallest / len(split), largest / len(split))
        return jnp.repeat(jnp.exp(draws), dims[dim] // shards_of).reshape((-1,) + (1,) * (len(dims) - dim - 1))

    loudness = one(*split[0])
    for cut in split[1:]:
        loudness = loudness * one(*cut)
    return loudness


def deal_out(own_key, own, number, rows, count, top, bound, slope):
    order = jax.random.permutation(own_key, count)
    heavy_load, usual = portions_of(count, rows * top, bound, slope, True), portions_of(count, rows * top, bound, slope, False)
    places = jnp.arange(count)

    def named(sizes, offset_by):
        used = int((sizes > 0).sum())
        fixed = max(1, used // 4)
        passed = fixed + (places - fixed + offset_by * (used - fixed)) % max(1, count - fixed)
        return jnp.zeros((count,), jnp.int32).at[order[jnp.where(places < fixed, places, passed)]].set(jnp.asarray(sizes, jnp.int32))

    sizes = jnp.where(number % 4 == 0, named(heavy_load, number // 4), named(usual, number - number // 4 - 1))
    mixed = jax.random.permutation(jax.random.fold_in(own, 3), count)
    donor, taker = mixed[0:count // 2 * 2:2], mixed[1:count // 2 * 2:2]
    room = jnp.minimum(sizes[donor] - 1, bound - sizes[taker]) // 2
    room = jnp.where((donor == order[0]) | (taker == order[0]) | (sizes[taker] == 0), 0, jnp.maximum(room, 0))
    passed = jax.random.randint(jax.random.fold_in(own, 4), (count // 2,), 0, 1 << 20) % (room + 1)
    sizes = sizes.at[donor].add(-passed).at[taker].add(passed)
    members = jnp.searchsorted(jnp.cumsum(sizes), jnp.arange(rows * top), side="right").astype(jnp.int32)
    listing = members.reshape(top, rows).T
    listing = listing[jax.random.permutation(jax.random.fold_in(own, 1), rows)]
    offset_by = jax.random.randint(jax.random.fold_in(own, 2), (rows, 1), 0, top)
    return jnp.take_along_axis(listing, (jnp.arange(top)[None, :] + offset_by) % top, axis=1)


def portions_of(amount, total, bound, skew, full):
    weights = [(1 << 20) // math.isqrt(rank ** skew) + 1 for rank in range(1, amount + 1)]
    largest = bound if full else min(bound, max(-(-total // amount), total * weights[0] // sum(weights)))
    least = 1 if total - largest >= amount - 1 else 0
    holding, surplus = [largest] + [least] * (amount - 1), total - largest - least * (amount - 1)
    while surplus > 0:
        candidates = [i for i in range(1, amount) if holding[i] < largest] or [i for i in range(1, amount) if holding[i] < bound]
        mass, budget = sum([weights[i] for i in candidates]), surplus
        for i in candidates:
            addition = min(bound - holding[i], max(1, budget * weights[i] // mass), surplus)
            holding[i] = holding[i] + addition
            surplus = surplus - addition
    return np.array(holding)


def centred(rng, dims, width, most, shards=(), kind=jnp.bfloat16):
    drawn = width * jax.random.normal(rng, dims, jnp.float32)
    if shards:
        drawn = drawn * levels(rng, dims, shards, -0.22, 0.18)
    return jnp.clip(drawn, -most, most).astype(kind)


def setup_inputs(seed: int = 0) -> dict:
    arg_keys = jax.random.split(jax.random.key(seed), 16)
    tokens = centred(arg_keys[0], (TOKENS, D), 1.0, 6.0, ((0, 32),))
    cotangent = centred(arg_keys[1], (TOKENS, D), 1.0, 6.0, ((0, 32),))
    routes_keys = jax.random.split(jax.random.fold_in(arg_keys[2], 1), TOKENS // ROWS)
    routes_turns = jax.random.permutation(jax.random.fold_in(arg_keys[2], 3), TOKENS // ROWS)
    routes = jax.vmap(lambda own, number: deal_out(jax.random.fold_in(arg_keys[2], 2), own, number, ROWS, EXPERTS, TOP, CAP, 1))(routes_keys, routes_turns).reshape((TOKENS, TOP))
    norm_in = jnp.clip(1.0 + 0.1 * jax.random.normal(arg_keys[3], (D,), jnp.float32), 0.5, 1.5)
    query_w = centred(arg_keys[4], (D, HEADS * HDIM), D ** -0.5, 0.125, ((1, 4),))
    key_w = centred(arg_keys[5], (D, HEADS * HDIM), D ** -0.5, 0.125, ((1, 4),))
    value_w = centred(arg_keys[6], (D, HEADS * HDIM), D ** -0.5, 0.125, ((1, 4),))
    out_w = centred(arg_keys[7], (HEADS * HDIM, D), (max(HEADS * HDIM // 64, 1)) ** -0.5, 1.0, ((0, 4),))
    query_gain = jnp.clip(1.0 + 0.18 * jax.random.normal(arg_keys[8], (HDIM,), jnp.float32), 0.1, 1.9)
    key_gain = jnp.clip(1.0 + 0.18 * jax.random.normal(arg_keys[9], (HDIM,), jnp.float32), 0.1, 1.9)
    norm_mid = jnp.clip(1.0 + 0.1 * jax.random.normal(arg_keys[10], (D,), jnp.float32), 0.5, 1.5)
    router_w = centred(arg_keys[11], (D, EXPERTS), (4 * D) ** -0.5, 0.0625, (), jnp.float32)
    gate_w = centred(arg_keys[12], (EXPERTS, D, FF), D ** -0.5, 0.125, ((0, 8),))
    up_w = centred(arg_keys[13], (EXPERTS, D, FF), D ** -0.5, 0.125, ((0, 8),))
    down_w = centred(arg_keys[14], (EXPERTS, FF, D), (max(FF // 20, 1)) ** -0.5, 0.875, ((0, 8),))
    return dict(tokens=tokens, cotangent=cotangent, routes=routes, norm_in=norm_in, query_w=query_w, key_w=key_w, value_w=value_w, out_w=out_w, query_gain=query_gain, key_gain=key_gain, norm_mid=norm_mid, router_w=router_w, gate_w=gate_w, up_w=up_w, down_w=down_w)


@jax.custom_vjp
def low(v):
    return lax.optimization_barrier(v.astype(jnp.bfloat16)).astype(jnp.float32)

@jax.custom_vjp
def low_back(v):
    return v

def low_keep(v):
    return (low(v), None)

def low_pass(kept, grad):
    return (grad,)

def back_keep(v):
    return (v, None)

def back_low(kept, grad):
    return (low(grad),)
low.defvjp(low_keep, low_pass)
low_back.defvjp(back_keep, back_low)
epsilon = 1e-06
highest = lax.Precision.HIGHEST

def product(left, right):
    return jnp.dot(left, right, precision=highest)

def rms_scale(values, norm_gain):
    return values * lax.rsqrt(lax.optimization_barrier(jnp.mean(values * values, axis=-1, keepdims=True)) + epsilon) * norm_gain

def rotate(values, cosine, sine_table):
    half_dim = values.shape[-1] // 2
    first_half = values[..., :half_dim]
    second_half = values[..., half_dim:]
    return jnp.concatenate([first_half * cosine - second_half * sine_table, second_half * cosine + first_half * sine_table], axis=-1)

def attend(inputs):
    query, key_rows, value_rows = inputs
    scores = low_back(jnp.einsum('qhd,khd->hqk', query, key_rows, precision=highest) / math.sqrt(query.shape[-1]))
    probs = low(jax.nn.softmax(scores, axis=-1))
    return jnp.einsum('hqk,khd->qhd', probs, value_rows, precision=highest)

def expert_block(inputs):
    rows_in, gate_mat, up_mat, down_mat = inputs
    gate_pre = low_back(product(rows_in, gate_mat))
    up_pre = low_back(product(rows_in, up_mat))
    hidden_low = low(gate_pre * jax.nn.sigmoid(gate_pre) * up_pre)
    return low(low_back(product(hidden_low, down_mat)))

def layer(routes, tokens, norm_in, query_w, key_w, value_w, out_w, query_gain, key_gain, norm_mid, router_w, gate_w, up_w, down_w):
    normed = low(rms_scale(tokens, norm_in))
    query_pre = low_back(product(normed, query_w)).reshape(N_EXPERT, SEQ_LEN, HEADS, HDIM)
    key_pre = low_back(product(normed, key_w)).reshape(N_EXPERT, SEQ_LEN, HEADS, HDIM)
    value_all = low(low_back(product(normed, value_w))).reshape(N_EXPERT, SEQ_LEN, HEADS, HDIM)
    half_dim = HDIM // 2
    frequency = jnp.exp(-math.log(10000.0) * 2.0 * jnp.arange(half_dim).astype(jnp.float32) / HDIM)
    angles = jnp.arange(SEQ_LEN).astype(jnp.float32)[:, None] * frequency[None, :]
    cosine = jnp.cos(angles)[:, None, :]
    sine_table = jnp.sin(angles)[:, None, :]
    query_all = low(rotate(rms_scale(query_pre, query_gain), cosine, sine_table))
    key_all = low(rotate(rms_scale(key_pre, key_gain), cosine, sine_table))
    attended = lax.map(jax.checkpoint(attend), (query_all, key_all, value_all))
    attended = low(low_back(attended.reshape(TOKENS, HEADS * HDIM)))
    middle = tokens + low_back(product(attended, out_w))
    normed_mid = rms_scale(middle, norm_mid)
    logits = product(normed_mid, router_w)
    gating = jax.nn.softmax(jnp.take_along_axis(logits, routes, axis=1), axis=-1)
    flat_routes = routes.reshape(-1).astype(jnp.int32)
    route_mask = (flat_routes[:, None] == jnp.arange(EXPERTS, dtype=jnp.int32)[None, :]).astype(jnp.int32)
    devices_all = TOKENS // ROWS
    running = jnp.cumsum(route_mask.reshape(devices_all, ROWS * TOP, EXPERTS), axis=1).reshape(TOKENS * TOP, EXPERTS)
    slot_index = lax.optimization_barrier(jnp.sum((running - 1) * route_mask, axis=1)).astype(jnp.int32)
    device_index = (jnp.arange(TOKENS * TOP, dtype=jnp.int32) // (ROWS * TOP)).astype(jnp.int32)
    positions = ((flat_routes * devices_all + device_index) * CAP + slot_index).astype(jnp.int32)
    route_rows = low_back(jnp.repeat(low(normed_mid), TOP, axis=0))
    buffers = jnp.zeros((EXPERTS * devices_all * CAP, D), jnp.float32).at[positions].set(route_rows)
    outputs = lax.map(jax.checkpoint(expert_block), (buffers.reshape(EXPERTS, devices_all * CAP, D), gate_w, up_w, down_w))
    per_route = outputs.reshape(EXPERTS * devices_all * CAP, D)[positions].reshape(TOKENS, TOP, D)
    return middle + lax.optimization_barrier(jnp.sum(gating[:, :, None] * per_route, axis=1))

def reference(tokens, cotangent, routes, norm_in, query_w, key_w, value_w, out_w, query_gain, key_gain, norm_mid, router_w, gate_w, up_w, down_w):
    params = [arr.astype(jnp.float32) for arr in (tokens, norm_in, query_w, key_w, value_w, out_w, query_gain, key_gain, norm_mid, router_w, gate_w, up_w, down_w)]
    output, pullback = jax.vjp(partial(layer, routes), *params)
    grads = pullback(cotangent.astype(jnp.float32))
    return (output.astype(jnp.bfloat16), grads[0], grads[1], grads[2], grads[3], grads[4], grads[5], grads[6], grads[7], grads[8], grads[9], grads[10], grads[11], grads[12])
```

```python
import math

import jax
import jax.numpy as jnp
from jax import lax
from jax.sharding import PartitionSpec as P

epsilon = 1e-06
highest = lax.Precision.HIGHEST
contract_last = (((1,), (1,)), ((), ()))
contract_first = (((0,), (0,)), ((), ()))


def inverse_rms(values):
    return lax.rsqrt(jnp.mean(values * values, axis=-1, keepdims=True) + epsilon)


def norm_backward(grad_norm, values, inverse, norm_gain):
    weighted = grad_norm * norm_gain
    inner_mean = jnp.mean(weighted * values, axis=-1, keepdims=True)
    return inverse * weighted - values * inverse * inverse * inverse * inner_mean


def rotary_tables(length, head_width):
    half_dim = head_width // 2
    frequency = jnp.exp(
        -math.log(10000.0) * 2.0 * jnp.arange(half_dim, dtype=jnp.float32) / head_width
    )
    angles = jnp.arange(length, dtype=jnp.float32)[:, None] * frequency[None, :]
    return (jnp.cos(angles)[:, None, :], jnp.sin(angles)[:, None, :])


def rotate(values, cosine, sine_table):
    half_dim = values.shape[-1] // 2
    first_half = values[..., :half_dim]
    second_half = values[..., half_dim:]
    return jnp.concatenate(
        [
            first_half * cosine - second_half * sine_table,
            second_half * cosine + first_half * sine_table,
        ],
        axis=-1,
    )


def rotate_back(gradient, cosine, sine_table):
    half_dim = gradient.shape[-1] // 2
    first_half = gradient[..., :half_dim]
    second_half = gradient[..., half_dim:]
    return jnp.concatenate(
        [
            first_half * cosine + second_half * sine_table,
            second_half * cosine - first_half * sine_table,
        ],
        axis=-1,
    )


def swiglu_back(hidden_grad, gate_pre, up_pre):
    sigmoid_part = jax.nn.sigmoid(gate_pre)
    gate_back = (
        hidden_grad * up_pre * sigmoid_part * (1.0 + gate_pre * (1.0 - sigmoid_part))
    ).astype(jnp.bfloat16)
    up_back = (hidden_grad * gate_pre * sigmoid_part).astype(jnp.bfloat16)
    return (gate_back, up_back)


def per_device(
    tokens,
    cotangent,
    routes,
    norm_in,
    query_w,
    key_w,
    value_w,
    out_w,
    query_gain,
    key_gain,
    norm_mid,
    router_w,
    gate_w,
    up_w,
    down_w,
):
    rows_own = tokens.shape[0]
    model_width = tokens.shape[1]
    tensor_count = lax.axis_size("tensor")
    expert_count = lax.axis_size("expert")
    head_width = query_gain.shape[0]
    local_heads = query_w.shape[1] // head_width
    experts_local = gate_w.shape[0]
    experts_all = router_w.shape[1]
    top_count = routes.shape[1]
    hidden_width = gate_w.shape[2]
    factor = 1.0 / math.sqrt(head_width)
    cot_all = lax.all_gather(cotangent, "expert", axis=0, tiled=True)
    source = tokens.astype(jnp.float32)
    scale_in = inverse_rms(source)
    normed_low = (source * scale_in * norm_in).astype(jnp.bfloat16)
    gathered = lax.all_gather(normed_low, "tensor", axis=0, tiled=True)
    seq_len = gathered.shape[0]
    query_pre = jnp.dot(gathered, query_w, preferred_element_type=jnp.float32)
    key_pre = jnp.dot(gathered, key_w, preferred_element_type=jnp.float32)
    value_low = jnp.dot(gathered, value_w, preferred_element_type=jnp.float32).astype(jnp.bfloat16)
    cosine, sine_table = rotary_tables(seq_len, head_width)
    query_heads = query_pre.reshape(seq_len, local_heads, head_width)
    key_heads = key_pre.reshape(seq_len, local_heads, head_width)
    query_scale = inverse_rms(query_heads)
    key_scale = inverse_rms(key_heads)
    query_low = rotate(query_heads * query_scale * query_gain, cosine, sine_table).astype(
        jnp.bfloat16
    )
    key_low = rotate(key_heads * key_scale * key_gain, cosine, sine_table).astype(jnp.bfloat16)
    value_heads = value_low.reshape(seq_len, local_heads, head_width)
    block_rows = min(512, seq_len)
    block_count = seq_len // block_rows
    query_blocks = query_low.reshape(block_count, block_rows, local_heads, head_width)

    def attend(query_block):
        scores = (
            jnp.einsum("qhd,khd->hqk", query_block, key_low, preferred_element_type=jnp.float32)
            * factor
        )
        row_max = jnp.max(scores, axis=-1, keepdims=True)
        shifted = jnp.exp(scores - row_max)
        row_sum = jnp.sum(shifted, axis=-1, keepdims=True)
        probs_low = (shifted / row_sum).astype(jnp.bfloat16)
        mixture = jnp.einsum(
            "hqk,khd->qhd", probs_low, value_heads, preferred_element_type=jnp.float32
        )
        return (mixture.astype(jnp.bfloat16), (row_max + jnp.log(row_sum))[..., 0])

    attended_blocks, log_sums = lax.map(attend, query_blocks)
    attended = attended_blocks.reshape(seq_len, local_heads * head_width)
    attn_out = lax.psum_scatter(
        jnp.dot(attended, out_w, preferred_element_type=jnp.float32).astype(jnp.bfloat16),
        "tensor",
        scatter_dimension=0,
        tiled=True,
    ).astype(jnp.float32)
    middle = source + attn_out
    scale_mid = inverse_rms(middle)
    normed_mid = middle * scale_mid * norm_mid
    mid_low = normed_mid.astype(jnp.bfloat16)
    logits = jnp.dot(normed_mid, router_w, precision=highest, preferred_element_type=jnp.float32)
    route_mask = routes[:, :, None] == jnp.arange(experts_all, dtype=jnp.int32)[None, None, :]
    mask_float = route_mask.astype(jnp.float32)
    chosen = jnp.sum(mask_float * logits[:, None, :], axis=-1)
    gating = jax.nn.softmax(chosen, axis=-1)
    upstream = cotangent.astype(jnp.float32)
    gates = jnp.sum(mask_float * gating[:, :, None], axis=1)
    x_all = lax.all_gather(mid_low, "expert", axis=0, tiled=True)
    gates_all = lax.all_gather(gates, "expert", axis=0, tiled=True)
    first_expert = lax.axis_index("expert") * experts_local
    own_gates = lax.dynamic_slice_in_dim(gates_all, first_expert, experts_local, 1)
    part_width = hidden_width // tensor_count
    rows_all = x_all.shape[0]
    y_part = jnp.zeros((rows_all, model_width), jnp.float32)
    x_grad_part = jnp.zeros((rows_all, model_width), jnp.float32)
    gate_grads, gate_parts, up_parts, down_parts = [], [], [], []
    for e in range(experts_local):
        hidden_raw = lax.dot_general(
            cot_all, down_w[e], contract_last, preferred_element_type=jnp.float32
        )
        gate_pre = jnp.dot(x_all, gate_w[e], preferred_element_type=jnp.float32)
        up_pre = jnp.dot(x_all, up_w[e], preferred_element_type=jnp.float32)
        weight = own_gates[:, e : e + 1]
        hidden = gate_pre * jax.nn.sigmoid(gate_pre) * up_pre
        gate_grads.append(jnp.sum(hidden * hidden_raw, axis=1))
        hidden_low = (hidden * weight).astype(jnp.bfloat16)
        gate_back, up_back = swiglu_back(hidden_raw * weight, gate_pre, up_pre)
        y_part = y_part + jnp.dot(hidden_low, down_w[e], preferred_element_type=jnp.float32)
        x_grad_part = x_grad_part + lax.dot_general(
            gate_back, gate_w[e], contract_last, preferred_element_type=jnp.float32
        )
        x_grad_part = x_grad_part + lax.dot_general(
            up_back, up_w[e], contract_last, preferred_element_type=jnp.float32
        )
        gate_parts.append(
            jnp.einsum(
                "nd,ntf->tdf",
                x_all,
                gate_back.reshape(rows_all, tensor_count, part_width),
                preferred_element_type=jnp.float32,
            ).astype(jnp.bfloat16)
        )
        up_parts.append(
            jnp.einsum(
                "nd,ntf->tdf",
                x_all,
                up_back.reshape(rows_all, tensor_count, part_width),
                preferred_element_type=jnp.float32,
            ).astype(jnp.bfloat16)
        )
        down_parts.append(
            lax.dot_general(
                hidden_low, cot_all, contract_first, preferred_element_type=jnp.float32
            ).astype(jnp.bfloat16)
        )
    x_grad = lax.psum_scatter(
        x_grad_part.astype(jnp.bfloat16), "expert", scatter_dimension=0, tiled=True
    )
    expert_input_grad = x_grad.astype(jnp.float32)
    gate_grad_sent = jnp.stack(gate_grads, axis=-1)
    gate_grad_all = lax.all_to_all(gate_grad_sent, "expert", split_axis=0, concat_axis=0, tiled=True)
    gate_grad_dense = (
        gate_grad_all.reshape(expert_count, rows_own, experts_local)
        .transpose(1, 0, 2)
        .reshape(rows_own, experts_all)
    )
    gate_grad = jnp.sum(mask_float * gate_grad_dense[:, None, :], axis=-1)
    y_sum = lax.psum_scatter(
        y_part.astype(jnp.bfloat16), "expert", scatter_dimension=0, tiled=True
    )
    output = (middle + y_sum.astype(jnp.float32)).astype(jnp.bfloat16)

    def own_part(parts):
        return [
            lax.psum_scatter(p, "tensor", scatter_dimension=0, tiled=True).astype(jnp.float32)
            for p in parts
        ]

    gate_w_grad = jnp.concatenate(own_part(gate_parts), axis=0)
    up_w_grad = jnp.concatenate(own_part(up_parts), axis=0)
    down_w_grad = jnp.stack(own_part(down_parts), axis=0)
    inner_gate = jnp.sum(gating * gate_grad, axis=-1, keepdims=True)
    chosen_grad = gating * (gate_grad - inner_gate)
    logit_grad = jnp.sum(chosen_grad[:, :, None] * mask_float, axis=1)
    router_part = lax.dot_general(
        normed_mid,
        logit_grad,
        contract_first,
        precision=highest,
        preferred_element_type=jnp.float32,
    )
    normed_mid_grad = expert_input_grad + lax.dot_general(
        logit_grad, router_w, contract_last, precision=highest, preferred_element_type=jnp.float32
    )
    norm_mid_part = jnp.sum(normed_mid_grad * middle * scale_mid, axis=0)
    middle_grad = upstream + norm_backward(normed_mid_grad, middle, scale_mid, norm_mid)
    branch_low = middle_grad.astype(jnp.bfloat16)
    branch_all = lax.all_gather(branch_low, "tensor", axis=0, tiled=True)
    attended_grad = lax.dot_general(
        branch_all, out_w, contract_last, preferred_element_type=jnp.float32
    ).astype(jnp.bfloat16)
    out_w_part = lax.dot_general(
        attended, branch_all, contract_first, preferred_element_type=jnp.float32
    )
    grad_blocks = attended_grad.reshape(block_count, block_rows, local_heads, head_width)

    def attend_back(carry, inputs):
        key_total, value_total = carry
        query_block, grad_block, log_block = inputs
        scores = (
            jnp.einsum("qhd,khd->hqk", query_block, key_low, preferred_element_type=jnp.float32)
            * factor
        )
        probs = jnp.exp(scores - log_block[:, :, None])
        probs_low = probs.astype(jnp.bfloat16)
        value_total = value_total + jnp.einsum(
            "hqk,qhd->khd", probs_low, grad_block, preferred_element_type=jnp.float32
        )
        prob_grad = jnp.einsum(
            "qhd,khd->hqk", grad_block, value_heads, preferred_element_type=jnp.float32
        )
        delta = jnp.sum(probs * prob_grad, axis=-1, keepdims=True)
        score_low = (probs * (prob_grad - delta)).astype(jnp.bfloat16)
        query_part = (
            jnp.einsum("hqk,khd->qhd", score_low, key_low, preferred_element_type=jnp.float32)
            * factor
        )
        key_total = (
            key_total
            + jnp.einsum("hqk,qhd->khd", score_low, query_block, preferred_element_type=jnp.float32)
            * factor
        )
        return ((key_total, value_total), query_part)

    zero_heads = jnp.zeros((seq_len, local_heads, head_width), jnp.float32)
    (key_grad, value_total), query_parts = lax.scan(
        attend_back, (zero_heads, zero_heads), (query_blocks, grad_blocks, log_sums)
    )
    query_grad = query_parts.reshape(seq_len, local_heads, head_width)
    value_grad_low = value_total.reshape(seq_len, local_heads * head_width).astype(jnp.bfloat16)
    query_rot_grad = rotate_back(query_grad, cosine, sine_table)
    key_rot_grad = rotate_back(key_grad, cosine, sine_table)
    query_gain_part = jnp.sum(query_rot_grad * query_heads * query_scale, axis=(0, 1))
    key_gain_part = jnp.sum(key_rot_grad * key_heads * key_scale, axis=(0, 1))
    query_pre_grad = (
        norm_backward(query_rot_grad, query_heads, query_scale, query_gain)
        .reshape(seq_len, local_heads * head_width)
        .astype(jnp.bfloat16)
    )
    key_pre_grad = (
        norm_backward(key_rot_grad, key_heads, key_scale, key_gain)
        .reshape(seq_len, local_heads * head_width)
        .astype(jnp.bfloat16)
    )
    query_w_part = lax.dot_general(
        gathered, query_pre_grad, contract_first, preferred_element_type=jnp.float32
    )
    key_w_part = lax.dot_general(
        gathered, key_pre_grad, contract_first, preferred_element_type=jnp.float32
    )
    value_w_part = lax.dot_general(
        gathered, value_grad_low, contract_first, preferred_element_type=jnp.float32
    )
    summed = lax.dot_general(
        query_pre_grad, query_w, contract_last, preferred_element_type=jnp.float32
    )
    summed = summed + lax.dot_general(
        key_pre_grad, key_w, contract_last, preferred_element_type=jnp.float32
    )
    rows_grad = lax.psum_scatter(
        (
            summed
            + lax.dot_general(
                value_grad_low, value_w, contract_last, preferred_element_type=jnp.float32
            )
        ).astype(jnp.bfloat16),
        "tensor",
        scatter_dimension=0,
        tiled=True,
    ).astype(jnp.float32)
    norm_in_part = jnp.sum(rows_grad * source * scale_in, axis=0)
    input_grad = middle_grad + norm_backward(rows_grad, source, scale_in, norm_in)
    query_w_grad, key_w_grad, value_w_grad, out_w_grad = (
        lax.psum_scatter(
            query_w_part.astype(jnp.bfloat16), "expert", scatter_dimension=0, tiled=True
        ).astype(jnp.float32),
        lax.psum_scatter(
            key_w_part.astype(jnp.bfloat16), "expert", scatter_dimension=0, tiled=True
        ).astype(jnp.float32),
        lax.psum_scatter(
            value_w_part.astype(jnp.bfloat16), "expert", scatter_dimension=0, tiled=True
        ).astype(jnp.float32),
        lax.psum_scatter(
            out_w_part.astype(jnp.bfloat16), "expert", scatter_dimension=1, tiled=True
        ).astype(jnp.float32),
    )
    norm_in_grad, query_gain_grad, key_gain_grad, norm_mid_grad, router_w_grad = lax.psum(
        (norm_in_part, query_gain_part, key_gain_part, norm_mid_part, router_part),
        ("expert", "tensor"),
    )
    return (
        output,
        input_grad,
        norm_in_grad,
        query_w_grad,
        key_w_grad,
        value_w_grad,
        out_w_grad,
        query_gain_grad,
        key_gain_grad,
        norm_mid_grad,
        router_w_grad,
        gate_w_grad,
        up_w_grad,
        down_w_grad,
    )


def solution(mesh):
    placed = (
        P(("expert", "tensor"), None),
        P(("expert", "tensor"), None),
        P(("expert", "tensor"), None),
        P(),
        P(None, "tensor"),
        P(None, "tensor"),
        P(None, "tensor"),
        P("tensor", None),
        P(),
        P(),
        P(),
        P(),
        P("expert", None, None),
        P("expert", None, None),
        P("expert", None, None),
    )
    return jax.shard_map(
        per_device,
        mesh=mesh,
        in_specs=placed,
        out_specs=(
            P(("expert", "tensor"), None),
            P(("expert", "tensor"), None),
            P(),
            P("expert", "tensor"),
            P("expert", "tensor"),
            P("expert", "tensor"),
            P("tensor", "expert"),
            P(),
            P(),
            P(),
            P(),
            P("expert", None, "tensor"),
            P("expert", None, "tensor"),
            P("expert", "tensor", None),
        ),
        check_vma=False,
    )
```

```python
import functools
import math

import jax
import jax.numpy as jnp
from jax import lax
from jax.experimental import pallas as pl
from jax.experimental.pallas import tpu as pltpu
from jax.sharding import PartitionSpec as P

epsilon = 1e-06
highest = lax.Precision.HIGHEST
contract_last = (((1,), (1,)), ((), ()))
contract_first = (((0,), (0,)), ((), ()))


def inverse_rms(values):
    return lax.rsqrt(jnp.mean(values * values, axis=-1, keepdims=True) + epsilon)


def norm_backward(grad_norm, values, inverse, norm_gain):
    weighted = grad_norm * norm_gain
    inner_mean = jnp.mean(weighted * values, axis=-1, keepdims=True)
    return inverse * weighted - values * inverse * inverse * inverse * inner_mean


def rotary_tables(length, head_width):
    half_dim = head_width // 2
    frequency = jnp.exp(
        -math.log(10000.0) * 2.0 * jnp.arange(half_dim, dtype=jnp.float32) / head_width
    )
    angles = jnp.arange(length, dtype=jnp.float32)[:, None] * frequency[None, :]
    return (jnp.cos(angles)[:, None, :], jnp.sin(angles)[:, None, :])


def rotate(values, cosine, sine_table):
    half_dim = values.shape[-1] // 2
    first_half = values[..., :half_dim]
    second_half = values[..., half_dim:]
    return jnp.concatenate(
        [
            first_half * cosine - second_half * sine_table,
            second_half * cosine + first_half * sine_table,
        ],
        axis=-1,
    )


def rotate_back(gradient, cosine, sine_table):
    half_dim = gradient.shape[-1] // 2
    first_half = gradient[..., :half_dim]
    second_half = gradient[..., half_dim:]
    return jnp.concatenate(
        [
            first_half * cosine + second_half * sine_table,
            second_half * cosine - first_half * sine_table,
        ],
        axis=-1,
    )


def swiglu_back(hidden_grad, gate_pre, up_pre):
    sigmoid_part = jax.nn.sigmoid(gate_pre)
    gate_back = (
        hidden_grad * up_pre * sigmoid_part * (1.0 + gate_pre * (1.0 - sigmoid_part))
    ).astype(jnp.bfloat16)
    up_back = (hidden_grad * gate_pre * sigmoid_part).astype(jnp.bfloat16)
    return (gate_back, up_back)


chunks = 4


def pick(index, values):
    result = values[-1]
    for j in reversed(range(len(values) - 1)):
        result = jnp.where(index == j, values[j], result)
    return result


def expert_kernel(
    experts_all,
    own_rows,
    raw_all,
    gate_hbm,
    up_hbm,
    rows_all,
    hidden_all,
    gate_all,
    up_all,
    total,
    gate_v,
    up_v,
    rows_v,
    raw_v,
    hidden_v,
    gate_b,
    up_b,
    parts,
    side_in,
    line_in,
    weight_sem,
    own_sem,
    raw_sem,
    out_sem,
    rows_sem,
    gather_recv,
    gather_send,
    side_recv,
    side_send,
    line_recv,
    line_send,
):
    position = lax.axis_index("expert")
    peer = lax.axis_index("tensor")
    z = position // 2
    x = position % 2
    experts_local, width, hidden = gate_v.shape
    rows = rows_v.shape[1]
    chunk = rows // chunks
    middle = (z == 1) | (z == 2)
    ends = (z == 0) | (z == 3)
    line_slots = [
        z,
        pick(z, [1, 0, 3, 2]),
        pick(z, [2, 2, 1, 1]),
        pick(z, [3, 3, 0, 0]),
    ]

    def device(zz, xx):
        return (zz * 2 + xx, peer)

    def slot_z(k):
        return pick(k, line_slots)

    weight_copies = [
        pltpu.make_async_copy(gate_hbm, gate_v, weight_sem.at[0]),
        pltpu.make_async_copy(up_hbm, up_v, weight_sem.at[1]),
    ]
    own_copy = pltpu.make_async_copy(own_rows, rows_v.at[position], own_sem)
    own_copy.start()
    for copy in weight_copies:
        copy.start()

    barrier = pltpu.get_barrier_semaphore()
    pl.semaphore_signal(barrier, inc=1, device_id=device(z, 1 - x), device_id_type=pl.DeviceIdType.MESH)

    @pl.when(z < 3)
    def _():
        pl.semaphore_signal(barrier, inc=1, device_id=device(z + 1, x), device_id_type=pl.DeviceIdType.MESH)

    @pl.when(z > 0)
    def _():
        pl.semaphore_signal(barrier, inc=1, device_id=device(z - 1, x), device_id_type=pl.DeviceIdType.MESH)

    pl.semaphore_wait(barrier, 2 + middle.astype(jnp.int32))

    def gather_copy(source, block, index, zz, xx):
        return pltpu.make_async_remote_copy(
            src_ref=source,
            dst_ref=rows_v.at[block],
            send_sem=gather_send.at[index],
            recv_sem=gather_recv.at[block],
            device_id=device(zz, xx),
            device_id_type=pl.DeviceIdType.MESH,
        )

    def own_send(index, zz, xx):
        return gather_copy(own_rows, position, index, zz, xx)

    own_send(0, z, 1 - x).start()

    @pl.when(z < 3)
    def _():
        own_send(1, z + 1, x).start()

    @pl.when(z > 0)
    def _():
        own_send(2, z - 1, x).start()

    def forward_side(k):
        block = slot_z(k) * 2 + x
        return gather_copy(rows_v.at[block], block, 2 + k, z, 1 - x)

    def forward_line(k):
        block = slot_z(k) * 2 + x
        target = jnp.where(slot_z(k) < z, z + 1, z - 1)
        return gather_copy(rows_v.at[block], block, 5 + k, jnp.clip(target, 0, 3), x)

    def arrived(block):
        gather_copy(own_rows, block, 0, z, 1 - x).wait_recv()
        pltpu.make_async_copy(rows_v.at[block], rows_all.at[block], rows_sem.at[block]).start()

    def arrive(k):
        arrived(slot_z(k) * 2 + x)
        forward_side(k).start()

        @pl.when(middle)
        def _():
            forward_line(k).start()

    def side_copy(k, c):
        area = pl.ds(c * chunk, chunk)
        return pltpu.make_async_remote_copy(
            src_ref=parts.at[4 + k, area],
            dst_ref=side_in.at[k, area],
            send_sem=side_send.at[k, c],
            recv_sem=side_recv.at[k, c],
            device_id=device(z, 1 - x),
            device_id_type=pl.DeviceIdType.MESH,
        )

    def line_slot(k):
        target = slot_z(k)
        return jnp.where(target < z, target, target + 1)

    def line_copy(k, c):
        area = pl.ds(c * chunk, chunk)
        target = jnp.where(slot_z(k) < z, z - 1, z + 1)
        return pltpu.make_async_remote_copy(
            src_ref=parts.at[k, area],
            dst_ref=line_in.at[line_slot(k), area],
            send_sem=line_send.at[k - 1, c],
            recv_sem=line_recv.at[line_slot(k), c],
            device_id=device(jnp.clip(target, 0, 3), x),
            device_id_type=pl.DeviceIdType.MESH,
        )

    def line_wait(slot, c):
        area = pl.ds(c * chunk, chunk)
        pltpu.make_async_remote_copy(
            src_ref=parts.at[0, area],
            dst_ref=line_in.at[slot, area],
            send_sem=line_send.at[0, c],
            recv_sem=line_recv.at[slot, c],
            device_id=device(z, 1 - x),
            device_id_type=pl.DeviceIdType.MESH,
        ).wait_recv()

    def relay(k, c, has_line):
        area = pl.ds(c * chunk, chunk)
        side_copy(k, c).wait_recv()
        summed = parts[k, area].astype(jnp.float32) + side_in[k, area].astype(jnp.float32)
        if has_line is False:
            parts[k, area] = summed.astype(jnp.bfloat16)
        else:

            @pl.when(middle)
            def _():
                line_wait(line_slot(k), c)
                parts[k, area] = (
                    summed + line_in[line_slot(k), area].astype(jnp.float32)
                ).astype(jnp.bfloat16)

            if has_line is None:

                @pl.when(ends)
                def _():
                    parts[k, area] = summed.astype(jnp.bfloat16)

        line_copy(k, c).start()

    def block_of(step):
        k = pick(step, [0, 1, 0, 2, 1, 3, 2, 3])
        side = pick(step, [0, 0, 1, 0, 1, 0, 1, 1])
        return k, side, slot_z(k) * 2 + jnp.where(side == 1, 1 - x, x)

    def raw_copy(step, slot):
        return pltpu.make_async_copy(raw_all.at[block_of(step)[2]], raw_v.at[slot], raw_sem.at[slot])

    def out_copies(block):
        return [
            pltpu.make_async_copy(hidden_v, hidden_all.at[block], out_sem.at[0]),
            pltpu.make_async_copy(gate_b, gate_all.at[block], out_sem.at[1]),
            pltpu.make_async_copy(up_b, up_all.at[block], out_sem.at[2]),
        ]

    raw_copy(0, 0).start()
    own_copy.wait()
    pltpu.make_async_copy(rows_v.at[position], rows_all.at[position], rows_sem.at[position]).start()
    for copy in weight_copies:
        copy.wait()

    def one_step(step, carry):
        k, side, block = block_of(step)
        slot = step % 2

        @pl.when(step == 1)
        def _():
            arrive(1)

            @pl.when(middle)
            def _():
                arrive(2)

        @pl.when(step == 3)
        def _():
            @pl.when(ends)
            def _():
                arrive(2)

            @pl.when(middle)
            def _():
                arrive(3)

        @pl.when((step == 5) & ends)
        def _():
            arrive(3)

        @pl.when(side == 1)
        def _():
            arrived(block)

        @pl.when((step == 7) & ends)
        def _():
            def one(c, carry):
                relay(1, c, False)
                return carry

            lax.fori_loop(0, chunks, one, 0)

        @pl.when(step < 7)
        def _():
            raw_copy(step + 1, 1 - slot).start()

        @pl.when(step > 0)
        def _():
            for copy in out_copies(block):
                copy.wait()

        raw_copy(step, slot).wait()
        rows_low = rows_v[block, :, :width]
        extra = rows_v[block, :, width:].astype(jnp.float32)
        lane = lax.broadcasted_iota(jnp.int32, extra.shape, 1)
        ext = jnp.zeros(extra.shape, jnp.float32)
        for e in range(experts_local):
            expert = position * experts_local + e
            high = lane == expert
            low = lane == expert + experts_all
            weight = jnp.sum(jnp.where(high | low, extra, 0.0), axis=1, keepdims=True)
            gate_grad = jnp.zeros((rows, 1), jnp.float32)
            for f in range(hidden // 512):
                columns = pl.ds(f * 512, 512)
                gate_pre = jnp.dot(rows_low, gate_v[e, :, columns], preferred_element_type=jnp.float32)
                up_pre = jnp.dot(rows_low, up_v[e, :, columns], preferred_element_type=jnp.float32)
                target = pl.ds(e * hidden + f * 512, 512)
                raw = raw_v[slot, :, target].astype(jnp.float32)
                sig = jax.nn.sigmoid(gate_pre)
                act = gate_pre * sig
                hid = act * up_pre
                gate_grad = gate_grad + jnp.sum(hid * raw, axis=1, keepdims=True)
                hidden_v[:, target] = (hid * weight).astype(jnp.bfloat16)
                grad = raw * weight
                gate_b[:, target] = (grad * up_pre * sig * (1.0 + gate_pre * (1.0 - sig))).astype(jnp.bfloat16)
                up_b[:, target] = (grad * act).astype(jnp.bfloat16)
            grad_high = gate_grad.astype(jnp.bfloat16).astype(jnp.float32)
            ext = jnp.where(high, grad_high, ext)
            ext = jnp.where(low, gate_grad - grad_high, ext)
        place = side * 4 + k
        parts[place, :, width:] = ext.astype(jnp.bfloat16)
        for copy in out_copies(block):
            copy.start()
        for d in range(width // 1024):
            span = pl.ds(d * 1024, 1024)
            summed = jnp.zeros((rows, 1024), jnp.float32)
            for e in range(experts_local):
                target = pl.ds(e * hidden, hidden)
                summed = summed + lax.dot_general(
                    gate_b[:, target], gate_v[e, span, :], contract_last, preferred_element_type=jnp.float32
                )
                summed = summed + lax.dot_general(
                    up_b[:, target], up_v[e, span, :], contract_last, preferred_element_type=jnp.float32
                )
            parts[place, :, span] = summed.astype(jnp.bfloat16)

        @pl.when(side == 1)
        def _():
            for c in range(chunks):
                side_copy(k, c).start()

        return carry

    lax.fori_loop(0, 8, one_step, 0)

    def relay_two(c, carry):
        relay(2, c, None)
        return carry

    lax.fori_loop(0, chunks, relay_two, 0)

    def relay_rest(c, carry):
        relay(3, c, None)

        @pl.when(middle)
        def _():
            relay(1, c, True)

        return carry

    lax.fori_loop(0, chunks, relay_rest, 0)

    def finish(c, carry):
        area = pl.ds(c * chunk, chunk)
        side_copy(0, c).wait_recv()
        total[area] = parts[0, area].astype(jnp.float32) + side_in[0, area].astype(jnp.float32)

        @pl.when(z < 3)
        def _():
            line_wait(z, c)
            total[area] += line_in[z, area].astype(jnp.float32)

        @pl.when(z > 0)
        def _():
            line_wait(z + 1, c)
            total[area] += line_in[z + 1, area].astype(jnp.float32)

        for k in range(4):
            side_copy(k, c).wait_send()
        for k in range(1, 4):
            line_copy(k, c).wait_send()
        return carry

    lax.fori_loop(0, chunks, finish, 0)

    own_send(0, z, 1 - x).wait_send()

    @pl.when(z < 3)
    def _():
        own_send(1, z + 1, x).wait_send()

    @pl.when(z > 0)
    def _():
        own_send(2, z - 1, x).wait_send()

    for k in range(1, 4):
        forward_side(k).wait_send()

        @pl.when(middle)
        def _(k=k):
            forward_line(k).wait_send()

    for copy in out_copies(position):
        copy.wait()
    for block in range(8):
        pltpu.make_async_copy(rows_v.at[block], rows_all.at[block], rows_sem.at[block]).wait()


def expert_pass(own_rows, raw_all, gate_w, up_w, experts_all, collective):
    rows, wide = own_rows.shape
    experts_local, width, hidden = gate_w.shape
    inner = experts_local * hidden
    any_space = pl.BlockSpec(memory_space=pl.ANY)
    low = jnp.bfloat16
    dma = pltpu.SemaphoreType.DMA
    return pl.pallas_call(
        functools.partial(expert_kernel, experts_all),
        name="expert_pass",
        out_shape=(
            jax.ShapeDtypeStruct((8, rows, wide), low),
            jax.ShapeDtypeStruct((8, rows, inner), low),
            jax.ShapeDtypeStruct((8, rows, inner), low),
            jax.ShapeDtypeStruct((8, rows, inner), low),
            jax.ShapeDtypeStruct((rows, wide), jnp.float32),
        ),
        in_specs=[any_space] * 4,
        out_specs=(any_space,) * 4 + (pl.BlockSpec(memory_space=pltpu.VMEM),),
        scratch_shapes=[
            pltpu.VMEM((experts_local, width, hidden), low),
            pltpu.VMEM((experts_local, width, hidden), low),
            pltpu.VMEM((8, rows, wide), low),
            pltpu.VMEM((2, rows, inner), low),
            pltpu.VMEM((rows, inner), low),
            pltpu.VMEM((rows, inner), low),
            pltpu.VMEM((rows, inner), low),
            pltpu.VMEM((8, rows, wide), low),
            pltpu.VMEM((4, rows, wide), low),
            pltpu.VMEM((5, rows, wide), low),
            dma((2,)),
            dma,
            dma((2,)),
            dma((3,)),
            dma((8,)),
            dma((8,)),
            dma((9,)),
            dma((4, chunks)),
            dma((4, chunks)),
            dma((5, chunks)),
            dma((3, chunks)),
        ],
        compiler_params=pltpu.CompilerParams(
            collective_id=collective, has_side_effects=True, vmem_limit_bytes=60 << 20
        ),
        cost_estimate=pl.CostEstimate(
            flops=2 * 4 * 8 * rows * width * inner, bytes_accessed=64 << 20, transcendentals=8 * rows * inner
        ),
    )(own_rows, raw_all, gate_w, up_w)


def scatter_kernel(
    parts, total, own, side_in, line_in, own_sem, side_recv, side_send, line_recv, line_send
):
    position = lax.axis_index("expert")
    peer = lax.axis_index("tensor")
    z = position // 2
    x = position % 2
    chunk = own.shape[1] // chunks
    middle = (z == 1) | (z == 2)
    line_slots = [
        z,
        pick(z, [1, 0, 3, 2]),
        pick(z, [2, 2, 1, 1]),
        pick(z, [3, 3, 0, 0]),
    ]
    mesh_ids = pl.DeviceIdType.MESH

    def device(zz, xx):
        return (zz * 2 + xx, peer)

    own_copies = [
        pltpu.make_async_copy(parts.at[line_slots[k] * 2 + x], own.at[k], own_sem.at[k]) for k in range(4)
    ]
    for k in (3, 2, 1, 0):
        own_copies[k].start()

    barrier = pltpu.get_barrier_semaphore()
    pl.semaphore_signal(barrier, inc=1, device_id=device(z, 1 - x), device_id_type=mesh_ids)

    @pl.when(z < 3)
    def _():
        pl.semaphore_signal(barrier, inc=1, device_id=device(z + 1, x), device_id_type=mesh_ids)

    @pl.when(z > 0)
    def _():
        pl.semaphore_signal(barrier, inc=1, device_id=device(z - 1, x), device_id_type=mesh_ids)

    pl.semaphore_wait(barrier, 2 + middle.astype(jnp.int32))

    def side_copy(k, c):
        area = pl.ds(c * chunk, chunk)
        return pltpu.make_async_remote_copy(
            src_ref=parts.at[pick(k, line_slots) * 2 + 1 - x, area],
            dst_ref=side_in.at[k, area],
            send_sem=side_send.at[k, c],
            recv_sem=side_recv.at[k, c],
            device_id=device(z, 1 - x),
            device_id_type=mesh_ids,
        )

    def line_slot(k):
        target = pick(k, line_slots)
        return jnp.where(target < z, target, target + 1)

    def line_copy(k, c):
        area = pl.ds(c * chunk, chunk)
        target = jnp.where(pick(k, line_slots) < z, z - 1, z + 1)
        return pltpu.make_async_remote_copy(
            src_ref=own.at[k, area],
            dst_ref=line_in.at[line_slot(k), area],
            send_sem=line_send.at[k - 1, c],
            recv_sem=line_recv.at[line_slot(k), c],
            device_id=device(jnp.clip(target, 0, 3), x),
            device_id_type=mesh_ids,
        )

    def line_wait(slot, c):
        area = pl.ds(c * chunk, chunk)
        pltpu.make_async_remote_copy(
            src_ref=own.at[0, area],
            dst_ref=line_in.at[slot, area],
            send_sem=line_send.at[0, c],
            recv_sem=line_recv.at[slot, c],
            device_id=device(z, 1 - x),
            device_id_type=mesh_ids,
        ).wait_recv()

    def send_order(i):
        return jnp.where(middle, pick(i, [3, 1, 2, 0]), pick(i, [3, 2, 1, 0]))

    def start_side(i, carry):
        for c in range(chunks):
            side_copy(send_order(i), c).start()
        return carry

    lax.fori_loop(0, 4, start_side, 0)
    for k in (3, 2, 1, 0):
        own_copies[k].wait()

    def relay(i, carry):
        k = send_order(i // chunks)
        c = i % chunks
        area = pl.ds(c * chunk, chunk)
        side_copy(k, c).wait_recv()
        own[k, area] = (
            own[k, area].astype(jnp.float32) + side_in[k, area].astype(jnp.float32)
        ).astype(jnp.bfloat16)

        @pl.when(middle)
        def _():
            line_wait(line_slot(k), c)
            own[k, area] = (
                own[k, area].astype(jnp.float32) + line_in[line_slot(k), area].astype(jnp.float32)
            ).astype(jnp.bfloat16)

        line_copy(k, c).start()
        return carry

    lax.fori_loop(0, 3 * chunks, relay, 0)

    def finish(c, carry):
        area = pl.ds(c * chunk, chunk)
        side_copy(0, c).wait_recv()
        total[area] = own[0, area].astype(jnp.float32) + side_in[0, area].astype(jnp.float32)

        @pl.when(z < 3)
        def _():
            line_wait(z, c)
            total[area] += line_in[z, area].astype(jnp.float32)

        @pl.when(z > 0)
        def _():
            line_wait(z + 1, c)
            total[area] += line_in[z + 1, area].astype(jnp.float32)

        for k in range(4):
            side_copy(k, c).wait_send()
        for k in range(1, 4):
            line_copy(k, c).wait_send()
        return carry

    lax.fori_loop(0, chunks, finish, 0)


def scatter_parts(parts, collective):
    rows, wide = parts.shape[1:]
    low = jnp.bfloat16
    dma = pltpu.SemaphoreType.DMA
    return pl.pallas_call(
        scatter_kernel,
        name="scatter_parts",
        out_shape=jax.ShapeDtypeStruct((rows, wide), jnp.float32),
        in_specs=[pl.BlockSpec(memory_space=pl.ANY)],
        out_specs=pl.BlockSpec(memory_space=pltpu.VMEM),
        scratch_shapes=[
            pltpu.VMEM((4, rows, wide), low),
            pltpu.VMEM((4, rows, wide), low),
            pltpu.VMEM((5, rows, wide), low),
            dma((4,)),
            dma((4, chunks)),
            dma((4, chunks)),
            dma((5, chunks)),
            dma((3, chunks)),
        ],
        compiler_params=pltpu.CompilerParams(
            collective_id=collective, has_side_effects=True, vmem_limit_bytes=40 << 20
        ),
        cost_estimate=pl.CostEstimate(flops=8 * rows * wide, bytes_accessed=300 << 20, transcendentals=0),
    )(parts)


def sum_kernel(own, total, incoming, recv, send):
    position = lax.axis_index("expert")
    peer = lax.axis_index("tensor")
    mesh_ids = pl.DeviceIdType.MESH

    def flip(index, bit):
        return index + bit - 2 * bit * ((index // bit) % 2)

    partners = [
        (position, flip(peer, 1)),
        (position, flip(peer, 2)),
        (flip(position, 1), peer),
        (flip(position, 2), peer),
        (flip(position, 4), peer),
    ]
    barrier = pltpu.get_barrier_semaphore()
    for partner in partners:
        pl.semaphore_signal(barrier, inc=1, device_id=partner, device_id_type=mesh_ids)
    pl.semaphore_wait(barrier, len(partners))
    total[0] = own[...]
    for i, partner in enumerate(partners):
        copy = pltpu.make_async_remote_copy(
            src_ref=total.at[i],
            dst_ref=incoming.at[i],
            send_sem=send.at[i],
            recv_sem=recv.at[i],
            device_id=partner,
            device_id_type=mesh_ids,
        )
        copy.start()
        copy.wait()
        total[i + 1] = total[i] + incoming[i]


def sum_everywhere(own, collective):
    steps = 5
    return pl.pallas_call(
        sum_kernel,
        name="sum_everywhere",
        out_shape=jax.ShapeDtypeStruct((steps + 1,) + own.shape, jnp.float32),
        in_specs=[pl.BlockSpec(memory_space=pltpu.VMEM)],
        out_specs=pl.BlockSpec(memory_space=pltpu.VMEM),
        scratch_shapes=[
            pltpu.VMEM((steps,) + own.shape, jnp.float32),
            pltpu.SemaphoreType.DMA((steps,)),
            pltpu.SemaphoreType.DMA((steps,)),
        ],
        compiler_params=pltpu.CompilerParams(collective_id=collective, has_side_effects=True),
        cost_estimate=pl.CostEstimate(flops=own.size * steps, bytes_accessed=40 << 20, transcendentals=0),
    )(own)[steps]


def weight_kernel(order, left, right, out):
    wide = left.shape[1]
    step = min(512, wide)
    for d in range(out.shape[2] // step):
        span = pl.ds(d * step, step)
        out[0, 0, span, :] = lax.dot_general(
            left[:, span], right[...], contract_first, preferred_element_type=jnp.float32
        ).astype(out.dtype)


def input_weight_parts(order, rows_all, grads, width, experts_local):
    count, wide = rows_all.shape
    hidden = grads.shape[1] // experts_local
    part = hidden // 4
    pieces = order.shape[0]
    return pl.pallas_call(
        weight_kernel,
        name="input_weight_parts",
        out_shape=jax.ShapeDtypeStruct((pieces, experts_local, width, part), jnp.bfloat16),
        grid_spec=pltpu.PrefetchScalarGridSpec(
            num_scalar_prefetch=1,
            grid=(pieces, experts_local),
            in_specs=[
                pl.BlockSpec((count, width), lambda r, e, order: (0, 0), pipeline_mode=pl.Buffered(1)),
                pl.BlockSpec((count, part), lambda r, e, order: (0, e * 4 + order[r])),
            ],
            out_specs=pl.BlockSpec((1, 1, width, part), lambda r, e, order: (r, e, 0, 0)),
        ),
        compiler_params=pltpu.CompilerParams(vmem_limit_bytes=48 << 20),
        cost_estimate=pl.CostEstimate(
            flops=2 * pieces * experts_local * count * width * part,
            bytes_accessed=2 * count * width + 2 * pieces * experts_local * part * (count + width),
            transcendentals=0,
        ),
    )(order, rows_all, grads)


def output_weight_parts(order, hidden_all, grads, experts_local):
    count, width = grads.shape
    hidden = hidden_all.shape[1] // experts_local
    part = hidden // 4
    pieces = order.shape[0]
    return pl.pallas_call(
        weight_kernel,
        name="output_weight_parts",
        out_shape=jax.ShapeDtypeStruct((pieces, experts_local, part, width), jnp.bfloat16),
        grid_spec=pltpu.PrefetchScalarGridSpec(
            num_scalar_prefetch=1,
            grid=(pieces, experts_local),
            in_specs=[
                pl.BlockSpec((count, part), lambda r, e, order: (0, e * 4 + order[r])),
                pl.BlockSpec((count, width), lambda r, e, order: (0, 0), pipeline_mode=pl.Buffered(1)),
            ],
            out_specs=pl.BlockSpec((1, 1, part, width), lambda r, e, order: (r, e, 0, 0)),
        ),
        compiler_params=pltpu.CompilerParams(vmem_limit_bytes=48 << 20),
        cost_estimate=pl.CostEstimate(
            flops=2 * pieces * experts_local * count * width * part,
            bytes_accessed=2 * count * width + 2 * pieces * experts_local * part * (count + width),
            transcendentals=0,
        ),
    )(order, hidden_all, grads)


def exchange(pieces_far, pieces_near):
    swap_core = [(0, 1), (1, 0), (2, 3), (3, 2)]
    swap_line = [(0, 2), (1, 3), (2, 0), (3, 1)]
    arrived = lax.ppermute(pieces_far, "tensor", swap_core)
    own = pieces_near[0].astype(jnp.float32) + arrived[0].astype(jnp.float32)
    sent = (pieces_near[1].astype(jnp.float32) + arrived[1].astype(jnp.float32)).astype(jnp.bfloat16)
    return own + lax.ppermute(sent, "tensor", swap_line).astype(jnp.float32)


def per_device(
    tokens,
    cotangent,
    routes,
    norm_in,
    query_w,
    key_w,
    value_w,
    out_w,
    query_gain,
    key_gain,
    norm_mid,
    router_w,
    gate_w,
    up_w,
    down_w,
):
    rows_own = tokens.shape[0]
    model_width = tokens.shape[1]
    expert_count = lax.axis_size("expert")
    head_width = query_gain.shape[0]
    local_heads = query_w.shape[1] // head_width
    experts_local = gate_w.shape[0]
    experts_all = router_w.shape[1]
    top_count = routes.shape[1]
    hidden_width = gate_w.shape[2]
    factor = 1.0 / math.sqrt(head_width)
    cot_all = lax.all_gather(cotangent, "expert", axis=0, tiled=True)
    source = tokens.astype(jnp.float32)
    scale_in = inverse_rms(source)
    normed_low = (source * scale_in * norm_in).astype(jnp.bfloat16)
    gathered = lax.all_gather(normed_low, "tensor", axis=0, tiled=True)
    seq_len = gathered.shape[0]
    query_pre = jnp.dot(gathered, query_w, preferred_element_type=jnp.float32)
    key_pre = jnp.dot(gathered, key_w, preferred_element_type=jnp.float32)
    value_low = jnp.dot(gathered, value_w, preferred_element_type=jnp.float32).astype(jnp.bfloat16)
    cosine, sine_table = rotary_tables(seq_len, head_width)
    query_heads = query_pre.reshape(seq_len, local_heads, head_width)
    key_heads = key_pre.reshape(seq_len, local_heads, head_width)
    query_scale = inverse_rms(query_heads)
    key_scale = inverse_rms(key_heads)
    query_low = rotate(query_heads * query_scale * query_gain, cosine, sine_table).astype(
        jnp.bfloat16
    )
    key_low = rotate(key_heads * key_scale * key_gain, cosine, sine_table).astype(jnp.bfloat16)
    value_heads = value_low.reshape(seq_len, local_heads, head_width)
    block_rows = min(512, seq_len)
    block_count = seq_len // block_rows
    query_blocks = query_low.reshape(block_count, block_rows, local_heads, head_width)

    def attend(query_block):
        scores = (
            jnp.einsum("qhd,khd->hqk", query_block, key_low, preferred_element_type=jnp.float32)
            * factor
        )
        row_max = jnp.max(scores, axis=-1, keepdims=True)
        shifted = jnp.exp(scores - row_max)
        row_sum = jnp.sum(shifted, axis=-1, keepdims=True)
        probs_low = (shifted / row_sum).astype(jnp.bfloat16)
        mixture = jnp.einsum(
            "hqk,khd->qhd", probs_low, value_heads, preferred_element_type=jnp.float32
        )
        return (mixture.astype(jnp.bfloat16), (row_max + jnp.log(row_sum))[..., 0])

    attended_blocks, log_sums = lax.map(attend, query_blocks)
    attended = attended_blocks.reshape(seq_len, local_heads * head_width)
    attn_out = lax.psum_scatter(
        jnp.dot(attended, out_w, preferred_element_type=jnp.float32).astype(jnp.bfloat16),
        "tensor",
        scatter_dimension=0,
        tiled=True,
    ).astype(jnp.float32)
    middle = source + attn_out
    scale_mid = inverse_rms(middle)
    normed_mid = middle * scale_mid * norm_mid
    mid_low = normed_mid.astype(jnp.bfloat16)
    logits = jnp.dot(normed_mid, router_w, precision=highest, preferred_element_type=jnp.float32)
    route_mask = routes[:, :, None] == jnp.arange(experts_all, dtype=jnp.int32)[None, None, :]
    mask_float = route_mask.astype(jnp.float32)
    chosen = jnp.sum(mask_float * logits[:, None, :], axis=-1)
    gating = jax.nn.softmax(chosen, axis=-1)
    upstream = cotangent.astype(jnp.float32)
    gates = jnp.sum(mask_float * gating[:, :, None], axis=1)
    gates_high = gates.astype(jnp.bfloat16)
    gates_low = (gates - gates_high.astype(jnp.float32)).astype(jnp.bfloat16)
    spare = jnp.zeros((rows_own, 128 - 2 * experts_all), jnp.bfloat16)
    own_rows = jnp.concatenate([mid_low, gates_high, gates_low, spare], axis=1)
    blocks = (expert_count, rows_own, experts_local * hidden_width)
    raw_all = jnp.concatenate(
        [
            lax.dot_general(
                cot_all, down_w[e], contract_last, preferred_element_type=jnp.float32
            ).astype(jnp.bfloat16)
            for e in range(experts_local)
        ],
        axis=1,
    ).reshape(blocks)
    rows_all, hidden_all, gate_all, up_all, row_total = expert_pass(
        own_rows, raw_all, gate_w, up_w, experts_all, 1
    )
    expert_input_grad = row_total[:, :model_width]
    gate_grad_dense = (
        row_total[:, model_width : model_width + experts_all]
        + row_total[:, model_width + experts_all : model_width + 2 * experts_all]
    )
    gate_grad = jnp.sum(mask_float * gate_grad_dense[:, None, :], axis=-1)
    count = expert_count * rows_own
    inner_all = experts_local * hidden_width
    rows_all = rows_all.reshape(count, own_rows.shape[1])
    hidden_all = hidden_all.reshape(count, inner_all)
    gate_all = gate_all.reshape(count, inner_all)
    up_all = up_all.reshape(count, inner_all)
    y_part = jnp.dot(
        hidden_all, down_w.reshape(inner_all, model_width), preferred_element_type=jnp.float32
    ).astype(jnp.bfloat16)
    y_sum = lax.psum_scatter(y_part, "expert", scatter_dimension=0, tiled=True)
    output = (middle + y_sum.astype(jnp.float32)).astype(jnp.bfloat16)
    me = lax.axis_index("tensor")
    far = jnp.stack([me ^ 1, me ^ 3]).astype(jnp.int32)
    near = jnp.stack([me, me ^ 2]).astype(jnp.int32)
    gate_w_grad = exchange(
        input_weight_parts(far, rows_all, gate_all, model_width, experts_local),
        input_weight_parts(near, rows_all, gate_all, model_width, experts_local),
    )
    up_w_grad = exchange(
        input_weight_parts(far, rows_all, up_all, model_width, experts_local),
        input_weight_parts(near, rows_all, up_all, model_width, experts_local),
    )
    down_w_grad = exchange(
        output_weight_parts(far, hidden_all, cot_all, experts_local),
        output_weight_parts(near, hidden_all, cot_all, experts_local),
    )
    inner_gate = jnp.sum(gating * gate_grad, axis=-1, keepdims=True)
    chosen_grad = gating * (gate_grad - inner_gate)
    logit_grad = jnp.sum(chosen_grad[:, :, None] * mask_float, axis=1)
    router_part = lax.dot_general(
        normed_mid,
        logit_grad,
        contract_first,
        precision=highest,
        preferred_element_type=jnp.float32,
    )
    normed_mid_grad = expert_input_grad + lax.dot_general(
        logit_grad, router_w, contract_last, precision=highest, preferred_element_type=jnp.float32
    )
    norm_mid_part = jnp.sum(normed_mid_grad * middle * scale_mid, axis=0)
    middle_grad = upstream + norm_backward(normed_mid_grad, middle, scale_mid, norm_mid)
    branch_low = middle_grad.astype(jnp.bfloat16)
    branch_all = lax.all_gather(branch_low, "tensor", axis=0, tiled=True)
    attended_grad = lax.dot_general(
        branch_all, out_w, contract_last, preferred_element_type=jnp.float32
    ).astype(jnp.bfloat16)
    out_w_part = lax.dot_general(
        attended, branch_all, contract_first, preferred_element_type=jnp.float32
    )
    grad_blocks = attended_grad.reshape(block_count, block_rows, local_heads, head_width)

    def attend_back(carry, inputs):
        key_total, value_total = carry
        query_block, grad_block, log_block = inputs
        scores = (
            jnp.einsum("qhd,khd->hqk", query_block, key_low, preferred_element_type=jnp.float32)
            * factor
        )
        probs = jnp.exp(scores - log_block[:, :, None])
        probs_low = probs.astype(jnp.bfloat16)
        value_total = value_total + jnp.einsum(
            "hqk,qhd->khd", probs_low, grad_block, preferred_element_type=jnp.float32
        )
        prob_grad = jnp.einsum(
            "qhd,khd->hqk", grad_block, value_heads, preferred_element_type=jnp.float32
        )
        delta = jnp.sum(probs * prob_grad, axis=-1, keepdims=True)
        score_low = (probs * (prob_grad - delta)).astype(jnp.bfloat16)
        query_part = (
            jnp.einsum("hqk,khd->qhd", score_low, key_low, preferred_element_type=jnp.float32)
            * factor
        )
        key_total = (
            key_total
            + jnp.einsum("hqk,qhd->khd", score_low, query_block, preferred_element_type=jnp.float32)
            * factor
        )
        return ((key_total, value_total), query_part)

    zero_heads = jnp.zeros((seq_len, local_heads, head_width), jnp.float32)
    (key_grad, value_total), query_parts = lax.scan(
        attend_back, (zero_heads, zero_heads), (query_blocks, grad_blocks, log_sums)
    )
    query_grad = query_parts.reshape(seq_len, local_heads, head_width)
    value_grad_low = value_total.reshape(seq_len, local_heads * head_width).astype(jnp.bfloat16)
    query_rot_grad = rotate_back(query_grad, cosine, sine_table)
    key_rot_grad = rotate_back(key_grad, cosine, sine_table)
    query_gain_part = jnp.sum(query_rot_grad * query_heads * query_scale, axis=(0, 1))
    key_gain_part = jnp.sum(key_rot_grad * key_heads * key_scale, axis=(0, 1))
    query_pre_grad = (
        norm_backward(query_rot_grad, query_heads, query_scale, query_gain)
        .reshape(seq_len, local_heads * head_width)
        .astype(jnp.bfloat16)
    )
    key_pre_grad = (
        norm_backward(key_rot_grad, key_heads, key_scale, key_gain)
        .reshape(seq_len, local_heads * head_width)
        .astype(jnp.bfloat16)
    )
    query_w_part = lax.dot_general(
        gathered, query_pre_grad, contract_first, preferred_element_type=jnp.float32
    )
    key_w_part = lax.dot_general(
        gathered, key_pre_grad, contract_first, preferred_element_type=jnp.float32
    )
    value_w_part = lax.dot_general(
        gathered, value_grad_low, contract_first, preferred_element_type=jnp.float32
    )
    summed = lax.dot_general(
        query_pre_grad, query_w, contract_last, preferred_element_type=jnp.float32
    )
    summed = summed + lax.dot_general(
        key_pre_grad, key_w, contract_last, preferred_element_type=jnp.float32
    )
    rows_grad = lax.psum_scatter(
        (
            summed
            + lax.dot_general(
                value_grad_low, value_w, contract_last, preferred_element_type=jnp.float32
            )
        ).astype(jnp.bfloat16),
        "tensor",
        scatter_dimension=0,
        tiled=True,
    ).astype(jnp.float32)
    norm_in_part = jnp.sum(rows_grad * source * scale_in, axis=0)
    input_grad = middle_grad + norm_backward(rows_grad, source, scale_in, norm_in)
    out_w_grad = lax.psum_scatter(
        out_w_part.astype(jnp.bfloat16), "expert", scatter_dimension=1, tiled=True
    ).astype(jnp.float32)
    part_rows = model_width // expert_count
    local_width = local_heads * head_width
    weight_parts = jnp.concatenate(
        [p.astype(jnp.bfloat16) for p in (query_w_part, key_w_part, value_w_part)], axis=1
    ).reshape(expert_count, part_rows, 3 * local_width)
    weight_sums = scatter_parts(weight_parts, 2)
    query_w_grad = weight_sums[:, :local_width]
    key_w_grad = weight_sums[:, local_width : 2 * local_width]
    value_w_grad = weight_sums[:, 2 * local_width :]
    norm_mid_grad, router_w_grad = lax.psum((norm_mid_part, router_part), ("expert", "tensor"))
    small = jnp.concatenate(
        [
            norm_in_part,
            query_gain_part,
            key_gain_part,
            jnp.zeros((-(model_width + 2 * head_width) % 1024,), jnp.float32),
        ]
    ).reshape(-1, 128)
    sums = sum_everywhere(small, 3).reshape(-1)
    norm_in_grad = sums[:model_width]
    query_gain_grad = sums[model_width : model_width + head_width]
    key_gain_grad = sums[model_width + head_width : model_width + 2 * head_width]
    return (
        output,
        input_grad,
        norm_in_grad,
        query_w_grad,
        key_w_grad,
        value_w_grad,
        out_w_grad,
        query_gain_grad,
        key_gain_grad,
        norm_mid_grad,
        router_w_grad,
        gate_w_grad,
        up_w_grad,
        down_w_grad,
    )


def per_device_general(
    tokens,
    cotangent,
    routes,
    norm_in,
    query_w,
    key_w,
    value_w,
    out_w,
    query_gain,
    key_gain,
    norm_mid,
    router_w,
    gate_w,
    up_w,
    down_w,
):
    rows_own = tokens.shape[0]
    model_width = tokens.shape[1]
    tensor_count = lax.axis_size("tensor")
    expert_count = lax.axis_size("expert")
    head_width = query_gain.shape[0]
    local_heads = query_w.shape[1] // head_width
    experts_local = gate_w.shape[0]
    experts_all = router_w.shape[1]
    top_count = routes.shape[1]
    hidden_width = gate_w.shape[2]
    factor = 1.0 / math.sqrt(head_width)
    cot_all = lax.all_gather(cotangent, "expert", axis=0, tiled=True)
    source = tokens.astype(jnp.float32)
    scale_in = inverse_rms(source)
    normed_low = (source * scale_in * norm_in).astype(jnp.bfloat16)
    gathered = lax.all_gather(normed_low, "tensor", axis=0, tiled=True)
    seq_len = gathered.shape[0]
    query_pre = jnp.dot(gathered, query_w, preferred_element_type=jnp.float32)
    key_pre = jnp.dot(gathered, key_w, preferred_element_type=jnp.float32)
    value_low = jnp.dot(gathered, value_w, preferred_element_type=jnp.float32).astype(jnp.bfloat16)
    cosine, sine_table = rotary_tables(seq_len, head_width)
    query_heads = query_pre.reshape(seq_len, local_heads, head_width)
    key_heads = key_pre.reshape(seq_len, local_heads, head_width)
    query_scale = inverse_rms(query_heads)
    key_scale = inverse_rms(key_heads)
    query_low = rotate(query_heads * query_scale * query_gain, cosine, sine_table).astype(
        jnp.bfloat16
    )
    key_low = rotate(key_heads * key_scale * key_gain, cosine, sine_table).astype(jnp.bfloat16)
    value_heads = value_low.reshape(seq_len, local_heads, head_width)
    block_rows = min(512, seq_len)
    block_count = seq_len // block_rows
    query_blocks = query_low.reshape(block_count, block_rows, local_heads, head_width)

    def attend(query_block):
        scores = (
            jnp.einsum("qhd,khd->hqk", query_block, key_low, preferred_element_type=jnp.float32)
            * factor
        )
        row_max = jnp.max(scores, axis=-1, keepdims=True)
        shifted = jnp.exp(scores - row_max)
        row_sum = jnp.sum(shifted, axis=-1, keepdims=True)
        probs_low = (shifted / row_sum).astype(jnp.bfloat16)
        mixture = jnp.einsum(
            "hqk,khd->qhd", probs_low, value_heads, preferred_element_type=jnp.float32
        )
        return (mixture.astype(jnp.bfloat16), (row_max + jnp.log(row_sum))[..., 0])

    attended_blocks, log_sums = lax.map(attend, query_blocks)
    attended = attended_blocks.reshape(seq_len, local_heads * head_width)
    attn_out = lax.psum_scatter(
        jnp.dot(attended, out_w, preferred_element_type=jnp.float32).astype(jnp.bfloat16),
        "tensor",
        scatter_dimension=0,
        tiled=True,
    ).astype(jnp.float32)
    middle = source + attn_out
    scale_mid = inverse_rms(middle)
    normed_mid = middle * scale_mid * norm_mid
    mid_low = normed_mid.astype(jnp.bfloat16)
    logits = jnp.dot(normed_mid, router_w, precision=highest, preferred_element_type=jnp.float32)
    route_mask = routes[:, :, None] == jnp.arange(experts_all, dtype=jnp.int32)[None, None, :]
    mask_float = route_mask.astype(jnp.float32)
    chosen = jnp.sum(mask_float * logits[:, None, :], axis=-1)
    gating = jax.nn.softmax(chosen, axis=-1)
    upstream = cotangent.astype(jnp.float32)
    gates = jnp.sum(mask_float * gating[:, :, None], axis=1)
    x_all = lax.all_gather(mid_low, "expert", axis=0, tiled=True)
    gates_all = lax.all_gather(gates, "expert", axis=0, tiled=True)
    first_expert = lax.axis_index("expert") * experts_local
    own_gates = lax.dynamic_slice_in_dim(gates_all, first_expert, experts_local, 1)
    part_width = hidden_width // tensor_count
    rows_all = x_all.shape[0]
    y_part = jnp.zeros((rows_all, model_width), jnp.float32)
    x_grad_part = jnp.zeros((rows_all, model_width), jnp.float32)
    gate_grads, gate_parts, up_parts, down_parts = [], [], [], []
    for e in range(experts_local):
        hidden_raw = lax.dot_general(
            cot_all, down_w[e], contract_last, preferred_element_type=jnp.float32
        )
        gate_pre = jnp.dot(x_all, gate_w[e], preferred_element_type=jnp.float32)
        up_pre = jnp.dot(x_all, up_w[e], preferred_element_type=jnp.float32)
        weight = own_gates[:, e : e + 1]
        hidden = gate_pre * jax.nn.sigmoid(gate_pre) * up_pre
        gate_grads.append(jnp.sum(hidden * hidden_raw, axis=1))
        hidden_low = (hidden * weight).astype(jnp.bfloat16)
        gate_back, up_back = swiglu_back(hidden_raw * weight, gate_pre, up_pre)
        y_part = y_part + jnp.dot(hidden_low, down_w[e], preferred_element_type=jnp.float32)
        x_grad_part = x_grad_part + lax.dot_general(
            gate_back, gate_w[e], contract_last, preferred_element_type=jnp.float32
        )
        x_grad_part = x_grad_part + lax.dot_general(
            up_back, up_w[e], contract_last, preferred_element_type=jnp.float32
        )
        gate_parts.append(
            jnp.einsum(
                "nd,ntf->tdf",
                x_all,
                gate_back.reshape(rows_all, tensor_count, part_width),
                preferred_element_type=jnp.float32,
            ).astype(jnp.bfloat16)
        )
        up_parts.append(
            jnp.einsum(
                "nd,ntf->tdf",
                x_all,
                up_back.reshape(rows_all, tensor_count, part_width),
                preferred_element_type=jnp.float32,
            ).astype(jnp.bfloat16)
        )
        down_parts.append(
            lax.dot_general(
                hidden_low, cot_all, contract_first, preferred_element_type=jnp.float32
            ).astype(jnp.bfloat16)
        )
    x_grad = lax.psum_scatter(
        x_grad_part.astype(jnp.bfloat16), "expert", scatter_dimension=0, tiled=True
    )
    expert_input_grad = x_grad.astype(jnp.float32)
    gate_grad_sent = jnp.stack(gate_grads, axis=-1)
    gate_grad_all = lax.all_to_all(gate_grad_sent, "expert", split_axis=0, concat_axis=0, tiled=True)
    gate_grad_dense = (
        gate_grad_all.reshape(expert_count, rows_own, experts_local)
        .transpose(1, 0, 2)
        .reshape(rows_own, experts_all)
    )
    gate_grad = jnp.sum(mask_float * gate_grad_dense[:, None, :], axis=-1)
    y_sum = lax.psum_scatter(
        y_part.astype(jnp.bfloat16), "expert", scatter_dimension=0, tiled=True
    )
    output = (middle + y_sum.astype(jnp.float32)).astype(jnp.bfloat16)

    def own_part(parts):
        return [
            lax.psum_scatter(p, "tensor", scatter_dimension=0, tiled=True).astype(jnp.float32)
            for p in parts
        ]

    gate_w_grad = jnp.concatenate(own_part(gate_parts), axis=0)
    up_w_grad = jnp.concatenate(own_part(up_parts), axis=0)
    down_w_grad = jnp.stack(own_part(down_parts), axis=0)
    inner_gate = jnp.sum(gating * gate_grad, axis=-1, keepdims=True)
    chosen_grad = gating * (gate_grad - inner_gate)
    logit_grad = jnp.sum(chosen_grad[:, :, None] * mask_float, axis=1)
    router_part = lax.dot_general(
        normed_mid,
        logit_grad,
        contract_first,
        precision=highest,
        preferred_element_type=jnp.float32,
    )
    normed_mid_grad = expert_input_grad + lax.dot_general(
        logit_grad, router_w, contract_last, precision=highest, preferred_element_type=jnp.float32
    )
    norm_mid_part = jnp.sum(normed_mid_grad * middle * scale_mid, axis=0)
    middle_grad = upstream + norm_backward(normed_mid_grad, middle, scale_mid, norm_mid)
    branch_low = middle_grad.astype(jnp.bfloat16)
    branch_all = lax.all_gather(branch_low, "tensor", axis=0, tiled=True)
    attended_grad = lax.dot_general(
        branch_all, out_w, contract_last, preferred_element_type=jnp.float32
    ).astype(jnp.bfloat16)
    out_w_part = lax.dot_general(
        attended, branch_all, contract_first, preferred_element_type=jnp.float32
    )
    grad_blocks = attended_grad.reshape(block_count, block_rows, local_heads, head_width)

    def attend_back(carry, inputs):
        key_total, value_total = carry
        query_block, grad_block, log_block = inputs
        scores = (
            jnp.einsum("qhd,khd->hqk", query_block, key_low, preferred_element_type=jnp.float32)
            * factor
        )
        probs = jnp.exp(scores - log_block[:, :, None])
        probs_low = probs.astype(jnp.bfloat16)
        value_total = value_total + jnp.einsum(
            "hqk,qhd->khd", probs_low, grad_block, preferred_element_type=jnp.float32
        )
        prob_grad = jnp.einsum(
            "qhd,khd->hqk", grad_block, value_heads, preferred_element_type=jnp.float32
        )
        delta = jnp.sum(probs * prob_grad, axis=-1, keepdims=True)
        score_low = (probs * (prob_grad - delta)).astype(jnp.bfloat16)
        query_part = (
            jnp.einsum("hqk,khd->qhd", score_low, key_low, preferred_element_type=jnp.float32)
            * factor
        )
        key_total = (
            key_total
            + jnp.einsum("hqk,qhd->khd", score_low, query_block, preferred_element_type=jnp.float32)
            * factor
        )
        return ((key_total, value_total), query_part)

    zero_heads = jnp.zeros((seq_len, local_heads, head_width), jnp.float32)
    (key_grad, value_total), query_parts = lax.scan(
        attend_back, (zero_heads, zero_heads), (query_blocks, grad_blocks, log_sums)
    )
    query_grad = query_parts.reshape(seq_len, local_heads, head_width)
    value_grad_low = value_total.reshape(seq_len, local_heads * head_width).astype(jnp.bfloat16)
    query_rot_grad = rotate_back(query_grad, cosine, sine_table)
    key_rot_grad = rotate_back(key_grad, cosine, sine_table)
    query_gain_part = jnp.sum(query_rot_grad * query_heads * query_scale, axis=(0, 1))
    key_gain_part = jnp.sum(key_rot_grad * key_heads * key_scale, axis=(0, 1))
    query_pre_grad = (
        norm_backward(query_rot_grad, query_heads, query_scale, query_gain)
        .reshape(seq_len, local_heads * head_width)
        .astype(jnp.bfloat16)
    )
    key_pre_grad = (
        norm_backward(key_rot_grad, key_heads, key_scale, key_gain)
        .reshape(seq_len, local_heads * head_width)
        .astype(jnp.bfloat16)
    )
    query_w_part = lax.dot_general(
        gathered, query_pre_grad, contract_first, preferred_element_type=jnp.float32
    )
    key_w_part = lax.dot_general(
        gathered, key_pre_grad, contract_first, preferred_element_type=jnp.float32
    )
    value_w_part = lax.dot_general(
        gathered, value_grad_low, contract_first, preferred_element_type=jnp.float32
    )
    summed = lax.dot_general(
        query_pre_grad, query_w, contract_last, preferred_element_type=jnp.float32
    )
    summed = summed + lax.dot_general(
        key_pre_grad, key_w, contract_last, preferred_element_type=jnp.float32
    )
    rows_grad = lax.psum_scatter(
        (
            summed
            + lax.dot_general(
                value_grad_low, value_w, contract_last, preferred_element_type=jnp.float32
            )
        ).astype(jnp.bfloat16),
        "tensor",
        scatter_dimension=0,
        tiled=True,
    ).astype(jnp.float32)
    norm_in_part = jnp.sum(rows_grad * source * scale_in, axis=0)
    input_grad = middle_grad + norm_backward(rows_grad, source, scale_in, norm_in)
    query_w_grad, key_w_grad, value_w_grad, out_w_grad = (
        lax.psum_scatter(
            query_w_part.astype(jnp.bfloat16), "expert", scatter_dimension=0, tiled=True
        ).astype(jnp.float32),
        lax.psum_scatter(
            key_w_part.astype(jnp.bfloat16), "expert", scatter_dimension=0, tiled=True
        ).astype(jnp.float32),
        lax.psum_scatter(
            value_w_part.astype(jnp.bfloat16), "expert", scatter_dimension=0, tiled=True
        ).astype(jnp.float32),
        lax.psum_scatter(
            out_w_part.astype(jnp.bfloat16), "expert", scatter_dimension=1, tiled=True
        ).astype(jnp.float32),
    )
    norm_in_grad, query_gain_grad, key_gain_grad, norm_mid_grad, router_w_grad = lax.psum(
        (norm_in_part, query_gain_part, key_gain_part, norm_mid_part, router_part),
        ("expert", "tensor"),
    )
    return (
        output,
        input_grad,
        norm_in_grad,
        query_w_grad,
        key_w_grad,
        value_w_grad,
        out_w_grad,
        query_gain_grad,
        key_gain_grad,
        norm_mid_grad,
        router_w_grad,
        gate_w_grad,
        up_w_grad,
        down_w_grad,
    )


def solution(mesh):
    placed = (
        P(("expert", "tensor"), None),
        P(("expert", "tensor"), None),
        P(("expert", "tensor"), None),
        P(),
        P(None, "tensor"),
        P(None, "tensor"),
        P(None, "tensor"),
        P("tensor", None),
        P(),
        P(),
        P(),
        P(),
        P("expert", None, None),
        P("expert", None, None),
        P("expert", None, None),
    )
    return jax.shard_map(
        per_device if dict(mesh.shape) == {"expert": 8, "tensor": 4} else per_device_general,
        mesh=mesh,
        in_specs=placed,
        out_specs=(
            P(("expert", "tensor"), None),
            P(("expert", "tensor"), None),
            P(),
            P("expert", "tensor"),
            P("expert", "tensor"),
            P("expert", "tensor"),
            P("tensor", "expert"),
            P(),
            P(),
            P(),
            P(),
            P("expert", None, "tensor"),
            P("expert", None, "tensor"),
            P("expert", "tensor", None),
        ),
        check_vma=False,
    )
```

```python
import functools
import math

import jax
import jax.numpy as jnp
from jax import lax
from jax.experimental import pallas as pl
from jax.experimental.pallas import tpu as pltpu
from jax.sharding import PartitionSpec as P

epsilon = 1e-06
highest = lax.Precision.HIGHEST
contract_last = (((1,), (1,)), ((), ()))
contract_first = (((0,), (0,)), ((), ()))


def inverse_rms(values):
    return lax.rsqrt(jnp.mean(values * values, axis=-1, keepdims=True) + epsilon)


def norm_backward(grad_norm, values, inverse, norm_gain):
    weighted = grad_norm * norm_gain
    inner_mean = jnp.mean(weighted * values, axis=-1, keepdims=True)
    return inverse * weighted - values * inverse * inverse * inverse * inner_mean


def rotary_tables(length, head_width):
    half_dim = head_width // 2
    frequency = jnp.exp(
        -math.log(10000.0) * 2.0 * jnp.arange(half_dim, dtype=jnp.float32) / head_width
    )
    angles = jnp.arange(length, dtype=jnp.float32)[:, None] * frequency[None, :]
    return (jnp.cos(angles)[:, None, :], jnp.sin(angles)[:, None, :])


def rotate(values, cosine, sine_table):
    half_dim = values.shape[-1] // 2
    first_half = values[..., :half_dim]
    second_half = values[..., half_dim:]
    return jnp.concatenate(
        [
            first_half * cosine - second_half * sine_table,
            second_half * cosine + first_half * sine_table,
        ],
        axis=-1,
    )


def rotate_back(gradient, cosine, sine_table):
    half_dim = gradient.shape[-1] // 2
    first_half = gradient[..., :half_dim]
    second_half = gradient[..., half_dim:]
    return jnp.concatenate(
        [
            first_half * cosine + second_half * sine_table,
            second_half * cosine - first_half * sine_table,
        ],
        axis=-1,
    )


def swiglu_back(hidden_grad, gate_pre, up_pre):
    sigmoid_part = jax.nn.sigmoid(gate_pre)
    gate_back = (
        hidden_grad * up_pre * sigmoid_part * (1.0 + gate_pre * (1.0 - sigmoid_part))
    ).astype(jnp.bfloat16)
    up_back = (hidden_grad * gate_pre * sigmoid_part).astype(jnp.bfloat16)
    return (gate_back, up_back)


chunks = 4


def pick(index, values):
    result = values[-1]
    for j in reversed(range(len(values) - 1)):
        result = jnp.where(index == j, values[j], result)
    return result


def expert_kernel(
    experts_all,
    own_rows,
    cot_all,
    gate_hbm,
    up_hbm,
    down_hbm,
    rows_all,
    hidden_all,
    gate_all,
    up_all,
    y_all,
    total,
    gate_v,
    up_v,
    down_v,
    rows_v,
    cot_v,
    hidden_v,
    gate_b,
    up_b,
    y_v,
    stage,
    parts,
    side_in,
    line_in,
    weight_sem,
    own_sem,
    cot_sem,
    out_sem,
    rows_sem,
    gather_recv,
    gather_send,
    side_recv,
    side_send,
    line_recv,
    line_send,
):
    position = lax.axis_index("expert")
    peer = lax.axis_index("tensor")
    z = position // 2
    x = position % 2
    experts_local, width, hidden = gate_v.shape
    rows = rows_v.shape[1]
    chunk = rows // chunks
    middle = (z == 1) | (z == 2)
    ends = (z == 0) | (z == 3)
    line_slots = [
        z,
        pick(z, [1, 0, 3, 2]),
        pick(z, [2, 2, 1, 1]),
        pick(z, [3, 3, 0, 0]),
    ]

    def device(zz, xx):
        return (zz * 2 + xx, peer)

    def slot_z(k):
        return pick(k, line_slots)

    weight_copies = [
        pltpu.make_async_copy(gate_hbm, gate_v, weight_sem.at[0]),
        pltpu.make_async_copy(up_hbm, up_v, weight_sem.at[1]),
        pltpu.make_async_copy(down_hbm, down_v, weight_sem.at[2]),
    ]
    own_copy = pltpu.make_async_copy(own_rows, rows_v.at[position], own_sem)
    own_copy.start()
    for copy in weight_copies:
        copy.start()

    barrier = pltpu.get_barrier_semaphore()
    pl.semaphore_signal(barrier, inc=1, device_id=device(z, 1 - x), device_id_type=pl.DeviceIdType.MESH)

    @pl.when(z < 3)
    def _():
        pl.semaphore_signal(barrier, inc=1, device_id=device(z + 1, x), device_id_type=pl.DeviceIdType.MESH)

    @pl.when(z > 0)
    def _():
        pl.semaphore_signal(barrier, inc=1, device_id=device(z - 1, x), device_id_type=pl.DeviceIdType.MESH)

    pl.semaphore_wait(barrier, 2 + middle.astype(jnp.int32))

    def gather_copy(source, block, index, zz, xx):
        return pltpu.make_async_remote_copy(
            src_ref=source,
            dst_ref=rows_v.at[block],
            send_sem=gather_send.at[index],
            recv_sem=gather_recv.at[block],
            device_id=device(zz, xx),
            device_id_type=pl.DeviceIdType.MESH,
        )

    def own_send(index, zz, xx):
        return gather_copy(own_rows, position, index, zz, xx)

    own_send(0, z, 1 - x).start()

    @pl.when(z < 3)
    def _():
        own_send(1, z + 1, x).start()

    @pl.when(z > 0)
    def _():
        own_send(2, z - 1, x).start()

    def forward_side(k):
        block = slot_z(k) * 2 + x
        return gather_copy(rows_v.at[block], block, 2 + k, z, 1 - x)

    def forward_line(k):
        block = slot_z(k) * 2 + x
        target = jnp.where(slot_z(k) < z, z + 1, z - 1)
        return gather_copy(rows_v.at[block], block, 5 + k, jnp.clip(target, 0, 3), x)

    def arrived(block):
        gather_copy(own_rows, block, 0, z, 1 - x).wait_recv()
        pltpu.make_async_copy(rows_v.at[block], rows_all.at[block], rows_sem.at[block]).start()

    def arrive(k):
        arrived(slot_z(k) * 2 + x)
        forward_side(k).start()

        @pl.when(middle)
        def _():
            forward_line(k).start()

    def side_copy(k, c):
        area = pl.ds(c * chunk, chunk)
        return pltpu.make_async_remote_copy(
            src_ref=parts.at[4 + k, area],
            dst_ref=side_in.at[k, area],
            send_sem=side_send.at[k, c],
            recv_sem=side_recv.at[k, c],
            device_id=device(z, 1 - x),
            device_id_type=pl.DeviceIdType.MESH,
        )

    def line_slot(k):
        target = slot_z(k)
        return jnp.where(target < z, target, target + 1)

    def line_copy(k, c):
        area = pl.ds(c * chunk, chunk)
        target = jnp.where(slot_z(k) < z, z - 1, z + 1)
        return pltpu.make_async_remote_copy(
            src_ref=parts.at[k, area],
            dst_ref=line_in.at[line_slot(k), area],
            send_sem=line_send.at[k - 1, c],
            recv_sem=line_recv.at[line_slot(k), c],
            device_id=device(jnp.clip(target, 0, 3), x),
            device_id_type=pl.DeviceIdType.MESH,
        )

    def line_wait(slot, c):
        area = pl.ds(c * chunk, chunk)
        pltpu.make_async_remote_copy(
            src_ref=parts.at[0, area],
            dst_ref=line_in.at[slot, area],
            send_sem=line_send.at[0, c],
            recv_sem=line_recv.at[slot, c],
            device_id=device(z, 1 - x),
            device_id_type=pl.DeviceIdType.MESH,
        ).wait_recv()

    def relay(k, c, has_line):
        area = pl.ds(c * chunk, chunk)
        side_copy(k, c).wait_recv()
        summed = parts[k, area].astype(jnp.float32) + side_in[k, area].astype(jnp.float32)
        if has_line is False:
            parts[k, area] = summed.astype(jnp.bfloat16)
        else:

            @pl.when(middle)
            def _():
                line_wait(line_slot(k), c)
                parts[k, area] = (
                    summed + line_in[line_slot(k), area].astype(jnp.float32)
                ).astype(jnp.bfloat16)

            if has_line is None:

                @pl.when(ends)
                def _():
                    parts[k, area] = summed.astype(jnp.bfloat16)

        line_copy(k, c).start()

    def block_of(step):
        k = pick(step, [0, 1, 0, 2, 1, 3, 2, 3])
        side = pick(step, [0, 0, 1, 0, 1, 0, 1, 1])
        return k, side, slot_z(k) * 2 + jnp.where(side == 1, 1 - x, x)

    def cot_copy(step):
        return pltpu.make_async_copy(cot_all.at[block_of(step)[2]], cot_v, cot_sem)

    def y_copy(block):
        return pltpu.make_async_copy(y_v, y_all.at[block], out_sem.at[3])

    def out_copies(block):
        return [
            pltpu.make_async_copy(hidden_v, hidden_all.at[block], out_sem.at[0]),
            pltpu.make_async_copy(gate_b, gate_all.at[block], out_sem.at[1]),
            pltpu.make_async_copy(up_b, up_all.at[block], out_sem.at[2]),
        ]

    cot_copy(0).start()
    own_copy.wait()
    pltpu.make_async_copy(rows_v.at[position], rows_all.at[position], rows_sem.at[position]).start()
    for copy in weight_copies:
        copy.wait()

    def one_step(step, carry):
        k, side, block = block_of(step)

        @pl.when(step == 1)
        def _():
            arrive(1)

            @pl.when(middle)
            def _():
                arrive(2)

        @pl.when(step == 3)
        def _():
            @pl.when(ends)
            def _():
                arrive(2)

            @pl.when(middle)
            def _():
                arrive(3)

        @pl.when((step == 5) & ends)
        def _():
            arrive(3)

        @pl.when(side == 1)
        def _():
            arrived(block)

        @pl.when((step == 7) & ends)
        def _():
            def one(c, carry):
                relay(1, c, False)
                return carry

            lax.fori_loop(0, chunks, one, 0)

        @pl.when(step > 0)
        def _():
            for copy in out_copies(block):
                copy.wait()

        cot_copy(step).wait()
        rows_low = rows_v[block, :, :width]
        extra = rows_v[block, :, width:].astype(jnp.float32)
        lane = lax.broadcasted_iota(jnp.int32, extra.shape, 1)
        ext = jnp.zeros(extra.shape, jnp.float32)
        for e in range(experts_local):
            expert = position * experts_local + e
            high = lane == expert
            low = lane == expert + experts_all
            weight = jnp.sum(jnp.where(high | low, extra, 0.0), axis=1, keepdims=True)
            gate_grad = jnp.zeros((rows, 1), jnp.float32)
            for f in range(hidden // 512):
                columns = pl.ds(f * 512, 512)
                gate_pre = jnp.dot(rows_low, gate_v[e, :, columns], preferred_element_type=jnp.float32)
                up_pre = jnp.dot(rows_low, up_v[e, :, columns], preferred_element_type=jnp.float32)
                target = pl.ds(e * hidden + f * 512, 512)
                raw = lax.dot_general(
                    cot_v[...],
                    down_v[e, columns, :],
                    contract_last,
                    preferred_element_type=jnp.float32,
                )
                sig = jax.nn.sigmoid(gate_pre)
                act = gate_pre * sig
                hid = act * up_pre
                gate_grad = gate_grad + jnp.sum(hid * raw, axis=1, keepdims=True)
                hidden_v[:, target] = (hid * weight).astype(jnp.bfloat16)
                grad = raw * weight
                gate_b[:, target] = (grad * up_pre * sig * (1.0 + gate_pre * (1.0 - sig))).astype(jnp.bfloat16)
                up_b[:, target] = (grad * act).astype(jnp.bfloat16)
            grad_high = gate_grad.astype(jnp.bfloat16).astype(jnp.float32)
            ext = jnp.where(high, grad_high, ext)
            ext = jnp.where(low, gate_grad - grad_high, ext)

        @pl.when(step < 7)
        def _():
            cot_copy(step + 1).start()

        place = side * 4 + k
        parts[place, :, width:] = ext.astype(jnp.bfloat16)
        for copy in out_copies(block):
            copy.start()
        for d in range(width // 1024):
            span = pl.ds(d * 1024, 1024)
            summed = jnp.zeros((rows, 1024), jnp.float32)
            for e in range(experts_local):
                target = pl.ds(e * hidden, hidden)
                summed = summed + lax.dot_general(
                    gate_b[:, target], gate_v[e, span, :], contract_last, preferred_element_type=jnp.float32
                )
                summed = summed + lax.dot_general(
                    up_b[:, target], up_v[e, span, :], contract_last, preferred_element_type=jnp.float32
                )
            parts[place, :, span] = summed.astype(jnp.bfloat16)

        @pl.when(side == 1)
        def _():
            for c in range(chunks):
                side_copy(k, c).start()

        @pl.when(step > 0)
        def _():
            y_copy(block).wait()

        for d in range(width // 1024):
            span = pl.ds(d * 1024, 1024)
            summed = jnp.zeros((rows, 1024), jnp.float32)
            for e in range(experts_local):
                summed = summed + jnp.dot(
                    hidden_v[:, pl.ds(e * hidden, hidden)],
                    down_v[e, :, span],
                    preferred_element_type=jnp.float32,
                )
            y_v[:, span] = summed.astype(jnp.bfloat16)
        y_copy(block).start()
        return carry

    lax.fori_loop(0, 8, one_step, 0)

    def relay_two(c, carry):
        relay(2, c, None)
        return carry

    lax.fori_loop(0, chunks, relay_two, 0)

    def relay_rest(c, carry):
        relay(3, c, None)

        @pl.when(middle)
        def _():
            relay(1, c, True)

        return carry

    lax.fori_loop(0, chunks, relay_rest, 0)

    def finish(c, carry):
        area = pl.ds(c * chunk, chunk)
        side_copy(0, c).wait_recv()
        stage[...] = parts[0, area].astype(jnp.float32) + side_in[0, area].astype(jnp.float32)

        @pl.when(z < 3)
        def _():
            line_wait(z, c)
            stage[...] += line_in[z, area].astype(jnp.float32)

        @pl.when(z > 0)
        def _():
            line_wait(z + 1, c)
            stage[...] += line_in[z + 1, area].astype(jnp.float32)

        result = pltpu.make_async_copy(stage, total.at[area], own_sem)
        result.start()
        result.wait()
        for k in range(4):
            side_copy(k, c).wait_send()
        for k in range(1, 4):
            line_copy(k, c).wait_send()
        return carry

    lax.fori_loop(0, chunks, finish, 0)

    own_send(0, z, 1 - x).wait_send()

    @pl.when(z < 3)
    def _():
        own_send(1, z + 1, x).wait_send()

    @pl.when(z > 0)
    def _():
        own_send(2, z - 1, x).wait_send()

    for k in range(1, 4):
        forward_side(k).wait_send()

        @pl.when(middle)
        def _(k=k):
            forward_line(k).wait_send()

    for copy in out_copies(position):
        copy.wait()
    y_copy(position).wait()
    for block in range(8):
        pltpu.make_async_copy(rows_v.at[block], rows_all.at[block], rows_sem.at[block]).wait()


def expert_pass(own_rows, cot_all, gate_w, up_w, down_w, experts_all, collective):
    rows, wide = own_rows.shape
    experts_local, width, hidden = gate_w.shape
    inner = experts_local * hidden
    any_space = pl.BlockSpec(memory_space=pl.ANY)
    low = jnp.bfloat16
    dma = pltpu.SemaphoreType.DMA
    return pl.pallas_call(
        functools.partial(expert_kernel, experts_all),
        name="expert_pass",
        out_shape=(
            jax.ShapeDtypeStruct((8, rows, wide), low),
            jax.ShapeDtypeStruct((8, rows, inner), low),
            jax.ShapeDtypeStruct((8, rows, inner), low),
            jax.ShapeDtypeStruct((8, rows, inner), low),
            jax.ShapeDtypeStruct((8, rows, width), low),
            jax.ShapeDtypeStruct((rows, wide), jnp.float32),
        ),
        in_specs=[any_space] * 5,
        out_specs=(any_space,) * 6,
        scratch_shapes=[
            pltpu.VMEM((experts_local, width, hidden), low),
            pltpu.VMEM((experts_local, width, hidden), low),
            pltpu.VMEM((experts_local, hidden, width), low),
            pltpu.VMEM((8, rows, wide), low),
            pltpu.VMEM((rows, width), low),
            pltpu.VMEM((rows, inner), low),
            pltpu.VMEM((rows, inner), low),
            pltpu.VMEM((rows, inner), low),
            pltpu.VMEM((rows, width), low),
            pltpu.VMEM((rows // chunks, wide), jnp.float32),
            pltpu.VMEM((8, rows, wide), low),
            pltpu.VMEM((4, rows, wide), low),
            pltpu.VMEM((5, rows, wide), low),
            dma((3,)),
            dma,
            dma,
            dma((4,)),
            dma((8,)),
            dma((8,)),
            dma((9,)),
            dma((4, chunks)),
            dma((4, chunks)),
            dma((5, chunks)),
            dma((3, chunks)),
        ],
        compiler_params=pltpu.CompilerParams(
            collective_id=collective, has_side_effects=True, vmem_limit_bytes=60 << 20
        ),
        cost_estimate=pl.CostEstimate(
            flops=2 * 6 * 8 * rows * width * inner, bytes_accessed=64 << 20, transcendentals=8 * rows * inner
        ),
    )(own_rows, cot_all, gate_w, up_w, down_w)


def line_gather(source, target, recv, send):
    position = lax.axis_index("expert")
    peer = lax.axis_index("tensor")
    z = position // 2
    x = position % 2
    middle = (z == 1) | (z == 2)
    slots = [z, pick(z, [1, 0, 3, 2]), pick(z, [2, 2, 1, 1]), pick(z, [3, 3, 0, 0])]

    def copy(block_source, block, index, zz, xx):
        return pltpu.make_async_remote_copy(
            src_ref=block_source,
            dst_ref=target.at[block],
            send_sem=send.at[index],
            recv_sem=recv.at[block],
            device_id=(zz * 2 + xx, peer),
            device_id_type=pl.DeviceIdType.MESH,
        )

    def own_up():
        return copy(source, position, 1, z + 1, x)

    def own_down():
        return copy(source, position, 2, z - 1, x)

    def own_side():
        return copy(source, position, 0, z, 1 - x)

    def side(k):
        block = slots[k] * 2 + x
        return copy(target.at[block], block, 2 + k, z, 1 - x)

    def line(k):
        block = slots[k] * 2 + x
        onward = jnp.where(slots[k] < z, z + 1, z - 1)
        return copy(target.at[block], block, 5 + k, jnp.clip(onward, 0, 3), x)

    def start():
        own_side().start()

        @pl.when(z < 3)
        def _():
            own_up().start()

        @pl.when(z > 0)
        def _():
            own_down().start()

    def wait_block(block):
        copy(source, block, 0, z, 1 - x).wait_recv()

    def arrive(k):
        wait_block(slots[k] * 2 + x)
        side(k).start()

        @pl.when(middle)
        def _():
            line(k).start()

    def arrive_side(k):
        wait_block(slots[k] * 2 + 1 - x)

    def drain():
        own_side().wait_send()

        @pl.when(z < 3)
        def _():
            own_up().wait_send()

        @pl.when(z > 0)
        def _():
            own_down().wait_send()

        for k in range(1, 4):
            side(k).wait_send()

            @pl.when(middle)
            def _(k=k):
                line(k).wait_send()

    return middle, start, arrive, arrive_side, drain


def attention_kernel(
    own,
    cot,
    query_w,
    key_w,
    value_w,
    out_w,
    query_gain,
    key_gain,
    cosine,
    sine,
    gathered,
    query_pre,
    key_pre,
    query_low,
    key_low,
    value_low,
    attended,
    log_sums,
    attn_sum,
    cot_all,
    rows_v,
    weights_v,
    out_v,
    pre_v,
    low_v,
    mixed_v,
    log_v,
    parts,
    own_part,
    core_in,
    line_in,
    load_sem,
    store_sem,
    rows_recv,
    rows_send,
    part_recv,
    part_send,
    cot_recv,
    cot_send,
    cot_sem,
):
    position = lax.axis_index("expert")
    t = lax.axis_index("tensor")
    z = position // 2
    x = position % 2
    y = t // 2
    c = t % 2
    near = y * 2 + 1 - c
    across = (1 - y) * 2 + c
    opposite = (1 - y) * 2 + 1 - c
    rows = own.shape[0]
    heads = low_v.shape[2] // 128
    factor = 1.0 / math.sqrt(128.0)
    mesh_ids = pl.DeviceIdType.MESH
    middle, gather_start, gather_arrive, gather_side, gather_drain = line_gather(
        cot, cot_all, cot_recv, cot_send
    )

    loads = [
        pltpu.make_async_copy(own, rows_v.at[t], load_sem.at[0]),
        pltpu.make_async_copy(query_w, weights_v.at[0], load_sem.at[1]),
        pltpu.make_async_copy(key_w, weights_v.at[1], load_sem.at[2]),
        pltpu.make_async_copy(value_w, weights_v.at[2], load_sem.at[3]),
        pltpu.make_async_copy(out_w, out_v, load_sem.at[4]),
    ]
    for load in loads:
        load.start()
    cot_copy = pltpu.make_async_copy(cot, cot_all.at[position], cot_sem)
    cot_copy.start()

    barrier = pltpu.get_barrier_semaphore()
    for place in ((position, near), (position, across), (z * 2 + 1 - x, t)):
        pl.semaphore_signal(barrier, inc=1, device_id=place, device_id_type=mesh_ids)

    @pl.when(z < 3)
    def _():
        pl.semaphore_signal(barrier, inc=1, device_id=(position + 2, t), device_id_type=mesh_ids)

    @pl.when(z > 0)
    def _():
        pl.semaphore_signal(barrier, inc=1, device_id=(position - 2, t), device_id_type=mesh_ids)

    pl.semaphore_wait(barrier, 4 + middle.astype(jnp.int32))

    def rows_copy(source, block, index, to):
        return pltpu.make_async_remote_copy(
            src_ref=source,
            dst_ref=rows_v.at[block],
            send_sem=rows_send.at[index - 1],
            recv_sem=rows_recv.at[index - 1],
            device_id=(position, to),
            device_id_type=mesh_ids,
        )

    to_across = rows_copy(own, t, 2, across)
    to_near = rows_copy(own, t, 1, near)
    forward = rows_copy(rows_v.at[across], across, 3, near)
    to_across.start()
    to_near.start()
    gather_start()
    for load in loads:
        load.wait()

    def project(i, carry):
        block = pick(i, [t, near, across, opposite])

        @pl.when(i == 1)
        def _():
            to_near.wait_recv()

        @pl.when(i == 2)
        def _():
            to_across.wait_recv()
            forward.start()
            gather_arrive(1)

            @pl.when(middle)
            def _():
                gather_arrive(2)

        @pl.when(i == 3)
        def _():
            forward.wait_recv()

        area = pl.ds(block * rows, rows)
        values = rows_v[block]
        for which, gain in ((0, query_gain), (1, key_gain)):
            pre = jnp.dot(values, weights_v[which], preferred_element_type=jnp.float32)
            pre_v[which, area] = pre
            for h in range(heads):
                span = slice(h * 128, (h + 1) * 128)
                head = pre[:, span]
                scale = lax.rsqrt(jnp.mean(head * head, axis=-1, keepdims=True) + epsilon)
                normed = head * scale * gain[...]
                turned = normed * cosine[area] + pltpu.roll(normed, 64, 1) * sine[area]
                low_v[which, area, span] = turned.astype(jnp.bfloat16)
        low_v[2, area] = jnp.dot(
            values, weights_v[2], preferred_element_type=jnp.float32
        ).astype(jnp.bfloat16)
        return carry

    lax.fori_loop(0, 4, project, 0)
    stores = [
        pltpu.make_async_copy(rows_v, gathered, store_sem.at[0]),
        pltpu.make_async_copy(pre_v.at[0], query_pre, store_sem.at[1]),
        pltpu.make_async_copy(pre_v.at[1], key_pre, store_sem.at[2]),
        pltpu.make_async_copy(low_v.at[0], query_low, store_sem.at[3]),
        pltpu.make_async_copy(low_v.at[1], key_low, store_sem.at[4]),
        pltpu.make_async_copy(low_v.at[2], value_low, store_sem.at[5]),
    ]
    for store in stores:
        store.start()

    def part_copy(source, target, index, to):
        return pltpu.make_async_remote_copy(
            src_ref=source,
            dst_ref=target,
            send_sem=part_send.at[index],
            recv_sem=part_recv.at[index],
            device_id=(position, to),
            device_id_type=mesh_ids,
        )

    core_first = part_copy(parts.at[0], core_in.at[0], 0, near)
    line_copy = part_copy(parts.at[1], line_in, 1, across)
    core_second = part_copy(parts.at[2], core_in.at[1], 2, near)

    def attend(i, carry):
        block = pick(i, [opposite, across, near, t])
        area = pl.ds(block * rows, rows)
        for h in range(heads):
            span = slice(h * 128, (h + 1) * 128)
            scores = lax.dot_general(
                low_v[0, area, span], low_v[1, :, span], contract_last, preferred_element_type=jnp.float32
            )
            highest_score = jnp.max(scores, axis=-1, keepdims=True)
            weights = jnp.exp((scores - highest_score) * factor)
            total = jnp.sum(weights, axis=-1, keepdims=True)
            mixed = jnp.dot(
                weights.astype(jnp.bfloat16), low_v[2, :, span], preferred_element_type=jnp.float32
            )
            mixed_v[area, span] = (mixed / total).astype(jnp.bfloat16)
            log_v[area, h : h + 1] = highest_score * factor + jnp.log(total)
        own_part[...] = jnp.dot(mixed_v[area], out_v[...], preferred_element_type=jnp.float32)

        @pl.when(i == 0)
        def _():
            parts[0] = own_part[...].astype(jnp.bfloat16)
            core_first.start()

        @pl.when(i == 1)
        def _():
            core_first.wait_recv()
            parts[1] = (own_part[...] + core_in[0].astype(jnp.float32)).astype(jnp.bfloat16)
            line_copy.start()

            @pl.when(middle)
            def _():
                gather_arrive(3)

        @pl.when(i == 2)
        def _():
            parts[2] = own_part[...].astype(jnp.bfloat16)
            core_second.start()

            @pl.when(middle == False)
            def _():
                gather_arrive(2)

        return carry

    lax.fori_loop(0, 4, attend, 0)
    more = [
        pltpu.make_async_copy(mixed_v, attended, store_sem.at[6]),
        pltpu.make_async_copy(log_v, log_sums, store_sem.at[7]),
    ]
    for store in more:
        store.start()
    core_second.wait_recv()
    own_part[...] += core_in[1].astype(jnp.float32)
    line_copy.wait_recv()
    own_part[...] += line_in[...].astype(jnp.float32)
    last = pltpu.make_async_copy(own_part, attn_sum, store_sem.at[8])
    last.start()

    @pl.when(middle == False)
    def _():
        gather_arrive(3)

    for k in range(4):
        gather_side(k)
    gather_drain()
    for copy in (to_across, to_near, forward, core_first, line_copy, core_second):
        copy.wait_send()
    for store in [*stores, *more, last, cot_copy]:
        store.wait()


def attention_forward(own, cot, weights, out_w, gains, tables, collective):
    rows, width = own.shape
    local = out_w.shape[0]
    length = 4 * rows
    any_space = pl.BlockSpec(memory_space=pl.ANY)
    vector = pl.BlockSpec(memory_space=pltpu.VMEM)
    low, full = jnp.bfloat16, jnp.float32
    dma = pltpu.SemaphoreType.DMA
    return pl.pallas_call(
        attention_kernel,
        name="attention_forward",
        out_shape=(
            jax.ShapeDtypeStruct((4, rows, width), low),
            jax.ShapeDtypeStruct((length, local), full),
            jax.ShapeDtypeStruct((length, local), full),
            jax.ShapeDtypeStruct((length, local), low),
            jax.ShapeDtypeStruct((length, local), low),
            jax.ShapeDtypeStruct((length, local), low),
            jax.ShapeDtypeStruct((length, local), low),
            jax.ShapeDtypeStruct((length, 128), full),
            jax.ShapeDtypeStruct((rows, width), full),
            jax.ShapeDtypeStruct((8, rows, width), low),
        ),
        in_specs=[any_space] * 6 + [vector] * 4,
        out_specs=(any_space,) * 10,
        scratch_shapes=[
            pltpu.VMEM((4, rows, width), low),
            pltpu.VMEM((3, width, local), low),
            pltpu.VMEM((local, width), low),
            pltpu.VMEM((2, length, local), full),
            pltpu.VMEM((3, length, local), low),
            pltpu.VMEM((length, local), low),
            pltpu.VMEM((length, 128), full),
            pltpu.VMEM((3, rows, width), low),
            pltpu.VMEM((rows, width), full),
            pltpu.VMEM((2, rows, width), low),
            pltpu.VMEM((rows, width), low),
            dma((5,)),
            dma((9,)),
            dma((3,)),
            dma((3,)),
            dma((3,)),
            dma((3,)),
            dma((8,)),
            dma((9,)),
            dma,
        ],
        compiler_params=pltpu.CompilerParams(
            collective_id=collective, has_side_effects=True, vmem_limit_bytes=60 << 20
        ),
        cost_estimate=pl.CostEstimate(
            flops=8 * length * width * local, bytes_accessed=64 << 20, transcendentals=length * length * 4
        ),
    )(own, cot, *weights, out_w, *gains, *tables)


def scatter_kernel(
    count,
    *refs,
):
    parts, totals = refs[:count], refs[count : 2 * count]
    own, side_in, line_in, own_sem, side_recv, side_send, line_recv, line_send = refs[2 * count :]
    position = lax.axis_index("expert")
    peer = lax.axis_index("tensor")
    z = position // 2
    x = position % 2
    middle = (z == 1) | (z == 2)
    line_slots = [
        z,
        pick(z, [1, 0, 3, 2]),
        pick(z, [2, 2, 1, 1]),
        pick(z, [3, 3, 0, 0]),
    ]
    mesh_ids = pl.DeviceIdType.MESH

    def device(zz, xx):
        return (zz * 2 + xx, peer)

    own_copies = [
        pltpu.make_async_copy(parts[c].at[line_slots[k] * 2 + x], own.at[k, c], own_sem.at[k, c])
        for k in (3, 2, 1, 0)
        for c in range(count)
    ]
    for copy in own_copies:
        copy.start()

    barrier = pltpu.get_barrier_semaphore()
    pl.semaphore_signal(barrier, inc=1, device_id=device(z, 1 - x), device_id_type=mesh_ids)

    @pl.when(z < 3)
    def _():
        pl.semaphore_signal(barrier, inc=1, device_id=device(z + 1, x), device_id_type=mesh_ids)

    @pl.when(z > 0)
    def _():
        pl.semaphore_signal(barrier, inc=1, device_id=device(z - 1, x), device_id_type=mesh_ids)

    pl.semaphore_wait(barrier, 2 + middle.astype(jnp.int32))

    def side_copy(k, c):
        return pltpu.make_async_remote_copy(
            src_ref=parts[c].at[pick(k, line_slots) * 2 + 1 - x],
            dst_ref=side_in.at[k, c],
            send_sem=side_send.at[k, c],
            recv_sem=side_recv.at[k, c],
            device_id=device(z, 1 - x),
            device_id_type=mesh_ids,
        )

    def line_slot(k):
        target = pick(k, line_slots)
        return jnp.where(target < z, target, target + 1)

    def line_copy(k, c):
        target = jnp.where(pick(k, line_slots) < z, z - 1, z + 1)
        return pltpu.make_async_remote_copy(
            src_ref=own.at[k, c],
            dst_ref=line_in.at[line_slot(k), c],
            send_sem=line_send.at[k - 1, c],
            recv_sem=line_recv.at[line_slot(k), c],
            device_id=device(jnp.clip(target, 0, 3), x),
            device_id_type=mesh_ids,
        )

    def line_wait(slot, c):
        pltpu.make_async_remote_copy(
            src_ref=own.at[0, c],
            dst_ref=line_in.at[slot, c],
            send_sem=line_send.at[0, c],
            recv_sem=line_recv.at[slot, c],
            device_id=device(z, 1 - x),
            device_id_type=mesh_ids,
        ).wait_recv()

    def send_order(i):
        return jnp.where(middle, pick(i, [3, 1, 2, 0]), pick(i, [3, 2, 1, 0]))

    def start_side(i, carry):
        for c in range(count):
            side_copy(send_order(i), c).start()
        return carry

    lax.fori_loop(0, 4, start_side, 0)
    for copy in own_copies:
        copy.wait()

    def relay(i, carry):
        k = send_order(i)
        for c in range(count):
            side_copy(k, c).wait_recv()
            own[k, c] = (
                own[k, c].astype(jnp.float32) + side_in[k, c].astype(jnp.float32)
            ).astype(jnp.bfloat16)

            @pl.when(middle)
            def _(c=c):
                line_wait(line_slot(k), c)
                own[k, c] = (
                    own[k, c].astype(jnp.float32) + line_in[line_slot(k), c].astype(jnp.float32)
                ).astype(jnp.bfloat16)

            line_copy(k, c).start()
        return carry

    lax.fori_loop(0, 3, relay, 0)
    for c in range(count):
        total = totals[c]
        side_copy(0, c).wait_recv()
        total[...] = own[0, c].astype(jnp.float32) + side_in[0, c].astype(jnp.float32)

        @pl.when(z < 3)
        def _(c=c, total=total):
            line_wait(z, c)
            total[...] += line_in[z, c].astype(jnp.float32)

        @pl.when(z > 0)
        def _(c=c, total=total):
            line_wait(z + 1, c)
            total[...] += line_in[z + 1, c].astype(jnp.float32)

        for k in range(4):
            side_copy(k, c).wait_send()
        for k in range(1, 4):
            line_copy(k, c).wait_send()


def scatter_parts(parts, collective):
    count = len(parts)
    rows, wide = parts[0].shape[1:]
    low = jnp.bfloat16
    dma = pltpu.SemaphoreType.DMA
    return pl.pallas_call(
        functools.partial(scatter_kernel, count),
        name="scatter_parts",
        out_shape=(jax.ShapeDtypeStruct((rows, wide), jnp.float32),) * count,
        in_specs=[pl.BlockSpec(memory_space=pl.ANY)] * count,
        out_specs=(pl.BlockSpec(memory_space=pltpu.VMEM),) * count,
        scratch_shapes=[
            pltpu.VMEM((4, count, rows, wide), low),
            pltpu.VMEM((4, count, rows, wide), low),
            pltpu.VMEM((5, count, rows, wide), low),
            dma((4, count)),
            dma((4, count)),
            dma((4, count)),
            dma((5, count)),
            dma((3, count)),
        ],
        compiler_params=pltpu.CompilerParams(
            collective_id=collective, has_side_effects=True, vmem_limit_bytes=40 << 20
        ),
        cost_estimate=pl.CostEstimate(
            flops=8 * rows * wide * count, bytes_accessed=300 << 20, transcendentals=0
        ),
    )(*parts)


def sum_kernel(own, total, incoming, recv, send):
    position = lax.axis_index("expert")
    peer = lax.axis_index("tensor")
    mesh_ids = pl.DeviceIdType.MESH

    def flip(index, bit):
        return index + bit - 2 * bit * ((index // bit) % 2)

    partners = [
        (position, flip(peer, 1)),
        (position, flip(peer, 2)),
        (flip(position, 1), peer),
        (flip(position, 2), peer),
        (flip(position, 4), peer),
    ]
    barrier = pltpu.get_barrier_semaphore()
    for partner in partners:
        pl.semaphore_signal(barrier, inc=1, device_id=partner, device_id_type=mesh_ids)
    pl.semaphore_wait(barrier, len(partners))
    total[0] = own[...]
    for i, partner in enumerate(partners):
        copy = pltpu.make_async_remote_copy(
            src_ref=total.at[i],
            dst_ref=incoming.at[i],
            send_sem=send.at[i],
            recv_sem=recv.at[i],
            device_id=partner,
            device_id_type=mesh_ids,
        )
        copy.start()
        copy.wait()
        total[i + 1] = total[i] + incoming[i]


def sum_everywhere(own, collective):
    steps = 5
    return pl.pallas_call(
        sum_kernel,
        name="sum_everywhere",
        out_shape=jax.ShapeDtypeStruct((steps + 1,) + own.shape, jnp.float32),
        in_specs=[pl.BlockSpec(memory_space=pltpu.VMEM)],
        out_specs=pl.BlockSpec(memory_space=pltpu.VMEM),
        scratch_shapes=[
            pltpu.VMEM((steps,) + own.shape, jnp.float32),
            pltpu.SemaphoreType.DMA((steps,)),
            pltpu.SemaphoreType.DMA((steps,)),
        ],
        compiler_params=pltpu.CompilerParams(collective_id=collective, has_side_effects=True),
        cost_estimate=pl.CostEstimate(flops=own.size * steps, bytes_accessed=40 << 20, transcendentals=0),
    )(own)[steps]


def weight_kernel(order, left, right, out):
    wide = left.shape[1]
    step = min(512, wide)
    for d in range(out.shape[2] // step):
        span = pl.ds(d * step, step)
        out[0, 0, span, :] = lax.dot_general(
            left[:, span], right[...], contract_first, preferred_element_type=jnp.float32
        ).astype(out.dtype)


def input_weight_parts(order, rows_all, grads, width, experts_local):
    count, wide = rows_all.shape
    hidden = grads.shape[1] // experts_local
    part = hidden // 4
    pieces = order.shape[0]
    return pl.pallas_call(
        weight_kernel,
        name="input_weight_parts",
        out_shape=jax.ShapeDtypeStruct((pieces, experts_local, width, part), jnp.bfloat16),
        grid_spec=pltpu.PrefetchScalarGridSpec(
            num_scalar_prefetch=1,
            grid=(pieces, experts_local),
            in_specs=[
                pl.BlockSpec((count, width), lambda r, e, order: (0, 0), pipeline_mode=pl.Buffered(1)),
                pl.BlockSpec((count, part), lambda r, e, order: (0, e * 4 + order[r])),
            ],
            out_specs=pl.BlockSpec((1, 1, width, part), lambda r, e, order: (r, e, 0, 0)),
        ),
        compiler_params=pltpu.CompilerParams(vmem_limit_bytes=48 << 20),
        cost_estimate=pl.CostEstimate(
            flops=2 * pieces * experts_local * count * width * part,
            bytes_accessed=2 * count * width + 2 * pieces * experts_local * part * (count + width),
            transcendentals=0,
        ),
    )(order, rows_all, grads)


def output_weight_parts(order, hidden_all, grads, experts_local):
    count, width = grads.shape
    hidden = hidden_all.shape[1] // experts_local
    part = hidden // 4
    pieces = order.shape[0]
    return pl.pallas_call(
        weight_kernel,
        name="output_weight_parts",
        out_shape=jax.ShapeDtypeStruct((pieces, experts_local, part, width), jnp.bfloat16),
        grid_spec=pltpu.PrefetchScalarGridSpec(
            num_scalar_prefetch=1,
            grid=(pieces, experts_local),
            in_specs=[
                pl.BlockSpec((count, part), lambda r, e, order: (0, e * 4 + order[r])),
                pl.BlockSpec((count, width), lambda r, e, order: (0, 0), pipeline_mode=pl.Buffered(1)),
            ],
            out_specs=pl.BlockSpec((1, 1, part, width), lambda r, e, order: (r, e, 0, 0)),
        ),
        compiler_params=pltpu.CompilerParams(vmem_limit_bytes=48 << 20),
        cost_estimate=pl.CostEstimate(
            flops=2 * pieces * experts_local * count * width * part,
            bytes_accessed=2 * count * width + 2 * pieces * experts_local * part * (count + width),
            transcendentals=0,
        ),
    )(order, hidden_all, grads)


def exchange(pieces_far, pieces_near):
    swap_core = [(0, 1), (1, 0), (2, 3), (3, 2)]
    swap_line = [(0, 2), (1, 3), (2, 0), (3, 1)]
    arrived = lax.ppermute(pieces_far, "tensor", swap_core)
    own = pieces_near[0].astype(jnp.float32) + arrived[0].astype(jnp.float32)
    sent = (pieces_near[1].astype(jnp.float32) + arrived[1].astype(jnp.float32)).astype(jnp.bfloat16)
    return own + lax.ppermute(sent, "tensor", swap_line).astype(jnp.float32)


def per_device(
    tokens,
    cotangent,
    routes,
    norm_in,
    query_w,
    key_w,
    value_w,
    out_w,
    query_gain,
    key_gain,
    norm_mid,
    router_w,
    gate_w,
    up_w,
    down_w,
):
    rows_own = tokens.shape[0]
    model_width = tokens.shape[1]
    expert_count = lax.axis_size("expert")
    head_width = query_gain.shape[0]
    local_heads = query_w.shape[1] // head_width
    experts_local = gate_w.shape[0]
    experts_all = router_w.shape[1]
    top_count = routes.shape[1]
    hidden_width = gate_w.shape[2]
    factor = 1.0 / math.sqrt(head_width)
    source = tokens.astype(jnp.float32)
    scale_in = inverse_rms(source)
    normed_low = (source * scale_in * norm_in).astype(jnp.bfloat16)
    seq_len = 4 * rows_own
    cosine, sine_table = rotary_tables(seq_len, head_width)
    turn_cosine = jnp.concatenate([cosine[:, 0], cosine[:, 0]], axis=1)
    turn_sine = jnp.concatenate([-sine_table[:, 0], sine_table[:, 0]], axis=1)
    (
        gathered,
        query_pre,
        key_pre,
        query_low,
        key_low,
        value_low,
        attended,
        log_rows,
        attn_out,
        cot_all,
    ) = attention_forward(
        normed_low,
        cotangent,
        (query_w, key_w, value_w),
        out_w,
        (query_gain[None], key_gain[None]),
        (turn_cosine, turn_sine),
        4,
    )
    gathered = gathered.reshape(seq_len, model_width)
    heads_shape = (seq_len, local_heads, head_width)
    query_heads = query_pre.reshape(heads_shape)
    key_heads = key_pre.reshape(heads_shape)
    query_scale = inverse_rms(query_heads)
    key_scale = inverse_rms(key_heads)
    key_low = key_low.reshape(heads_shape)
    value_heads = value_low.reshape(heads_shape)
    block_rows = min(512, seq_len)
    block_count = seq_len // block_rows
    query_blocks = query_low.reshape(block_count, block_rows, local_heads, head_width)
    log_sums = (
        log_rows[:, :local_heads].T.reshape(local_heads, block_count, block_rows).transpose(1, 0, 2)
    )
    middle = source + attn_out
    scale_mid = inverse_rms(middle)
    normed_mid = middle * scale_mid * norm_mid
    mid_low = normed_mid.astype(jnp.bfloat16)
    logits = jnp.dot(normed_mid, router_w, precision=highest, preferred_element_type=jnp.float32)
    route_mask = routes[:, :, None] == jnp.arange(experts_all, dtype=jnp.int32)[None, None, :]
    mask_float = route_mask.astype(jnp.float32)
    chosen = jnp.sum(mask_float * logits[:, None, :], axis=-1)
    gating = jax.nn.softmax(chosen, axis=-1)
    upstream = cotangent.astype(jnp.float32)
    gates = jnp.sum(mask_float * gating[:, :, None], axis=1)
    gates_high = gates.astype(jnp.bfloat16)
    gates_low = (gates - gates_high.astype(jnp.float32)).astype(jnp.bfloat16)
    spare = jnp.zeros((rows_own, 128 - 2 * experts_all), jnp.bfloat16)
    own_rows = jnp.concatenate([mid_low, gates_high, gates_low, spare], axis=1)
    rows_all, hidden_all, gate_all, up_all, y_all, row_total = expert_pass(
        own_rows, cot_all, gate_w, up_w, down_w, experts_all, 1
    )
    expert_input_grad = row_total[:, :model_width]
    cot_all = cot_all.reshape(expert_count * rows_own, model_width)
    gate_grad_dense = (
        row_total[:, model_width : model_width + experts_all]
        + row_total[:, model_width + experts_all : model_width + 2 * experts_all]
    )
    gate_grad = jnp.sum(mask_float * gate_grad_dense[:, None, :], axis=-1)
    count = expert_count * rows_own
    inner_all = experts_local * hidden_width
    rows_all = rows_all.reshape(count, own_rows.shape[1])
    hidden_all = hidden_all.reshape(count, inner_all)
    gate_all = gate_all.reshape(count, inner_all)
    up_all = up_all.reshape(count, inner_all)
    y_part = y_all.reshape(count, model_width)
    y_sum = lax.psum_scatter(y_part, "expert", scatter_dimension=0, tiled=True)
    output = (middle + y_sum.astype(jnp.float32)).astype(jnp.bfloat16)
    me = lax.axis_index("tensor")
    far = jnp.stack([me ^ 1, me ^ 3]).astype(jnp.int32)
    near = jnp.stack([me, me ^ 2]).astype(jnp.int32)
    gate_far = input_weight_parts(far, rows_all, gate_all, model_width, experts_local)
    up_far = input_weight_parts(far, rows_all, up_all, model_width, experts_local)
    down_far = output_weight_parts(far, hidden_all, cot_all, experts_local)
    gate_near = input_weight_parts(near, rows_all, gate_all, model_width, experts_local)
    up_near = input_weight_parts(near, rows_all, up_all, model_width, experts_local)
    down_near = output_weight_parts(near, hidden_all, cot_all, experts_local)
    inner_gate = jnp.sum(gating * gate_grad, axis=-1, keepdims=True)
    chosen_grad = gating * (gate_grad - inner_gate)
    logit_grad = jnp.sum(chosen_grad[:, :, None] * mask_float, axis=1)
    router_part = lax.dot_general(
        normed_mid,
        logit_grad,
        contract_first,
        precision=highest,
        preferred_element_type=jnp.float32,
    )
    normed_mid_grad = expert_input_grad + lax.dot_general(
        logit_grad, router_w, contract_last, precision=highest, preferred_element_type=jnp.float32
    )
    norm_mid_part = jnp.sum(normed_mid_grad * middle * scale_mid, axis=0)
    middle_grad = upstream + norm_backward(normed_mid_grad, middle, scale_mid, norm_mid)
    branch_low = middle_grad.astype(jnp.bfloat16)
    branch_all = lax.all_gather(branch_low, "tensor", axis=0, tiled=True)
    branch_all, gate_far, up_far = lax.optimization_barrier((branch_all, gate_far, up_far))
    attended_grad = lax.dot_general(
        branch_all, out_w, contract_last, preferred_element_type=jnp.float32
    ).astype(jnp.bfloat16)
    out_w_part = lax.dot_general(
        attended, branch_all, contract_first, preferred_element_type=jnp.float32
    )
    grad_blocks = attended_grad.reshape(block_count, block_rows, local_heads, head_width)

    def attend_back(carry, inputs):
        key_total, value_total = carry
        query_block, grad_block, log_block = inputs
        scores = (
            jnp.einsum("qhd,khd->hqk", query_block, key_low, preferred_element_type=jnp.float32)
            * factor
        )
        probs = jnp.exp(scores - log_block[:, :, None])
        probs_low = probs.astype(jnp.bfloat16)
        value_total = value_total + jnp.einsum(
            "hqk,qhd->khd", probs_low, grad_block, preferred_element_type=jnp.float32
        )
        prob_grad = jnp.einsum(
            "qhd,khd->hqk", grad_block, value_heads, preferred_element_type=jnp.float32
        )
        delta = jnp.sum(probs * prob_grad, axis=-1, keepdims=True)
        score_low = (probs * (prob_grad - delta)).astype(jnp.bfloat16)
        query_part = (
            jnp.einsum("hqk,khd->qhd", score_low, key_low, preferred_element_type=jnp.float32)
            * factor
        )
        key_total = (
            key_total
            + jnp.einsum("hqk,qhd->khd", score_low, query_block, preferred_element_type=jnp.float32)
            * factor
        )
        return ((key_total, value_total), query_part)

    zero_heads = jnp.zeros((seq_len, local_heads, head_width), jnp.float32)
    (key_grad, value_total), query_parts = lax.scan(
        attend_back, (zero_heads, zero_heads), (query_blocks, grad_blocks, log_sums)
    )
    query_grad = query_parts.reshape(seq_len, local_heads, head_width)
    value_grad_low = value_total.reshape(seq_len, local_heads * head_width).astype(jnp.bfloat16)
    query_rot_grad = rotate_back(query_grad, cosine, sine_table)
    key_rot_grad = rotate_back(key_grad, cosine, sine_table)
    query_gain_part = jnp.sum(query_rot_grad * query_heads * query_scale, axis=(0, 1))
    key_gain_part = jnp.sum(key_rot_grad * key_heads * key_scale, axis=(0, 1))
    query_pre_grad = (
        norm_backward(query_rot_grad, query_heads, query_scale, query_gain)
        .reshape(seq_len, local_heads * head_width)
        .astype(jnp.bfloat16)
    )
    key_pre_grad = (
        norm_backward(key_rot_grad, key_heads, key_scale, key_gain)
        .reshape(seq_len, local_heads * head_width)
        .astype(jnp.bfloat16)
    )
    query_w_part = lax.dot_general(
        gathered, query_pre_grad, contract_first, preferred_element_type=jnp.float32
    )
    key_w_part = lax.dot_general(
        gathered, key_pre_grad, contract_first, preferred_element_type=jnp.float32
    )
    value_w_part = lax.dot_general(
        gathered, value_grad_low, contract_first, preferred_element_type=jnp.float32
    )
    summed = lax.dot_general(
        query_pre_grad, query_w, contract_last, preferred_element_type=jnp.float32
    )
    summed = summed + lax.dot_general(
        key_pre_grad, key_w, contract_last, preferred_element_type=jnp.float32
    )
    rows_grad = lax.psum_scatter(
        (
            summed
            + lax.dot_general(
                value_grad_low, value_w, contract_last, preferred_element_type=jnp.float32
            )
        ).astype(jnp.bfloat16),
        "tensor",
        scatter_dimension=0,
        tiled=True,
    ).astype(jnp.float32)
    norm_in_part = jnp.sum(rows_grad * source * scale_in, axis=0)
    input_grad = middle_grad + norm_backward(rows_grad, source, scale_in, norm_in)
    out_w_grad = lax.psum_scatter(
        out_w_part.astype(jnp.bfloat16), "expert", scatter_dimension=1, tiled=True
    ).astype(jnp.float32)
    part_rows = model_width // expert_count
    local_width = local_heads * head_width
    query_w_grad, key_w_grad, value_w_grad = scatter_parts(
        [
            p.astype(jnp.bfloat16).reshape(expert_count, part_rows, local_width)
            for p in (query_w_part, key_w_part, value_w_part)
        ],
        2,
    )
    gate_w_grad = exchange(gate_far, gate_near)
    up_w_grad = exchange(up_far, up_near)
    down_w_grad = exchange(down_far, down_near)
    router_w_grad = lax.psum(router_part, ("expert", "tensor"))
    small = jnp.concatenate(
        [
            norm_in_part,
            query_gain_part,
            key_gain_part,
            norm_mid_part,
            jnp.zeros((-(2 * model_width + 2 * head_width) % 1024,), jnp.float32),
        ]
    ).reshape(-1, 128)
    sums = sum_everywhere(small, 3).reshape(-1)
    norm_in_grad = sums[:model_width]
    query_gain_grad = sums[model_width : model_width + head_width]
    key_gain_grad = sums[model_width + head_width : model_width + 2 * head_width]
    norm_mid_grad = sums[model_width + 2 * head_width : 2 * model_width + 2 * head_width]
    return (
        output,
        input_grad,
        norm_in_grad,
        query_w_grad,
        key_w_grad,
        value_w_grad,
        out_w_grad,
        query_gain_grad,
        key_gain_grad,
        norm_mid_grad,
        router_w_grad,
        gate_w_grad,
        up_w_grad,
        down_w_grad,
    )


def per_device_general(
    tokens,
    cotangent,
    routes,
    norm_in,
    query_w,
    key_w,
    value_w,
    out_w,
    query_gain,
    key_gain,
    norm_mid,
    router_w,
    gate_w,
    up_w,
    down_w,
):
    rows_own = tokens.shape[0]
    model_width = tokens.shape[1]
    tensor_count = lax.axis_size("tensor")
    expert_count = lax.axis_size("expert")
    head_width = query_gain.shape[0]
    local_heads = query_w.shape[1] // head_width
    experts_local = gate_w.shape[0]
    experts_all = router_w.shape[1]
    top_count = routes.shape[1]
    hidden_width = gate_w.shape[2]
    factor = 1.0 / math.sqrt(head_width)
    cot_all = lax.all_gather(cotangent, "expert", axis=0, tiled=True)
    source = tokens.astype(jnp.float32)
    scale_in = inverse_rms(source)
    normed_low = (source * scale_in * norm_in).astype(jnp.bfloat16)
    gathered = lax.all_gather(normed_low, "tensor", axis=0, tiled=True)
    seq_len = gathered.shape[0]
    query_pre = jnp.dot(gathered, query_w, preferred_element_type=jnp.float32)
    key_pre = jnp.dot(gathered, key_w, preferred_element_type=jnp.float32)
    value_low = jnp.dot(gathered, value_w, preferred_element_type=jnp.float32).astype(jnp.bfloat16)
    cosine, sine_table = rotary_tables(seq_len, head_width)
    query_heads = query_pre.reshape(seq_len, local_heads, head_width)
    key_heads = key_pre.reshape(seq_len, local_heads, head_width)
    query_scale = inverse_rms(query_heads)
    key_scale = inverse_rms(key_heads)
    query_low = rotate(query_heads * query_scale * query_gain, cosine, sine_table).astype(
        jnp.bfloat16
    )
    key_low = rotate(key_heads * key_scale * key_gain, cosine, sine_table).astype(jnp.bfloat16)
    value_heads = value_low.reshape(seq_len, local_heads, head_width)
    block_rows = min(512, seq_len)
    block_count = seq_len // block_rows
    query_blocks = query_low.reshape(block_count, block_rows, local_heads, head_width)

    def attend(query_block):
        scores = (
            jnp.einsum("qhd,khd->hqk", query_block, key_low, preferred_element_type=jnp.float32)
            * factor
        )
        row_max = jnp.max(scores, axis=-1, keepdims=True)
        shifted = jnp.exp(scores - row_max)
        row_sum = jnp.sum(shifted, axis=-1, keepdims=True)
        probs_low = (shifted / row_sum).astype(jnp.bfloat16)
        mixture = jnp.einsum(
            "hqk,khd->qhd", probs_low, value_heads, preferred_element_type=jnp.float32
        )
        return (mixture.astype(jnp.bfloat16), (row_max + jnp.log(row_sum))[..., 0])

    attended_blocks, log_sums = lax.map(attend, query_blocks)
    attended = attended_blocks.reshape(seq_len, local_heads * head_width)
    attn_out = lax.psum_scatter(
        jnp.dot(attended, out_w, preferred_element_type=jnp.float32).astype(jnp.bfloat16),
        "tensor",
        scatter_dimension=0,
        tiled=True,
    ).astype(jnp.float32)
    middle = source + attn_out
    scale_mid = inverse_rms(middle)
    normed_mid = middle * scale_mid * norm_mid
    mid_low = normed_mid.astype(jnp.bfloat16)
    logits = jnp.dot(normed_mid, router_w, precision=highest, preferred_element_type=jnp.float32)
    route_mask = routes[:, :, None] == jnp.arange(experts_all, dtype=jnp.int32)[None, None, :]
    mask_float = route_mask.astype(jnp.float32)
    chosen = jnp.sum(mask_float * logits[:, None, :], axis=-1)
    gating = jax.nn.softmax(chosen, axis=-1)
    upstream = cotangent.astype(jnp.float32)
    gates = jnp.sum(mask_float * gating[:, :, None], axis=1)
    x_all = lax.all_gather(mid_low, "expert", axis=0, tiled=True)
    gates_all = lax.all_gather(gates, "expert", axis=0, tiled=True)
    first_expert = lax.axis_index("expert") * experts_local
    own_gates = lax.dynamic_slice_in_dim(gates_all, first_expert, experts_local, 1)
    part_width = hidden_width // tensor_count
    rows_all = x_all.shape[0]
    y_part = jnp.zeros((rows_all, model_width), jnp.float32)
    x_grad_part = jnp.zeros((rows_all, model_width), jnp.float32)
    gate_grads, gate_parts, up_parts, down_parts = [], [], [], []
    for e in range(experts_local):
        hidden_raw = lax.dot_general(
            cot_all, down_w[e], contract_last, preferred_element_type=jnp.float32
        )
        gate_pre = jnp.dot(x_all, gate_w[e], preferred_element_type=jnp.float32)
        up_pre = jnp.dot(x_all, up_w[e], preferred_element_type=jnp.float32)
        weight = own_gates[:, e : e + 1]
        hidden = gate_pre * jax.nn.sigmoid(gate_pre) * up_pre
        gate_grads.append(jnp.sum(hidden * hidden_raw, axis=1))
        hidden_low = (hidden * weight).astype(jnp.bfloat16)
        gate_back, up_back = swiglu_back(hidden_raw * weight, gate_pre, up_pre)
        y_part = y_part + jnp.dot(hidden_low, down_w[e], preferred_element_type=jnp.float32)
        x_grad_part = x_grad_part + lax.dot_general(
            gate_back, gate_w[e], contract_last, preferred_element_type=jnp.float32
        )
        x_grad_part = x_grad_part + lax.dot_general(
            up_back, up_w[e], contract_last, preferred_element_type=jnp.float32
        )
        gate_parts.append(
            jnp.einsum(
                "nd,ntf->tdf",
                x_all,
                gate_back.reshape(rows_all, tensor_count, part_width),
                preferred_element_type=jnp.float32,
            ).astype(jnp.bfloat16)
        )
        up_parts.append(
            jnp.einsum(
                "nd,ntf->tdf",
                x_all,
                up_back.reshape(rows_all, tensor_count, part_width),
                preferred_element_type=jnp.float32,
            ).astype(jnp.bfloat16)
        )
        down_parts.append(
            lax.dot_general(
                hidden_low, cot_all, contract_first, preferred_element_type=jnp.float32
            ).astype(jnp.bfloat16)
        )
    x_grad = lax.psum_scatter(
        x_grad_part.astype(jnp.bfloat16), "expert", scatter_dimension=0, tiled=True
    )
    expert_input_grad = x_grad.astype(jnp.float32)
    gate_grad_sent = jnp.stack(gate_grads, axis=-1)
    gate_grad_all = lax.all_to_all(gate_grad_sent, "expert", split_axis=0, concat_axis=0, tiled=True)
    gate_grad_dense = (
        gate_grad_all.reshape(expert_count, rows_own, experts_local)
        .transpose(1, 0, 2)
        .reshape(rows_own, experts_all)
    )
    gate_grad = jnp.sum(mask_float * gate_grad_dense[:, None, :], axis=-1)
    y_sum = lax.psum_scatter(
        y_part.astype(jnp.bfloat16), "expert", scatter_dimension=0, tiled=True
    )
    output = (middle + y_sum.astype(jnp.float32)).astype(jnp.bfloat16)

    def own_part(parts):
        return [
            lax.psum_scatter(p, "tensor", scatter_dimension=0, tiled=True).astype(jnp.float32)
            for p in parts
        ]

    gate_w_grad = jnp.concatenate(own_part(gate_parts), axis=0)
    up_w_grad = jnp.concatenate(own_part(up_parts), axis=0)
    down_w_grad = jnp.stack(own_part(down_parts), axis=0)
    inner_gate = jnp.sum(gating * gate_grad, axis=-1, keepdims=True)
    chosen_grad = gating * (gate_grad - inner_gate)
    logit_grad = jnp.sum(chosen_grad[:, :, None] * mask_float, axis=1)
    router_part = lax.dot_general(
        normed_mid,
        logit_grad,
        contract_first,
        precision=highest,
        preferred_element_type=jnp.float32,
    )
    normed_mid_grad = expert_input_grad + lax.dot_general(
        logit_grad, router_w, contract_last, precision=highest, preferred_element_type=jnp.float32
    )
    norm_mid_part = jnp.sum(normed_mid_grad * middle * scale_mid, axis=0)
    middle_grad = upstream + norm_backward(normed_mid_grad, middle, scale_mid, norm_mid)
    branch_low = middle_grad.astype(jnp.bfloat16)
    branch_all = lax.all_gather(branch_low, "tensor", axis=0, tiled=True)
    attended_grad = lax.dot_general(
        branch_all, out_w, contract_last, preferred_element_type=jnp.float32
    ).astype(jnp.bfloat16)
    out_w_part = lax.dot_general(
        attended, branch_all, contract_first, preferred_element_type=jnp.float32
    )
    grad_blocks = attended_grad.reshape(block_count, block_rows, local_heads, head_width)

    def attend_back(carry, inputs):
        key_total, value_total = carry
        query_block, grad_block, log_block = inputs
        scores = (
            jnp.einsum("qhd,khd->hqk", query_block, key_low, preferred_element_type=jnp.float32)
            * factor
        )
        probs = jnp.exp(scores - log_block[:, :, None])
        probs_low = probs.astype(jnp.bfloat16)
        value_total = value_total + jnp.einsum(
            "hqk,qhd->khd", probs_low, grad_block, preferred_element_type=jnp.float32
        )
        prob_grad = jnp.einsum(
            "qhd,khd->hqk", grad_block, value_heads, preferred_element_type=jnp.float32
        )
        delta = jnp.sum(probs * prob_grad, axis=-1, keepdims=True)
        score_low = (probs * (prob_grad - delta)).astype(jnp.bfloat16)
        query_part = (
            jnp.einsum("hqk,khd->qhd", score_low, key_low, preferred_element_type=jnp.float32)
            * factor
        )
        key_total = (
            key_total
            + jnp.einsum("hqk,qhd->khd", score_low, query_block, preferred_element_type=jnp.float32)
            * factor
        )
        return ((key_total, value_total), query_part)

    zero_heads = jnp.zeros((seq_len, local_heads, head_width), jnp.float32)
    (key_grad, value_total), query_parts = lax.scan(
        attend_back, (zero_heads, zero_heads), (query_blocks, grad_blocks, log_sums)
    )
    query_grad = query_parts.reshape(seq_len, local_heads, head_width)
    value_grad_low = value_total.reshape(seq_len, local_heads * head_width).astype(jnp.bfloat16)
    query_rot_grad = rotate_back(query_grad, cosine, sine_table)
    key_rot_grad = rotate_back(key_grad, cosine, sine_table)
    query_gain_part = jnp.sum(query_rot_grad * query_heads * query_scale, axis=(0, 1))
    key_gain_part = jnp.sum(key_rot_grad * key_heads * key_scale, axis=(0, 1))
    query_pre_grad = (
        norm_backward(query_rot_grad, query_heads, query_scale, query_gain)
        .reshape(seq_len, local_heads * head_width)
        .astype(jnp.bfloat16)
    )
    key_pre_grad = (
        norm_backward(key_rot_grad, key_heads, key_scale, key_gain)
        .reshape(seq_len, local_heads * head_width)
        .astype(jnp.bfloat16)
    )
    query_w_part = lax.dot_general(
        gathered, query_pre_grad, contract_first, preferred_element_type=jnp.float32
    )
    key_w_part = lax.dot_general(
        gathered, key_pre_grad, contract_first, preferred_element_type=jnp.float32
    )
    value_w_part = lax.dot_general(
        gathered, value_grad_low, contract_first, preferred_element_type=jnp.float32
    )
    summed = lax.dot_general(
        query_pre_grad, query_w, contract_last, preferred_element_type=jnp.float32
    )
    summed = summed + lax.dot_general(
        key_pre_grad, key_w, contract_last, preferred_element_type=jnp.float32
    )
    rows_grad = lax.psum_scatter(
        (
            summed
            + lax.dot_general(
                value_grad_low, value_w, contract_last, preferred_element_type=jnp.float32
            )
        ).astype(jnp.bfloat16),
        "tensor",
        scatter_dimension=0,
        tiled=True,
    ).astype(jnp.float32)
    norm_in_part = jnp.sum(rows_grad * source * scale_in, axis=0)
    input_grad = middle_grad + norm_backward(rows_grad, source, scale_in, norm_in)
    query_w_grad, key_w_grad, value_w_grad, out_w_grad = (
        lax.psum_scatter(
            query_w_part.astype(jnp.bfloat16), "expert", scatter_dimension=0, tiled=True
        ).astype(jnp.float32),
        lax.psum_scatter(
            key_w_part.astype(jnp.bfloat16), "expert", scatter_dimension=0, tiled=True
        ).astype(jnp.float32),
        lax.psum_scatter(
            value_w_part.astype(jnp.bfloat16), "expert", scatter_dimension=0, tiled=True
        ).astype(jnp.float32),
        lax.psum_scatter(
            out_w_part.astype(jnp.bfloat16), "expert", scatter_dimension=1, tiled=True
        ).astype(jnp.float32),
    )
    norm_in_grad, query_gain_grad, key_gain_grad, norm_mid_grad, router_w_grad = lax.psum(
        (norm_in_part, query_gain_part, key_gain_part, norm_mid_part, router_part),
        ("expert", "tensor"),
    )
    return (
        output,
        input_grad,
        norm_in_grad,
        query_w_grad,
        key_w_grad,
        value_w_grad,
        out_w_grad,
        query_gain_grad,
        key_gain_grad,
        norm_mid_grad,
        router_w_grad,
        gate_w_grad,
        up_w_grad,
        down_w_grad,
    )


def solution(mesh):
    placed = (
        P(("expert", "tensor"), None),
        P(("expert", "tensor"), None),
        P(("expert", "tensor"), None),
        P(),
        P(None, "tensor"),
        P(None, "tensor"),
        P(None, "tensor"),
        P("tensor", None),
        P(),
        P(),
        P(),
        P(),
        P("expert", None, None),
        P("expert", None, None),
        P("expert", None, None),
    )
    return jax.shard_map(
        per_device if dict(mesh.shape) == {"expert": 8, "tensor": 4} else per_device_general,
        mesh=mesh,
        in_specs=placed,
        out_specs=(
            P(("expert", "tensor"), None),
            P(("expert", "tensor"), None),
            P(),
            P("expert", "tensor"),
            P("expert", "tensor"),
            P("expert", "tensor"),
            P("tensor", "expert"),
            P(),
            P(),
            P(),
            P(),
            P("expert", None, "tensor"),
            P("expert", None, "tensor"),
            P("expert", "tensor", None),
        ),
        check_vma=False,
    )
```

```python
import functools
import math

import jax
import jax.numpy as jnp
from jax import lax
from jax.experimental import pallas as pl
from jax.experimental.pallas import tpu as pltpu
from jax.sharding import PartitionSpec as P

epsilon = 1e-06
highest = lax.Precision.HIGHEST
contract_last = (((1,), (1,)), ((), ()))
contract_first = (((0,), (0,)), ((), ()))


def inverse_rms(values):
    return lax.rsqrt(jnp.mean(values * values, axis=-1, keepdims=True) + epsilon)


def norm_backward(grad_norm, values, inverse, norm_gain):
    weighted = grad_norm * norm_gain
    inner_mean = jnp.mean(weighted * values, axis=-1, keepdims=True)
    return inverse * weighted - values * inverse * inverse * inverse * inner_mean


def rotary_tables(length, head_width):
    half_dim = head_width // 2
    frequency = jnp.exp(
        -math.log(10000.0) * 2.0 * jnp.arange(half_dim, dtype=jnp.float32) / head_width
    )
    angles = jnp.arange(length, dtype=jnp.float32)[:, None] * frequency[None, :]
    return (jnp.cos(angles)[:, None, :], jnp.sin(angles)[:, None, :])


def rotate(values, cosine, sine_table):
    half_dim = values.shape[-1] // 2
    first_half = values[..., :half_dim]
    second_half = values[..., half_dim:]
    return jnp.concatenate(
        [
            first_half * cosine - second_half * sine_table,
            second_half * cosine + first_half * sine_table,
        ],
        axis=-1,
    )


def rotate_back(gradient, cosine, sine_table):
    half_dim = gradient.shape[-1] // 2
    first_half = gradient[..., :half_dim]
    second_half = gradient[..., half_dim:]
    return jnp.concatenate(
        [
            first_half * cosine + second_half * sine_table,
            second_half * cosine - first_half * sine_table,
        ],
        axis=-1,
    )


def swiglu_back(hidden_grad, gate_pre, up_pre):
    sigmoid_part = jax.nn.sigmoid(gate_pre)
    gate_back = (
        hidden_grad * up_pre * sigmoid_part * (1.0 + gate_pre * (1.0 - sigmoid_part))
    ).astype(jnp.bfloat16)
    up_back = (hidden_grad * gate_pre * sigmoid_part).astype(jnp.bfloat16)
    return (gate_back, up_back)


chunks = 4


def pick(index, values):
    result = values[-1]
    for j in reversed(range(len(values) - 1)):
        result = jnp.where(index == j, values[j], result)
    return result


def expert_kernel(
    experts_all,
    own_rows,
    cot_all,
    gate_hbm,
    up_hbm,
    down_hbm,
    hidden_all,
    grads_all,
    y_all,
    total,
    far_input,
    near_input,
    far_output,
    near_output,
    gate_v,
    up_v,
    down_v,
    rows_v,
    cot_v,
    hidden_v,
    gate_b,
    up_b,
    y_v,
    stage,
    parts,
    side_in,
    cross_in,
    line_in,
    weight_sem,
    own_sem,
    cot_sem,
    out_sem,
    item_in,
    item_out,
    gather_recv,
    gather_send,
    side_recv,
    side_send,
    cross_recv,
    cross_send,
    line_recv,
    line_send,
):
    position = lax.axis_index("expert")
    peer = lax.axis_index("tensor")
    z = position // 2
    x = position % 2
    experts_local, width, hidden = gate_v.shape
    rows = cot_v.shape[0]
    part = hidden // 4
    y = peer // 2
    core = peer % 2
    chunk = rows // chunks
    middle = (z == 1) | (z == 2)
    ends = (z == 0) | (z == 3)
    pair = z + 1 - 2 * (z % 2)
    line_slots = [
        z,
        pick(z, [1, 0, 3, 2]),
        pick(z, [2, 2, 1, 1]),
        pick(z, [3, 3, 0, 0]),
    ]

    def block_rows(block):
        return pl.ds(pl.multiple_of(block * rows, rows), rows)

    def device(zz, xx):
        return (zz * 2 + xx, peer)

    def slot_z(k):
        return pick(k, line_slots)

    weight_copies = [
        pltpu.make_async_copy(gate_hbm, gate_v, weight_sem.at[0]),
        pltpu.make_async_copy(up_hbm, up_v, weight_sem.at[1]),
        pltpu.make_async_copy(down_hbm, down_v, weight_sem.at[2]),
    ]
    own_copy = pltpu.make_async_copy(own_rows, rows_v.at[block_rows(position)], own_sem)
    own_copy.start()
    for copy in weight_copies:
        copy.start()

    barrier = pltpu.get_barrier_semaphore()
    pl.semaphore_signal(barrier, inc=1, device_id=device(z, 1 - x), device_id_type=pl.DeviceIdType.MESH)

    @pl.when(z < 3)
    def _():
        pl.semaphore_signal(barrier, inc=1, device_id=device(z + 1, x), device_id_type=pl.DeviceIdType.MESH)

    @pl.when(z > 0)
    def _():
        pl.semaphore_signal(barrier, inc=1, device_id=device(z - 1, x), device_id_type=pl.DeviceIdType.MESH)

    pl.semaphore_wait(barrier, 2 + middle.astype(jnp.int32))

    def gather_copy(source, block, index, zz, xx):
        return pltpu.make_async_remote_copy(
            src_ref=source,
            dst_ref=rows_v.at[block_rows(block)],
            send_sem=gather_send.at[index],
            recv_sem=gather_recv.at[block],
            device_id=device(zz, xx),
            device_id_type=pl.DeviceIdType.MESH,
        )

    def own_send(index, zz, xx):
        return gather_copy(own_rows, position, index, zz, xx)

    own_send(0, z, 1 - x).start()

    @pl.when(z < 3)
    def _():
        own_send(1, z + 1, x).start()

    @pl.when(z > 0)
    def _():
        own_send(2, z - 1, x).start()

    def forward_side(k):
        block = slot_z(k) * 2 + x
        return gather_copy(rows_v.at[block_rows(block)], block, 2 + k, z, 1 - x)

    def forward_line(k):
        block = slot_z(k) * 2 + x
        target = jnp.where(slot_z(k) < z, z + 1, z - 1)
        return gather_copy(rows_v.at[block_rows(block)], block, 5 + k, jnp.clip(target, 0, 3), x)

    def arrived(block):
        gather_copy(own_rows, block, 0, z, 1 - x).wait_recv()

    def arrive(k):
        arrived(slot_z(k) * 2 + x)
        if k < 3:

            @pl.when(ends)
            def _():
                forward_side(k).start()

        @pl.when(middle)
        def _():
            if k > 1:
                forward_side(k).start()
            forward_line(k).start()

    def forward_cross():
        block = jnp.where(ends, z, slot_z(3)) * 2 + 1 - x
        return gather_copy(rows_v.at[block_rows(block)], block, 9, pair, x)

    def cross_copy(c):
        area = pl.ds(c * chunk, chunk)
        return pltpu.make_async_remote_copy(
            src_ref=parts.at[5, area],
            dst_ref=cross_in.at[area],
            send_sem=cross_send.at[c],
            recv_sem=cross_recv.at[c],
            device_id=device(pair, x),
            device_id_type=pl.DeviceIdType.MESH,
        )

    def cross_add(c):
        area = pl.ds(c * chunk, chunk)
        cross_copy(c).wait_recv()
        parts[4, area] = (
            parts[4, area].astype(jnp.float32) + cross_in[area].astype(jnp.float32)
        ).astype(jnp.bfloat16)
        side_copy(0, c).start()

    def side_slot(k):
        return jnp.maximum(k - 1, 0)

    def side_copy(k, c):
        area = pl.ds(c * chunk, chunk)
        return pltpu.make_async_remote_copy(
            src_ref=parts.at[4 + k, area],
            dst_ref=side_in.at[side_slot(k), area],
            send_sem=side_send.at[side_slot(k), c],
            recv_sem=side_recv.at[side_slot(k), c],
            device_id=device(z, 1 - x),
            device_id_type=pl.DeviceIdType.MESH,
        )

    def line_slot(k):
        target = slot_z(k)
        return jnp.where(target < z, target, target + 1)

    def line_copy(k, c):
        area = pl.ds(c * chunk, chunk)
        target = jnp.where(slot_z(k) < z, z - 1, z + 1)
        return pltpu.make_async_remote_copy(
            src_ref=parts.at[k, area],
            dst_ref=line_in.at[line_slot(k), area],
            send_sem=line_send.at[k - 1, c],
            recv_sem=line_recv.at[line_slot(k), c],
            device_id=device(jnp.clip(target, 0, 3), x),
            device_id_type=pl.DeviceIdType.MESH,
        )

    def line_wait(slot, c):
        area = pl.ds(c * chunk, chunk)
        pltpu.make_async_remote_copy(
            src_ref=parts.at[0, area],
            dst_ref=line_in.at[slot, area],
            send_sem=line_send.at[0, c],
            recv_sem=line_recv.at[slot, c],
            device_id=device(z, 1 - x),
            device_id_type=pl.DeviceIdType.MESH,
        ).wait_recv()

    def relay(k, c):
        area = pl.ds(c * chunk, chunk)
        if k > 1:
            side_copy(k, c).wait_recv()
            parts[k, area] = (
                parts[k, area].astype(jnp.float32) + side_in[k - 1, area].astype(jnp.float32)
            ).astype(jnp.bfloat16)

        @pl.when(middle)
        def _():
            line_wait(line_slot(k), c)
            parts[k, area] = (
                parts[k, area].astype(jnp.float32) + line_in[line_slot(k), area].astype(jnp.float32)
            ).astype(jnp.bfloat16)

        line_copy(k, c).start()

    def block_of(step):
        k = pick(step, [0, 1, 0, 1, 2, 2, 3, 3])
        side = pick(step, [0, 0, 1, 1, 0, 1, 1, 0])
        return k, side, slot_z(k) * 2 + jnp.where(side == 1, 1 - x, x)

    def cot_copy(step):
        return pltpu.make_async_copy(cot_all.at[block_rows(block_of(step)[2])], cot_v, cot_sem)

    def y_copy(block):
        return pltpu.make_async_copy(y_v, y_all.at[block], out_sem.at[3])

    def out_copies(block):
        return [
            pltpu.make_async_copy(hidden_v, hidden_all.at[block_rows(block)], out_sem.at[0]),
            pltpu.make_async_copy(gate_b, grads_all.at[0, block_rows(block)], out_sem.at[1]),
            pltpu.make_async_copy(up_b, grads_all.at[1, block_rows(block)], out_sem.at[2]),
        ]

    cot_copy(0).start()
    own_copy.wait()
    for copy in weight_copies:
        copy.wait()

    def one_step(step, carry):
        k, side, block = block_of(step)

        @pl.when(step == 1)
        def _():
            arrive(1)

            @pl.when(middle)
            def _():
                arrive(2)

            arrived(z * 2 + 1 - x)

            @pl.when(ends)
            def _():
                forward_cross().start()

        @pl.when(step == 3)
        def _():
            @pl.when(ends)
            def _():
                arrive(2)

            @pl.when(middle)
            def _():
                arrive(3)

            arrived(slot_z(1) * 2 + 1 - x)

        @pl.when(step == 5)
        def _():
            arrived(slot_z(2) * 2 + 1 - x)

        @pl.when((step == 6) & ends)
        def _():
            arrived(slot_z(3) * 2 + 1 - x)

        @pl.when((step == 7) & ends)
        def _():
            arrive(3)

        @pl.when(step > 0)
        def _():
            for copy in out_copies(block):
                copy.wait()

        cot_copy(step).wait()
        rows_low = rows_v[block_rows(block), :width]
        extra = rows_v[block_rows(block), width:].astype(jnp.float32)
        lane = lax.broadcasted_iota(jnp.int32, extra.shape, 1)
        ext = jnp.zeros(extra.shape, jnp.float32)
        for e in range(experts_local):
            expert = position * experts_local + e
            high = lane == expert
            low = lane == expert + experts_all
            weight = jnp.sum(jnp.where(high | low, extra, 0.0), axis=1, keepdims=True)
            gate_grad = jnp.zeros((rows, 1), jnp.float32)
            for f in range(hidden // 512):
                columns = pl.ds(f * 512, 512)
                gate_pre = jnp.dot(rows_low, gate_v[e, :, columns], preferred_element_type=jnp.float32)
                up_pre = jnp.dot(rows_low, up_v[e, :, columns], preferred_element_type=jnp.float32)
                target = pl.ds(e * hidden + f * 512, 512)
                raw = lax.dot_general(
                    cot_v[...],
                    down_v[e, columns, :],
                    contract_last,
                    preferred_element_type=jnp.float32,
                )
                sig = jax.nn.sigmoid(gate_pre)
                act = gate_pre * sig
                hid = act * up_pre
                gate_grad = gate_grad + jnp.sum(hid * raw, axis=1, keepdims=True)
                hidden_v[:, target] = (hid * weight).astype(jnp.bfloat16)
                grad = raw * weight
                gate_b[:, target] = (grad * up_pre * sig * (1.0 + gate_pre * (1.0 - sig))).astype(jnp.bfloat16)
                up_b[:, target] = (grad * act).astype(jnp.bfloat16)
            grad_high = gate_grad.astype(jnp.bfloat16).astype(jnp.float32)
            ext = jnp.where(high, grad_high, ext)
            ext = jnp.where(low, gate_grad - grad_high, ext)

        @pl.when(step < 7)
        def _():
            cot_copy(step + 1).start()

        @pl.when((step == 4) & middle)
        def _():
            arrived(slot_z(3) * 2 + 1 - x)
            forward_cross().start()

        place = side * 4 + k
        parts[place, :, width:] = ext.astype(jnp.bfloat16)
        for copy in out_copies(block):
            copy.start()
        for d in range(width // 1024):
            span = pl.ds(d * 1024, 1024)
            summed = jnp.zeros((rows, 1024), jnp.float32)
            for e in range(experts_local):
                target = pl.ds(e * hidden, hidden)
                summed = summed + lax.dot_general(
                    gate_b[:, target], gate_v[e, span, :], contract_last, preferred_element_type=jnp.float32
                )
                summed = summed + lax.dot_general(
                    up_b[:, target], up_v[e, span, :], contract_last, preferred_element_type=jnp.float32
                )
            parts[place, :, span] = summed.astype(jnp.bfloat16)

        @pl.when((side == 1) & (k > 1))
        def _():
            for c in range(chunks):
                side_copy(k, c).start()

        @pl.when(step == 3)
        def _():
            for c in range(chunks):
                cross_copy(c).start()

        @pl.when((step == 1) & ends)
        def _():
            for c in range(chunks):
                line_copy(1, c).start()

        @pl.when(step > 0)
        def _():
            y_copy(block).wait()

        for d in range(width // 1024):
            span = pl.ds(d * 1024, 1024)
            summed = jnp.zeros((rows, 1024), jnp.float32)
            for e in range(experts_local):
                summed = summed + jnp.dot(
                    hidden_v[:, pl.ds(e * hidden, hidden)],
                    down_v[e, :, span],
                    preferred_element_type=jnp.float32,
                )
            y_v[:, span] = summed.astype(jnp.bfloat16)
        y_copy(block).start()
        return carry

    lax.fori_loop(0, 8, one_step, 0)

    for copy in out_copies(position):
        copy.wait()
    y_copy(position).wait()
    whole_cot = [
        pltpu.make_async_copy(cot_all.at[:, pl.ds(h * hidden, hidden)], up_v.at[h], weight_sem.at[h])
        for h in range(2)
    ]
    for copy in whole_cot:
        copy.start()

    def columns_of(pair, q):
        column_y = jnp.where(q == 0, y, 1 - y)
        column_core = jnp.where(pair == 0, 1 - core, core)
        return column_y * 2 + column_core

    def item_source(i):
        pair = i // 6
        kind = (i % 6) // 2
        e = i % 2
        return pair, kind, e

    def item_loads(i, act):
        pair, kind, e = item_source(i)
        slot = i % 2
        for q in range(2):
            start = pl.multiple_of(e * hidden + columns_of(pair, q) * part, part)
            place = gate_v.at[0, :, pl.ds(pl.multiple_of(slot * 2 * part + q * part, part), part)]
            sem = item_in.at[slot, q]

            @pl.when(kind < 2)
            def _(start=start, place=place, sem=sem):
                act(
                    pltpu.make_async_copy(
                        grads_all.at[jnp.minimum(kind, 1), :, pl.ds(start, part)], place, sem
                    )
                )

            @pl.when(kind == 2)
            def _(start=start, place=place, sem=sem):
                act(pltpu.make_async_copy(hidden_all.at[:, pl.ds(start, part)], place, sem))

    def item_stores(i, act):
        pair, kind, e = item_source(i)
        slot = i % 2
        for q in range(2):
            wide_place = gate_v.at[1, :, pl.ds(pl.multiple_of(slot * 2 * part + q * part, part), part)]
            tall_place = down_v.at[slot, pl.ds(q * part, part)]
            sem = item_out.at[slot, q]
            for which, wide_out, tall_out in (
                (0, far_input, far_output),
                (1, near_input, near_output),
            ):

                @pl.when((pair == which) & (kind < 2))
                def _(wide_place=wide_place, sem=sem, wide_out=wide_out, q=q):
                    act(
                        pltpu.make_async_copy(wide_place, wide_out.at[jnp.minimum(kind, 1), q, e], sem)
                    )

                @pl.when((pair == which) & (kind == 2))
                def _(tall_place=tall_place, sem=sem, tall_out=tall_out, q=q):
                    act(pltpu.make_async_copy(tall_place, tall_out.at[q, e], sem))

    item_loads(0, lambda copy: copy.start())
    for copy in whole_cot:
        copy.wait()

    def at(index, first, gap):
        return (index >= first) & (index < first + gap * chunks) & ((index - first) % gap == 0)

    def item(index, carry):
        i = index // 4
        d = index % 4
        kind = (i % 6) // 2
        slot = i % 2

        @pl.when(d == 0)
        def _():
            item_loads(i, lambda copy: copy.wait())

            @pl.when(i < 11)
            def _():
                item_loads(i + 1, lambda copy: copy.start())

            @pl.when(i > 1)
            def _():
                item_stores(i - 2, lambda copy: copy.wait())

        columns = pl.ds(pl.multiple_of(slot * 2 * part, 2 * part), 2 * part)
        span = pl.ds(pl.multiple_of(d * (width // 4), width // 4), width // 4)

        @pl.when(kind < 2)
        def _():
            gate_v[1, span, columns] = lax.dot_general(
                rows_v[:, span], gate_v[0, :, columns], contract_first, preferred_element_type=jnp.float32
            ).astype(jnp.bfloat16)

        @pl.when(kind == 2)
        def _():
            half = pl.ds(pl.multiple_of((d % 2) * (hidden // 2), hidden // 2), hidden // 2)
            down_v[slot, : 2 * part, span] = lax.dot_general(
                gate_v[0, :, columns],
                up_v[d // 2, :, half],
                contract_first,
                preferred_element_type=jnp.float32,
            ).astype(jnp.bfloat16)

        @pl.when(d == 3)
        def _():
            item_stores(i, lambda copy: copy.start())

        @pl.when(at(index, 1, 1))
        def _():
            cross_add(index - 1)

        @pl.when(at(index, 5, 4))
        def _():
            relay(3, (index - 5) // 4)

        @pl.when(at(index, 11, 4) & middle)
        def _():
            relay(1, (index - 11) // 4)

        @pl.when(at(index, 18, 1) & ends)
        def _():
            relay(2, index - 18)

        @pl.when(at(index, 24, 4) & middle)
        def _():
            relay(2, (index - 24) // 4)

        return carry

    lax.fori_loop(0, 48, item, 0)
    for last in (10, 11):
        item_stores(last, lambda copy: copy.wait())

    def finish(c, carry):
        area = pl.ds(c * chunk, chunk)
        side_copy(0, c).wait_recv()
        stage[...] = parts[0, area].astype(jnp.float32) + side_in[0, area].astype(jnp.float32)

        @pl.when(z < 3)
        def _():
            line_wait(z, c)
            stage[...] += line_in[z, area].astype(jnp.float32)

        @pl.when(z > 0)
        def _():
            line_wait(z + 1, c)
            stage[...] += line_in[z + 1, area].astype(jnp.float32)

        result = pltpu.make_async_copy(stage, total.at[area], own_sem)
        result.start()
        result.wait()
        for k in (0, 2, 3):
            side_copy(k, c).wait_send()
        cross_copy(c).wait_send()
        for k in range(1, 4):
            line_copy(k, c).wait_send()
        return carry

    lax.fori_loop(0, chunks, finish, 0)

    own_send(0, z, 1 - x).wait_send()

    @pl.when(z < 3)
    def _():
        own_send(1, z + 1, x).wait_send()

    @pl.when(z > 0)
    def _():
        own_send(2, z - 1, x).wait_send()

    forward_cross().wait_send()
    forward_side(2).wait_send()

    @pl.when(ends)
    def _():
        forward_side(1).wait_send()

    @pl.when(middle)
    def _():
        forward_side(3).wait_send()
        for k in range(1, 4):
            forward_line(k).wait_send()


def expert_pass(own_rows, cot_all, gate_w, up_w, down_w, experts_all, collective):
    rows, wide = own_rows.shape
    experts_local, width, hidden = gate_w.shape
    inner = experts_local * hidden
    any_space = pl.BlockSpec(memory_space=pl.ANY)
    low = jnp.bfloat16
    dma = pltpu.SemaphoreType.DMA
    return pl.pallas_call(
        functools.partial(expert_kernel, experts_all),
        name="expert_pass",
        out_shape=(
            jax.ShapeDtypeStruct((8 * rows, inner), low),
            jax.ShapeDtypeStruct((2, 8 * rows, inner), low),
            jax.ShapeDtypeStruct((8, rows, width), low),
            jax.ShapeDtypeStruct((rows, wide), jnp.float32),
            *(jax.ShapeDtypeStruct((2, 2, experts_local, width, hidden // 4), low),) * 2,
            *(jax.ShapeDtypeStruct((2, experts_local, hidden // 4, width), low),) * 2,
        ),
        in_specs=[any_space] * 5,
        out_specs=(any_space,) * 8,
        scratch_shapes=[
            pltpu.VMEM((experts_local, width, hidden), low),
            pltpu.VMEM((experts_local, width, hidden), low),
            pltpu.VMEM((experts_local, hidden, width), low),
            pltpu.VMEM((8 * rows, wide), low),
            pltpu.VMEM((rows, width), low),
            pltpu.VMEM((rows, inner), low),
            pltpu.VMEM((rows, inner), low),
            pltpu.VMEM((rows, inner), low),
            pltpu.VMEM((rows, width), low),
            pltpu.VMEM((rows // chunks, wide), jnp.float32),
            pltpu.VMEM((8, rows, wide), low),
            pltpu.VMEM((3, rows, wide), low),
            pltpu.VMEM((rows, wide), low),
            pltpu.VMEM((5, rows, wide), low),
            dma((3,)),
            dma,
            dma,
            dma((4,)),
            dma((2, 2)),
            dma((2, 2)),
            dma((8,)),
            dma((10,)),
            dma((3, chunks)),
            dma((3, chunks)),
            dma((chunks,)),
            dma((chunks,)),
            dma((5, chunks)),
            dma((3, chunks)),
        ],
        compiler_params=pltpu.CompilerParams(
            collective_id=collective, has_side_effects=True, vmem_limit_bytes=60 << 20
        ),
        cost_estimate=pl.CostEstimate(
            flops=2 * 9 * 8 * rows * width * inner, bytes_accessed=64 << 20, transcendentals=8 * rows * inner
        ),
    )(own_rows, cot_all, gate_w, up_w, down_w)


def line_gather(source, target, recv, send):
    position = lax.axis_index("expert")
    peer = lax.axis_index("tensor")
    z = position // 2
    x = position % 2
    middle = (z == 1) | (z == 2)
    slots = [z, pick(z, [1, 0, 3, 2]), pick(z, [2, 2, 1, 1]), pick(z, [3, 3, 0, 0])]

    def copy(block_source, block, index, zz, xx):
        return pltpu.make_async_remote_copy(
            src_ref=block_source,
            dst_ref=target.at[block],
            send_sem=send.at[index],
            recv_sem=recv.at[block],
            device_id=(zz * 2 + xx, peer),
            device_id_type=pl.DeviceIdType.MESH,
        )

    def own_up():
        return copy(source, position, 1, z + 1, x)

    def own_down():
        return copy(source, position, 2, z - 1, x)

    def own_side():
        return copy(source, position, 0, z, 1 - x)

    def side(k):
        block = slots[k] * 2 + x
        return copy(target.at[block], block, 2 + k, z, 1 - x)

    def line(k):
        block = slots[k] * 2 + x
        onward = jnp.where(slots[k] < z, z + 1, z - 1)
        return copy(target.at[block], block, 5 + k, jnp.clip(onward, 0, 3), x)

    def start():
        own_side().start()

        @pl.when(z < 3)
        def _():
            own_up().start()

        @pl.when(z > 0)
        def _():
            own_down().start()

    def wait_block(block):
        copy(source, block, 0, z, 1 - x).wait_recv()

    def arrive(k):
        wait_block(slots[k] * 2 + x)
        side(k).start()

        @pl.when(middle)
        def _():
            line(k).start()

    def arrive_side(k):
        wait_block(slots[k] * 2 + 1 - x)

    def drain():
        own_side().wait_send()

        @pl.when(z < 3)
        def _():
            own_up().wait_send()

        @pl.when(z > 0)
        def _():
            own_down().wait_send()

        for k in range(1, 4):
            side(k).wait_send()

            @pl.when(middle)
            def _(k=k):
                line(k).wait_send()

    return middle, start, arrive, arrive_side, drain


def attention_kernel(
    own,
    cot,
    query_w,
    key_w,
    value_w,
    out_w,
    query_gain,
    key_gain,
    cosine,
    sine,
    gathered,
    query_unit,
    key_unit,
    query_low,
    key_low,
    value_low,
    attended,
    log_sums,
    attn_sum,
    cot_all,
    rows_v,
    weights_v,
    out_v,
    pre_v,
    low_v,
    mixed_v,
    log_v,
    parts,
    own_part,
    core_in,
    line_in,
    load_sem,
    store_sem,
    rows_recv,
    rows_send,
    part_recv,
    part_send,
    cot_recv,
    cot_send,
    cot_sem,
):
    position = lax.axis_index("expert")
    t = lax.axis_index("tensor")
    z = position // 2
    x = position % 2
    y = t // 2
    c = t % 2
    near = y * 2 + 1 - c
    across = (1 - y) * 2 + c
    opposite = (1 - y) * 2 + 1 - c
    rows = own.shape[0]
    heads = low_v.shape[2] // 128
    factor = 1.0 / math.sqrt(128.0)
    mesh_ids = pl.DeviceIdType.MESH
    middle, gather_start, gather_arrive, gather_side, gather_drain = line_gather(
        cot, cot_all, cot_recv, cot_send
    )

    loads = [
        pltpu.make_async_copy(own, rows_v.at[t], load_sem.at[0]),
        pltpu.make_async_copy(query_w, weights_v.at[0], load_sem.at[1]),
        pltpu.make_async_copy(key_w, weights_v.at[1], load_sem.at[2]),
        pltpu.make_async_copy(value_w, weights_v.at[2], load_sem.at[3]),
        pltpu.make_async_copy(out_w, out_v, load_sem.at[4]),
    ]
    for load in loads:
        load.start()
    cot_copy = pltpu.make_async_copy(cot, cot_all.at[position], cot_sem)
    cot_copy.start()

    barrier = pltpu.get_barrier_semaphore()
    for place in ((position, near), (position, across), (z * 2 + 1 - x, t)):
        pl.semaphore_signal(barrier, inc=1, device_id=place, device_id_type=mesh_ids)

    @pl.when(z < 3)
    def _():
        pl.semaphore_signal(barrier, inc=1, device_id=(position + 2, t), device_id_type=mesh_ids)

    @pl.when(z > 0)
    def _():
        pl.semaphore_signal(barrier, inc=1, device_id=(position - 2, t), device_id_type=mesh_ids)

    pl.semaphore_wait(barrier, 4 + middle.astype(jnp.int32))

    def rows_copy(source, block, index, to):
        return pltpu.make_async_remote_copy(
            src_ref=source,
            dst_ref=rows_v.at[block],
            send_sem=rows_send.at[index - 1],
            recv_sem=rows_recv.at[index - 1],
            device_id=(position, to),
            device_id_type=mesh_ids,
        )

    to_across = rows_copy(own, t, 2, across)
    to_near = rows_copy(own, t, 1, near)
    forward = rows_copy(rows_v.at[across], across, 3, near)
    to_across.start()
    to_near.start()
    gather_start()
    for load in loads:
        load.wait()

    def project(i, carry):
        block = pick(i, [t, near, across, opposite])

        @pl.when(i == 1)
        def _():
            to_near.wait_recv()

        @pl.when(i == 2)
        def _():
            to_across.wait_recv()
            forward.start()
            gather_arrive(1)

            @pl.when(middle)
            def _():
                gather_arrive(2)

        @pl.when(i == 3)
        def _():
            forward.wait_recv()

        area = pl.ds(block * rows, rows)
        values = rows_v[block]
        for which, gain in ((0, query_gain), (1, key_gain)):
            pre = jnp.dot(values, weights_v[which], preferred_element_type=jnp.float32)
            for h in range(heads):
                span = slice(h * 128, (h + 1) * 128)
                head = pre[:, span]
                scale = lax.rsqrt(jnp.mean(head * head, axis=-1, keepdims=True) + epsilon)
                unit = head * scale
                pre_v[which, area, span] = unit.astype(jnp.bfloat16)
                lane = 4 + which * 4 + h
                log_v[area, lane : lane + 1] = scale
                normed = unit * gain[...]
                turned = normed * cosine[area] + pltpu.roll(normed, 64, 1) * sine[area]
                low_v[which, area, span] = turned.astype(jnp.bfloat16)
        low_v[2, area] = jnp.dot(
            values, weights_v[2], preferred_element_type=jnp.float32
        ).astype(jnp.bfloat16)
        return carry

    lax.fori_loop(0, 4, project, 0)
    stores = [
        pltpu.make_async_copy(rows_v, gathered, store_sem.at[0]),
        pltpu.make_async_copy(pre_v.at[0], query_unit, store_sem.at[1]),
        pltpu.make_async_copy(pre_v.at[1], key_unit, store_sem.at[2]),
        pltpu.make_async_copy(low_v.at[0], query_low, store_sem.at[3]),
        pltpu.make_async_copy(low_v.at[1], key_low, store_sem.at[4]),
        pltpu.make_async_copy(low_v.at[2], value_low, store_sem.at[5]),
    ]
    for store in stores:
        store.start()

    def part_copy(source, target, index, to):
        return pltpu.make_async_remote_copy(
            src_ref=source,
            dst_ref=target,
            send_sem=part_send.at[index],
            recv_sem=part_recv.at[index],
            device_id=(position, to),
            device_id_type=mesh_ids,
        )

    core_first = part_copy(parts.at[0], core_in.at[0], 0, near)
    line_copy = part_copy(parts.at[1], line_in, 1, across)
    core_second = part_copy(parts.at[2], core_in.at[1], 2, near)

    def attend(i, carry):
        block = pick(i, [opposite, across, near, t])
        area = pl.ds(block * rows, rows)
        for h in range(heads):
            span = slice(h * 128, (h + 1) * 128)
            scores = lax.dot_general(
                low_v[0, area, span], low_v[1, :, span], contract_last, preferred_element_type=jnp.float32
            )
            highest_score = jnp.max(scores, axis=-1, keepdims=True)
            weights = jnp.exp((scores - highest_score) * factor)
            total = jnp.sum(weights, axis=-1, keepdims=True)
            mixed = jnp.dot(
                weights.astype(jnp.bfloat16), low_v[2, :, span], preferred_element_type=jnp.float32
            )
            mixed_v[area, span] = (mixed / total).astype(jnp.bfloat16)
            log_v[area, h : h + 1] = highest_score * factor + jnp.log(total)
        own_part[...] = jnp.dot(mixed_v[area], out_v[...], preferred_element_type=jnp.float32)

        @pl.when(i == 0)
        def _():
            parts[0] = own_part[...].astype(jnp.bfloat16)
            core_first.start()

        @pl.when(i == 1)
        def _():
            core_first.wait_recv()
            parts[1] = (own_part[...] + core_in[0].astype(jnp.float32)).astype(jnp.bfloat16)
            line_copy.start()

            @pl.when(middle)
            def _():
                gather_arrive(3)

        @pl.when(i == 2)
        def _():
            parts[2] = own_part[...].astype(jnp.bfloat16)
            core_second.start()

            @pl.when(middle == False)
            def _():
                gather_arrive(2)

        return carry

    lax.fori_loop(0, 4, attend, 0)
    more = [
        pltpu.make_async_copy(mixed_v, attended, store_sem.at[6]),
        pltpu.make_async_copy(log_v, log_sums, store_sem.at[7]),
    ]
    for store in more:
        store.start()
    core_second.wait_recv()
    own_part[...] += core_in[1].astype(jnp.float32)
    line_copy.wait_recv()
    own_part[...] += line_in[...].astype(jnp.float32)
    last = pltpu.make_async_copy(own_part, attn_sum, store_sem.at[8])
    last.start()

    @pl.when(middle == False)
    def _():
        gather_arrive(3)

    for k in range(4):
        gather_side(k)
    gather_drain()
    for copy in (to_across, to_near, forward, core_first, line_copy, core_second):
        copy.wait_send()
    for store in [*stores, *more, last, cot_copy]:
        store.wait()


def attention_forward(own, cot, weights, out_w, gains, tables, collective):
    rows, width = own.shape
    local = out_w.shape[0]
    length = 4 * rows
    any_space = pl.BlockSpec(memory_space=pl.ANY)
    vector = pl.BlockSpec(memory_space=pltpu.VMEM)
    low, full = jnp.bfloat16, jnp.float32
    dma = pltpu.SemaphoreType.DMA
    return pl.pallas_call(
        attention_kernel,
        name="attention_forward",
        out_shape=(
            jax.ShapeDtypeStruct((4, rows, width), low),
            jax.ShapeDtypeStruct((length, local), low),
            jax.ShapeDtypeStruct((length, local), low),
            jax.ShapeDtypeStruct((length, local), low),
            jax.ShapeDtypeStruct((length, local), low),
            jax.ShapeDtypeStruct((length, local), low),
            jax.ShapeDtypeStruct((length, local), low),
            jax.ShapeDtypeStruct((length, 128), full),
            jax.ShapeDtypeStruct((rows, width), full),
            jax.ShapeDtypeStruct((8, rows, width), low),
        ),
        in_specs=[any_space] * 6 + [vector] * 4,
        out_specs=(any_space,) * 10,
        scratch_shapes=[
            pltpu.VMEM((4, rows, width), low),
            pltpu.VMEM((3, width, local), low),
            pltpu.VMEM((local, width), low),
            pltpu.VMEM((2, length, local), low),
            pltpu.VMEM((3, length, local), low),
            pltpu.VMEM((length, local), low),
            pltpu.VMEM((length, 128), full),
            pltpu.VMEM((3, rows, width), low),
            pltpu.VMEM((rows, width), full),
            pltpu.VMEM((2, rows, width), low),
            pltpu.VMEM((rows, width), low),
            dma((5,)),
            dma((9,)),
            dma((3,)),
            dma((3,)),
            dma((3,)),
            dma((3,)),
            dma((8,)),
            dma((9,)),
            dma,
        ],
        compiler_params=pltpu.CompilerParams(
            collective_id=collective, has_side_effects=True, vmem_limit_bytes=60 << 20
        ),
        cost_estimate=pl.CostEstimate(
            flops=8 * length * width * local, bytes_accessed=64 << 20, transcendentals=length * length * 4
        ),
    )(own, cot, *weights, out_w, *gains, *tables)


def attention_back_kernel(
    branch,
    gathered,
    query_unit,
    key_unit,
    query_low,
    key_low,
    value_low,
    attended,
    log_sums,
    query_w,
    key_w,
    value_w,
    out_w,
    query_gain,
    key_gain,
    cosine,
    sine,
    rows_grad,
    out_total,
    value_total,
    key_total,
    query_total,
    gain_sums,
    branch_v,
    rows_v,
    weights_v,
    out_v,
    unit_v,
    low_v,
    log_v,
    grads_v,
    key_acc,
    value_acc,
    scattered,
    side_in,
    line_in,
    own_part,
    core_in,
    across_in,
    load_sem,
    store_sem,
    branch_recv,
    branch_send,
    part_recv,
    part_send,
    side_recv,
    side_send,
    line_recv,
    line_send,
):
    position = lax.axis_index("expert")
    t = lax.axis_index("tensor")
    z = position // 2
    x = position % 2
    y = t // 2
    core = t % 2
    near = y * 2 + 1 - core
    across = (1 - y) * 2 + core
    opposite = (1 - y) * 2 + 1 - core
    rows = branch.shape[0]
    local = out_v.shape[0]
    heads = local // 128
    kinds = scattered.shape[0]
    factor = 1.0 / math.sqrt(128.0)
    middle = (z == 1) | (z == 2)
    mesh_ids = pl.DeviceIdType.MESH
    slots = [z, pick(z, [1, 0, 3, 2]), pick(z, [2, 2, 1, 1]), pick(z, [3, 3, 0, 0])]

    loads = [
        pltpu.make_async_copy(branch, branch_v.at[t], load_sem.at[0]),
        pltpu.make_async_copy(out_w, out_v, load_sem.at[1]),
        pltpu.make_async_copy(query_low, low_v.at[0], load_sem.at[2]),
        pltpu.make_async_copy(key_low, low_v.at[1], load_sem.at[3]),
        pltpu.make_async_copy(value_low, low_v.at[2], load_sem.at[4]),
        pltpu.make_async_copy(log_sums, log_v, load_sem.at[5]),
        pltpu.make_async_copy(query_unit, unit_v.at[0], load_sem.at[6]),
        pltpu.make_async_copy(key_unit, unit_v.at[1], load_sem.at[7]),
        pltpu.make_async_copy(attended, low_v.at[3], load_sem.at[8]),
        pltpu.make_async_copy(gathered, rows_v, load_sem.at[9]),
        pltpu.make_async_copy(query_w, weights_v.at[0], load_sem.at[10]),
        pltpu.make_async_copy(key_w, weights_v.at[1], load_sem.at[11]),
        pltpu.make_async_copy(value_w, weights_v.at[2], load_sem.at[12]),
    ]
    for load in loads:
        load.start()

    barrier = pltpu.get_barrier_semaphore()
    for place in ((position, near), (position, across), (z * 2 + 1 - x, t)):
        pl.semaphore_signal(barrier, inc=1, device_id=place, device_id_type=mesh_ids)

    @pl.when(z < 3)
    def _():
        pl.semaphore_signal(barrier, inc=1, device_id=(position + 2, t), device_id_type=mesh_ids)

    @pl.when(z > 0)
    def _():
        pl.semaphore_signal(barrier, inc=1, device_id=(position - 2, t), device_id_type=mesh_ids)

    pl.semaphore_wait(barrier, 4 + middle.astype(jnp.int32))

    def branch_copy(source, block, index, to):
        return pltpu.make_async_remote_copy(
            src_ref=source,
            dst_ref=branch_v.at[block],
            send_sem=branch_send.at[index - 1],
            recv_sem=branch_recv.at[index - 1],
            device_id=(position, to),
            device_id_type=mesh_ids,
        )

    to_across = branch_copy(branch, t, 2, across)
    to_near = branch_copy(branch, t, 1, near)
    forward = branch_copy(branch_v.at[across], across, 3, near)
    to_across.start()
    to_near.start()

    def side_copy(k, c):
        return pltpu.make_async_remote_copy(
            src_ref=scattered.at[c, pick(k, slots) * 2 + 1 - x],
            dst_ref=side_in.at[c, k],
            send_sem=side_send.at[c, k],
            recv_sem=side_recv.at[c, k],
            device_id=(z * 2 + 1 - x, t),
            device_id_type=mesh_ids,
        )

    def line_slot(k):
        target = pick(k, slots)
        return jnp.where(target < z, target, target + 1)

    def line_copy(k, c):
        target = jnp.where(pick(k, slots) < z, z - 1, z + 1)
        return pltpu.make_async_remote_copy(
            src_ref=scattered.at[c, pick(k, slots) * 2 + x],
            dst_ref=line_in.at[c, line_slot(k)],
            send_sem=line_send.at[c, k - 1],
            recv_sem=line_recv.at[c, line_slot(k)],
            device_id=(jnp.clip(target, 0, 3) * 2 + x, t),
            device_id_type=mesh_ids,
        )

    def line_wait(slot, c):
        pltpu.make_async_remote_copy(
            src_ref=scattered.at[c, position],
            dst_ref=line_in.at[c, slot],
            send_sem=line_send.at[c, 0],
            recv_sem=line_recv.at[c, slot],
            device_id=(z * 2 + 1 - x, t),
            device_id_type=mesh_ids,
        ).wait_recv()

    def send_order(i):
        return jnp.where(middle, pick(i, [3, 1, 2, 0]), pick(i, [3, 2, 1, 0]))

    def start_side(c):
        def one(i, carry):
            side_copy(send_order(i), c).start()
            return carry

        lax.fori_loop(0, 4, one, 0)

    def weight_part(c, left, right):
        for d in range(8 // 2):
            span = pl.ds(d * 512, 512)
            product = jnp.zeros((512, local), jnp.float32)
            for b in range(4):
                product = product + lax.dot_general(
                    left[b, :, span],
                    right[pl.ds(b * rows, rows)],
                    contract_first,
                    preferred_element_type=jnp.float32,
                )
            scattered[c, 2 * d] = product[:256].astype(jnp.bfloat16)
            scattered[c, 2 * d + 1] = product[256:].astype(jnp.bfloat16)

    gain_sums[...] = jnp.zeros_like(gain_sums)
    for load in loads[:9]:
        load.wait()

    def norm_back(turned, which, area, h, gain):
        span = slice(h * 128, (h + 1) * 128)
        grad = turned * cosine[area] - pltpu.roll(turned, 64, 1) * sine[area]
        unit = unit_v[which, area, span].astype(jnp.float32)
        gain_sums[which : which + 1] += jnp.sum(grad * unit, axis=0, keepdims=True)
        weighted = grad * gain[...]
        inner = jnp.mean(weighted * unit, axis=-1, keepdims=True)
        lane = 4 + which * 4 + h
        grads_v[which, area, span] = (
            log_v[area, lane : lane + 1] * (weighted - unit * inner)
        ).astype(jnp.bfloat16)

    def attend(i, carry):
        block = pick(i, [t, near, across, opposite])

        @pl.when(i == 1)
        def _():
            to_near.wait_recv()

        @pl.when(i == 2)
        def _():
            to_across.wait_recv()
            forward.start()

        @pl.when(i == 3)
        def _():
            forward.wait_recv()
            weight_part(0, branch_v, low_v.at[3])
            start_side(0)

        area = pl.ds(block * rows, rows)
        mixed_grad = lax.dot_general(
            branch_v[block], out_v[...], contract_last, preferred_element_type=jnp.float32
        ).astype(jnp.bfloat16)
        for h in range(heads):
            span = slice(h * 128, (h + 1) * 128)
            query = low_v[0, area, span]
            key = low_v[1, :, span]
            grad = mixed_grad[:, span]
            scores = lax.dot_general(query, key, contract_last, preferred_element_type=jnp.float32)
            probs = jnp.exp(scores * factor - log_v[area, h : h + 1])
            prob_grad = lax.dot_general(
                grad, low_v[2, :, span], contract_last, preferred_element_type=jnp.float32
            )
            delta = jnp.sum(probs * prob_grad, axis=-1, keepdims=True)
            score_grad = (probs * (prob_grad - delta)).astype(jnp.bfloat16)
            query_grad = jnp.dot(score_grad, key, preferred_element_type=jnp.float32) * factor
            key_part = lax.dot_general(
                score_grad, query, contract_first, preferred_element_type=jnp.float32
            )
            value_part = lax.dot_general(
                probs.astype(jnp.bfloat16), grad, contract_first, preferred_element_type=jnp.float32
            )
            first = i == 0
            key_acc[:, span] = jnp.where(first, 0.0, key_acc[:, span]) + key_part
            value_acc[:, span] = jnp.where(first, 0.0, value_acc[:, span]) + value_part
            norm_back(query_grad, 0, area, h, query_gain)
        return carry

    key_acc[...] = jnp.zeros_like(key_acc)
    value_acc[...] = jnp.zeros_like(value_acc)
    lax.fori_loop(0, 4, attend, 0)
    for load in loads[9:]:
        load.wait()
    grads_v[2] = value_acc[...].astype(jnp.bfloat16)
    weight_part(1, rows_v, grads_v.at[2])
    start_side(1)

    def key_back(b, carry):
        area = pl.ds(b * rows, rows)
        for h in range(heads):
            norm_back(key_acc[area, h * 128 : (h + 1) * 128] * factor, 1, area, h, key_gain)
        return carry

    lax.fori_loop(0, 4, key_back, 0)
    weight_part(2, rows_v, grads_v.at[1])
    start_side(2)
    weight_part(3, rows_v, grads_v.at[0])
    start_side(3)

    def part_copy(source, target, index, to):
        return pltpu.make_async_remote_copy(
            src_ref=source,
            dst_ref=target,
            send_sem=part_send.at[index],
            recv_sem=part_recv.at[index],
            device_id=(position, to),
            device_id_type=mesh_ids,
        )

    for copy in (to_across, to_near, forward):
        copy.wait_send()
    core_first = part_copy(branch_v.at[0], core_in.at[0], 0, near)
    across_copy = part_copy(branch_v.at[1], across_in, 1, across)
    core_second = part_copy(branch_v.at[2], core_in.at[1], 2, near)

    def relay(k, c):
        block = pick(k, slots) * 2 + x
        side_copy(k, c).wait_recv()
        scattered[c, block] = (
            scattered[c, block].astype(jnp.float32) + side_in[c, k].astype(jnp.float32)
        ).astype(jnp.bfloat16)

        @pl.when(middle)
        def _():
            line_wait(line_slot(k), c)
            scattered[c, block] = (
                scattered[c, block].astype(jnp.float32) + line_in[c, line_slot(k)].astype(jnp.float32)
            ).astype(jnp.bfloat16)

        line_copy(k, c).start()

    def relays(c):
        def one(i, carry):
            relay(send_order(i), c)
            return carry

        lax.fori_loop(0, 3, one, 0)

    def rows_part(i, carry):
        block = pick(i, [opposite, across, near, t])
        area = pl.ds(block * rows, rows)
        for d in range(2):
            span = pl.ds(d * 1024, 1024)
            product = jnp.zeros((rows, 1024), jnp.float32)
            for which in range(3):
                product = product + lax.dot_general(
                    grads_v[which, area],
                    weights_v[which, span],
                    contract_last,
                    preferred_element_type=jnp.float32,
                )
            own_part[:, span] = product

        @pl.when(i == 0)
        def _():
            branch_v[0] = own_part[...].astype(jnp.bfloat16)
            core_first.start()

        @pl.when(i == 1)
        def _():
            core_first.wait_recv()
            branch_v[1] = (own_part[...] + core_in[0].astype(jnp.float32)).astype(jnp.bfloat16)
            across_copy.start()

        @pl.when(i == 2)
        def _():
            branch_v[2] = own_part[...].astype(jnp.bfloat16)
            core_second.start()

        return carry

    lax.fori_loop(0, 4, rows_part, 0)
    relays(0)
    relays(1)
    core_second.wait_recv()
    own_part[...] += core_in[1].astype(jnp.float32)
    across_copy.wait_recv()
    own_part[...] += across_in[...].astype(jnp.float32)
    last = pltpu.make_async_copy(own_part, rows_grad, store_sem)
    last.start()
    relays(2)
    relays(3)
    for c, total in enumerate((out_total, value_total, key_total, query_total)):
        side_copy(0, c).wait_recv()
        total[...] = scattered[c, position].astype(jnp.float32) + side_in[c, 0].astype(jnp.float32)

        @pl.when(z < 3)
        def _(c=c, total=total):
            line_wait(z, c)
            total[...] += line_in[c, z].astype(jnp.float32)

        @pl.when(z > 0)
        def _(c=c, total=total):
            line_wait(z + 1, c)
            total[...] += line_in[c, z + 1].astype(jnp.float32)

        for k in range(4):
            side_copy(k, c).wait_send()
        for k in range(1, 4):
            line_copy(k, c).wait_send()
    for copy in (core_first, across_copy, core_second):
        copy.wait_send()
    last.wait()


def attention_backward(branch, saved, weights, out_w, gains, tables, collective):
    rows, width = branch.shape
    local = out_w.shape[0]
    length = 4 * rows
    any_space = pl.BlockSpec(memory_space=pl.ANY)
    vector = pl.BlockSpec(memory_space=pltpu.VMEM)
    low, full = jnp.bfloat16, jnp.float32
    dma = pltpu.SemaphoreType.DMA
    return pl.pallas_call(
        attention_back_kernel,
        name="attention_backward",
        out_shape=(jax.ShapeDtypeStruct((rows, width), full),)
        + (jax.ShapeDtypeStruct((width // 8, local), full),) * 4
        + (jax.ShapeDtypeStruct((8, 128), full),),
        in_specs=[any_space] * 13 + [vector] * 4,
        out_specs=(any_space,) + (vector,) * 5,
        scratch_shapes=[
            pltpu.VMEM((4, rows, width), low),
            pltpu.VMEM((4, rows, width), low),
            pltpu.VMEM((3, width, local), low),
            pltpu.VMEM((local, width), low),
            pltpu.VMEM((2, length, local), low),
            pltpu.VMEM((4, length, local), low),
            pltpu.VMEM((length, 128), full),
            pltpu.VMEM((3, length, local), low),
            pltpu.VMEM((length, local), full),
            pltpu.VMEM((length, local), full),
            pltpu.VMEM((4, 8, width // 8, local), low),
            pltpu.VMEM((4, 4, width // 8, local), low),
            pltpu.VMEM((4, 5, width // 8, local), low),
            pltpu.VMEM((rows, width), full),
            pltpu.VMEM((2, rows, width), low),
            pltpu.VMEM((rows, width), low),
            dma((13,)),
            dma,
            dma((3,)),
            dma((3,)),
            dma((3,)),
            dma((3,)),
            dma((4, 4)),
            dma((4, 4)),
            dma((4, 5)),
            dma((4, 3)),
        ],
        compiler_params=pltpu.CompilerParams(
            collective_id=collective, has_side_effects=True, vmem_limit_bytes=60 << 20
        ),
        cost_estimate=pl.CostEstimate(
            flops=16 * length * width * local, bytes_accessed=64 << 20, transcendentals=length * length * 4
        ),
    )(branch, *saved, *weights, out_w, *gains, *tables)


def sum_kernel(own, total, incoming, recv, send):
    position = lax.axis_index("expert")
    peer = lax.axis_index("tensor")
    mesh_ids = pl.DeviceIdType.MESH

    def flip(index, bit):
        return index + bit - 2 * bit * ((index // bit) % 2)

    partners = [
        (position, flip(peer, 1)),
        (position, flip(peer, 2)),
        (flip(position, 1), peer),
        (flip(position, 2), peer),
        (flip(position, 4), peer),
    ]
    barrier = pltpu.get_barrier_semaphore()
    for partner in partners:
        pl.semaphore_signal(barrier, inc=1, device_id=partner, device_id_type=mesh_ids)
    pl.semaphore_wait(barrier, len(partners))
    total[0] = own[...]
    for i, partner in enumerate(partners):
        copy = pltpu.make_async_remote_copy(
            src_ref=total.at[i],
            dst_ref=incoming.at[i],
            send_sem=send.at[i],
            recv_sem=recv.at[i],
            device_id=partner,
            device_id_type=mesh_ids,
        )
        copy.start()
        copy.wait()
        total[i + 1] = total[i] + incoming[i]


def sum_everywhere(own, collective):
    steps = 5
    return pl.pallas_call(
        sum_kernel,
        name="sum_everywhere",
        out_shape=jax.ShapeDtypeStruct((steps + 1,) + own.shape, jnp.float32),
        in_specs=[pl.BlockSpec(memory_space=pltpu.VMEM)],
        out_specs=pl.BlockSpec(memory_space=pltpu.VMEM),
        scratch_shapes=[
            pltpu.VMEM((steps,) + own.shape, jnp.float32),
            pltpu.SemaphoreType.DMA((steps,)),
            pltpu.SemaphoreType.DMA((steps,)),
        ],
        compiler_params=pltpu.CompilerParams(collective_id=collective, has_side_effects=True),
        cost_estimate=pl.CostEstimate(flops=own.size * steps, bytes_accessed=40 << 20, transcendentals=0),
    )(own)[steps]


def exchange(pieces_far, pieces_near, axis):
    swap_core = [(0, 1), (1, 0), (2, 3), (3, 2)]
    swap_line = [(0, 2), (1, 3), (2, 0), (3, 1)]
    arrived = lax.ppermute(pieces_far, "tensor", swap_core)
    summed = pieces_near.astype(jnp.float32) + arrived.astype(jnp.float32)
    own = lax.index_in_dim(summed, 0, axis, keepdims=False)
    sent = lax.index_in_dim(summed, 1, axis, keepdims=False).astype(jnp.bfloat16)
    return own + lax.ppermute(sent, "tensor", swap_line).astype(jnp.float32)


def per_device(
    tokens,
    cotangent,
    routes,
    norm_in,
    query_w,
    key_w,
    value_w,
    out_w,
    query_gain,
    key_gain,
    norm_mid,
    router_w,
    gate_w,
    up_w,
    down_w,
):
    rows_own = tokens.shape[0]
    model_width = tokens.shape[1]
    expert_count = lax.axis_size("expert")
    head_width = query_gain.shape[0]
    experts_all = router_w.shape[1]
    source = tokens.astype(jnp.float32)
    scale_in = inverse_rms(source)
    normed_low = (source * scale_in * norm_in).astype(jnp.bfloat16)
    cosine, sine_table = rotary_tables(4 * rows_own, head_width)
    tables = (
        jnp.concatenate([cosine[:, 0], cosine[:, 0]], axis=1),
        jnp.concatenate([-sine_table[:, 0], sine_table[:, 0]], axis=1),
    )
    gains = (query_gain[None], key_gain[None])
    *saved, attn_out, cot_all = attention_forward(
        normed_low, cotangent, (query_w, key_w, value_w), out_w, gains, tables, 1
    )
    middle = source + attn_out
    scale_mid = inverse_rms(middle)
    normed_mid = middle * scale_mid * norm_mid
    mid_low = normed_mid.astype(jnp.bfloat16)
    logits = jnp.dot(normed_mid, router_w, precision=highest, preferred_element_type=jnp.float32)
    route_mask = routes[:, :, None] == jnp.arange(experts_all, dtype=jnp.int32)[None, None, :]
    mask_float = route_mask.astype(jnp.float32)
    chosen = jnp.sum(mask_float * logits[:, None, :], axis=-1)
    gating = jax.nn.softmax(chosen, axis=-1)
    gates = jnp.sum(mask_float * gating[:, :, None], axis=1)
    gates_high = gates.astype(jnp.bfloat16)
    gates_low = (gates - gates_high.astype(jnp.float32)).astype(jnp.bfloat16)
    spare = jnp.zeros((rows_own, 128 - 2 * experts_all), jnp.bfloat16)
    own_rows = jnp.concatenate([mid_low, gates_high, gates_low, spare], axis=1)
    _, _, y_all, row_total, far_input, near_input, far_output, near_output = expert_pass(
        own_rows, cot_all.reshape(-1, model_width), gate_w, up_w, down_w, experts_all, 2
    )
    expert_input_grad = row_total[:, :model_width]
    gate_grad_dense = (
        row_total[:, model_width : model_width + experts_all]
        + row_total[:, model_width + experts_all : model_width + 2 * experts_all]
    )
    gate_grad = jnp.sum(mask_float * gate_grad_dense[:, None, :], axis=-1)
    inner_gate = jnp.sum(gating * gate_grad, axis=-1, keepdims=True)
    chosen_grad = gating * (gate_grad - inner_gate)
    logit_grad = jnp.sum(chosen_grad[:, :, None] * mask_float, axis=1)
    normed_mid_grad = expert_input_grad + lax.dot_general(
        logit_grad, router_w, contract_last, precision=highest, preferred_element_type=jnp.float32
    )
    norm_mid_part = jnp.sum(normed_mid_grad * middle * scale_mid, axis=0)
    upstream = cotangent.astype(jnp.float32)
    middle_grad = upstream + norm_backward(normed_mid_grad, middle, scale_mid, norm_mid)
    branch_low = middle_grad.astype(jnp.bfloat16)
    rows_grad, out_w_turned, value_w_grad, key_w_grad, query_w_grad, gain_sums = attention_backward(
        branch_low, saved, (query_w, key_w, value_w), out_w, gains, tables, 3
    )
    out_w_grad = out_w_turned.T
    router_part = lax.dot_general(
        normed_mid,
        logit_grad,
        contract_first,
        precision=highest,
        preferred_element_type=jnp.float32,
    )
    y_sum = lax.psum_scatter(
        y_all.reshape(expert_count * rows_own, model_width),
        "expert",
        scatter_dimension=0,
        tiled=True,
    )
    output = (middle + y_sum.astype(jnp.float32)).astype(jnp.bfloat16)
    input_parts = exchange(far_input, near_input, 1)
    gate_w_grad, up_w_grad = input_parts[0], input_parts[1]
    down_w_grad = exchange(far_output, near_output, 0)
    norm_in_part = jnp.sum(rows_grad * source * scale_in, axis=0)
    input_grad = middle_grad + norm_backward(rows_grad, source, scale_in, norm_in)
    router_w_grad = lax.psum(router_part, ("expert", "tensor"))
    small = jnp.concatenate(
        [
            norm_in_part,
            norm_mid_part,
            gain_sums[0],
            gain_sums[1],
            jnp.zeros((-(2 * model_width + 2 * head_width) % 1024,), jnp.float32),
        ]
    ).reshape(-1, 128)
    sums = sum_everywhere(small, 4).reshape(-1)
    norm_in_grad = sums[:model_width]
    norm_mid_grad = sums[model_width : 2 * model_width]
    query_gain_grad = sums[2 * model_width : 2 * model_width + head_width]
    key_gain_grad = sums[2 * model_width + head_width : 2 * model_width + 2 * head_width]
    return (
        output,
        input_grad,
        norm_in_grad,
        query_w_grad,
        key_w_grad,
        value_w_grad,
        out_w_grad,
        query_gain_grad,
        key_gain_grad,
        norm_mid_grad,
        router_w_grad,
        gate_w_grad,
        up_w_grad,
        down_w_grad,
    )


def per_device_general(
    tokens,
    cotangent,
    routes,
    norm_in,
    query_w,
    key_w,
    value_w,
    out_w,
    query_gain,
    key_gain,
    norm_mid,
    router_w,
    gate_w,
    up_w,
    down_w,
):
    rows_own = tokens.shape[0]
    model_width = tokens.shape[1]
    tensor_count = lax.axis_size("tensor")
    expert_count = lax.axis_size("expert")
    head_width = query_gain.shape[0]
    local_heads = query_w.shape[1] // head_width
    experts_local = gate_w.shape[0]
    experts_all = router_w.shape[1]
    top_count = routes.shape[1]
    hidden_width = gate_w.shape[2]
    factor = 1.0 / math.sqrt(head_width)
    cot_all = lax.all_gather(cotangent, "expert", axis=0, tiled=True)
    source = tokens.astype(jnp.float32)
    scale_in = inverse_rms(source)
    normed_low = (source * scale_in * norm_in).astype(jnp.bfloat16)
    gathered = lax.all_gather(normed_low, "tensor", axis=0, tiled=True)
    seq_len = gathered.shape[0]
    query_pre = jnp.dot(gathered, query_w, preferred_element_type=jnp.float32)
    key_pre = jnp.dot(gathered, key_w, preferred_element_type=jnp.float32)
    value_low = jnp.dot(gathered, value_w, preferred_element_type=jnp.float32).astype(jnp.bfloat16)
    cosine, sine_table = rotary_tables(seq_len, head_width)
    query_heads = query_pre.reshape(seq_len, local_heads, head_width)
    key_heads = key_pre.reshape(seq_len, local_heads, head_width)
    query_scale = inverse_rms(query_heads)
    key_scale = inverse_rms(key_heads)
    query_low = rotate(query_heads * query_scale * query_gain, cosine, sine_table).astype(
        jnp.bfloat16
    )
    key_low = rotate(key_heads * key_scale * key_gain, cosine, sine_table).astype(jnp.bfloat16)
    value_heads = value_low.reshape(seq_len, local_heads, head_width)
    block_rows = min(512, seq_len)
    block_count = seq_len // block_rows
    query_blocks = query_low.reshape(block_count, block_rows, local_heads, head_width)

    def attend(query_block):
        scores = (
            jnp.einsum("qhd,khd->hqk", query_block, key_low, preferred_element_type=jnp.float32)
            * factor
        )
        row_max = jnp.max(scores, axis=-1, keepdims=True)
        shifted = jnp.exp(scores - row_max)
        row_sum = jnp.sum(shifted, axis=-1, keepdims=True)
        probs_low = (shifted / row_sum).astype(jnp.bfloat16)
        mixture = jnp.einsum(
            "hqk,khd->qhd", probs_low, value_heads, preferred_element_type=jnp.float32
        )
        return (mixture.astype(jnp.bfloat16), (row_max + jnp.log(row_sum))[..., 0])

    attended_blocks, log_sums = lax.map(attend, query_blocks)
    attended = attended_blocks.reshape(seq_len, local_heads * head_width)
    attn_out = lax.psum_scatter(
        jnp.dot(attended, out_w, preferred_element_type=jnp.float32).astype(jnp.bfloat16),
        "tensor",
        scatter_dimension=0,
        tiled=True,
    ).astype(jnp.float32)
    middle = source + attn_out
    scale_mid = inverse_rms(middle)
    normed_mid = middle * scale_mid * norm_mid
    mid_low = normed_mid.astype(jnp.bfloat16)
    logits = jnp.dot(normed_mid, router_w, precision=highest, preferred_element_type=jnp.float32)
    route_mask = routes[:, :, None] == jnp.arange(experts_all, dtype=jnp.int32)[None, None, :]
    mask_float = route_mask.astype(jnp.float32)
    chosen = jnp.sum(mask_float * logits[:, None, :], axis=-1)
    gating = jax.nn.softmax(chosen, axis=-1)
    upstream = cotangent.astype(jnp.float32)
    gates = jnp.sum(mask_float * gating[:, :, None], axis=1)
    x_all = lax.all_gather(mid_low, "expert", axis=0, tiled=True)
    gates_all = lax.all_gather(gates, "expert", axis=0, tiled=True)
    first_expert = lax.axis_index("expert") * experts_local
    own_gates = lax.dynamic_slice_in_dim(gates_all, first_expert, experts_local, 1)
    part_width = hidden_width // tensor_count
    rows_all = x_all.shape[0]
    y_part = jnp.zeros((rows_all, model_width), jnp.float32)
    x_grad_part = jnp.zeros((rows_all, model_width), jnp.float32)
    gate_grads, gate_parts, up_parts, down_parts = [], [], [], []
    for e in range(experts_local):
        hidden_raw = lax.dot_general(
            cot_all, down_w[e], contract_last, preferred_element_type=jnp.float32
        )
        gate_pre = jnp.dot(x_all, gate_w[e], preferred_element_type=jnp.float32)
        up_pre = jnp.dot(x_all, up_w[e], preferred_element_type=jnp.float32)
        weight = own_gates[:, e : e + 1]
        hidden = gate_pre * jax.nn.sigmoid(gate_pre) * up_pre
        gate_grads.append(jnp.sum(hidden * hidden_raw, axis=1))
        hidden_low = (hidden * weight).astype(jnp.bfloat16)
        gate_back, up_back = swiglu_back(hidden_raw * weight, gate_pre, up_pre)
        y_part = y_part + jnp.dot(hidden_low, down_w[e], preferred_element_type=jnp.float32)
        x_grad_part = x_grad_part + lax.dot_general(
            gate_back, gate_w[e], contract_last, preferred_element_type=jnp.float32
        )
        x_grad_part = x_grad_part + lax.dot_general(
            up_back, up_w[e], contract_last, preferred_element_type=jnp.float32
        )
        gate_parts.append(
            jnp.einsum(
                "nd,ntf->tdf",
                x_all,
                gate_back.reshape(rows_all, tensor_count, part_width),
                preferred_element_type=jnp.float32,
            ).astype(jnp.bfloat16)
        )
        up_parts.append(
            jnp.einsum(
                "nd,ntf->tdf",
                x_all,
                up_back.reshape(rows_all, tensor_count, part_width),
                preferred_element_type=jnp.float32,
            ).astype(jnp.bfloat16)
        )
        down_parts.append(
            lax.dot_general(
                hidden_low, cot_all, contract_first, preferred_element_type=jnp.float32
            ).astype(jnp.bfloat16)
        )
    x_grad = lax.psum_scatter(
        x_grad_part.astype(jnp.bfloat16), "expert", scatter_dimension=0, tiled=True
    )
    expert_input_grad = x_grad.astype(jnp.float32)
    gate_grad_sent = jnp.stack(gate_grads, axis=-1)
    gate_grad_all = lax.all_to_all(gate_grad_sent, "expert", split_axis=0, concat_axis=0, tiled=True)
    gate_grad_dense = (
        gate_grad_all.reshape(expert_count, rows_own, experts_local)
        .transpose(1, 0, 2)
        .reshape(rows_own, experts_all)
    )
    gate_grad = jnp.sum(mask_float * gate_grad_dense[:, None, :], axis=-1)
    y_sum = lax.psum_scatter(
        y_part.astype(jnp.bfloat16), "expert", scatter_dimension=0, tiled=True
    )
    output = (middle + y_sum.astype(jnp.float32)).astype(jnp.bfloat16)

    def own_part(parts):
        return [
            lax.psum_scatter(p, "tensor", scatter_dimension=0, tiled=True).astype(jnp.float32)
            for p in parts
        ]

    gate_w_grad = jnp.concatenate(own_part(gate_parts), axis=0)
    up_w_grad = jnp.concatenate(own_part(up_parts), axis=0)
    down_w_grad = jnp.stack(own_part(down_parts), axis=0)
    inner_gate = jnp.sum(gating * gate_grad, axis=-1, keepdims=True)
    chosen_grad = gating * (gate_grad - inner_gate)
    logit_grad = jnp.sum(chosen_grad[:, :, None] * mask_float, axis=1)
    router_part = lax.dot_general(
        normed_mid,
        logit_grad,
        contract_first,
        precision=highest,
        preferred_element_type=jnp.float32,
    )
    normed_mid_grad = expert_input_grad + lax.dot_general(
        logit_grad, router_w, contract_last, precision=highest, preferred_element_type=jnp.float32
    )
    norm_mid_part = jnp.sum(normed_mid_grad * middle * scale_mid, axis=0)
    middle_grad = upstream + norm_backward(normed_mid_grad, middle, scale_mid, norm_mid)
    branch_low = middle_grad.astype(jnp.bfloat16)
    branch_all = lax.all_gather(branch_low, "tensor", axis=0, tiled=True)
    attended_grad = lax.dot_general(
        branch_all, out_w, contract_last, preferred_element_type=jnp.float32
    ).astype(jnp.bfloat16)
    out_w_part = lax.dot_general(
        attended, branch_all, contract_first, preferred_element_type=jnp.float32
    )
    grad_blocks = attended_grad.reshape(block_count, block_rows, local_heads, head_width)

    def attend_back(carry, inputs):
        key_total, value_total = carry
        query_block, grad_block, log_block = inputs
        scores = (
            jnp.einsum("qhd,khd->hqk", query_block, key_low, preferred_element_type=jnp.float32)
            * factor
        )
        probs = jnp.exp(scores - log_block[:, :, None])
        probs_low = probs.astype(jnp.bfloat16)
        value_total = value_total + jnp.einsum(
            "hqk,qhd->khd", probs_low, grad_block, preferred_element_type=jnp.float32
        )
        prob_grad = jnp.einsum(
            "qhd,khd->hqk", grad_block, value_heads, preferred_element_type=jnp.float32
        )
        delta = jnp.sum(probs * prob_grad, axis=-1, keepdims=True)
        score_low = (probs * (prob_grad - delta)).astype(jnp.bfloat16)
        query_part = (
            jnp.einsum("hqk,khd->qhd", score_low, key_low, preferred_element_type=jnp.float32)
            * factor
        )
        key_total = (
            key_total
            + jnp.einsum("hqk,qhd->khd", score_low, query_block, preferred_element_type=jnp.float32)
            * factor
        )
        return ((key_total, value_total), query_part)

    zero_heads = jnp.zeros((seq_len, local_heads, head_width), jnp.float32)
    (key_grad, value_total), query_parts = lax.scan(
        attend_back, (zero_heads, zero_heads), (query_blocks, grad_blocks, log_sums)
    )
    query_grad = query_parts.reshape(seq_len, local_heads, head_width)
    value_grad_low = value_total.reshape(seq_len, local_heads * head_width).astype(jnp.bfloat16)
    query_rot_grad = rotate_back(query_grad, cosine, sine_table)
    key_rot_grad = rotate_back(key_grad, cosine, sine_table)
    query_gain_part = jnp.sum(query_rot_grad * query_heads * query_scale, axis=(0, 1))
    key_gain_part = jnp.sum(key_rot_grad * key_heads * key_scale, axis=(0, 1))
    query_pre_grad = (
        norm_backward(query_rot_grad, query_heads, query_scale, query_gain)
        .reshape(seq_len, local_heads * head_width)
        .astype(jnp.bfloat16)
    )
    key_pre_grad = (
        norm_backward(key_rot_grad, key_heads, key_scale, key_gain)
        .reshape(seq_len, local_heads * head_width)
        .astype(jnp.bfloat16)
    )
    query_w_part = lax.dot_general(
        gathered, query_pre_grad, contract_first, preferred_element_type=jnp.float32
    )
    key_w_part = lax.dot_general(
        gathered, key_pre_grad, contract_first, preferred_element_type=jnp.float32
    )
    value_w_part = lax.dot_general(
        gathered, value_grad_low, contract_first, preferred_element_type=jnp.float32
    )
    summed = lax.dot_general(
        query_pre_grad, query_w, contract_last, preferred_element_type=jnp.float32
    )
    summed = summed + lax.dot_general(
        key_pre_grad, key_w, contract_last, preferred_element_type=jnp.float32
    )
    rows_grad = lax.psum_scatter(
        (
            summed
            + lax.dot_general(
                value_grad_low, value_w, contract_last, preferred_element_type=jnp.float32
            )
        ).astype(jnp.bfloat16),
        "tensor",
        scatter_dimension=0,
        tiled=True,
    ).astype(jnp.float32)
    norm_in_part = jnp.sum(rows_grad * source * scale_in, axis=0)
    input_grad = middle_grad + norm_backward(rows_grad, source, scale_in, norm_in)
    query_w_grad, key_w_grad, value_w_grad, out_w_grad = (
        lax.psum_scatter(
            query_w_part.astype(jnp.bfloat16), "expert", scatter_dimension=0, tiled=True
        ).astype(jnp.float32),
        lax.psum_scatter(
            key_w_part.astype(jnp.bfloat16), "expert", scatter_dimension=0, tiled=True
        ).astype(jnp.float32),
        lax.psum_scatter(
            value_w_part.astype(jnp.bfloat16), "expert", scatter_dimension=0, tiled=True
        ).astype(jnp.float32),
        lax.psum_scatter(
            out_w_part.astype(jnp.bfloat16), "expert", scatter_dimension=1, tiled=True
        ).astype(jnp.float32),
    )
    norm_in_grad, query_gain_grad, key_gain_grad, norm_mid_grad, router_w_grad = lax.psum(
        (norm_in_part, query_gain_part, key_gain_part, norm_mid_part, router_part),
        ("expert", "tensor"),
    )
    return (
        output,
        input_grad,
        norm_in_grad,
        query_w_grad,
        key_w_grad,
        value_w_grad,
        out_w_grad,
        query_gain_grad,
        key_gain_grad,
        norm_mid_grad,
        router_w_grad,
        gate_w_grad,
        up_w_grad,
        down_w_grad,
    )


def solution(mesh):
    placed = (
        P(("expert", "tensor"), None),
        P(("expert", "tensor"), None),
        P(("expert", "tensor"), None),
        P(),
        P(None, "tensor"),
        P(None, "tensor"),
        P(None, "tensor"),
        P("tensor", None),
        P(),
        P(),
        P(),
        P(),
        P("expert", None, None),
        P("expert", None, None),
        P("expert", None, None),
    )
    return jax.shard_map(
        per_device if dict(mesh.shape) == {"expert": 8, "tensor": 4} else per_device_general,
        mesh=mesh,
        in_specs=placed,
        out_specs=(
            P(("expert", "tensor"), None),
            P(("expert", "tensor"), None),
            P(),
            P("expert", "tensor"),
            P("expert", "tensor"),
            P("expert", "tensor"),
            P("tensor", "expert"),
            P(),
            P(),
            P(),
            P(),
            P("expert", None, "tensor"),
            P("expert", None, "tensor"),
            P("expert", "tensor", None),
        ),
        check_vma=False,
    )
```

```python
import functools
import math

import jax
import jax.numpy as jnp
from jax import lax
from jax.experimental import pallas as pl
from jax.experimental.pallas import tpu as pltpu
from jax.sharding import PartitionSpec as P

epsilon = 1e-06
highest = lax.Precision.HIGHEST
contract_last = (((1,), (1,)), ((), ()))
contract_first = (((0,), (0,)), ((), ()))


def inverse_rms(values):
    return lax.rsqrt(jnp.mean(values * values, axis=-1, keepdims=True) + epsilon)


def norm_backward(grad_norm, values, inverse, norm_gain):
    weighted = grad_norm * norm_gain
    inner_mean = jnp.mean(weighted * values, axis=-1, keepdims=True)
    return inverse * weighted - values * inverse * inverse * inverse * inner_mean


def rotary_tables(length, head_width):
    half_dim = head_width // 2
    frequency = jnp.exp(
        -math.log(10000.0) * 2.0 * jnp.arange(half_dim, dtype=jnp.float32) / head_width
    )
    angles = jnp.arange(length, dtype=jnp.float32)[:, None] * frequency[None, :]
    return (jnp.cos(angles)[:, None, :], jnp.sin(angles)[:, None, :])


def rotate(values, cosine, sine_table):
    half_dim = values.shape[-1] // 2
    first_half = values[..., :half_dim]
    second_half = values[..., half_dim:]
    return jnp.concatenate(
        [
            first_half * cosine - second_half * sine_table,
            second_half * cosine + first_half * sine_table,
        ],
        axis=-1,
    )


def rotate_back(gradient, cosine, sine_table):
    half_dim = gradient.shape[-1] // 2
    first_half = gradient[..., :half_dim]
    second_half = gradient[..., half_dim:]
    return jnp.concatenate(
        [
            first_half * cosine + second_half * sine_table,
            second_half * cosine - first_half * sine_table,
        ],
        axis=-1,
    )


def swiglu_back(hidden_grad, gate_pre, up_pre):
    sigmoid_part = jax.nn.sigmoid(gate_pre)
    gate_back = (
        hidden_grad * up_pre * sigmoid_part * (1.0 + gate_pre * (1.0 - sigmoid_part))
    ).astype(jnp.bfloat16)
    up_back = (hidden_grad * gate_pre * sigmoid_part).astype(jnp.bfloat16)
    return (gate_back, up_back)


chunks = 4


def pick(index, values):
    result = values[-1]
    for j in reversed(range(len(values) - 1)):
        result = jnp.where(index == j, values[j], result)
    return result


def expert_kernel(
    experts_all,
    own_rows,
    cot_all,
    gate_hbm,
    up_hbm,
    down_hbm,
    hidden_all,
    grads_all,
    y_all,
    total,
    core_input,
    near_input,
    core_output,
    near_output,
    gate_v,
    up_v,
    down_v,
    rows_v,
    cot_v,
    hidden_v,
    gate_b,
    up_b,
    y_v,
    stage,
    parts,
    side_in,
    cross_in,
    line_in,
    weight_sem,
    own_sem,
    cot_sem,
    out_sem,
    item_in,
    item_out,
    core_recv,
    gather_recv,
    gather_send,
    side_recv,
    side_send,
    cross_recv,
    cross_send,
    line_recv,
    line_send,
):
    position = lax.axis_index("expert")
    peer = lax.axis_index("tensor")
    z = position // 2
    x = position % 2
    experts_local, width, hidden = gate_v.shape
    rows = cot_v.shape[0]
    part = hidden // 4
    y = peer // 2
    core = peer % 2
    chunk = rows // chunks
    middle = (z == 1) | (z == 2)
    ends = (z == 0) | (z == 3)
    pair = z + 1 - 2 * (z % 2)
    line_slots = [
        z,
        pick(z, [1, 0, 3, 2]),
        pick(z, [2, 2, 1, 1]),
        pick(z, [3, 3, 0, 0]),
    ]

    def block_rows(block):
        return pl.ds(pl.multiple_of(block * rows, rows), rows)

    def device(zz, xx):
        return (zz * 2 + xx, peer)

    def slot_z(k):
        return pick(k, line_slots)

    weight_copies = [
        pltpu.make_async_copy(gate_hbm, gate_v, weight_sem.at[0]),
        pltpu.make_async_copy(up_hbm, up_v, weight_sem.at[1]),
        pltpu.make_async_copy(down_hbm, down_v, weight_sem.at[2]),
    ]
    own_copy = pltpu.make_async_copy(own_rows, rows_v.at[block_rows(position)], own_sem)
    own_copy.start()
    for copy in weight_copies:
        copy.start()

    barrier = pltpu.get_barrier_semaphore()
    pl.semaphore_signal(barrier, inc=1, device_id=device(z, 1 - x), device_id_type=pl.DeviceIdType.MESH)
    core_peer = (position, y * 2 + 1 - core)
    pl.semaphore_signal(barrier, inc=1, device_id=core_peer, device_id_type=pl.DeviceIdType.MESH)

    @pl.when(z < 3)
    def _():
        pl.semaphore_signal(barrier, inc=1, device_id=device(z + 1, x), device_id_type=pl.DeviceIdType.MESH)

    @pl.when(z > 0)
    def _():
        pl.semaphore_signal(barrier, inc=1, device_id=device(z - 1, x), device_id_type=pl.DeviceIdType.MESH)

    pl.semaphore_wait(barrier, 3 + middle.astype(jnp.int32))

    def gather_copy(source, block, index, zz, xx):
        return pltpu.make_async_remote_copy(
            src_ref=source,
            dst_ref=rows_v.at[block_rows(block)],
            send_sem=gather_send.at[index],
            recv_sem=gather_recv.at[block],
            device_id=device(zz, xx),
            device_id_type=pl.DeviceIdType.MESH,
        )

    def own_send(index, zz, xx):
        return gather_copy(own_rows, position, index, zz, xx)

    own_send(0, z, 1 - x).start()

    @pl.when(z < 3)
    def _():
        own_send(1, z + 1, x).start()

    @pl.when(z > 0)
    def _():
        own_send(2, z - 1, x).start()

    def forward_side(k):
        block = slot_z(k) * 2 + x
        return gather_copy(rows_v.at[block_rows(block)], block, 2 + k, z, 1 - x)

    def forward_line(k):
        block = slot_z(k) * 2 + x
        target = jnp.where(slot_z(k) < z, z + 1, z - 1)
        return gather_copy(rows_v.at[block_rows(block)], block, 5 + k, jnp.clip(target, 0, 3), x)

    def arrived(block):
        gather_copy(own_rows, block, 0, z, 1 - x).wait_recv()

    def arrive(k):
        arrived(slot_z(k) * 2 + x)
        if k < 3:

            @pl.when(ends)
            def _():
                forward_side(k).start()

        @pl.when(middle)
        def _():
            if k > 1:
                forward_side(k).start()
            forward_line(k).start()

    def forward_cross():
        block = jnp.where(ends, z, slot_z(3)) * 2 + 1 - x
        return gather_copy(rows_v.at[block_rows(block)], block, 9, pair, x)

    def cross_copy(c):
        area = pl.ds(c * chunk, chunk)
        return pltpu.make_async_remote_copy(
            src_ref=parts.at[5, area],
            dst_ref=cross_in.at[area],
            send_sem=cross_send.at[c],
            recv_sem=cross_recv.at[c],
            device_id=device(pair, x),
            device_id_type=pl.DeviceIdType.MESH,
        )

    def cross_add(c):
        area = pl.ds(c * chunk, chunk)
        cross_copy(c).wait_recv()
        parts[4, area] = (
            parts[4, area].astype(jnp.float32) + cross_in[area].astype(jnp.float32)
        ).astype(jnp.bfloat16)
        side_copy(0, c).start()

    def side_slot(k):
        return jnp.maximum(k - 1, 0)

    def side_copy(k, c):
        area = pl.ds(c * chunk, chunk)
        return pltpu.make_async_remote_copy(
            src_ref=parts.at[4 + k, area],
            dst_ref=side_in.at[side_slot(k), area],
            send_sem=side_send.at[side_slot(k), c],
            recv_sem=side_recv.at[side_slot(k), c],
            device_id=device(z, 1 - x),
            device_id_type=pl.DeviceIdType.MESH,
        )

    def line_slot(k):
        target = slot_z(k)
        return jnp.where(target < z, target, target + 1)

    def line_copy(k, c):
        area = pl.ds(c * chunk, chunk)
        target = jnp.where(slot_z(k) < z, z - 1, z + 1)
        return pltpu.make_async_remote_copy(
            src_ref=parts.at[k, area],
            dst_ref=line_in.at[line_slot(k), area],
            send_sem=line_send.at[k - 1, c],
            recv_sem=line_recv.at[line_slot(k), c],
            device_id=device(jnp.clip(target, 0, 3), x),
            device_id_type=pl.DeviceIdType.MESH,
        )

    def line_wait(slot, c):
        area = pl.ds(c * chunk, chunk)
        pltpu.make_async_remote_copy(
            src_ref=parts.at[0, area],
            dst_ref=line_in.at[slot, area],
            send_sem=line_send.at[0, c],
            recv_sem=line_recv.at[slot, c],
            device_id=device(z, 1 - x),
            device_id_type=pl.DeviceIdType.MESH,
        ).wait_recv()

    def relay(k, c):
        area = pl.ds(c * chunk, chunk)
        if k > 1:
            side_copy(k, c).wait_recv()
            parts[k, area] = (
                parts[k, area].astype(jnp.float32) + side_in[k - 1, area].astype(jnp.float32)
            ).astype(jnp.bfloat16)

        @pl.when(middle)
        def _():
            line_wait(line_slot(k), c)
            parts[k, area] = (
                parts[k, area].astype(jnp.float32) + line_in[line_slot(k), area].astype(jnp.float32)
            ).astype(jnp.bfloat16)

        line_copy(k, c).start()

    def block_of(step):
        k = pick(step, [0, 1, 0, 1, 2, 2, 3, 3])
        side = pick(step, [0, 0, 1, 1, 0, 1, 1, 0])
        return k, side, slot_z(k) * 2 + jnp.where(side == 1, 1 - x, x)

    def cot_copy(step):
        return pltpu.make_async_copy(cot_all.at[block_rows(block_of(step)[2])], cot_v, cot_sem)

    def y_copy(block):
        return pltpu.make_async_copy(y_v, y_all.at[block], out_sem.at[3])

    def out_copies(block):
        return [
            pltpu.make_async_copy(hidden_v, hidden_all.at[block_rows(block)], out_sem.at[0]),
            pltpu.make_async_copy(gate_b, grads_all.at[0, block_rows(block)], out_sem.at[1]),
            pltpu.make_async_copy(up_b, grads_all.at[1, block_rows(block)], out_sem.at[2]),
        ]

    cot_copy(0).start()
    own_copy.wait()
    for copy in weight_copies:
        copy.wait()

    def one_step(step, carry):
        k, side, block = block_of(step)

        @pl.when(step == 1)
        def _():
            arrive(1)

            @pl.when(middle)
            def _():
                arrive(2)

            arrived(z * 2 + 1 - x)

            @pl.when(ends)
            def _():
                forward_cross().start()

        @pl.when(step == 3)
        def _():
            @pl.when(ends)
            def _():
                arrive(2)

            @pl.when(middle)
            def _():
                arrive(3)

            arrived(slot_z(1) * 2 + 1 - x)

        @pl.when(step == 5)
        def _():
            arrived(slot_z(2) * 2 + 1 - x)

        @pl.when((step == 6) & ends)
        def _():
            arrived(slot_z(3) * 2 + 1 - x)

        @pl.when((step == 7) & ends)
        def _():
            arrive(3)

        @pl.when(step > 0)
        def _():
            for copy in out_copies(block):
                copy.wait()

        cot_copy(step).wait()
        rows_low = rows_v[block_rows(block), :width]
        extra = rows_v[block_rows(block), width:].astype(jnp.float32)
        lane = lax.broadcasted_iota(jnp.int32, extra.shape, 1)
        ext = jnp.zeros(extra.shape, jnp.float32)
        for e in range(experts_local):
            expert = position * experts_local + e
            high = lane == expert
            low = lane == expert + experts_all
            weight = jnp.sum(jnp.where(high | low, extra, 0.0), axis=1, keepdims=True)
            gate_grad = jnp.zeros((rows, 1), jnp.float32)
            for f in range(hidden // 512):
                columns = pl.ds(f * 512, 512)
                gate_pre = jnp.dot(rows_low, gate_v[e, :, columns], preferred_element_type=jnp.float32)
                up_pre = jnp.dot(rows_low, up_v[e, :, columns], preferred_element_type=jnp.float32)
                target = pl.ds(e * hidden + f * 512, 512)
                raw = lax.dot_general(
                    cot_v[...],
                    down_v[e, columns, :],
                    contract_last,
                    preferred_element_type=jnp.float32,
                )
                sig = jax.nn.sigmoid(gate_pre)
                act = gate_pre * sig
                hid = act * up_pre
                gate_grad = gate_grad + jnp.sum(hid * raw, axis=1, keepdims=True)
                hidden_v[:, target] = (hid * weight).astype(jnp.bfloat16)
                grad = raw * weight
                gate_b[:, target] = (grad * up_pre * sig * (1.0 + gate_pre * (1.0 - sig))).astype(jnp.bfloat16)
                up_b[:, target] = (grad * act).astype(jnp.bfloat16)
            grad_high = gate_grad.astype(jnp.bfloat16).astype(jnp.float32)
            ext = jnp.where(high, grad_high, ext)
            ext = jnp.where(low, gate_grad - grad_high, ext)

        @pl.when(step < 7)
        def _():
            cot_copy(step + 1).start()

        @pl.when((step == 4) & middle)
        def _():
            arrived(slot_z(3) * 2 + 1 - x)
            forward_cross().start()

        place = side * 4 + k
        parts[place, :, width:] = ext.astype(jnp.bfloat16)
        for copy in out_copies(block):
            copy.start()
        for d in range(width // 1024):
            span = pl.ds(d * 1024, 1024)
            summed = jnp.zeros((rows, 1024), jnp.float32)
            for e in range(experts_local):
                target = pl.ds(e * hidden, hidden)
                summed = summed + lax.dot_general(
                    gate_b[:, target], gate_v[e, span, :], contract_last, preferred_element_type=jnp.float32
                )
                summed = summed + lax.dot_general(
                    up_b[:, target], up_v[e, span, :], contract_last, preferred_element_type=jnp.float32
                )
            parts[place, :, span] = summed.astype(jnp.bfloat16)

        @pl.when((side == 1) & (k > 1))
        def _():
            for c in range(chunks):
                side_copy(k, c).start()

        @pl.when(step == 3)
        def _():
            for c in range(chunks):
                cross_copy(c).start()

        @pl.when((step == 1) & ends)
        def _():
            for c in range(chunks):
                line_copy(1, c).start()

        @pl.when(step > 0)
        def _():
            y_copy(block).wait()

        for d in range(width // 1024):
            span = pl.ds(d * 1024, 1024)
            summed = jnp.zeros((rows, 1024), jnp.float32)
            for e in range(experts_local):
                summed = summed + jnp.dot(
                    hidden_v[:, pl.ds(e * hidden, hidden)],
                    down_v[e, :, span],
                    preferred_element_type=jnp.float32,
                )
            y_v[:, span] = summed.astype(jnp.bfloat16)
        y_copy(block).start()
        return carry

    lax.fori_loop(0, 8, one_step, 0)

    for copy in out_copies(position):
        copy.wait()
    y_copy(position).wait()
    whole_cot = [
        pltpu.make_async_copy(cot_all.at[:, pl.ds(h * hidden, hidden)], up_v.at[h], weight_sem.at[h])
        for h in range(2)
    ]
    for copy in whole_cot:
        copy.start()

    def columns_of(pair, q):
        column_y = jnp.where(q == 0, y, 1 - y)
        column_core = jnp.where(pair == 0, 1 - core, core)
        return column_y * 2 + column_core

    def item_source(i):
        return i // 6, (i % 6) // 2, i % 2

    def item_loads(i, act):
        pair_of, kind, e = item_source(i)
        slot = i % 2
        for q in range(2):
            start = pl.multiple_of(e * hidden + columns_of(pair_of, q) * part, part)
            place = gate_v.at[0, :, pl.ds(pl.multiple_of(slot * 2 * part + q * part, part), part)]
            sem = item_in.at[slot, q]

            @pl.when(kind < 2)
            def _(start=start, place=place, sem=sem):
                act(
                    pltpu.make_async_copy(
                        grads_all.at[jnp.minimum(kind, 1), :, pl.ds(start, part)], place, sem
                    )
                )

            @pl.when(kind == 2)
            def _(start=start, place=place, sem=sem):
                act(pltpu.make_async_copy(hidden_all.at[:, pl.ds(start, part)], place, sem))

    def core_copy(source, target, slot, number, q):
        return pltpu.make_async_remote_copy(
            src_ref=source,
            dst_ref=target,
            send_sem=item_out.at[slot, q],
            recv_sem=core_recv.at[number, q],
            device_id=core_peer,
            device_id_type=pl.DeviceIdType.MESH,
        )

    def item_stores(i, starting):
        pair_of, kind, e = item_source(i)
        slot = i % 2
        number = i % 6
        wide_kind = jnp.minimum(kind, 1)
        for q in range(2):
            wide_place = gate_v.at[1, :, pl.ds(pl.multiple_of(slot * 2 * part + q * part, part), part)]
            tall_place = down_v.at[slot, pl.ds(q * part, part)]

            def far(source, target, q=q):
                copy = core_copy(source, target, slot, number, q)
                if starting:
                    copy.start()
                else:
                    copy.wait_send()

            def own(source, target, q=q):
                copy = pltpu.make_async_copy(source, target, item_out.at[slot, q])
                if starting:
                    copy.start()
                else:
                    copy.wait()

            for which, move, wide_out, tall_out in (
                (0, far, core_input, core_output),
                (1, own, near_input, near_output),
            ):

                @pl.when((pair_of == which) & (kind < 2))
                def _(move=move, wide_place=wide_place, wide_out=wide_out, q=q):
                    move(wide_place, wide_out.at[q, wide_kind, e])

                @pl.when((pair_of == which) & (kind == 2))
                def _(move=move, tall_place=tall_place, tall_out=tall_out, q=q):
                    move(tall_place, tall_out.at[q, e])

    item_loads(0, lambda copy: copy.start())
    for copy in whole_cot:
        copy.wait()

    def at(index, first, gap):
        return (index >= first) & (index < first + gap * chunks) & ((index - first) % gap == 0)

    def item(index, carry):
        i = index // 4
        d = index % 4
        kind = (i % 6) // 2
        slot = i % 2

        @pl.when(d == 0)
        def _():
            item_loads(i, lambda copy: copy.wait())

            @pl.when(i < 11)
            def _():
                item_loads(i + 1, lambda copy: copy.start())

            @pl.when(i > 1)
            def _():
                item_stores(i - 2, False)

        columns = pl.ds(pl.multiple_of(slot * 2 * part, 2 * part), 2 * part)
        span = pl.ds(pl.multiple_of(d * (width // 4), width // 4), width // 4)

        @pl.when(kind < 2)
        def _():
            gate_v[1, span, columns] = lax.dot_general(
                rows_v[:, span], gate_v[0, :, columns], contract_first, preferred_element_type=jnp.float32
            ).astype(jnp.bfloat16)

        @pl.when(kind == 2)
        def _():
            half = pl.ds(pl.multiple_of((d % 2) * (hidden // 2), hidden // 2), hidden // 2)
            down_v[slot, : 2 * part, span] = lax.dot_general(
                gate_v[0, :, columns],
                up_v[d // 2, :, half],
                contract_first,
                preferred_element_type=jnp.float32,
            ).astype(jnp.bfloat16)

        @pl.when(d == 3)
        def _():
            item_stores(i, True)

        @pl.when(at(index, 1, 1))
        def _():
            cross_add(index - 1)

        @pl.when(at(index, 5, 4))
        def _():
            relay(3, (index - 5) // 4)

        @pl.when(at(index, 11, 4) & middle)
        def _():
            relay(1, (index - 11) // 4)

        @pl.when(at(index, 18, 1) & ends)
        def _():
            relay(2, index - 18)

        @pl.when(at(index, 24, 4) & middle)
        def _():
            relay(2, (index - 24) // 4)

        return carry

    lax.fori_loop(0, 48, item, 0)
    for last in (10, 11):
        item_stores(last, False)
    for number in range(6):
        for q in range(2):
            if number < 4:
                core_copy(
                    gate_v.at[1, :, pl.ds(0, part)],
                    core_input.at[q, number // 2, number % 2],
                    0,
                    number,
                    q,
                ).wait_recv()
            else:
                core_copy(
                    down_v.at[0, pl.ds(0, part)], core_output.at[q, number % 2], 0, number, q
                ).wait_recv()

    def finish(c, carry):
        area = pl.ds(c * chunk, chunk)
        side_copy(0, c).wait_recv()
        stage[...] = parts[0, area].astype(jnp.float32) + side_in[0, area].astype(jnp.float32)

        @pl.when(z < 3)
        def _():
            line_wait(z, c)
            stage[...] += line_in[z, area].astype(jnp.float32)

        @pl.when(z > 0)
        def _():
            line_wait(z + 1, c)
            stage[...] += line_in[z + 1, area].astype(jnp.float32)

        result = pltpu.make_async_copy(stage, total.at[area], own_sem)
        result.start()
        result.wait()
        for k in (0, 2, 3):
            side_copy(k, c).wait_send()
        cross_copy(c).wait_send()
        for k in range(1, 4):
            line_copy(k, c).wait_send()
        return carry

    lax.fori_loop(0, chunks, finish, 0)

    own_send(0, z, 1 - x).wait_send()

    @pl.when(z < 3)
    def _():
        own_send(1, z + 1, x).wait_send()

    @pl.when(z > 0)
    def _():
        own_send(2, z - 1, x).wait_send()

    forward_cross().wait_send()
    forward_side(2).wait_send()

    @pl.when(ends)
    def _():
        forward_side(1).wait_send()

    @pl.when(middle)
    def _():
        forward_side(3).wait_send()
        for k in range(1, 4):
            forward_line(k).wait_send()


def expert_pass(own_rows, cot_all, gate_w, up_w, down_w, experts_all, collective):
    rows, wide = own_rows.shape
    experts_local, width, hidden = gate_w.shape
    inner = experts_local * hidden
    any_space = pl.BlockSpec(memory_space=pl.ANY)
    low = jnp.bfloat16
    dma = pltpu.SemaphoreType.DMA
    return pl.pallas_call(
        functools.partial(expert_kernel, experts_all),
        name="expert_pass",
        out_shape=(
            jax.ShapeDtypeStruct((8 * rows, inner), low),
            jax.ShapeDtypeStruct((2, 8 * rows, inner), low),
            jax.ShapeDtypeStruct((8, rows, width), low),
            jax.ShapeDtypeStruct((rows, wide), jnp.float32),
            *(jax.ShapeDtypeStruct((2, 2, experts_local, width, hidden // 4), low),) * 2,
            *(jax.ShapeDtypeStruct((2, experts_local, hidden // 4, width), low),) * 2,
        ),
        in_specs=[any_space] * 5,
        out_specs=(any_space,) * 8,
        scratch_shapes=[
            pltpu.VMEM((experts_local, width, hidden), low),
            pltpu.VMEM((experts_local, width, hidden), low),
            pltpu.VMEM((experts_local, hidden, width), low),
            pltpu.VMEM((8 * rows, wide), low),
            pltpu.VMEM((rows, width), low),
            pltpu.VMEM((rows, inner), low),
            pltpu.VMEM((rows, inner), low),
            pltpu.VMEM((rows, inner), low),
            pltpu.VMEM((rows, width), low),
            pltpu.VMEM((rows // chunks, wide), jnp.float32),
            pltpu.VMEM((8, rows, wide), low),
            pltpu.VMEM((3, rows, wide), low),
            pltpu.VMEM((rows, wide), low),
            pltpu.VMEM((5, rows, wide), low),
            dma((3,)),
            dma,
            dma,
            dma((4,)),
            dma((2, 2)),
            dma((2, 2)),
            dma((6, 2)),
            dma((8,)),
            dma((10,)),
            dma((3, chunks)),
            dma((3, chunks)),
            dma((chunks,)),
            dma((chunks,)),
            dma((5, chunks)),
            dma((3, chunks)),
        ],
        compiler_params=pltpu.CompilerParams(
            collective_id=collective, has_side_effects=True, vmem_limit_bytes=60 << 20
        ),
        cost_estimate=pl.CostEstimate(
            flops=2 * 9 * 8 * rows * width * inner, bytes_accessed=64 << 20, transcendentals=8 * rows * inner
        ),
    )(own_rows, cot_all, gate_w, up_w, down_w)


def line_gather(source, target, recv, send):
    position = lax.axis_index("expert")
    peer = lax.axis_index("tensor")
    z = position // 2
    x = position % 2
    middle = (z == 1) | (z == 2)
    slots = [z, pick(z, [1, 0, 3, 2]), pick(z, [2, 2, 1, 1]), pick(z, [3, 3, 0, 0])]

    def copy(block_source, block, index, zz, xx):
        return pltpu.make_async_remote_copy(
            src_ref=block_source,
            dst_ref=target.at[block],
            send_sem=send.at[index],
            recv_sem=recv.at[block],
            device_id=(zz * 2 + xx, peer),
            device_id_type=pl.DeviceIdType.MESH,
        )

    def own_up():
        return copy(source, position, 1, z + 1, x)

    def own_down():
        return copy(source, position, 2, z - 1, x)

    def own_side():
        return copy(source, position, 0, z, 1 - x)

    def side(k):
        block = slots[k] * 2 + x
        return copy(target.at[block], block, 2 + k, z, 1 - x)

    def line(k):
        block = slots[k] * 2 + x
        onward = jnp.where(slots[k] < z, z + 1, z - 1)
        return copy(target.at[block], block, 5 + k, jnp.clip(onward, 0, 3), x)

    def start():
        own_side().start()

        @pl.when(z < 3)
        def _():
            own_up().start()

        @pl.when(z > 0)
        def _():
            own_down().start()

    def wait_block(block):
        copy(source, block, 0, z, 1 - x).wait_recv()

    def arrive(k):
        wait_block(slots[k] * 2 + x)
        side(k).start()

        @pl.when(middle)
        def _():
            line(k).start()

    def arrive_side(k):
        wait_block(slots[k] * 2 + 1 - x)

    def drain():
        own_side().wait_send()

        @pl.when(z < 3)
        def _():
            own_up().wait_send()

        @pl.when(z > 0)
        def _():
            own_down().wait_send()

        for k in range(1, 4):
            side(k).wait_send()

            @pl.when(middle)
            def _(k=k):
                line(k).wait_send()

    return middle, start, arrive, arrive_side, drain


def attention_kernel(
    own,
    cot,
    query_w,
    key_w,
    value_w,
    out_w,
    query_gain,
    key_gain,
    cosine,
    sine,
    gathered,
    query_unit,
    key_unit,
    query_low,
    key_low,
    value_low,
    attended,
    log_sums,
    attn_sum,
    cot_all,
    rows_v,
    weights_v,
    out_v,
    pre_v,
    low_v,
    mixed_v,
    log_v,
    parts,
    own_part,
    core_in,
    line_in,
    load_sem,
    store_sem,
    rows_recv,
    rows_send,
    part_recv,
    part_send,
    cot_recv,
    cot_send,
    cot_sem,
):
    position = lax.axis_index("expert")
    t = lax.axis_index("tensor")
    z = position // 2
    x = position % 2
    y = t // 2
    c = t % 2
    near = y * 2 + 1 - c
    across = (1 - y) * 2 + c
    opposite = (1 - y) * 2 + 1 - c
    rows = own.shape[0]
    heads = low_v.shape[2] // 128
    factor = 1.0 / math.sqrt(128.0)
    mesh_ids = pl.DeviceIdType.MESH
    middle, gather_start, gather_arrive, gather_side, gather_drain = line_gather(
        cot, cot_all, cot_recv, cot_send
    )

    loads = [
        pltpu.make_async_copy(own, rows_v.at[t], load_sem.at[0]),
        pltpu.make_async_copy(query_w, weights_v.at[0], load_sem.at[1]),
        pltpu.make_async_copy(key_w, weights_v.at[1], load_sem.at[2]),
        pltpu.make_async_copy(value_w, weights_v.at[2], load_sem.at[3]),
        pltpu.make_async_copy(out_w, out_v, load_sem.at[4]),
    ]
    for load in loads:
        load.start()
    cot_copy = pltpu.make_async_copy(cot, cot_all.at[position], cot_sem)
    cot_copy.start()

    barrier = pltpu.get_barrier_semaphore()
    for place in ((position, near), (position, across), (z * 2 + 1 - x, t)):
        pl.semaphore_signal(barrier, inc=1, device_id=place, device_id_type=mesh_ids)

    @pl.when(z < 3)
    def _():
        pl.semaphore_signal(barrier, inc=1, device_id=(position + 2, t), device_id_type=mesh_ids)

    @pl.when(z > 0)
    def _():
        pl.semaphore_signal(barrier, inc=1, device_id=(position - 2, t), device_id_type=mesh_ids)

    pl.semaphore_wait(barrier, 4 + middle.astype(jnp.int32))

    def rows_copy(source, block, index, to):
        return pltpu.make_async_remote_copy(
            src_ref=source,
            dst_ref=rows_v.at[block],
            send_sem=rows_send.at[index - 1],
            recv_sem=rows_recv.at[index - 1],
            device_id=(position, to),
            device_id_type=mesh_ids,
        )

    to_across = rows_copy(own, t, 2, across)
    to_near = rows_copy(own, t, 1, near)
    forward = rows_copy(rows_v.at[across], across, 3, near)
    to_across.start()
    to_near.start()
    gather_start()
    for load in loads:
        load.wait()

    def project(i, carry):
        block = pick(i, [t, near, across, opposite])

        @pl.when(i == 1)
        def _():
            to_near.wait_recv()

        @pl.when(i == 2)
        def _():
            to_across.wait_recv()
            forward.start()
            gather_arrive(1)

            @pl.when(middle)
            def _():
                gather_arrive(2)

        @pl.when(i == 3)
        def _():
            forward.wait_recv()

        area = pl.ds(block * rows, rows)
        values = rows_v[block]
        for which, gain in ((0, query_gain), (1, key_gain)):
            pre = jnp.dot(values, weights_v[which], preferred_element_type=jnp.float32)
            for h in range(heads):
                span = slice(h * 128, (h + 1) * 128)
                head = pre[:, span]
                scale = lax.rsqrt(jnp.mean(head * head, axis=-1, keepdims=True) + epsilon)
                unit = head * scale
                pre_v[which, area, span] = unit.astype(jnp.bfloat16)
                lane = 4 + which * 4 + h
                log_v[area, lane : lane + 1] = scale
                normed = unit * gain[...]
                turned = normed * cosine[area] + pltpu.roll(normed, 64, 1) * sine[area]
                low_v[which, area, span] = turned.astype(jnp.bfloat16)
        low_v[2, area] = jnp.dot(
            values, weights_v[2], preferred_element_type=jnp.float32
        ).astype(jnp.bfloat16)
        return carry

    lax.fori_loop(0, 4, project, 0)
    stores = [
        pltpu.make_async_copy(rows_v, gathered, store_sem.at[0]),
        pltpu.make_async_copy(pre_v.at[0], query_unit, store_sem.at[1]),
        pltpu.make_async_copy(pre_v.at[1], key_unit, store_sem.at[2]),
        pltpu.make_async_copy(low_v.at[0], query_low, store_sem.at[3]),
        pltpu.make_async_copy(low_v.at[1], key_low, store_sem.at[4]),
        pltpu.make_async_copy(low_v.at[2], value_low, store_sem.at[5]),
    ]
    for store in stores:
        store.start()

    def part_copy(source, target, index, to):
        return pltpu.make_async_remote_copy(
            src_ref=source,
            dst_ref=target,
            send_sem=part_send.at[index],
            recv_sem=part_recv.at[index],
            device_id=(position, to),
            device_id_type=mesh_ids,
        )

    core_first = part_copy(parts.at[0], core_in.at[0], 0, near)
    line_copy = part_copy(parts.at[1], line_in, 1, across)
    core_second = part_copy(parts.at[2], core_in.at[1], 2, near)

    def attend(i, carry):
        block = pick(i, [opposite, across, near, t])
        area = pl.ds(block * rows, rows)
        for h in range(heads):
            span = slice(h * 128, (h + 1) * 128)
            scores = lax.dot_general(
                low_v[0, area, span], low_v[1, :, span], contract_last, preferred_element_type=jnp.float32
            )
            highest_score = jnp.max(scores, axis=-1, keepdims=True)
            weights = jnp.exp((scores - highest_score) * factor)
            total = jnp.sum(weights, axis=-1, keepdims=True)
            mixed = jnp.dot(
                weights.astype(jnp.bfloat16), low_v[2, :, span], preferred_element_type=jnp.float32
            )
            mixed_v[area, span] = (mixed / total).astype(jnp.bfloat16)
            log_v[area, h : h + 1] = highest_score * factor + jnp.log(total)
        own_part[...] = jnp.dot(mixed_v[area], out_v[...], preferred_element_type=jnp.float32)

        @pl.when(i == 0)
        def _():
            parts[0] = own_part[...].astype(jnp.bfloat16)
            core_first.start()

        @pl.when(i == 1)
        def _():
            core_first.wait_recv()
            parts[1] = (own_part[...] + core_in[0].astype(jnp.float32)).astype(jnp.bfloat16)
            line_copy.start()

            @pl.when(middle)
            def _():
                gather_arrive(3)

        @pl.when(i == 2)
        def _():
            parts[2] = own_part[...].astype(jnp.bfloat16)
            core_second.start()

            @pl.when(middle == False)
            def _():
                gather_arrive(2)

        return carry

    lax.fori_loop(0, 4, attend, 0)
    more = [
        pltpu.make_async_copy(mixed_v, attended, store_sem.at[6]),
        pltpu.make_async_copy(log_v, log_sums, store_sem.at[7]),
    ]
    for store in more:
        store.start()
    core_second.wait_recv()
    own_part[...] += core_in[1].astype(jnp.float32)
    line_copy.wait_recv()
    own_part[...] += line_in[...].astype(jnp.float32)
    last = pltpu.make_async_copy(own_part, attn_sum, store_sem.at[8])
    last.start()

    @pl.when(middle == False)
    def _():
        gather_arrive(3)

    for k in range(4):
        gather_side(k)
    gather_drain()
    for copy in (to_across, to_near, forward, core_first, line_copy, core_second):
        copy.wait_send()
    for store in [*stores, *more, last, cot_copy]:
        store.wait()


def attention_forward(own, cot, weights, out_w, gains, tables, collective):
    rows, width = own.shape
    local = out_w.shape[0]
    length = 4 * rows
    any_space = pl.BlockSpec(memory_space=pl.ANY)
    vector = pl.BlockSpec(memory_space=pltpu.VMEM)
    low, full = jnp.bfloat16, jnp.float32
    dma = pltpu.SemaphoreType.DMA
    return pl.pallas_call(
        attention_kernel,
        name="attention_forward",
        out_shape=(
            jax.ShapeDtypeStruct((4, rows, width), low),
            jax.ShapeDtypeStruct((length, local), low),
            jax.ShapeDtypeStruct((length, local), low),
            jax.ShapeDtypeStruct((length, local), low),
            jax.ShapeDtypeStruct((length, local), low),
            jax.ShapeDtypeStruct((length, local), low),
            jax.ShapeDtypeStruct((length, local), low),
            jax.ShapeDtypeStruct((length, 128), full),
            jax.ShapeDtypeStruct((rows, width), full),
            jax.ShapeDtypeStruct((8, rows, width), low),
        ),
        in_specs=[any_space] * 6 + [vector] * 4,
        out_specs=(any_space,) * 10,
        scratch_shapes=[
            pltpu.VMEM((4, rows, width), low),
            pltpu.VMEM((3, width, local), low),
            pltpu.VMEM((local, width), low),
            pltpu.VMEM((2, length, local), low),
            pltpu.VMEM((3, length, local), low),
            pltpu.VMEM((length, local), low),
            pltpu.VMEM((length, 128), full),
            pltpu.VMEM((3, rows, width), low),
            pltpu.VMEM((rows, width), full),
            pltpu.VMEM((2, rows, width), low),
            pltpu.VMEM((rows, width), low),
            dma((5,)),
            dma((9,)),
            dma((3,)),
            dma((3,)),
            dma((3,)),
            dma((3,)),
            dma((8,)),
            dma((9,)),
            dma,
        ],
        compiler_params=pltpu.CompilerParams(
            collective_id=collective, has_side_effects=True, vmem_limit_bytes=60 << 20
        ),
        cost_estimate=pl.CostEstimate(
            flops=8 * length * width * local, bytes_accessed=64 << 20, transcendentals=length * length * 4
        ),
    )(own, cot, *weights, out_w, *gains, *tables)


def attention_back_kernel(
    branch,
    gathered,
    query_unit,
    key_unit,
    query_low,
    key_low,
    value_low,
    attended,
    log_sums,
    query_w,
    key_w,
    value_w,
    out_w,
    query_gain,
    key_gain,
    cosine,
    sine,
    sent_input,
    sent_output,
    y_all,
    rows_grad,
    arrived_input,
    arrived_output,
    y_total,
    y_side,
    y_cross,
    y_line,
    y_sums,
    out_total,
    value_total,
    key_total,
    query_total,
    gain_sums,
    branch_v,
    rows_v,
    weights_v,
    out_v,
    unit_v,
    low_v,
    log_v,
    grads_v,
    key_acc,
    value_acc,
    scattered,
    side_in,
    line_in,
    own_part,
    core_in,
    across_in,
    y_v,
    load_sem,
    store_sem,
    branch_recv,
    branch_send,
    part_recv,
    part_send,
    side_recv,
    side_send,
    line_recv,
    line_send,
    swap_recv,
    swap_send,
    y_load,
    y_store,
    y_side_recv,
    y_side_send,
    y_cross_sems,
    y_line_recv,
    y_line_send,
):
    position = lax.axis_index("expert")
    t = lax.axis_index("tensor")
    z = position // 2
    x = position % 2
    y = t // 2
    core = t % 2
    near = y * 2 + 1 - core
    across = (1 - y) * 2 + core
    opposite = (1 - y) * 2 + 1 - core
    rows = branch.shape[0]
    local = out_v.shape[0]
    heads = local // 128
    kinds = scattered.shape[0]
    factor = 1.0 / math.sqrt(128.0)
    middle = (z == 1) | (z == 2)
    mesh_ids = pl.DeviceIdType.MESH
    slots = [z, pick(z, [1, 0, 3, 2]), pick(z, [2, 2, 1, 1]), pick(z, [3, 3, 0, 0])]

    loads = [
        pltpu.make_async_copy(branch, branch_v.at[t], load_sem.at[0]),
        pltpu.make_async_copy(out_w, out_v, load_sem.at[1]),
        pltpu.make_async_copy(query_low, low_v.at[0], load_sem.at[2]),
        pltpu.make_async_copy(key_low, low_v.at[1], load_sem.at[3]),
        pltpu.make_async_copy(value_low, low_v.at[2], load_sem.at[4]),
        pltpu.make_async_copy(log_sums, log_v, load_sem.at[5]),
        pltpu.make_async_copy(query_unit, unit_v.at[0], load_sem.at[6]),
        pltpu.make_async_copy(key_unit, unit_v.at[1], load_sem.at[7]),
        pltpu.make_async_copy(attended, low_v.at[3], load_sem.at[8]),
        pltpu.make_async_copy(gathered, rows_v, load_sem.at[9]),
        pltpu.make_async_copy(query_w, weights_v.at[0], load_sem.at[10]),
        pltpu.make_async_copy(key_w, weights_v.at[1], load_sem.at[11]),
        pltpu.make_async_copy(value_w, weights_v.at[2], load_sem.at[12]),
    ]
    for load in loads:
        load.start()

    barrier = pltpu.get_barrier_semaphore()
    for place in ((position, near), (position, across), (z * 2 + 1 - x, t)):
        pl.semaphore_signal(barrier, inc=1, device_id=place, device_id_type=mesh_ids)

    @pl.when(z < 3)
    def _():
        pl.semaphore_signal(barrier, inc=1, device_id=(position + 2, t), device_id_type=mesh_ids)

    @pl.when(z > 0)
    def _():
        pl.semaphore_signal(barrier, inc=1, device_id=(position - 2, t), device_id_type=mesh_ids)

    pl.semaphore_wait(barrier, 4 + middle.astype(jnp.int32))

    def branch_copy(source, block, index, to):
        return pltpu.make_async_remote_copy(
            src_ref=source,
            dst_ref=branch_v.at[block],
            send_sem=branch_send.at[index - 1],
            recv_sem=branch_recv.at[index - 1],
            device_id=(position, to),
            device_id_type=mesh_ids,
        )

    to_across = branch_copy(branch, t, 2, across)
    to_near = branch_copy(branch, t, 1, near)
    forward = branch_copy(branch_v.at[across], across, 3, near)
    to_across.start()
    to_near.start()

    swaps = [
        pltpu.make_async_remote_copy(
            src_ref=sent,
            dst_ref=arrived,
            send_sem=swap_send.at[i],
            recv_sem=swap_recv.at[i],
            device_id=(position, across),
            device_id_type=mesh_ids,
        )
        for i, (sent, arrived) in enumerate(
            ((sent_input, arrived_input), (sent_output, arrived_output))
        )
    ]

    def side_copy(k, c):
        return pltpu.make_async_remote_copy(
            src_ref=scattered.at[c, pick(k, slots) * 2 + 1 - x],
            dst_ref=side_in.at[c, k],
            send_sem=side_send.at[c, k],
            recv_sem=side_recv.at[c, k],
            device_id=(z * 2 + 1 - x, t),
            device_id_type=mesh_ids,
        )

    def line_slot(k):
        target = pick(k, slots)
        return jnp.where(target < z, target, target + 1)

    def line_copy(k, c):
        target = jnp.where(pick(k, slots) < z, z - 1, z + 1)
        return pltpu.make_async_remote_copy(
            src_ref=scattered.at[c, pick(k, slots) * 2 + x],
            dst_ref=line_in.at[c, line_slot(k)],
            send_sem=line_send.at[c, k - 1],
            recv_sem=line_recv.at[c, line_slot(k)],
            device_id=(jnp.clip(target, 0, 3) * 2 + x, t),
            device_id_type=mesh_ids,
        )

    def line_wait(slot, c):
        pltpu.make_async_remote_copy(
            src_ref=scattered.at[c, position],
            dst_ref=line_in.at[c, slot],
            send_sem=line_send.at[c, 0],
            recv_sem=line_recv.at[c, slot],
            device_id=(z * 2 + 1 - x, t),
            device_id_type=mesh_ids,
        ).wait_recv()

    def send_order(i):
        return jnp.where(middle, pick(i, [3, 1, 2, 0]), pick(i, [3, 2, 1, 0]))

    pair = z + 1 - 2 * (z % 2)
    ends = (z == 0) | (z == 3)

    def y_remote(source, target, send_sem, recv_sem, zz, xx):
        return pltpu.make_async_remote_copy(
            src_ref=source,
            dst_ref=target,
            send_sem=send_sem,
            recv_sem=recv_sem,
            device_id=(zz * 2 + xx, t),
            device_id_type=mesh_ids,
        )

    def y_block(k, xx):
        return y_all.at[slots[k] * 2 + xx]

    def y_side_copy(k):
        slot = max(k - 1, 0)
        source = y_sums.at[0] if k == 0 else y_block(k, 1 - x)
        return y_remote(
            source, y_side.at[slot], y_side_send.at[slot], y_side_recv.at[slot], z, 1 - x
        )

    def y_cross_copy():
        return y_remote(
            y_block(1, 1 - x), y_cross, y_cross_sems.at[0], y_cross_sems.at[1], pair, x
        )

    def y_line_copy(k, source):
        target = jnp.where(slots[k] < z, z - 1, z + 1)
        return y_remote(
            source,
            y_line.at[line_slot(k)],
            y_line_send.at[k - 1],
            y_line_recv.at[line_slot(k)],
            jnp.clip(target, 0, 3),
            x,
        )

    def y_line_wait(slot):
        y_remote(
            y_all.at[0], y_line.at[slot], y_line_send.at[0], y_line_recv.at[slot], z, 1 - x
        ).wait_recv()

    def y_add(target, sources):
        half = rows // 2
        for part in range(2):
            area = pl.ds(part * half, half)

            def load(i, source, area=area):
                return pltpu.make_async_copy(source.at[area], y_v.at[i], y_load.at[i])

            for i, (source, needed) in enumerate(sources):
                if needed is None:
                    load(i, source).start()
                else:

                    @pl.when(needed)
                    def _(i=i, source=source, load=load):
                        load(i, source).start()

            for i, (source, needed) in enumerate(sources):
                if needed is None:
                    load(i, source).wait()
                else:

                    @pl.when(needed)
                    def _(i=i, source=source, load=load):
                        load(i, source).wait()

            for i, (source, needed) in enumerate(sources[1:], 1):

                def add(i=i):
                    y_v[0] = (y_v[0].astype(jnp.float32) + y_v[i].astype(jnp.float32)).astype(
                        jnp.bfloat16
                    )

                if needed is None:
                    add()
                else:
                    pl.when(needed)(add)
            store = pltpu.make_async_copy(y_v.at[0], target.at[area], y_store)
            store.start()
            store.wait()

    def y_relay(k):
        if k > 1:
            y_side_copy(k).wait_recv()
        sources = [(y_block(k, x), None)]
        if k > 1:
            sources.append((y_side.at[k - 1], None))

        @pl.when(middle)
        def _():
            y_line_wait(line_slot(k))

        y_add(y_sums.at[k], [*sources, (y_line.at[line_slot(k)], middle)])
        y_line_copy(k, y_sums.at[k]).start()

    y_side_copy(3).start()
    y_cross_copy().start()
    y_side_copy(2).start()

    @pl.when(ends)
    def _():
        y_line_copy(1, y_block(1, x)).start()

    def start_side(c):
        def one(i, carry):
            side_copy(send_order(i), c).start()
            return carry

        lax.fori_loop(0, 4, one, 0)

    def weight_part(c, left, right):
        for d in range(8 // 2):
            span = pl.ds(d * 512, 512)
            product = jnp.zeros((512, local), jnp.float32)
            for b in range(4):
                product = product + lax.dot_general(
                    left[b, :, span],
                    right[pl.ds(b * rows, rows)],
                    contract_first,
                    preferred_element_type=jnp.float32,
                )
            scattered[c, 2 * d] = product[:256].astype(jnp.bfloat16)
            scattered[c, 2 * d + 1] = product[256:].astype(jnp.bfloat16)

    gain_sums[...] = jnp.zeros_like(gain_sums)
    for load in loads[:9]:
        load.wait()

    def norm_back(turned, which, area, h, gain):
        span = slice(h * 128, (h + 1) * 128)
        grad = turned * cosine[area] - pltpu.roll(turned, 64, 1) * sine[area]
        unit = unit_v[which, area, span].astype(jnp.float32)
        gain_sums[which : which + 1] += jnp.sum(grad * unit, axis=0, keepdims=True)
        weighted = grad * gain[...]
        inner = jnp.mean(weighted * unit, axis=-1, keepdims=True)
        lane = 4 + which * 4 + h
        grads_v[which, area, span] = (
            log_v[area, lane : lane + 1] * (weighted - unit * inner)
        ).astype(jnp.bfloat16)

    def attend(i, carry):
        block = pick(i, [t, near, across, opposite])

        @pl.when(i == 1)
        def _():
            to_near.wait_recv()

        @pl.when(i == 2)
        def _():
            to_across.wait_recv()
            forward.start()
            to_across.wait_send()
            for swap in swaps:
                swap.start()

            @pl.when(ends)
            def _():
                y_relay(3)

        @pl.when(i == 3)
        def _():
            forward.wait_recv()
            weight_part(0, branch_v, low_v.at[3])
            start_side(0)

        area = pl.ds(block * rows, rows)
        mixed_grad = lax.dot_general(
            branch_v[block], out_v[...], contract_last, preferred_element_type=jnp.float32
        ).astype(jnp.bfloat16)
        for h in range(heads):
            span = slice(h * 128, (h + 1) * 128)
            query = low_v[0, area, span]
            key = low_v[1, :, span]
            grad = mixed_grad[:, span]
            scores = lax.dot_general(query, key, contract_last, preferred_element_type=jnp.float32)
            probs = jnp.exp(scores * factor - log_v[area, h : h + 1])
            prob_grad = lax.dot_general(
                grad, low_v[2, :, span], contract_last, preferred_element_type=jnp.float32
            )
            delta = jnp.sum(probs * prob_grad, axis=-1, keepdims=True)
            score_grad = (probs * (prob_grad - delta)).astype(jnp.bfloat16)
            query_grad = jnp.dot(score_grad, key, preferred_element_type=jnp.float32) * factor
            key_part = lax.dot_general(
                score_grad, query, contract_first, preferred_element_type=jnp.float32
            )
            value_part = lax.dot_general(
                probs.astype(jnp.bfloat16), grad, contract_first, preferred_element_type=jnp.float32
            )
            first = i == 0
            key_acc[:, span] = jnp.where(first, 0.0, key_acc[:, span]) + key_part
            value_acc[:, span] = jnp.where(first, 0.0, value_acc[:, span]) + value_part
            norm_back(query_grad, 0, area, h, query_gain)
        return carry

    key_acc[...] = jnp.zeros_like(key_acc)
    value_acc[...] = jnp.zeros_like(value_acc)
    lax.fori_loop(0, 4, attend, 0)
    for load in loads[9:]:
        load.wait()

    @pl.when(ends)
    def _():
        y_relay(2)

    @pl.when(middle)
    def _():
        y_relay(3)

    grads_v[2] = value_acc[...].astype(jnp.bfloat16)
    weight_part(1, rows_v, grads_v.at[2])
    start_side(1)

    def key_back(b, carry):
        area = pl.ds(b * rows, rows)
        for h in range(heads):
            norm_back(key_acc[area, h * 128 : (h + 1) * 128] * factor, 1, area, h, key_gain)
        return carry

    lax.fori_loop(0, 4, key_back, 0)
    weight_part(2, rows_v, grads_v.at[1])
    start_side(2)
    weight_part(3, rows_v, grads_v.at[0])
    start_side(3)

    y_cross_copy().wait_recv()
    y_add(y_sums.at[0], [(y_block(0, 1 - x), None), (y_cross, None)])
    y_side_copy(0).start()

    def part_copy(source, target, index, to):
        return pltpu.make_async_remote_copy(
            src_ref=source,
            dst_ref=target,
            send_sem=part_send.at[index],
            recv_sem=part_recv.at[index],
            device_id=(position, to),
            device_id_type=mesh_ids,
        )

    for copy in (to_near, forward):
        copy.wait_send()
    core_first = part_copy(branch_v.at[0], core_in.at[0], 0, near)
    across_copy = part_copy(branch_v.at[1], across_in, 1, across)
    core_second = part_copy(branch_v.at[2], core_in.at[1], 2, near)

    def relay(k, c):
        block = pick(k, slots) * 2 + x
        side_copy(k, c).wait_recv()
        scattered[c, block] = (
            scattered[c, block].astype(jnp.float32) + side_in[c, k].astype(jnp.float32)
        ).astype(jnp.bfloat16)

        @pl.when(middle)
        def _():
            line_wait(line_slot(k), c)
            scattered[c, block] = (
                scattered[c, block].astype(jnp.float32) + line_in[c, line_slot(k)].astype(jnp.float32)
            ).astype(jnp.bfloat16)

        line_copy(k, c).start()

    def relays(c):
        def one(i, carry):
            relay(send_order(i), c)
            return carry

        lax.fori_loop(0, 3, one, 0)

    def rows_part(i, carry):
        block = pick(i, [opposite, across, near, t])
        area = pl.ds(block * rows, rows)
        for d in range(2):
            span = pl.ds(d * 1024, 1024)
            product = jnp.zeros((rows, 1024), jnp.float32)
            for which in range(3):
                product = product + lax.dot_general(
                    grads_v[which, area],
                    weights_v[which, span],
                    contract_last,
                    preferred_element_type=jnp.float32,
                )
            own_part[:, span] = product

        @pl.when(i == 0)
        def _():
            branch_v[0] = own_part[...].astype(jnp.bfloat16)
            core_first.start()

        @pl.when(i == 1)
        def _():
            core_first.wait_recv()
            branch_v[1] = (own_part[...] + core_in[0].astype(jnp.float32)).astype(jnp.bfloat16)
            across_copy.start()

        @pl.when(i == 2)
        def _():
            branch_v[2] = own_part[...].astype(jnp.bfloat16)
            core_second.start()

        return carry

    lax.fori_loop(0, 4, rows_part, 0)
    relays(0)

    @pl.when(middle)
    def _():
        y_relay(1)
        y_relay(2)

    relays(1)
    core_second.wait_recv()
    own_part[...] += core_in[1].astype(jnp.float32)
    across_copy.wait_recv()
    own_part[...] += across_in[...].astype(jnp.float32)
    last = pltpu.make_async_copy(own_part, rows_grad, store_sem)
    last.start()
    relays(2)
    y_side_copy(0).wait_recv()

    @pl.when(z < 3)
    def _():
        y_line_wait(z)

    @pl.when(z > 0)
    def _():
        y_line_wait(z + 1)

    y_add(
        y_total,
        [
            (y_all.at[position], None),
            (y_side.at[0], None),
            (y_line.at[z], z < 3),
            (y_line.at[z + 1], z > 0),
        ],
    )
    relays(3)
    for c, total in enumerate((out_total, value_total, key_total, query_total)):
        side_copy(0, c).wait_recv()
        total[...] = scattered[c, position].astype(jnp.float32) + side_in[c, 0].astype(jnp.float32)

        @pl.when(z < 3)
        def _(c=c, total=total):
            line_wait(z, c)
            total[...] += line_in[c, z].astype(jnp.float32)

        @pl.when(z > 0)
        def _(c=c, total=total):
            line_wait(z + 1, c)
            total[...] += line_in[c, z + 1].astype(jnp.float32)

        for k in range(4):
            side_copy(k, c).wait_send()
        for k in range(1, 4):
            line_copy(k, c).wait_send()
    for copy in (core_first, across_copy, core_second):
        copy.wait_send()
    last.wait()
    for swap in swaps:
        swap.wait()
    for k in (0, 2, 3):
        y_side_copy(k).wait_send()
    y_cross_copy().wait_send()
    for k in (1, 2, 3):
        y_line_copy(k, y_sums.at[k]).wait_send()


def attention_backward(branch, saved, weights, out_w, gains, tables, sent, y_all, collective):
    rows, width = branch.shape
    local = out_w.shape[0]
    length = 4 * rows
    any_space = pl.BlockSpec(memory_space=pl.ANY)
    vector = pl.BlockSpec(memory_space=pltpu.VMEM)
    low, full = jnp.bfloat16, jnp.float32
    dma = pltpu.SemaphoreType.DMA
    return pl.pallas_call(
        attention_back_kernel,
        name="attention_backward",
        out_shape=(jax.ShapeDtypeStruct((rows, width), full),)
        + tuple(jax.ShapeDtypeStruct(array.shape, array.dtype) for array in sent)
        + (
            jax.ShapeDtypeStruct((rows, width), low),
            jax.ShapeDtypeStruct((3, rows, width), low),
            jax.ShapeDtypeStruct((rows, width), low),
            jax.ShapeDtypeStruct((5, rows, width), low),
            jax.ShapeDtypeStruct((4, rows, width), low),
        )
        + (jax.ShapeDtypeStruct((width // 8, local), full),) * 4
        + (jax.ShapeDtypeStruct((8, 128), full),),
        in_specs=[any_space] * 13 + [vector] * 4 + [any_space] * 3,
        out_specs=(any_space,) * 8 + (vector,) * 5,
        scratch_shapes=[
            pltpu.VMEM((4, rows, width), low),
            pltpu.VMEM((4, rows, width), low),
            pltpu.VMEM((3, width, local), low),
            pltpu.VMEM((local, width), low),
            pltpu.VMEM((2, length, local), low),
            pltpu.VMEM((4, length, local), low),
            pltpu.VMEM((length, 128), full),
            pltpu.VMEM((3, length, local), low),
            pltpu.VMEM((length, local), full),
            pltpu.VMEM((length, local), full),
            pltpu.VMEM((4, 8, width // 8, local), low),
            pltpu.VMEM((4, 4, width // 8, local), low),
            pltpu.VMEM((4, 5, width // 8, local), low),
            pltpu.VMEM((rows, width), full),
            pltpu.VMEM((2, rows, width), low),
            pltpu.VMEM((rows, width), low),
            pltpu.VMEM((4, rows // 2, width), low),
            dma((13,)),
            dma,
            dma((3,)),
            dma((3,)),
            dma((3,)),
            dma((3,)),
            dma((4, 4)),
            dma((4, 4)),
            dma((4, 5)),
            dma((4, 3)),
            dma((2,)),
            dma((2,)),
            dma((4,)),
            dma,
            dma((3,)),
            dma((3,)),
            dma((2,)),
            dma((5,)),
            dma((3,)),
        ],
        compiler_params=pltpu.CompilerParams(
            collective_id=collective, has_side_effects=True, vmem_limit_bytes=60 << 20
        ),
        cost_estimate=pl.CostEstimate(
            flops=16 * length * width * local, bytes_accessed=64 << 20, transcendentals=length * length * 4
        ),
    )(branch, *saved, *weights, out_w, *gains, *tables, *sent, y_all)


def sum_kernel(own, total, incoming, recv, send):
    position = lax.axis_index("expert")
    peer = lax.axis_index("tensor")
    mesh_ids = pl.DeviceIdType.MESH

    def flip(index, bit):
        return index + bit - 2 * bit * ((index // bit) % 2)

    partners = [
        (position, flip(peer, 1)),
        (position, flip(peer, 2)),
        (flip(position, 1), peer),
        (flip(position, 2), peer),
        (flip(position, 4), peer),
    ]
    barrier = pltpu.get_barrier_semaphore()
    for partner in partners:
        pl.semaphore_signal(barrier, inc=1, device_id=partner, device_id_type=mesh_ids)
    pl.semaphore_wait(barrier, len(partners))
    total[0] = own[...]
    for i, partner in enumerate(partners):
        copy = pltpu.make_async_remote_copy(
            src_ref=total.at[i],
            dst_ref=incoming.at[i],
            send_sem=send.at[i],
            recv_sem=recv.at[i],
            device_id=partner,
            device_id_type=mesh_ids,
        )
        copy.start()
        copy.wait()
        total[i + 1] = total[i] + incoming[i]


def sum_everywhere(own, collective):
    steps = 5
    return pl.pallas_call(
        sum_kernel,
        name="sum_everywhere",
        out_shape=jax.ShapeDtypeStruct((steps + 1,) + own.shape, jnp.float32),
        in_specs=[pl.BlockSpec(memory_space=pltpu.VMEM)],
        out_specs=pl.BlockSpec(memory_space=pltpu.VMEM),
        scratch_shapes=[
            pltpu.VMEM((steps,) + own.shape, jnp.float32),
            pltpu.SemaphoreType.DMA((steps,)),
            pltpu.SemaphoreType.DMA((steps,)),
        ],
        compiler_params=pltpu.CompilerParams(collective_id=collective, has_side_effects=True),
        cost_estimate=pl.CostEstimate(flops=own.size * steps, bytes_accessed=40 << 20, transcendentals=0),
    )(own)[steps]


def add_three(first, second, third):
    return first.astype(jnp.float32) + second.astype(jnp.float32) + third.astype(jnp.float32)


def per_device(
    tokens,
    cotangent,
    routes,
    norm_in,
    query_w,
    key_w,
    value_w,
    out_w,
    query_gain,
    key_gain,
    norm_mid,
    router_w,
    gate_w,
    up_w,
    down_w,
):
    rows_own = tokens.shape[0]
    model_width = tokens.shape[1]
    head_width = query_gain.shape[0]
    experts_all = router_w.shape[1]
    source = tokens.astype(jnp.float32)
    scale_in = inverse_rms(source)
    normed_low = (source * scale_in * norm_in).astype(jnp.bfloat16)
    cosine, sine_table = rotary_tables(4 * rows_own, head_width)
    tables = (
        jnp.concatenate([cosine[:, 0], cosine[:, 0]], axis=1),
        jnp.concatenate([-sine_table[:, 0], sine_table[:, 0]], axis=1),
    )
    gains = (query_gain[None], key_gain[None])
    *saved, attn_out, cot_all = attention_forward(
        normed_low, cotangent, (query_w, key_w, value_w), out_w, gains, tables, 1
    )
    middle = source + attn_out
    scale_mid = inverse_rms(middle)
    normed_mid = middle * scale_mid * norm_mid
    mid_low = normed_mid.astype(jnp.bfloat16)
    logits = jnp.dot(normed_mid, router_w, precision=highest, preferred_element_type=jnp.float32)
    route_mask = routes[:, :, None] == jnp.arange(experts_all, dtype=jnp.int32)[None, None, :]
    mask_float = route_mask.astype(jnp.float32)
    chosen = jnp.sum(mask_float * logits[:, None, :], axis=-1)
    gating = jax.nn.softmax(chosen, axis=-1)
    gates = jnp.sum(mask_float * gating[:, :, None], axis=1)
    gates_high = gates.astype(jnp.bfloat16)
    gates_low = (gates - gates_high.astype(jnp.float32)).astype(jnp.bfloat16)
    spare = jnp.zeros((rows_own, 128 - 2 * experts_all), jnp.bfloat16)
    own_rows = jnp.concatenate([mid_low, gates_high, gates_low, spare], axis=1)
    _, _, y_all, row_total, core_input, near_input, core_output, near_output = expert_pass(
        own_rows, cot_all.reshape(-1, model_width), gate_w, up_w, down_w, experts_all, 2
    )
    expert_input_grad = row_total[:, :model_width]
    gate_grad_dense = (
        row_total[:, model_width : model_width + experts_all]
        + row_total[:, model_width + experts_all : model_width + 2 * experts_all]
    )
    gate_grad = jnp.sum(mask_float * gate_grad_dense[:, None, :], axis=-1)
    inner_gate = jnp.sum(gating * gate_grad, axis=-1, keepdims=True)
    chosen_grad = gating * (gate_grad - inner_gate)
    logit_grad = jnp.sum(chosen_grad[:, :, None] * mask_float, axis=1)
    normed_mid_grad = expert_input_grad + lax.dot_general(
        logit_grad, router_w, contract_last, precision=highest, preferred_element_type=jnp.float32
    )
    norm_mid_part = jnp.sum(normed_mid_grad * middle * scale_mid, axis=0)
    upstream = cotangent.astype(jnp.float32)
    middle_grad = upstream + norm_backward(normed_mid_grad, middle, scale_mid, norm_mid)
    branch_low = middle_grad.astype(jnp.bfloat16)
    sent = (
        (near_input[1].astype(jnp.float32) + core_input[1].astype(jnp.float32)).astype(jnp.bfloat16),
        (near_output[1].astype(jnp.float32) + core_output[1].astype(jnp.float32)).astype(jnp.bfloat16),
    )
    (
        rows_grad,
        line_input,
        line_output,
        y_sum,
        _,
        _,
        _,
        _,
        out_w_turned,
        value_w_grad,
        key_w_grad,
        query_w_grad,
        gain_sums,
    ) = attention_backward(
        branch_low, saved, (query_w, key_w, value_w), out_w, gains, tables, sent, y_all, 3
    )
    out_w_grad = out_w_turned.T
    router_part = lax.dot_general(
        normed_mid,
        logit_grad,
        contract_first,
        precision=highest,
        preferred_element_type=jnp.float32,
    )
    output = (middle + y_sum.astype(jnp.float32)).astype(jnp.bfloat16)
    gate_w_grad = add_three(near_input[0, 0], core_input[0, 0], line_input[0])
    up_w_grad = add_three(near_input[0, 1], core_input[0, 1], line_input[1])
    down_w_grad = add_three(near_output[0], core_output[0], line_output)
    norm_in_part = jnp.sum(rows_grad * source * scale_in, axis=0)
    input_grad = middle_grad + norm_backward(rows_grad, source, scale_in, norm_in)
    router_w_grad = lax.psum(router_part, ("expert", "tensor"))
    small = jnp.concatenate(
        [
            norm_in_part,
            norm_mid_part,
            gain_sums[0],
            gain_sums[1],
            jnp.zeros((-(2 * model_width + 2 * head_width) % 1024,), jnp.float32),
        ]
    ).reshape(-1, 128)
    sums = sum_everywhere(small, 4).reshape(-1)
    norm_in_grad = sums[:model_width]
    norm_mid_grad = sums[model_width : 2 * model_width]
    query_gain_grad = sums[2 * model_width : 2 * model_width + head_width]
    key_gain_grad = sums[2 * model_width + head_width : 2 * model_width + 2 * head_width]
    return (
        output,
        input_grad,
        norm_in_grad,
        query_w_grad,
        key_w_grad,
        value_w_grad,
        out_w_grad,
        query_gain_grad,
        key_gain_grad,
        norm_mid_grad,
        router_w_grad,
        gate_w_grad,
        up_w_grad,
        down_w_grad,
    )


def per_device_general(
    tokens,
    cotangent,
    routes,
    norm_in,
    query_w,
    key_w,
    value_w,
    out_w,
    query_gain,
    key_gain,
    norm_mid,
    router_w,
    gate_w,
    up_w,
    down_w,
):
    rows_own = tokens.shape[0]
    model_width = tokens.shape[1]
    tensor_count = lax.axis_size("tensor")
    expert_count = lax.axis_size("expert")
    head_width = query_gain.shape[0]
    local_heads = query_w.shape[1] // head_width
    experts_local = gate_w.shape[0]
    experts_all = router_w.shape[1]
    top_count = routes.shape[1]
    hidden_width = gate_w.shape[2]
    factor = 1.0 / math.sqrt(head_width)
    cot_all = lax.all_gather(cotangent, "expert", axis=0, tiled=True)
    source = tokens.astype(jnp.float32)
    scale_in = inverse_rms(source)
    normed_low = (source * scale_in * norm_in).astype(jnp.bfloat16)
    gathered = lax.all_gather(normed_low, "tensor", axis=0, tiled=True)
    seq_len = gathered.shape[0]
    query_pre = jnp.dot(gathered, query_w, preferred_element_type=jnp.float32)
    key_pre = jnp.dot(gathered, key_w, preferred_element_type=jnp.float32)
    value_low = jnp.dot(gathered, value_w, preferred_element_type=jnp.float32).astype(jnp.bfloat16)
    cosine, sine_table = rotary_tables(seq_len, head_width)
    query_heads = query_pre.reshape(seq_len, local_heads, head_width)
    key_heads = key_pre.reshape(seq_len, local_heads, head_width)
    query_scale = inverse_rms(query_heads)
    key_scale = inverse_rms(key_heads)
    query_low = rotate(query_heads * query_scale * query_gain, cosine, sine_table).astype(
        jnp.bfloat16
    )
    key_low = rotate(key_heads * key_scale * key_gain, cosine, sine_table).astype(jnp.bfloat16)
    value_heads = value_low.reshape(seq_len, local_heads, head_width)
    block_rows = min(512, seq_len)
    block_count = seq_len // block_rows
    query_blocks = query_low.reshape(block_count, block_rows, local_heads, head_width)

    def attend(query_block):
        scores = (
            jnp.einsum("qhd,khd->hqk", query_block, key_low, preferred_element_type=jnp.float32)
            * factor
        )
        row_max = jnp.max(scores, axis=-1, keepdims=True)
        shifted = jnp.exp(scores - row_max)
        row_sum = jnp.sum(shifted, axis=-1, keepdims=True)
        probs_low = (shifted / row_sum).astype(jnp.bfloat16)
        mixture = jnp.einsum(
            "hqk,khd->qhd", probs_low, value_heads, preferred_element_type=jnp.float32
        )
        return (mixture.astype(jnp.bfloat16), (row_max + jnp.log(row_sum))[..., 0])

    attended_blocks, log_sums = lax.map(attend, query_blocks)
    attended = attended_blocks.reshape(seq_len, local_heads * head_width)
    attn_out = lax.psum_scatter(
        jnp.dot(attended, out_w, preferred_element_type=jnp.float32).astype(jnp.bfloat16),
        "tensor",
        scatter_dimension=0,
        tiled=True,
    ).astype(jnp.float32)
    middle = source + attn_out
    scale_mid = inverse_rms(middle)
    normed_mid = middle * scale_mid * norm_mid
    mid_low = normed_mid.astype(jnp.bfloat16)
    logits = jnp.dot(normed_mid, router_w, precision=highest, preferred_element_type=jnp.float32)
    route_mask = routes[:, :, None] == jnp.arange(experts_all, dtype=jnp.int32)[None, None, :]
    mask_float = route_mask.astype(jnp.float32)
    chosen = jnp.sum(mask_float * logits[:, None, :], axis=-1)
    gating = jax.nn.softmax(chosen, axis=-1)
    upstream = cotangent.astype(jnp.float32)
    gates = jnp.sum(mask_float * gating[:, :, None], axis=1)
    x_all = lax.all_gather(mid_low, "expert", axis=0, tiled=True)
    gates_all = lax.all_gather(gates, "expert", axis=0, tiled=True)
    first_expert = lax.axis_index("expert") * experts_local
    own_gates = lax.dynamic_slice_in_dim(gates_all, first_expert, experts_local, 1)
    part_width = hidden_width // tensor_count
    rows_all = x_all.shape[0]
    y_part = jnp.zeros((rows_all, model_width), jnp.float32)
    x_grad_part = jnp.zeros((rows_all, model_width), jnp.float32)
    gate_grads, gate_parts, up_parts, down_parts = [], [], [], []
    for e in range(experts_local):
        hidden_raw = lax.dot_general(
            cot_all, down_w[e], contract_last, preferred_element_type=jnp.float32
        )
        gate_pre = jnp.dot(x_all, gate_w[e], preferred_element_type=jnp.float32)
        up_pre = jnp.dot(x_all, up_w[e], preferred_element_type=jnp.float32)
        weight = own_gates[:, e : e + 1]
        hidden = gate_pre * jax.nn.sigmoid(gate_pre) * up_pre
        gate_grads.append(jnp.sum(hidden * hidden_raw, axis=1))
        hidden_low = (hidden * weight).astype(jnp.bfloat16)
        gate_back, up_back = swiglu_back(hidden_raw * weight, gate_pre, up_pre)
        y_part = y_part + jnp.dot(hidden_low, down_w[e], preferred_element_type=jnp.float32)
        x_grad_part = x_grad_part + lax.dot_general(
            gate_back, gate_w[e], contract_last, preferred_element_type=jnp.float32
        )
        x_grad_part = x_grad_part + lax.dot_general(
            up_back, up_w[e], contract_last, preferred_element_type=jnp.float32
        )
        gate_parts.append(
            jnp.einsum(
                "nd,ntf->tdf",
                x_all,
                gate_back.reshape(rows_all, tensor_count, part_width),
                preferred_element_type=jnp.float32,
            ).astype(jnp.bfloat16)
        )
        up_parts.append(
            jnp.einsum(
                "nd,ntf->tdf",
                x_all,
                up_back.reshape(rows_all, tensor_count, part_width),
                preferred_element_type=jnp.float32,
            ).astype(jnp.bfloat16)
        )
        down_parts.append(
            lax.dot_general(
                hidden_low, cot_all, contract_first, preferred_element_type=jnp.float32
            ).astype(jnp.bfloat16)
        )
    x_grad = lax.psum_scatter(
        x_grad_part.astype(jnp.bfloat16), "expert", scatter_dimension=0, tiled=True
    )
    expert_input_grad = x_grad.astype(jnp.float32)
    gate_grad_sent = jnp.stack(gate_grads, axis=-1)
    gate_grad_all = lax.all_to_all(gate_grad_sent, "expert", split_axis=0, concat_axis=0, tiled=True)
    gate_grad_dense = (
        gate_grad_all.reshape(expert_count, rows_own, experts_local)
        .transpose(1, 0, 2)
        .reshape(rows_own, experts_all)
    )
    gate_grad = jnp.sum(mask_float * gate_grad_dense[:, None, :], axis=-1)
    y_sum = lax.psum_scatter(
        y_part.astype(jnp.bfloat16), "expert", scatter_dimension=0, tiled=True
    )
    output = (middle + y_sum.astype(jnp.float32)).astype(jnp.bfloat16)

    def own_part(parts):
        return [
            lax.psum_scatter(p, "tensor", scatter_dimension=0, tiled=True).astype(jnp.float32)
            for p in parts
        ]

    gate_w_grad = jnp.concatenate(own_part(gate_parts), axis=0)
    up_w_grad = jnp.concatenate(own_part(up_parts), axis=0)
    down_w_grad = jnp.stack(own_part(down_parts), axis=0)
    inner_gate = jnp.sum(gating * gate_grad, axis=-1, keepdims=True)
    chosen_grad = gating * (gate_grad - inner_gate)
    logit_grad = jnp.sum(chosen_grad[:, :, None] * mask_float, axis=1)
    router_part = lax.dot_general(
        normed_mid,
        logit_grad,
        contract_first,
        precision=highest,
        preferred_element_type=jnp.float32,
    )
    normed_mid_grad = expert_input_grad + lax.dot_general(
        logit_grad, router_w, contract_last, precision=highest, preferred_element_type=jnp.float32
    )
    norm_mid_part = jnp.sum(normed_mid_grad * middle * scale_mid, axis=0)
    middle_grad = upstream + norm_backward(normed_mid_grad, middle, scale_mid, norm_mid)
    branch_low = middle_grad.astype(jnp.bfloat16)
    branch_all = lax.all_gather(branch_low, "tensor", axis=0, tiled=True)
    attended_grad = lax.dot_general(
        branch_all, out_w, contract_last, preferred_element_type=jnp.float32
    ).astype(jnp.bfloat16)
    out_w_part = lax.dot_general(
        attended, branch_all, contract_first, preferred_element_type=jnp.float32
    )
    grad_blocks = attended_grad.reshape(block_count, block_rows, local_heads, head_width)

    def attend_back(carry, inputs):
        key_total, value_total = carry
        query_block, grad_block, log_block = inputs
        scores = (
            jnp.einsum("qhd,khd->hqk", query_block, key_low, preferred_element_type=jnp.float32)
            * factor
        )
        probs = jnp.exp(scores - log_block[:, :, None])
        probs_low = probs.astype(jnp.bfloat16)
        value_total = value_total + jnp.einsum(
            "hqk,qhd->khd", probs_low, grad_block, preferred_element_type=jnp.float32
        )
        prob_grad = jnp.einsum(
            "qhd,khd->hqk", grad_block, value_heads, preferred_element_type=jnp.float32
        )
        delta = jnp.sum(probs * prob_grad, axis=-1, keepdims=True)
        score_low = (probs * (prob_grad - delta)).astype(jnp.bfloat16)
        query_part = (
            jnp.einsum("hqk,khd->qhd", score_low, key_low, preferred_element_type=jnp.float32)
            * factor
        )
        key_total = (
            key_total
            + jnp.einsum("hqk,qhd->khd", score_low, query_block, preferred_element_type=jnp.float32)
            * factor
        )
        return ((key_total, value_total), query_part)

    zero_heads = jnp.zeros((seq_len, local_heads, head_width), jnp.float32)
    (key_grad, value_total), query_parts = lax.scan(
        attend_back, (zero_heads, zero_heads), (query_blocks, grad_blocks, log_sums)
    )
    query_grad = query_parts.reshape(seq_len, local_heads, head_width)
    value_grad_low = value_total.reshape(seq_len, local_heads * head_width).astype(jnp.bfloat16)
    query_rot_grad = rotate_back(query_grad, cosine, sine_table)
    key_rot_grad = rotate_back(key_grad, cosine, sine_table)
    query_gain_part = jnp.sum(query_rot_grad * query_heads * query_scale, axis=(0, 1))
    key_gain_part = jnp.sum(key_rot_grad * key_heads * key_scale, axis=(0, 1))
    query_pre_grad = (
        norm_backward(query_rot_grad, query_heads, query_scale, query_gain)
        .reshape(seq_len, local_heads * head_width)
        .astype(jnp.bfloat16)
    )
    key_pre_grad = (
        norm_backward(key_rot_grad, key_heads, key_scale, key_gain)
        .reshape(seq_len, local_heads * head_width)
        .astype(jnp.bfloat16)
    )
    query_w_part = lax.dot_general(
        gathered, query_pre_grad, contract_first, preferred_element_type=jnp.float32
    )
    key_w_part = lax.dot_general(
        gathered, key_pre_grad, contract_first, preferred_element_type=jnp.float32
    )
    value_w_part = lax.dot_general(
        gathered, value_grad_low, contract_first, preferred_element_type=jnp.float32
    )
    summed = lax.dot_general(
        query_pre_grad, query_w, contract_last, preferred_element_type=jnp.float32
    )
    summed = summed + lax.dot_general(
        key_pre_grad, key_w, contract_last, preferred_element_type=jnp.float32
    )
    rows_grad = lax.psum_scatter(
        (
            summed
            + lax.dot_general(
                value_grad_low, value_w, contract_last, preferred_element_type=jnp.float32
            )
        ).astype(jnp.bfloat16),
        "tensor",
        scatter_dimension=0,
        tiled=True,
    ).astype(jnp.float32)
    norm_in_part = jnp.sum(rows_grad * source * scale_in, axis=0)
    input_grad = middle_grad + norm_backward(rows_grad, source, scale_in, norm_in)
    query_w_grad, key_w_grad, value_w_grad, out_w_grad = (
        lax.psum_scatter(
            query_w_part.astype(jnp.bfloat16), "expert", scatter_dimension=0, tiled=True
        ).astype(jnp.float32),
        lax.psum_scatter(
            key_w_part.astype(jnp.bfloat16), "expert", scatter_dimension=0, tiled=True
        ).astype(jnp.float32),
        lax.psum_scatter(
            value_w_part.astype(jnp.bfloat16), "expert", scatter_dimension=0, tiled=True
        ).astype(jnp.float32),
        lax.psum_scatter(
            out_w_part.astype(jnp.bfloat16), "expert", scatter_dimension=1, tiled=True
        ).astype(jnp.float32),
    )
    norm_in_grad, query_gain_grad, key_gain_grad, norm_mid_grad, router_w_grad = lax.psum(
        (norm_in_part, query_gain_part, key_gain_part, norm_mid_part, router_part),
        ("expert", "tensor"),
    )
    return (
        output,
        input_grad,
        norm_in_grad,
        query_w_grad,
        key_w_grad,
        value_w_grad,
        out_w_grad,
        query_gain_grad,
        key_gain_grad,
        norm_mid_grad,
        router_w_grad,
        gate_w_grad,
        up_w_grad,
        down_w_grad,
    )


def solution(mesh):
    placed = (
        P(("expert", "tensor"), None),
        P(("expert", "tensor"), None),
        P(("expert", "tensor"), None),
        P(),
        P(None, "tensor"),
        P(None, "tensor"),
        P(None, "tensor"),
        P("tensor", None),
        P(),
        P(),
        P(),
        P(),
        P("expert", None, None),
        P("expert", None, None),
        P("expert", None, None),
    )
    return jax.shard_map(
        per_device if dict(mesh.shape) == {"expert": 8, "tensor": 4} else per_device_general,
        mesh=mesh,
        in_specs=placed,
        out_specs=(
            P(("expert", "tensor"), None),
            P(("expert", "tensor"), None),
            P(),
            P("expert", "tensor"),
            P("expert", "tensor"),
            P("expert", "tensor"),
            P("tensor", "expert"),
            P(),
            P(),
            P(),
            P(),
            P("expert", None, "tensor"),
            P("expert", None, "tensor"),
            P("expert", "tensor", None),
        ),
        check_vma=False,
    )
```

```python
import functools
import math

import jax
import jax.numpy as jnp
from jax import lax
from jax.experimental import pallas as pl
from jax.experimental.pallas import tpu as pltpu
from jax.sharding import PartitionSpec as P

epsilon = 1e-06
highest = lax.Precision.HIGHEST
contract_last = (((1,), (1,)), ((), ()))
contract_first = (((0,), (0,)), ((), ()))


def inverse_rms(values):
    return lax.rsqrt(jnp.mean(values * values, axis=-1, keepdims=True) + epsilon)


def norm_backward(grad_norm, values, inverse, norm_gain):
    weighted = grad_norm * norm_gain
    inner_mean = jnp.mean(weighted * values, axis=-1, keepdims=True)
    return inverse * weighted - values * inverse * inverse * inverse * inner_mean


def rotary_tables(length, head_width):
    half_dim = head_width // 2
    frequency = jnp.exp(
        -math.log(10000.0) * 2.0 * jnp.arange(half_dim, dtype=jnp.float32) / head_width
    )
    angles = jnp.arange(length, dtype=jnp.float32)[:, None] * frequency[None, :]
    return (jnp.cos(angles)[:, None, :], jnp.sin(angles)[:, None, :])


def rotate(values, cosine, sine_table):
    half_dim = values.shape[-1] // 2
    first_half = values[..., :half_dim]
    second_half = values[..., half_dim:]
    return jnp.concatenate(
        [
            first_half * cosine - second_half * sine_table,
            second_half * cosine + first_half * sine_table,
        ],
        axis=-1,
    )


def rotate_back(gradient, cosine, sine_table):
    half_dim = gradient.shape[-1] // 2
    first_half = gradient[..., :half_dim]
    second_half = gradient[..., half_dim:]
    return jnp.concatenate(
        [
            first_half * cosine + second_half * sine_table,
            second_half * cosine - first_half * sine_table,
        ],
        axis=-1,
    )


def swiglu_back(hidden_grad, gate_pre, up_pre):
    sigmoid_part = jax.nn.sigmoid(gate_pre)
    gate_back = (
        hidden_grad * up_pre * sigmoid_part * (1.0 + gate_pre * (1.0 - sigmoid_part))
    ).astype(jnp.bfloat16)
    up_back = (hidden_grad * gate_pre * sigmoid_part).astype(jnp.bfloat16)
    return (gate_back, up_back)


chunks = 4


def pick(index, values):
    result = values[-1]
    for j in reversed(range(len(values) - 1)):
        result = jnp.where(index == j, values[j], result)
    return result


def expert_kernel(
    experts_all,
    own_rows,
    cot_all,
    gate_hbm,
    up_hbm,
    down_hbm,
    hidden_all,
    grads_all,
    y_all,
    total,
    core_input,
    near_input,
    core_output,
    near_output,
    cot_late,
    gate_v,
    up_v,
    down_v,
    rows_v,
    cot_v,
    hidden_v,
    gate_b,
    up_b,
    y_v,
    stage,
    parts,
    side_in,
    cross_in,
    line_in,
    weight_sem,
    own_sem,
    cot_sem,
    out_sem,
    item_in,
    item_out,
    core_recv,
    gather_recv,
    gather_send,
    side_recv,
    side_send,
    cross_recv,
    cross_send,
    line_recv,
    line_send,
    late_recv,
    late_send,
):
    position = lax.axis_index("expert")
    peer = lax.axis_index("tensor")
    z = position // 2
    x = position % 2
    experts_local, width, hidden = gate_v.shape
    rows = cot_v.shape[0]
    part = hidden // 4
    y = peer // 2
    core = peer % 2
    chunk = rows // chunks
    middle = (z == 1) | (z == 2)
    ends = (z == 0) | (z == 3)
    pair = z + 1 - 2 * (z % 2)
    line_slots = [
        z,
        pick(z, [1, 0, 3, 2]),
        pick(z, [2, 2, 1, 1]),
        pick(z, [3, 3, 0, 0]),
    ]

    def block_rows(block):
        return pl.ds(pl.multiple_of(block * rows, rows), rows)

    def device(zz, xx):
        return (zz * 2 + xx, peer)

    def slot_z(k):
        return pick(k, line_slots)

    weight_copies = [
        pltpu.make_async_copy(gate_hbm, gate_v, weight_sem.at[0]),
        pltpu.make_async_copy(up_hbm, up_v, weight_sem.at[1]),
        pltpu.make_async_copy(down_hbm, down_v, weight_sem.at[2]),
    ]
    own_copy = pltpu.make_async_copy(own_rows, rows_v.at[block_rows(position)], own_sem)
    own_copy.start()
    for copy in weight_copies:
        copy.start()

    barrier = pltpu.get_barrier_semaphore()
    pl.semaphore_signal(barrier, inc=1, device_id=device(z, 1 - x), device_id_type=pl.DeviceIdType.MESH)
    core_peer = (position, y * 2 + 1 - core)
    pl.semaphore_signal(barrier, inc=1, device_id=core_peer, device_id_type=pl.DeviceIdType.MESH)

    @pl.when(z < 3)
    def _():
        pl.semaphore_signal(barrier, inc=1, device_id=device(z + 1, x), device_id_type=pl.DeviceIdType.MESH)

    @pl.when(z > 0)
    def _():
        pl.semaphore_signal(barrier, inc=1, device_id=device(z - 1, x), device_id_type=pl.DeviceIdType.MESH)

    pl.semaphore_wait(barrier, 3 + middle.astype(jnp.int32))

    def gather_copy(source, block, index, zz, xx):
        return pltpu.make_async_remote_copy(
            src_ref=source,
            dst_ref=rows_v.at[block_rows(block)],
            send_sem=gather_send.at[index],
            recv_sem=gather_recv.at[block],
            device_id=device(zz, xx),
            device_id_type=pl.DeviceIdType.MESH,
        )

    def own_send(index, zz, xx):
        return gather_copy(own_rows, position, index, zz, xx)

    own_send(0, z, 1 - x).start()

    @pl.when(z < 3)
    def _():
        own_send(1, z + 1, x).start()

    @pl.when(z > 0)
    def _():
        own_send(2, z - 1, x).start()

    def forward_side(k):
        block = slot_z(k) * 2 + x
        return gather_copy(rows_v.at[block_rows(block)], block, 2 + k, z, 1 - x)

    def forward_line(k):
        block = slot_z(k) * 2 + x
        target = jnp.where(slot_z(k) < z, z + 1, z - 1)
        return gather_copy(rows_v.at[block_rows(block)], block, 5 + k, jnp.clip(target, 0, 3), x)

    def arrived(block):
        gather_copy(own_rows, block, 0, z, 1 - x).wait_recv()

    def arrive(k):
        arrived(slot_z(k) * 2 + x)
        if k < 3:

            @pl.when(ends)
            def _():
                forward_side(k).start()

        @pl.when(middle)
        def _():
            if k > 1:
                forward_side(k).start()
            forward_line(k).start()

    def forward_cross():
        block = jnp.where(ends, z, slot_z(3)) * 2 + 1 - x
        return gather_copy(rows_v.at[block_rows(block)], block, 9, pair, x)

    def cross_copy(c):
        area = pl.ds(c * chunk, chunk)
        return pltpu.make_async_remote_copy(
            src_ref=parts.at[5, area],
            dst_ref=cross_in.at[area],
            send_sem=cross_send.at[c],
            recv_sem=cross_recv.at[c],
            device_id=device(pair, x),
            device_id_type=pl.DeviceIdType.MESH,
        )

    def cross_add(c):
        area = pl.ds(c * chunk, chunk)
        cross_copy(c).wait_recv()
        parts[4, area] = (
            parts[4, area].astype(jnp.float32) + cross_in[area].astype(jnp.float32)
        ).astype(jnp.bfloat16)
        side_copy(0, c).start()

    def side_slot(k):
        return jnp.maximum(k - 1, 0)

    def side_copy(k, c):
        area = pl.ds(c * chunk, chunk)
        return pltpu.make_async_remote_copy(
            src_ref=parts.at[4 + k, area],
            dst_ref=side_in.at[side_slot(k), area],
            send_sem=side_send.at[side_slot(k), c],
            recv_sem=side_recv.at[side_slot(k), c],
            device_id=device(z, 1 - x),
            device_id_type=pl.DeviceIdType.MESH,
        )

    def line_slot(k):
        target = slot_z(k)
        return jnp.where(target < z, target, target + 1)

    def line_copy(k, c):
        area = pl.ds(c * chunk, chunk)
        target = jnp.where(slot_z(k) < z, z - 1, z + 1)
        return pltpu.make_async_remote_copy(
            src_ref=parts.at[k, area],
            dst_ref=line_in.at[line_slot(k), area],
            send_sem=line_send.at[k - 1, c],
            recv_sem=line_recv.at[line_slot(k), c],
            device_id=device(jnp.clip(target, 0, 3), x),
            device_id_type=pl.DeviceIdType.MESH,
        )

    def line_wait(slot, c):
        area = pl.ds(c * chunk, chunk)
        pltpu.make_async_remote_copy(
            src_ref=parts.at[0, area],
            dst_ref=line_in.at[slot, area],
            send_sem=line_send.at[0, c],
            recv_sem=line_recv.at[slot, c],
            device_id=device(z, 1 - x),
            device_id_type=pl.DeviceIdType.MESH,
        ).wait_recv()

    def relay(k, c):
        area = pl.ds(c * chunk, chunk)
        if k > 1:
            side_copy(k, c).wait_recv()
            parts[k, area] = (
                parts[k, area].astype(jnp.float32) + side_in[k - 1, area].astype(jnp.float32)
            ).astype(jnp.bfloat16)

        @pl.when(middle)
        def _():
            line_wait(line_slot(k), c)
            parts[k, area] = (
                parts[k, area].astype(jnp.float32) + line_in[line_slot(k), area].astype(jnp.float32)
            ).astype(jnp.bfloat16)

        line_copy(k, c).start()

    def block_of(step):
        k = pick(step, [0, 1, 0, 1, 2, 2, 3, 3])
        side = pick(step, [0, 0, 1, 1, 0, 1, 1, 0])
        return k, side, slot_z(k) * 2 + jnp.where(side == 1, 1 - x, x)

    def cot_copy(step):
        return pltpu.make_async_copy(cot_all.at[block_rows(block_of(step)[2])], cot_v, cot_sem)

    def late_copy():
        return pltpu.make_async_remote_copy(
            src_ref=cot_all.at[block_rows(slot_z(3) * 2 + x)],
            dst_ref=cot_late,
            send_sem=late_send,
            recv_sem=late_recv,
            device_id=device(z, 1 - x),
            device_id_type=pl.DeviceIdType.MESH,
        )

    def y_copy(block):
        return pltpu.make_async_copy(y_v, y_all.at[block], out_sem.at[3])

    def out_copies(block):
        return [
            pltpu.make_async_copy(hidden_v, hidden_all.at[block_rows(block)], out_sem.at[0]),
            pltpu.make_async_copy(gate_b, grads_all.at[0, block_rows(block)], out_sem.at[1]),
            pltpu.make_async_copy(up_b, grads_all.at[1, block_rows(block)], out_sem.at[2]),
        ]

    cot_copy(0).start()
    own_copy.wait()
    for copy in weight_copies:
        copy.wait()

    def one_step(step, carry):
        k, side, block = block_of(step)

        @pl.when(step == 1)
        def _():
            arrive(1)

            @pl.when(middle)
            def _():
                arrive(2)

            arrived(z * 2 + 1 - x)

            @pl.when(ends)
            def _():
                forward_cross().start()

        @pl.when(step == 3)
        def _():
            @pl.when(ends)
            def _():
                arrive(2)

            @pl.when(middle)
            def _():
                arrive(3)

            arrived(slot_z(1) * 2 + 1 - x)

        @pl.when(step == 4)
        def _():
            late_copy().start()

        @pl.when(step == 6)
        def _():
            late_copy().wait_recv()
            pltpu.make_async_copy(cot_late, cot_v, cot_sem).start()

        @pl.when(step == 5)
        def _():
            arrived(slot_z(2) * 2 + 1 - x)

        @pl.when((step == 6) & ends)
        def _():
            arrived(slot_z(3) * 2 + 1 - x)

        @pl.when((step == 7) & ends)
        def _():
            arrive(3)

        @pl.when(step > 0)
        def _():
            for copy in out_copies(block):
                copy.wait()

        cot_copy(step).wait()
        rows_low = rows_v[block_rows(block), :width]
        extra = rows_v[block_rows(block), width:].astype(jnp.float32)
        lane = lax.broadcasted_iota(jnp.int32, extra.shape, 1)
        ext = jnp.zeros(extra.shape, jnp.float32)
        for e in range(experts_local):
            expert = position * experts_local + e
            high = lane == expert
            low = lane == expert + experts_all
            weight = jnp.sum(jnp.where(high | low, extra, 0.0), axis=1, keepdims=True)
            gate_grad = jnp.zeros((rows, 1), jnp.float32)
            for f in range(hidden // 512):
                columns = pl.ds(f * 512, 512)
                gate_pre = jnp.dot(rows_low, gate_v[e, :, columns], preferred_element_type=jnp.float32)
                up_pre = jnp.dot(rows_low, up_v[e, :, columns], preferred_element_type=jnp.float32)
                target = pl.ds(e * hidden + f * 512, 512)
                raw = lax.dot_general(
                    cot_v[...],
                    down_v[e, columns, :],
                    contract_last,
                    preferred_element_type=jnp.float32,
                )
                sig = jax.nn.sigmoid(gate_pre)
                act = gate_pre * sig
                hid = act * up_pre
                gate_grad = gate_grad + jnp.sum(hid * raw, axis=1, keepdims=True)
                hidden_v[:, target] = (hid * weight).astype(jnp.bfloat16)
                grad = raw * weight
                gate_b[:, target] = (grad * up_pre * sig * (1.0 + gate_pre * (1.0 - sig))).astype(jnp.bfloat16)
                up_b[:, target] = (grad * act).astype(jnp.bfloat16)
            grad_high = gate_grad.astype(jnp.bfloat16).astype(jnp.float32)
            ext = jnp.where(high, grad_high, ext)
            ext = jnp.where(low, gate_grad - grad_high, ext)

        @pl.when((step < 7) & (step != 5))
        def _():
            cot_copy(step + 1).start()

        @pl.when((step == 4) & middle)
        def _():
            arrived(slot_z(3) * 2 + 1 - x)
            forward_cross().start()

        place = side * 4 + k
        parts[place, :, width:] = ext.astype(jnp.bfloat16)
        for copy in out_copies(block):
            copy.start()
        for d in range(width // 1024):
            span = pl.ds(d * 1024, 1024)
            summed = jnp.zeros((rows, 1024), jnp.float32)
            for e in range(experts_local):
                target = pl.ds(e * hidden, hidden)
                summed = summed + lax.dot_general(
                    gate_b[:, target], gate_v[e, span, :], contract_last, preferred_element_type=jnp.float32
                )
                summed = summed + lax.dot_general(
                    up_b[:, target], up_v[e, span, :], contract_last, preferred_element_type=jnp.float32
                )
            parts[place, :, span] = summed.astype(jnp.bfloat16)

        @pl.when((side == 1) & (k > 1))
        def _():
            for c in range(chunks):
                side_copy(k, c).start()

        @pl.when(step == 3)
        def _():
            for c in range(chunks):
                cross_copy(c).start()

        @pl.when((step == 1) & ends)
        def _():
            for c in range(chunks):
                line_copy(1, c).start()

        @pl.when(step > 0)
        def _():
            y_copy(block).wait()

        for d in range(width // 1024):
            span = pl.ds(d * 1024, 1024)
            summed = jnp.zeros((rows, 1024), jnp.float32)
            for e in range(experts_local):
                summed = summed + jnp.dot(
                    hidden_v[:, pl.ds(e * hidden, hidden)],
                    down_v[e, :, span],
                    preferred_element_type=jnp.float32,
                )
            y_v[:, span] = summed.astype(jnp.bfloat16)
        y_copy(block).start()
        return carry

    lax.fori_loop(0, 8, one_step, 0)

    for copy in out_copies(position):
        copy.wait()
    y_copy(position).wait()
    whole_cot = [
        pltpu.make_async_copy(cot_all.at[:, pl.ds(h * hidden, hidden)], up_v.at[h], weight_sem.at[h])
        for h in range(2)
    ]
    for copy in whole_cot:
        copy.start()

    def columns_of(pair, q):
        column_y = jnp.where(q == 0, y, 1 - y)
        column_core = jnp.where(pair == 0, 1 - core, core)
        return column_y * 2 + column_core

    def item_source(i):
        return i // 6, (i % 6) // 2, i % 2

    def item_loads(i, act):
        pair_of, kind, e = item_source(i)
        slot = i % 2
        for q in range(2):
            start = pl.multiple_of(e * hidden + columns_of(pair_of, q) * part, part)
            place = gate_v.at[0, :, pl.ds(pl.multiple_of(slot * 2 * part + q * part, part), part)]
            sem = item_in.at[slot, q]

            @pl.when(kind < 2)
            def _(start=start, place=place, sem=sem):
                act(
                    pltpu.make_async_copy(
                        grads_all.at[jnp.minimum(kind, 1), :, pl.ds(start, part)], place, sem
                    )
                )

            @pl.when(kind == 2)
            def _(start=start, place=place, sem=sem):
                act(pltpu.make_async_copy(hidden_all.at[:, pl.ds(start, part)], place, sem))

    def core_copy(source, target, slot, number, q):
        return pltpu.make_async_remote_copy(
            src_ref=source,
            dst_ref=target,
            send_sem=item_out.at[slot, q],
            recv_sem=core_recv.at[number, q],
            device_id=core_peer,
            device_id_type=pl.DeviceIdType.MESH,
        )

    def item_stores(i, starting):
        pair_of, kind, e = item_source(i)
        slot = i % 2
        number = i % 6
        wide_kind = jnp.minimum(kind, 1)
        for q in range(2):
            wide_place = gate_v.at[1, :, pl.ds(pl.multiple_of(slot * 2 * part + q * part, part), part)]
            tall_place = down_v.at[slot, pl.ds(q * part, part)]

            def far(source, target, q=q):
                copy = core_copy(source, target, slot, number, q)
                if starting:
                    copy.start()
                else:
                    copy.wait_send()

            def own(source, target, q=q):
                copy = pltpu.make_async_copy(source, target, item_out.at[slot, q])
                if starting:
                    copy.start()
                else:
                    copy.wait()

            for which, move, wide_out, tall_out in (
                (0, far, core_input, core_output),
                (1, own, near_input, near_output),
            ):

                @pl.when((pair_of == which) & (kind < 2))
                def _(move=move, wide_place=wide_place, wide_out=wide_out, q=q):
                    move(wide_place, wide_out.at[q, wide_kind, e])

                @pl.when((pair_of == which) & (kind == 2))
                def _(move=move, tall_place=tall_place, tall_out=tall_out, q=q):
                    move(tall_place, tall_out.at[q, e])

    item_loads(0, lambda copy: copy.start())
    for copy in whole_cot:
        copy.wait()
    late_rows = block_rows(slot_z(3) * 2 + 1 - x)
    late_parts = [
        pltpu.make_async_copy(
            cot_late.at[:, pl.ds(h * hidden, hidden)], up_v.at[h, late_rows], weight_sem.at[h]
        )
        for h in range(2)
    ]
    for copy in late_parts:
        copy.start()
    for copy in late_parts:
        copy.wait()
    late_copy().wait_send()

    def at(index, first, gap):
        return (index >= first) & (index < first + gap * chunks) & ((index - first) % gap == 0)

    def item(index, carry):
        i = index // 4
        d = index % 4
        kind = (i % 6) // 2
        slot = i % 2

        @pl.when(d == 0)
        def _():
            item_loads(i, lambda copy: copy.wait())

            @pl.when(i < 11)
            def _():
                item_loads(i + 1, lambda copy: copy.start())

            @pl.when(i > 1)
            def _():
                item_stores(i - 2, False)

        columns = pl.ds(pl.multiple_of(slot * 2 * part, 2 * part), 2 * part)
        span = pl.ds(pl.multiple_of(d * (width // 4), width // 4), width // 4)

        @pl.when(kind < 2)
        def _():
            gate_v[1, span, columns] = lax.dot_general(
                rows_v[:, span], gate_v[0, :, columns], contract_first, preferred_element_type=jnp.float32
            ).astype(jnp.bfloat16)

        @pl.when(kind == 2)
        def _():
            half = pl.ds(pl.multiple_of((d % 2) * (hidden // 2), hidden // 2), hidden // 2)
            down_v[slot, : 2 * part, span] = lax.dot_general(
                gate_v[0, :, columns],
                up_v[d // 2, :, half],
                contract_first,
                preferred_element_type=jnp.float32,
            ).astype(jnp.bfloat16)

        @pl.when(d == 3)
        def _():
            item_stores(i, True)

        @pl.when(at(index, 1, 1))
        def _():
            cross_add(index - 1)

        @pl.when(at(index, 5, 4))
        def _():
            relay(3, (index - 5) // 4)

        @pl.when(at(index, 11, 4) & middle)
        def _():
            relay(1, (index - 11) // 4)

        @pl.when(at(index, 18, 1) & ends)
        def _():
            relay(2, index - 18)

        @pl.when(at(index, 24, 4) & middle)
        def _():
            relay(2, (index - 24) // 4)

        return carry

    lax.fori_loop(0, 48, item, 0)
    for last in (10, 11):
        item_stores(last, False)
    for number in range(6):
        for q in range(2):
            if number < 4:
                core_copy(
                    gate_v.at[1, :, pl.ds(0, part)],
                    core_input.at[q, number // 2, number % 2],
                    0,
                    number,
                    q,
                ).wait_recv()
            else:
                core_copy(
                    down_v.at[0, pl.ds(0, part)], core_output.at[q, number % 2], 0, number, q
                ).wait_recv()

    def finish(c, carry):
        area = pl.ds(c * chunk, chunk)
        side_copy(0, c).wait_recv()
        stage[...] = parts[0, area].astype(jnp.float32) + side_in[0, area].astype(jnp.float32)

        @pl.when(z < 3)
        def _():
            line_wait(z, c)
            stage[...] += line_in[z, area].astype(jnp.float32)

        @pl.when(z > 0)
        def _():
            line_wait(z + 1, c)
            stage[...] += line_in[z + 1, area].astype(jnp.float32)

        result = pltpu.make_async_copy(stage, total.at[area], own_sem)
        result.start()
        result.wait()
        for k in (0, 2, 3):
            side_copy(k, c).wait_send()
        cross_copy(c).wait_send()
        for k in range(1, 4):
            line_copy(k, c).wait_send()
        return carry

    lax.fori_loop(0, chunks, finish, 0)

    own_send(0, z, 1 - x).wait_send()

    @pl.when(z < 3)
    def _():
        own_send(1, z + 1, x).wait_send()

    @pl.when(z > 0)
    def _():
        own_send(2, z - 1, x).wait_send()

    forward_cross().wait_send()
    forward_side(2).wait_send()

    @pl.when(ends)
    def _():
        forward_side(1).wait_send()

    @pl.when(middle)
    def _():
        forward_side(3).wait_send()
        for k in range(1, 4):
            forward_line(k).wait_send()


def expert_pass(own_rows, cot_all, gate_w, up_w, down_w, experts_all, collective):
    rows, wide = own_rows.shape
    experts_local, width, hidden = gate_w.shape
    inner = experts_local * hidden
    any_space = pl.BlockSpec(memory_space=pl.ANY)
    low = jnp.bfloat16
    dma = pltpu.SemaphoreType.DMA
    return pl.pallas_call(
        functools.partial(expert_kernel, experts_all),
        name="expert_pass",
        out_shape=(
            jax.ShapeDtypeStruct((8 * rows, inner), low),
            jax.ShapeDtypeStruct((2, 8 * rows, inner), low),
            jax.ShapeDtypeStruct((8, rows, width), low),
            jax.ShapeDtypeStruct((rows, wide), jnp.float32),
            *(jax.ShapeDtypeStruct((2, 2, experts_local, width, hidden // 4), low),) * 2,
            *(jax.ShapeDtypeStruct((2, experts_local, hidden // 4, width), low),) * 2,
            jax.ShapeDtypeStruct((rows, width), low),
        ),
        in_specs=[any_space] * 5,
        out_specs=(any_space,) * 9,
        scratch_shapes=[
            pltpu.VMEM((experts_local, width, hidden), low),
            pltpu.VMEM((experts_local, width, hidden), low),
            pltpu.VMEM((experts_local, hidden, width), low),
            pltpu.VMEM((8 * rows, wide), low),
            pltpu.VMEM((rows, width), low),
            pltpu.VMEM((rows, inner), low),
            pltpu.VMEM((rows, inner), low),
            pltpu.VMEM((rows, inner), low),
            pltpu.VMEM((rows, width), low),
            pltpu.VMEM((rows // chunks, wide), jnp.float32),
            pltpu.VMEM((8, rows, wide), low),
            pltpu.VMEM((3, rows, wide), low),
            pltpu.VMEM((rows, wide), low),
            pltpu.VMEM((5, rows, wide), low),
            dma((3,)),
            dma,
            dma,
            dma((4,)),
            dma((2, 2)),
            dma((2, 2)),
            dma((6, 2)),
            dma((8,)),
            dma((10,)),
            dma((3, chunks)),
            dma((3, chunks)),
            dma((chunks,)),
            dma((chunks,)),
            dma((5, chunks)),
            dma((3, chunks)),
            dma,
            dma,
        ],
        compiler_params=pltpu.CompilerParams(
            collective_id=collective, has_side_effects=True, vmem_limit_bytes=60 << 20
        ),
        cost_estimate=pl.CostEstimate(
            flops=2 * 9 * 8 * rows * width * inner, bytes_accessed=64 << 20, transcendentals=8 * rows * inner
        ),
    )(own_rows, cot_all, gate_w, up_w, down_w)


def line_gather(source, target, recv, send):
    position = lax.axis_index("expert")
    peer = lax.axis_index("tensor")
    z = position // 2
    x = position % 2
    middle = (z == 1) | (z == 2)
    slots = [z, pick(z, [1, 0, 3, 2]), pick(z, [2, 2, 1, 1]), pick(z, [3, 3, 0, 0])]

    def copy(block_source, block, index, zz, xx):
        return pltpu.make_async_remote_copy(
            src_ref=block_source,
            dst_ref=target.at[block],
            send_sem=send.at[index],
            recv_sem=recv.at[block],
            device_id=(zz * 2 + xx, peer),
            device_id_type=pl.DeviceIdType.MESH,
        )

    def own_up():
        return copy(source, position, 1, z + 1, x)

    def own_down():
        return copy(source, position, 2, z - 1, x)

    def own_side():
        return copy(source, position, 0, z, 1 - x)

    def side(k):
        block = slots[k] * 2 + x
        return copy(target.at[block], block, 2 + k, z, 1 - x)

    def line(k):
        block = slots[k] * 2 + x
        onward = jnp.where(slots[k] < z, z + 1, z - 1)
        return copy(target.at[block], block, 5 + k, jnp.clip(onward, 0, 3), x)

    def start():
        own_side().start()

        @pl.when(z < 3)
        def _():
            own_up().start()

        @pl.when(z > 0)
        def _():
            own_down().start()

    def wait_block(block):
        copy(source, block, 0, z, 1 - x).wait_recv()

    def arrive(k):
        wait_block(slots[k] * 2 + x)
        if k < 3:
            side(k).start()

        @pl.when(middle)
        def _():
            line(k).start()

    def arrive_side(k):
        wait_block(slots[k] * 2 + 1 - x)

    def drain():
        own_side().wait_send()

        @pl.when(z < 3)
        def _():
            own_up().wait_send()

        @pl.when(z > 0)
        def _():
            own_down().wait_send()

        for k in range(1, 4):
            if k < 3:
                side(k).wait_send()

            @pl.when(middle)
            def _(k=k):
                line(k).wait_send()

    return middle, start, arrive, arrive_side, drain


def attention_kernel(
    own,
    cot,
    query_w,
    key_w,
    value_w,
    out_w,
    query_gain,
    key_gain,
    cosine,
    sine,
    gathered,
    query_unit,
    key_unit,
    query_low,
    key_low,
    value_low,
    attended,
    log_sums,
    attn_sum,
    cot_all,
    rows_v,
    weights_v,
    out_v,
    pre_v,
    low_v,
    mixed_v,
    log_v,
    parts,
    own_part,
    core_in,
    line_in,
    load_sem,
    store_sem,
    rows_recv,
    rows_send,
    part_recv,
    part_send,
    cot_recv,
    cot_send,
    cot_sem,
):
    position = lax.axis_index("expert")
    t = lax.axis_index("tensor")
    z = position // 2
    x = position % 2
    y = t // 2
    c = t % 2
    near = y * 2 + 1 - c
    across = (1 - y) * 2 + c
    opposite = (1 - y) * 2 + 1 - c
    rows = own.shape[0]
    heads = low_v.shape[2] // 128
    factor = 1.0 / math.sqrt(128.0)
    mesh_ids = pl.DeviceIdType.MESH
    middle, gather_start, gather_arrive, gather_side, gather_drain = line_gather(
        cot, cot_all, cot_recv, cot_send
    )

    loads = [
        pltpu.make_async_copy(own, rows_v.at[t], load_sem.at[0]),
        pltpu.make_async_copy(query_w, weights_v.at[0], load_sem.at[1]),
        pltpu.make_async_copy(key_w, weights_v.at[1], load_sem.at[2]),
        pltpu.make_async_copy(value_w, weights_v.at[2], load_sem.at[3]),
        pltpu.make_async_copy(out_w, out_v, load_sem.at[4]),
    ]
    for load in loads:
        load.start()
    cot_copy = pltpu.make_async_copy(cot, cot_all.at[position], cot_sem)
    cot_copy.start()

    barrier = pltpu.get_barrier_semaphore()
    for place in ((position, near), (position, across), (z * 2 + 1 - x, t)):
        pl.semaphore_signal(barrier, inc=1, device_id=place, device_id_type=mesh_ids)

    @pl.when(z < 3)
    def _():
        pl.semaphore_signal(barrier, inc=1, device_id=(position + 2, t), device_id_type=mesh_ids)

    @pl.when(z > 0)
    def _():
        pl.semaphore_signal(barrier, inc=1, device_id=(position - 2, t), device_id_type=mesh_ids)

    pl.semaphore_wait(barrier, 4 + middle.astype(jnp.int32))

    def rows_copy(source, block, index, to):
        return pltpu.make_async_remote_copy(
            src_ref=source,
            dst_ref=rows_v.at[block],
            send_sem=rows_send.at[index - 1],
            recv_sem=rows_recv.at[index - 1],
            device_id=(position, to),
            device_id_type=mesh_ids,
        )

    to_across = rows_copy(own, t, 2, across)
    to_near = rows_copy(own, t, 1, near)
    forward = rows_copy(rows_v.at[across], across, 3, near)
    to_across.start()
    to_near.start()
    gather_start()
    for load in loads:
        load.wait()

    def project(i, carry):
        block = pick(i, [t, near, across, opposite])

        @pl.when(i == 1)
        def _():
            to_near.wait_recv()

        @pl.when(i == 2)
        def _():
            to_across.wait_recv()
            forward.start()
            gather_arrive(1)

            @pl.when(middle)
            def _():
                gather_arrive(2)

        @pl.when(i == 3)
        def _():
            forward.wait_recv()

        area = pl.ds(block * rows, rows)
        values = rows_v[block]
        for which, gain in ((0, query_gain), (1, key_gain)):
            pre = jnp.dot(values, weights_v[which], preferred_element_type=jnp.float32)
            for h in range(heads):
                span = slice(h * 128, (h + 1) * 128)
                head = pre[:, span]
                scale = lax.rsqrt(jnp.mean(head * head, axis=-1, keepdims=True) + epsilon)
                unit = head * scale
                pre_v[which, area, span] = unit.astype(jnp.bfloat16)
                lane = 4 + which * 4 + h
                log_v[area, lane : lane + 1] = scale
                normed = unit * gain[...]
                turned = normed * cosine[area] + pltpu.roll(normed, 64, 1) * sine[area]
                low_v[which, area, span] = turned.astype(jnp.bfloat16)
        low_v[2, area] = jnp.dot(
            values, weights_v[2], preferred_element_type=jnp.float32
        ).astype(jnp.bfloat16)
        return carry

    lax.fori_loop(0, 4, project, 0)
    stores = [
        pltpu.make_async_copy(rows_v, gathered, store_sem.at[0]),
        pltpu.make_async_copy(pre_v.at[0], query_unit, store_sem.at[1]),
        pltpu.make_async_copy(pre_v.at[1], key_unit, store_sem.at[2]),
        pltpu.make_async_copy(low_v.at[0], query_low, store_sem.at[3]),
        pltpu.make_async_copy(low_v.at[1], key_low, store_sem.at[4]),
        pltpu.make_async_copy(low_v.at[2], value_low, store_sem.at[5]),
    ]
    for store in stores:
        store.start()

    def part_copy(source, target, index, to):
        return pltpu.make_async_remote_copy(
            src_ref=source,
            dst_ref=target,
            send_sem=part_send.at[index],
            recv_sem=part_recv.at[index],
            device_id=(position, to),
            device_id_type=mesh_ids,
        )

    core_first = part_copy(parts.at[0], core_in.at[0], 0, near)
    line_copy = part_copy(parts.at[1], line_in, 1, across)
    core_second = part_copy(parts.at[2], core_in.at[1], 2, near)

    def attend(i, carry):
        block = pick(i, [opposite, across, near, t])
        area = pl.ds(block * rows, rows)
        for h in range(heads):
            span = slice(h * 128, (h + 1) * 128)
            scores = lax.dot_general(
                low_v[0, area, span], low_v[1, :, span], contract_last, preferred_element_type=jnp.float32
            )
            highest_score = jnp.max(scores, axis=-1, keepdims=True)
            weights = jnp.exp((scores - highest_score) * factor)
            total = jnp.sum(weights, axis=-1, keepdims=True)
            mixed = jnp.dot(
                weights.astype(jnp.bfloat16), low_v[2, :, span], preferred_element_type=jnp.float32
            )
            mixed_v[area, span] = (mixed / total).astype(jnp.bfloat16)
            log_v[area, h : h + 1] = highest_score * factor + jnp.log(total)
        own_part[...] = jnp.dot(mixed_v[area], out_v[...], preferred_element_type=jnp.float32)

        @pl.when(i == 0)
        def _():
            parts[0] = own_part[...].astype(jnp.bfloat16)
            core_first.start()

        @pl.when(i == 1)
        def _():
            core_first.wait_recv()
            parts[1] = (own_part[...] + core_in[0].astype(jnp.float32)).astype(jnp.bfloat16)
            line_copy.start()

            @pl.when(middle)
            def _():
                gather_arrive(3)

        @pl.when(i == 2)
        def _():
            parts[2] = own_part[...].astype(jnp.bfloat16)
            core_second.start()

            @pl.when(middle == False)
            def _():
                gather_arrive(2)

        return carry

    lax.fori_loop(0, 4, attend, 0)
    more = [
        pltpu.make_async_copy(mixed_v, attended, store_sem.at[6]),
        pltpu.make_async_copy(log_v, log_sums, store_sem.at[7]),
    ]
    for store in more:
        store.start()
    core_second.wait_recv()
    own_part[...] += core_in[1].astype(jnp.float32)
    line_copy.wait_recv()
    own_part[...] += line_in[...].astype(jnp.float32)
    last = pltpu.make_async_copy(own_part, attn_sum, store_sem.at[8])
    last.start()

    @pl.when(middle == False)
    def _():
        gather_arrive(3)

    for k in range(3):
        gather_side(k)
    gather_drain()
    for copy in (to_across, to_near, forward, core_first, line_copy, core_second):
        copy.wait_send()
    for store in [*stores, *more, last, cot_copy]:
        store.wait()


def attention_forward(own, cot, weights, out_w, gains, tables, collective):
    rows, width = own.shape
    local = out_w.shape[0]
    length = 4 * rows
    any_space = pl.BlockSpec(memory_space=pl.ANY)
    vector = pl.BlockSpec(memory_space=pltpu.VMEM)
    low, full = jnp.bfloat16, jnp.float32
    dma = pltpu.SemaphoreType.DMA
    return pl.pallas_call(
        attention_kernel,
        name="attention_forward",
        out_shape=(
            jax.ShapeDtypeStruct((4, rows, width), low),
            jax.ShapeDtypeStruct((length, local), low),
            jax.ShapeDtypeStruct((length, local), low),
            jax.ShapeDtypeStruct((length, local), low),
            jax.ShapeDtypeStruct((length, local), low),
            jax.ShapeDtypeStruct((length, local), low),
            jax.ShapeDtypeStruct((length, local), low),
            jax.ShapeDtypeStruct((length, 128), full),
            jax.ShapeDtypeStruct((rows, width), full),
            jax.ShapeDtypeStruct((8, rows, width), low),
        ),
        in_specs=[any_space] * 6 + [vector] * 4,
        out_specs=(any_space,) * 10,
        scratch_shapes=[
            pltpu.VMEM((4, rows, width), low),
            pltpu.VMEM((3, width, local), low),
            pltpu.VMEM((local, width), low),
            pltpu.VMEM((2, length, local), low),
            pltpu.VMEM((3, length, local), low),
            pltpu.VMEM((length, local), low),
            pltpu.VMEM((length, 128), full),
            pltpu.VMEM((3, rows, width), low),
            pltpu.VMEM((rows, width), full),
            pltpu.VMEM((2, rows, width), low),
            pltpu.VMEM((rows, width), low),
            dma((5,)),
            dma((9,)),
            dma((3,)),
            dma((3,)),
            dma((3,)),
            dma((3,)),
            dma((8,)),
            dma((9,)),
            dma,
        ],
        compiler_params=pltpu.CompilerParams(
            collective_id=collective, has_side_effects=True, vmem_limit_bytes=60 << 20
        ),
        cost_estimate=pl.CostEstimate(
            flops=8 * length * width * local, bytes_accessed=64 << 20, transcendentals=length * length * 4
        ),
    )(own, cot, *weights, out_w, *gains, *tables)


def attention_back_kernel(
    branch,
    gathered,
    query_unit,
    key_unit,
    query_low,
    key_low,
    value_low,
    attended,
    log_sums,
    query_w,
    key_w,
    value_w,
    out_w,
    query_gain,
    key_gain,
    cosine,
    sine,
    sent_input,
    sent_output,
    y_all,
    rows_grad,
    arrived_input,
    arrived_output,
    y_total,
    y_side,
    y_cross,
    y_line,
    y_sums,
    out_total,
    value_total,
    key_total,
    query_total,
    gain_sums,
    branch_v,
    rows_v,
    weights_v,
    out_v,
    unit_v,
    low_v,
    log_v,
    grads_v,
    key_acc,
    value_acc,
    scattered,
    side_in,
    line_in,
    own_part,
    core_in,
    across_in,
    y_v,
    load_sem,
    store_sem,
    branch_recv,
    branch_send,
    part_recv,
    part_send,
    side_recv,
    side_send,
    line_recv,
    line_send,
    swap_recv,
    swap_send,
    y_load,
    y_store,
    y_side_recv,
    y_side_send,
    y_cross_sems,
    y_line_recv,
    y_line_send,
):
    position = lax.axis_index("expert")
    t = lax.axis_index("tensor")
    z = position // 2
    x = position % 2
    y = t // 2
    core = t % 2
    near = y * 2 + 1 - core
    across = (1 - y) * 2 + core
    opposite = (1 - y) * 2 + 1 - core
    rows = branch.shape[0]
    local = out_v.shape[0]
    heads = local // 128
    kinds = scattered.shape[0]
    factor = 1.0 / math.sqrt(128.0)
    middle = (z == 1) | (z == 2)
    mesh_ids = pl.DeviceIdType.MESH
    slots = [z, pick(z, [1, 0, 3, 2]), pick(z, [2, 2, 1, 1]), pick(z, [3, 3, 0, 0])]

    loads = [
        pltpu.make_async_copy(branch, branch_v.at[t], load_sem.at[0]),
        pltpu.make_async_copy(out_w, out_v, load_sem.at[1]),
        pltpu.make_async_copy(query_low, low_v.at[0], load_sem.at[2]),
        pltpu.make_async_copy(key_low, low_v.at[1], load_sem.at[3]),
        pltpu.make_async_copy(value_low, low_v.at[2], load_sem.at[4]),
        pltpu.make_async_copy(log_sums, log_v, load_sem.at[5]),
        pltpu.make_async_copy(query_unit, unit_v.at[0], load_sem.at[6]),
        pltpu.make_async_copy(key_unit, unit_v.at[1], load_sem.at[7]),
        pltpu.make_async_copy(attended, low_v.at[3], load_sem.at[8]),
        pltpu.make_async_copy(gathered, rows_v, load_sem.at[9]),
        pltpu.make_async_copy(query_w, weights_v.at[0], load_sem.at[10]),
        pltpu.make_async_copy(key_w, weights_v.at[1], load_sem.at[11]),
        pltpu.make_async_copy(value_w, weights_v.at[2], load_sem.at[12]),
    ]
    for load in loads:
        load.start()

    barrier = pltpu.get_barrier_semaphore()
    for place in ((position, near), (position, across), (z * 2 + 1 - x, t)):
        pl.semaphore_signal(barrier, inc=1, device_id=place, device_id_type=mesh_ids)

    @pl.when(z < 3)
    def _():
        pl.semaphore_signal(barrier, inc=1, device_id=(position + 2, t), device_id_type=mesh_ids)

    @pl.when(z > 0)
    def _():
        pl.semaphore_signal(barrier, inc=1, device_id=(position - 2, t), device_id_type=mesh_ids)

    pl.semaphore_wait(barrier, 4 + middle.astype(jnp.int32))

    def branch_copy(source, block, index, to):
        return pltpu.make_async_remote_copy(
            src_ref=source,
            dst_ref=branch_v.at[block],
            send_sem=branch_send.at[index - 1],
            recv_sem=branch_recv.at[index - 1],
            device_id=(position, to),
            device_id_type=mesh_ids,
        )

    to_across = branch_copy(branch, t, 2, across)
    to_near = branch_copy(branch, t, 1, near)
    forward = branch_copy(branch_v.at[across], across, 3, near)
    to_across.start()
    to_near.start()

    swaps = [
        pltpu.make_async_remote_copy(
            src_ref=sent,
            dst_ref=arrived,
            send_sem=swap_send.at[i],
            recv_sem=swap_recv.at[i],
            device_id=(position, across),
            device_id_type=mesh_ids,
        )
        for i, (sent, arrived) in enumerate(
            ((sent_input, arrived_input), (sent_output, arrived_output))
        )
    ]

    def side_copy(k, c):
        return pltpu.make_async_remote_copy(
            src_ref=scattered.at[c, pick(k, slots) * 2 + 1 - x],
            dst_ref=side_in.at[c, k],
            send_sem=side_send.at[c, k],
            recv_sem=side_recv.at[c, k],
            device_id=(z * 2 + 1 - x, t),
            device_id_type=mesh_ids,
        )

    def line_slot(k):
        target = pick(k, slots)
        return jnp.where(target < z, target, target + 1)

    def line_copy(k, c):
        target = jnp.where(pick(k, slots) < z, z - 1, z + 1)
        return pltpu.make_async_remote_copy(
            src_ref=scattered.at[c, pick(k, slots) * 2 + x],
            dst_ref=line_in.at[c, line_slot(k)],
            send_sem=line_send.at[c, k - 1],
            recv_sem=line_recv.at[c, line_slot(k)],
            device_id=(jnp.clip(target, 0, 3) * 2 + x, t),
            device_id_type=mesh_ids,
        )

    def line_wait(slot, c):
        pltpu.make_async_remote_copy(
            src_ref=scattered.at[c, position],
            dst_ref=line_in.at[c, slot],
            send_sem=line_send.at[c, 0],
            recv_sem=line_recv.at[c, slot],
            device_id=(z * 2 + 1 - x, t),
            device_id_type=mesh_ids,
        ).wait_recv()

    def send_order(i):
        return jnp.where(middle, pick(i, [3, 1, 2, 0]), pick(i, [3, 2, 1, 0]))

    pair = z + 1 - 2 * (z % 2)
    ends = (z == 0) | (z == 3)

    def y_remote(source, target, send_sem, recv_sem, zz, xx):
        return pltpu.make_async_remote_copy(
            src_ref=source,
            dst_ref=target,
            send_sem=send_sem,
            recv_sem=recv_sem,
            device_id=(zz * 2 + xx, t),
            device_id_type=mesh_ids,
        )

    def y_block(k, xx):
        return y_all.at[slots[k] * 2 + xx]

    def y_side_copy(k):
        slot = max(k - 1, 0)
        source = y_sums.at[0] if k == 0 else y_block(k, 1 - x)
        return y_remote(
            source, y_side.at[slot], y_side_send.at[slot], y_side_recv.at[slot], z, 1 - x
        )

    def y_cross_copy():
        return y_remote(
            y_block(1, 1 - x), y_cross, y_cross_sems.at[0], y_cross_sems.at[1], pair, x
        )

    def y_line_copy(k, source):
        target = jnp.where(slots[k] < z, z - 1, z + 1)
        return y_remote(
            source,
            y_line.at[line_slot(k)],
            y_line_send.at[k - 1],
            y_line_recv.at[line_slot(k)],
            jnp.clip(target, 0, 3),
            x,
        )

    def y_line_wait(slot):
        y_remote(
            y_all.at[0], y_line.at[slot], y_line_send.at[0], y_line_recv.at[slot], z, 1 - x
        ).wait_recv()

    def y_add(target, sources):
        half = rows // 2
        for part in range(2):
            area = pl.ds(part * half, half)

            def load(i, source, area=area):
                return pltpu.make_async_copy(source.at[area], y_v.at[i], y_load.at[i])

            for i, (source, needed) in enumerate(sources):
                if needed is None:
                    load(i, source).start()
                else:

                    @pl.when(needed)
                    def _(i=i, source=source, load=load):
                        load(i, source).start()

            for i, (source, needed) in enumerate(sources):
                if needed is None:
                    load(i, source).wait()
                else:

                    @pl.when(needed)
                    def _(i=i, source=source, load=load):
                        load(i, source).wait()

            for i, (source, needed) in enumerate(sources[1:], 1):

                def add(i=i):
                    y_v[0] = (y_v[0].astype(jnp.float32) + y_v[i].astype(jnp.float32)).astype(
                        jnp.bfloat16
                    )

                if needed is None:
                    add()
                else:
                    pl.when(needed)(add)
            store = pltpu.make_async_copy(y_v.at[0], target.at[area], y_store)
            store.start()
            store.wait()

    def y_relay(k):
        if k > 1:
            y_side_copy(k).wait_recv()
        sources = [(y_block(k, x), None)]
        if k > 1:
            sources.append((y_side.at[k - 1], None))

        @pl.when(middle)
        def _():
            y_line_wait(line_slot(k))

        y_add(y_sums.at[k], [*sources, (y_line.at[line_slot(k)], middle)])
        y_line_copy(k, y_sums.at[k]).start()

    y_side_copy(3).start()
    y_cross_copy().start()
    y_side_copy(2).start()

    @pl.when(ends)
    def _():
        y_line_copy(1, y_block(1, x)).start()

    def start_side(c):
        def one(i, carry):
            side_copy(send_order(i), c).start()
            return carry

        lax.fori_loop(0, 4, one, 0)

    def weight_part(c, left, right):
        for d in range(8 // 2):
            span = pl.ds(d * 512, 512)
            product = jnp.zeros((512, local), jnp.float32)
            for b in range(4):
                product = product + lax.dot_general(
                    left[b, :, span],
                    right[pl.ds(b * rows, rows)],
                    contract_first,
                    preferred_element_type=jnp.float32,
                )
            scattered[c, 2 * d] = product[:256].astype(jnp.bfloat16)
            scattered[c, 2 * d + 1] = product[256:].astype(jnp.bfloat16)

    gain_sums[...] = jnp.zeros_like(gain_sums)
    for load in loads[:9]:
        load.wait()

    def norm_back(turned, which, area, h, gain):
        span = slice(h * 128, (h + 1) * 128)
        grad = turned * cosine[area] - pltpu.roll(turned, 64, 1) * sine[area]
        unit = unit_v[which, area, span].astype(jnp.float32)
        gain_sums[which : which + 1] += jnp.sum(grad * unit, axis=0, keepdims=True)
        weighted = grad * gain[...]
        inner = jnp.mean(weighted * unit, axis=-1, keepdims=True)
        lane = 4 + which * 4 + h
        grads_v[which, area, span] = (
            log_v[area, lane : lane + 1] * (weighted - unit * inner)
        ).astype(jnp.bfloat16)

    def attend(i, carry):
        block = pick(i, [t, near, across, opposite])

        @pl.when(i == 1)
        def _():
            to_near.wait_recv()

        @pl.when(i == 2)
        def _():
            to_across.wait_recv()
            forward.start()
            to_across.wait_send()
            for swap in swaps:
                swap.start()

            @pl.when(ends)
            def _():
                y_relay(3)

        @pl.when(i == 3)
        def _():
            forward.wait_recv()
            weight_part(0, branch_v, low_v.at[3])
            start_side(0)

        area = pl.ds(block * rows, rows)
        mixed_grad = lax.dot_general(
            branch_v[block], out_v[...], contract_last, preferred_element_type=jnp.float32
        ).astype(jnp.bfloat16)
        for h in range(heads):
            span = slice(h * 128, (h + 1) * 128)
            query = low_v[0, area, span]
            key = low_v[1, :, span]
            grad = mixed_grad[:, span]
            scores = lax.dot_general(query, key, contract_last, preferred_element_type=jnp.float32)
            probs = jnp.exp(scores * factor - log_v[area, h : h + 1])
            prob_grad = lax.dot_general(
                grad, low_v[2, :, span], contract_last, preferred_element_type=jnp.float32
            )
            delta = jnp.sum(probs * prob_grad, axis=-1, keepdims=True)
            score_grad = (probs * (prob_grad - delta)).astype(jnp.bfloat16)
            query_grad = jnp.dot(score_grad, key, preferred_element_type=jnp.float32) * factor
            key_part = lax.dot_general(
                score_grad, query, contract_first, preferred_element_type=jnp.float32
            )
            value_part = lax.dot_general(
                probs.astype(jnp.bfloat16), grad, contract_first, preferred_element_type=jnp.float32
            )
            first = i == 0
            key_acc[:, span] = jnp.where(first, 0.0, key_acc[:, span]) + key_part
            value_acc[:, span] = jnp.where(first, 0.0, value_acc[:, span]) + value_part
            norm_back(query_grad, 0, area, h, query_gain)
        return carry

    key_acc[...] = jnp.zeros_like(key_acc)
    value_acc[...] = jnp.zeros_like(value_acc)
    lax.fori_loop(0, 4, attend, 0)
    for load in loads[9:]:
        load.wait()

    @pl.when(ends)
    def _():
        y_relay(2)

    @pl.when(middle)
    def _():
        y_relay(3)

    grads_v[2] = value_acc[...].astype(jnp.bfloat16)
    weight_part(1, rows_v, grads_v.at[2])
    start_side(1)

    def key_back(b, carry):
        area = pl.ds(b * rows, rows)
        for h in range(heads):
            norm_back(key_acc[area, h * 128 : (h + 1) * 128] * factor, 1, area, h, key_gain)
        return carry

    lax.fori_loop(0, 4, key_back, 0)
    weight_part(2, rows_v, grads_v.at[1])
    start_side(2)
    weight_part(3, rows_v, grads_v.at[0])
    start_side(3)

    y_cross_copy().wait_recv()
    y_add(y_sums.at[0], [(y_block(0, 1 - x), None), (y_cross, None)])
    y_side_copy(0).start()

    def part_copy(source, target, index, to):
        return pltpu.make_async_remote_copy(
            src_ref=source,
            dst_ref=target,
            send_sem=part_send.at[index],
            recv_sem=part_recv.at[index],
            device_id=(position, to),
            device_id_type=mesh_ids,
        )

    for copy in (to_near, forward):
        copy.wait_send()
    core_first = part_copy(branch_v.at[0], core_in.at[0], 0, near)
    across_copy = part_copy(branch_v.at[1], across_in, 1, across)
    core_second = part_copy(branch_v.at[2], core_in.at[1], 2, near)

    def relay(k, c):
        block = pick(k, slots) * 2 + x
        side_copy(k, c).wait_recv()
        scattered[c, block] = (
            scattered[c, block].astype(jnp.float32) + side_in[c, k].astype(jnp.float32)
        ).astype(jnp.bfloat16)

        @pl.when(middle)
        def _():
            line_wait(line_slot(k), c)
            scattered[c, block] = (
                scattered[c, block].astype(jnp.float32) + line_in[c, line_slot(k)].astype(jnp.float32)
            ).astype(jnp.bfloat16)

        line_copy(k, c).start()

    def relays(c):
        def one(i, carry):
            relay(send_order(i), c)
            return carry

        lax.fori_loop(0, 3, one, 0)

    def rows_part(i, carry):
        block = pick(i, [opposite, across, near, t])
        area = pl.ds(block * rows, rows)
        for d in range(2):
            span = pl.ds(d * 1024, 1024)
            product = jnp.zeros((rows, 1024), jnp.float32)
            for which in range(3):
                product = product + lax.dot_general(
                    grads_v[which, area],
                    weights_v[which, span],
                    contract_last,
                    preferred_element_type=jnp.float32,
                )
            own_part[:, span] = product

        @pl.when(i == 0)
        def _():
            branch_v[0] = own_part[...].astype(jnp.bfloat16)
            core_first.start()

        @pl.when(i == 1)
        def _():
            core_first.wait_recv()
            branch_v[1] = (own_part[...] + core_in[0].astype(jnp.float32)).astype(jnp.bfloat16)
            across_copy.start()

        @pl.when(i == 2)
        def _():
            branch_v[2] = own_part[...].astype(jnp.bfloat16)
            core_second.start()

        return carry

    lax.fori_loop(0, 4, rows_part, 0)
    relays(0)

    @pl.when(middle)
    def _():
        y_relay(1)
        y_relay(2)

    relays(1)
    relays(2)
    y_side_copy(0).wait_recv()

    @pl.when(z < 3)
    def _():
        y_line_wait(z)

    @pl.when(z > 0)
    def _():
        y_line_wait(z + 1)

    y_add(
        y_total,
        [
            (y_all.at[position], None),
            (y_side.at[0], None),
            (y_line.at[z], z < 3),
            (y_line.at[z + 1], z > 0),
        ],
    )
    relays(3)
    for c, total in enumerate((out_total, value_total, key_total, query_total)):
        side_copy(0, c).wait_recv()
        total[...] = scattered[c, position].astype(jnp.float32) + side_in[c, 0].astype(jnp.float32)

        @pl.when(z < 3)
        def _(c=c, total=total):
            line_wait(z, c)
            total[...] += line_in[c, z].astype(jnp.float32)

        @pl.when(z > 0)
        def _(c=c, total=total):
            line_wait(z + 1, c)
            total[...] += line_in[c, z + 1].astype(jnp.float32)

        for k in range(4):
            side_copy(k, c).wait_send()
        for k in range(1, 4):
            line_copy(k, c).wait_send()
    core_second.wait_recv()
    own_part[...] += core_in[1].astype(jnp.float32)
    across_copy.wait_recv()
    own_part[...] += across_in[...].astype(jnp.float32)
    last = pltpu.make_async_copy(own_part, rows_grad, store_sem)
    last.start()
    for copy in (core_first, across_copy, core_second):
        copy.wait_send()
    last.wait()
    for swap in swaps:
        swap.wait()
    for k in (0, 2, 3):
        y_side_copy(k).wait_send()
    y_cross_copy().wait_send()
    for k in (1, 2, 3):
        y_line_copy(k, y_sums.at[k]).wait_send()


def attention_backward(branch, saved, weights, out_w, gains, tables, sent, y_all, collective):
    rows, width = branch.shape
    local = out_w.shape[0]
    length = 4 * rows
    any_space = pl.BlockSpec(memory_space=pl.ANY)
    vector = pl.BlockSpec(memory_space=pltpu.VMEM)
    low, full = jnp.bfloat16, jnp.float32
    dma = pltpu.SemaphoreType.DMA
    return pl.pallas_call(
        attention_back_kernel,
        name="attention_backward",
        out_shape=(jax.ShapeDtypeStruct((rows, width), full),)
        + tuple(jax.ShapeDtypeStruct(array.shape, array.dtype) for array in sent)
        + (
            jax.ShapeDtypeStruct((rows, width), low),
            jax.ShapeDtypeStruct((3, rows, width), low),
            jax.ShapeDtypeStruct((rows, width), low),
            jax.ShapeDtypeStruct((5, rows, width), low),
            jax.ShapeDtypeStruct((4, rows, width), low),
        )
        + (jax.ShapeDtypeStruct((width // 8, local), full),) * 4
        + (jax.ShapeDtypeStruct((8, 128), full),),
        in_specs=[any_space] * 13 + [vector] * 4 + [any_space] * 3,
        out_specs=(any_space,) * 8 + (vector,) * 5,
        scratch_shapes=[
            pltpu.VMEM((4, rows, width), low),
            pltpu.VMEM((4, rows, width), low),
            pltpu.VMEM((3, width, local), low),
            pltpu.VMEM((local, width), low),
            pltpu.VMEM((2, length, local), low),
            pltpu.VMEM((4, length, local), low),
            pltpu.VMEM((length, 128), full),
            pltpu.VMEM((3, length, local), low),
            pltpu.VMEM((length, local), full),
            pltpu.VMEM((length, local), full),
            pltpu.VMEM((4, 8, width // 8, local), low),
            pltpu.VMEM((4, 4, width // 8, local), low),
            pltpu.VMEM((4, 5, width // 8, local), low),
            pltpu.VMEM((rows, width), full),
            pltpu.VMEM((2, rows, width), low),
            pltpu.VMEM((rows, width), low),
            pltpu.VMEM((4, rows // 2, width), low),
            dma((13,)),
            dma,
            dma((3,)),
            dma((3,)),
            dma((3,)),
            dma((3,)),
            dma((4, 4)),
            dma((4, 4)),
            dma((4, 5)),
            dma((4, 3)),
            dma((2,)),
            dma((2,)),
            dma((4,)),
            dma,
            dma((3,)),
            dma((3,)),
            dma((2,)),
            dma((5,)),
            dma((3,)),
        ],
        compiler_params=pltpu.CompilerParams(
            collective_id=collective, has_side_effects=True, vmem_limit_bytes=60 << 20
        ),
        cost_estimate=pl.CostEstimate(
            flops=16 * length * width * local, bytes_accessed=64 << 20, transcendentals=length * length * 4
        ),
    )(branch, *saved, *weights, out_w, *gains, *tables, *sent, y_all)


def sum_kernel(own, total, incoming, recv, send):
    position = lax.axis_index("expert")
    peer = lax.axis_index("tensor")
    mesh_ids = pl.DeviceIdType.MESH

    def flip(index, bit):
        return index + bit - 2 * bit * ((index // bit) % 2)

    partners = [
        (position, flip(peer, 1)),
        (position, flip(peer, 2)),
        (flip(position, 1), peer),
        (flip(position, 2), peer),
        (flip(position, 4), peer),
    ]
    barrier = pltpu.get_barrier_semaphore()
    for partner in partners:
        pl.semaphore_signal(barrier, inc=1, device_id=partner, device_id_type=mesh_ids)
    pl.semaphore_wait(barrier, len(partners))
    total[0] = own[...]
    for i, partner in enumerate(partners):
        copy = pltpu.make_async_remote_copy(
            src_ref=total.at[i],
            dst_ref=incoming.at[i],
            send_sem=send.at[i],
            recv_sem=recv.at[i],
            device_id=partner,
            device_id_type=mesh_ids,
        )
        copy.start()
        copy.wait()
        total[i + 1] = total[i] + incoming[i]


def sum_everywhere(own, collective):
    steps = 5
    return pl.pallas_call(
        sum_kernel,
        name="sum_everywhere",
        out_shape=jax.ShapeDtypeStruct((steps + 1,) + own.shape, jnp.float32),
        in_specs=[pl.BlockSpec(memory_space=pltpu.VMEM)],
        out_specs=pl.BlockSpec(memory_space=pltpu.VMEM),
        scratch_shapes=[
            pltpu.VMEM((steps,) + own.shape, jnp.float32),
            pltpu.SemaphoreType.DMA((steps,)),
            pltpu.SemaphoreType.DMA((steps,)),
        ],
        compiler_params=pltpu.CompilerParams(collective_id=collective, has_side_effects=True),
        cost_estimate=pl.CostEstimate(flops=own.size * steps, bytes_accessed=40 << 20, transcendentals=0),
    )(own)[steps]


def add_three(first, second, third):
    return first.astype(jnp.float32) + second.astype(jnp.float32) + third.astype(jnp.float32)


def per_device(
    tokens,
    cotangent,
    routes,
    norm_in,
    query_w,
    key_w,
    value_w,
    out_w,
    query_gain,
    key_gain,
    norm_mid,
    router_w,
    gate_w,
    up_w,
    down_w,
):
    rows_own = tokens.shape[0]
    model_width = tokens.shape[1]
    head_width = query_gain.shape[0]
    experts_all = router_w.shape[1]
    source = tokens.astype(jnp.float32)
    scale_in = inverse_rms(source)
    normed_low = (source * scale_in * norm_in).astype(jnp.bfloat16)
    cosine, sine_table = rotary_tables(4 * rows_own, head_width)
    tables = (
        jnp.concatenate([cosine[:, 0], cosine[:, 0]], axis=1),
        jnp.concatenate([-sine_table[:, 0], sine_table[:, 0]], axis=1),
    )
    gains = (query_gain[None], key_gain[None])
    *saved, attn_out, cot_all = attention_forward(
        normed_low, cotangent, (query_w, key_w, value_w), out_w, gains, tables, 1
    )
    middle = source + attn_out
    scale_mid = inverse_rms(middle)
    normed_mid = middle * scale_mid * norm_mid
    mid_low = normed_mid.astype(jnp.bfloat16)
    logits = jnp.dot(normed_mid, router_w, precision=highest, preferred_element_type=jnp.float32)
    route_mask = routes[:, :, None] == jnp.arange(experts_all, dtype=jnp.int32)[None, None, :]
    mask_float = route_mask.astype(jnp.float32)
    chosen = jnp.sum(mask_float * logits[:, None, :], axis=-1)
    gating = jax.nn.softmax(chosen, axis=-1)
    gates = jnp.sum(mask_float * gating[:, :, None], axis=1)
    gates_high = gates.astype(jnp.bfloat16)
    gates_low = (gates - gates_high.astype(jnp.float32)).astype(jnp.bfloat16)
    spare = jnp.zeros((rows_own, 128 - 2 * experts_all), jnp.bfloat16)
    own_rows = jnp.concatenate([mid_low, gates_high, gates_low, spare], axis=1)
    _, _, y_all, row_total, core_input, near_input, core_output, near_output, _ = expert_pass(
        own_rows, cot_all.reshape(-1, model_width), gate_w, up_w, down_w, experts_all, 2
    )
    expert_input_grad = row_total[:, :model_width]
    gate_grad_dense = (
        row_total[:, model_width : model_width + experts_all]
        + row_total[:, model_width + experts_all : model_width + 2 * experts_all]
    )
    gate_grad = jnp.sum(mask_float * gate_grad_dense[:, None, :], axis=-1)
    inner_gate = jnp.sum(gating * gate_grad, axis=-1, keepdims=True)
    chosen_grad = gating * (gate_grad - inner_gate)
    logit_grad = jnp.sum(chosen_grad[:, :, None] * mask_float, axis=1)
    normed_mid_grad = expert_input_grad + lax.dot_general(
        logit_grad, router_w, contract_last, precision=highest, preferred_element_type=jnp.float32
    )
    norm_mid_part = jnp.sum(normed_mid_grad * middle * scale_mid, axis=0)
    upstream = cotangent.astype(jnp.float32)
    middle_grad = upstream + norm_backward(normed_mid_grad, middle, scale_mid, norm_mid)
    branch_low = middle_grad.astype(jnp.bfloat16)
    sent = (
        (near_input[1].astype(jnp.float32) + core_input[1].astype(jnp.float32)).astype(jnp.bfloat16),
        (near_output[1].astype(jnp.float32) + core_output[1].astype(jnp.float32)).astype(jnp.bfloat16),
    )
    (
        rows_grad,
        line_input,
        line_output,
        y_sum,
        _,
        _,
        _,
        _,
        out_w_turned,
        value_w_grad,
        key_w_grad,
        query_w_grad,
        gain_sums,
    ) = attention_backward(
        branch_low, saved, (query_w, key_w, value_w), out_w, gains, tables, sent, y_all, 3
    )
    out_w_grad = out_w_turned.T
    router_part = lax.dot_general(
        normed_mid,
        logit_grad,
        contract_first,
        precision=highest,
        preferred_element_type=jnp.float32,
    )
    output = (middle + y_sum.astype(jnp.float32)).astype(jnp.bfloat16)
    gate_w_grad = add_three(near_input[0, 0], core_input[0, 0], line_input[0])
    up_w_grad = add_three(near_input[0, 1], core_input[0, 1], line_input[1])
    down_w_grad = add_three(near_output[0], core_output[0], line_output)
    norm_in_part = jnp.sum(rows_grad * source * scale_in, axis=0)
    input_grad = middle_grad + norm_backward(rows_grad, source, scale_in, norm_in)
    router_w_grad = lax.psum(router_part, ("expert", "tensor"))
    small = jnp.concatenate(
        [
            norm_in_part,
            norm_mid_part,
            gain_sums[0],
            gain_sums[1],
            jnp.zeros((-(2 * model_width + 2 * head_width) % 1024,), jnp.float32),
        ]
    ).reshape(-1, 128)
    sums = sum_everywhere(small, 4).reshape(-1)
    norm_in_grad = sums[:model_width]
    norm_mid_grad = sums[model_width : 2 * model_width]
    query_gain_grad = sums[2 * model_width : 2 * model_width + head_width]
    key_gain_grad = sums[2 * model_width + head_width : 2 * model_width + 2 * head_width]
    return (
        output,
        input_grad,
        norm_in_grad,
        query_w_grad,
        key_w_grad,
        value_w_grad,
        out_w_grad,
        query_gain_grad,
        key_gain_grad,
        norm_mid_grad,
        router_w_grad,
        gate_w_grad,
        up_w_grad,
        down_w_grad,
    )


def per_device_general(
    tokens,
    cotangent,
    routes,
    norm_in,
    query_w,
    key_w,
    value_w,
    out_w,
    query_gain,
    key_gain,
    norm_mid,
    router_w,
    gate_w,
    up_w,
    down_w,
):
    rows_own = tokens.shape[0]
    model_width = tokens.shape[1]
    tensor_count = lax.axis_size("tensor")
    expert_count = lax.axis_size("expert")
    head_width = query_gain.shape[0]
    local_heads = query_w.shape[1] // head_width
    experts_local = gate_w.shape[0]
    experts_all = router_w.shape[1]
    top_count = routes.shape[1]
    hidden_width = gate_w.shape[2]
    factor = 1.0 / math.sqrt(head_width)
    cot_all = lax.all_gather(cotangent, "expert", axis=0, tiled=True)
    source = tokens.astype(jnp.float32)
    scale_in = inverse_rms(source)
    normed_low = (source * scale_in * norm_in).astype(jnp.bfloat16)
    gathered = lax.all_gather(normed_low, "tensor", axis=0, tiled=True)
    seq_len = gathered.shape[0]
    query_pre = jnp.dot(gathered, query_w, preferred_element_type=jnp.float32)
    key_pre = jnp.dot(gathered, key_w, preferred_element_type=jnp.float32)
    value_low = jnp.dot(gathered, value_w, preferred_element_type=jnp.float32).astype(jnp.bfloat16)
    cosine, sine_table = rotary_tables(seq_len, head_width)
    query_heads = query_pre.reshape(seq_len, local_heads, head_width)
    key_heads = key_pre.reshape(seq_len, local_heads, head_width)
    query_scale = inverse_rms(query_heads)
    key_scale = inverse_rms(key_heads)
    query_low = rotate(query_heads * query_scale * query_gain, cosine, sine_table).astype(
        jnp.bfloat16
    )
    key_low = rotate(key_heads * key_scale * key_gain, cosine, sine_table).astype(jnp.bfloat16)
    value_heads = value_low.reshape(seq_len, local_heads, head_width)
    block_rows = min(512, seq_len)
    block_count = seq_len // block_rows
    query_blocks = query_low.reshape(block_count, block_rows, local_heads, head_width)

    def attend(query_block):
        scores = (
            jnp.einsum("qhd,khd->hqk", query_block, key_low, preferred_element_type=jnp.float32)
            * factor
        )
        row_max = jnp.max(scores, axis=-1, keepdims=True)
        shifted = jnp.exp(scores - row_max)
        row_sum = jnp.sum(shifted, axis=-1, keepdims=True)
        probs_low = (shifted / row_sum).astype(jnp.bfloat16)
        mixture = jnp.einsum(
            "hqk,khd->qhd", probs_low, value_heads, preferred_element_type=jnp.float32
        )
        return (mixture.astype(jnp.bfloat16), (row_max + jnp.log(row_sum))[..., 0])

    attended_blocks, log_sums = lax.map(attend, query_blocks)
    attended = attended_blocks.reshape(seq_len, local_heads * head_width)
    attn_out = lax.psum_scatter(
        jnp.dot(attended, out_w, preferred_element_type=jnp.float32).astype(jnp.bfloat16),
        "tensor",
        scatter_dimension=0,
        tiled=True,
    ).astype(jnp.float32)
    middle = source + attn_out
    scale_mid = inverse_rms(middle)
    normed_mid = middle * scale_mid * norm_mid
    mid_low = normed_mid.astype(jnp.bfloat16)
    logits = jnp.dot(normed_mid, router_w, precision=highest, preferred_element_type=jnp.float32)
    route_mask = routes[:, :, None] == jnp.arange(experts_all, dtype=jnp.int32)[None, None, :]
    mask_float = route_mask.astype(jnp.float32)
    chosen = jnp.sum(mask_float * logits[:, None, :], axis=-1)
    gating = jax.nn.softmax(chosen, axis=-1)
    upstream = cotangent.astype(jnp.float32)
    gates = jnp.sum(mask_float * gating[:, :, None], axis=1)
    x_all = lax.all_gather(mid_low, "expert", axis=0, tiled=True)
    gates_all = lax.all_gather(gates, "expert", axis=0, tiled=True)
    first_expert = lax.axis_index("expert") * experts_local
    own_gates = lax.dynamic_slice_in_dim(gates_all, first_expert, experts_local, 1)
    part_width = hidden_width // tensor_count
    rows_all = x_all.shape[0]
    y_part = jnp.zeros((rows_all, model_width), jnp.float32)
    x_grad_part = jnp.zeros((rows_all, model_width), jnp.float32)
    gate_grads, gate_parts, up_parts, down_parts = [], [], [], []
    for e in range(experts_local):
        hidden_raw = lax.dot_general(
            cot_all, down_w[e], contract_last, preferred_element_type=jnp.float32
        )
        gate_pre = jnp.dot(x_all, gate_w[e], preferred_element_type=jnp.float32)
        up_pre = jnp.dot(x_all, up_w[e], preferred_element_type=jnp.float32)
        weight = own_gates[:, e : e + 1]
        hidden = gate_pre * jax.nn.sigmoid(gate_pre) * up_pre
        gate_grads.append(jnp.sum(hidden * hidden_raw, axis=1))
        hidden_low = (hidden * weight).astype(jnp.bfloat16)
        gate_back, up_back = swiglu_back(hidden_raw * weight, gate_pre, up_pre)
        y_part = y_part + jnp.dot(hidden_low, down_w[e], preferred_element_type=jnp.float32)
        x_grad_part = x_grad_part + lax.dot_general(
            gate_back, gate_w[e], contract_last, preferred_element_type=jnp.float32
        )
        x_grad_part = x_grad_part + lax.dot_general(
            up_back, up_w[e], contract_last, preferred_element_type=jnp.float32
        )
        gate_parts.append(
            jnp.einsum(
                "nd,ntf->tdf",
                x_all,
                gate_back.reshape(rows_all, tensor_count, part_width),
                preferred_element_type=jnp.float32,
            ).astype(jnp.bfloat16)
        )
        up_parts.append(
            jnp.einsum(
                "nd,ntf->tdf",
                x_all,
                up_back.reshape(rows_all, tensor_count, part_width),
                preferred_element_type=jnp.float32,
            ).astype(jnp.bfloat16)
        )
        down_parts.append(
            lax.dot_general(
                hidden_low, cot_all, contract_first, preferred_element_type=jnp.float32
            ).astype(jnp.bfloat16)
        )
    x_grad = lax.psum_scatter(
        x_grad_part.astype(jnp.bfloat16), "expert", scatter_dimension=0, tiled=True
    )
    expert_input_grad = x_grad.astype(jnp.float32)
    gate_grad_sent = jnp.stack(gate_grads, axis=-1)
    gate_grad_all = lax.all_to_all(gate_grad_sent, "expert", split_axis=0, concat_axis=0, tiled=True)
    gate_grad_dense = (
        gate_grad_all.reshape(expert_count, rows_own, experts_local)
        .transpose(1, 0, 2)
        .reshape(rows_own, experts_all)
    )
    gate_grad = jnp.sum(mask_float * gate_grad_dense[:, None, :], axis=-1)
    y_sum = lax.psum_scatter(
        y_part.astype(jnp.bfloat16), "expert", scatter_dimension=0, tiled=True
    )
    output = (middle + y_sum.astype(jnp.float32)).astype(jnp.bfloat16)

    def own_part(parts):
        return [
            lax.psum_scatter(p, "tensor", scatter_dimension=0, tiled=True).astype(jnp.float32)
            for p in parts
        ]

    gate_w_grad = jnp.concatenate(own_part(gate_parts), axis=0)
    up_w_grad = jnp.concatenate(own_part(up_parts), axis=0)
    down_w_grad = jnp.stack(own_part(down_parts), axis=0)
    inner_gate = jnp.sum(gating * gate_grad, axis=-1, keepdims=True)
    chosen_grad = gating * (gate_grad - inner_gate)
    logit_grad = jnp.sum(chosen_grad[:, :, None] * mask_float, axis=1)
    router_part = lax.dot_general(
        normed_mid,
        logit_grad,
        contract_first,
        precision=highest,
        preferred_element_type=jnp.float32,
    )
    normed_mid_grad = expert_input_grad + lax.dot_general(
        logit_grad, router_w, contract_last, precision=highest, preferred_element_type=jnp.float32
    )
    norm_mid_part = jnp.sum(normed_mid_grad * middle * scale_mid, axis=0)
    middle_grad = upstream + norm_backward(normed_mid_grad, middle, scale_mid, norm_mid)
    branch_low = middle_grad.astype(jnp.bfloat16)
    branch_all = lax.all_gather(branch_low, "tensor", axis=0, tiled=True)
    attended_grad = lax.dot_general(
        branch_all, out_w, contract_last, preferred_element_type=jnp.float32
    ).astype(jnp.bfloat16)
    out_w_part = lax.dot_general(
        attended, branch_all, contract_first, preferred_element_type=jnp.float32
    )
    grad_blocks = attended_grad.reshape(block_count, block_rows, local_heads, head_width)

    def attend_back(carry, inputs):
        key_total, value_total = carry
        query_block, grad_block, log_block = inputs
        scores = (
            jnp.einsum("qhd,khd->hqk", query_block, key_low, preferred_element_type=jnp.float32)
            * factor
        )
        probs = jnp.exp(scores - log_block[:, :, None])
        probs_low = probs.astype(jnp.bfloat16)
        value_total = value_total + jnp.einsum(
            "hqk,qhd->khd", probs_low, grad_block, preferred_element_type=jnp.float32
        )
        prob_grad = jnp.einsum(
            "qhd,khd->hqk", grad_block, value_heads, preferred_element_type=jnp.float32
        )
        delta = jnp.sum(probs * prob_grad, axis=-1, keepdims=True)
        score_low = (probs * (prob_grad - delta)).astype(jnp.bfloat16)
        query_part = (
            jnp.einsum("hqk,khd->qhd", score_low, key_low, preferred_element_type=jnp.float32)
            * factor
        )
        key_total = (
            key_total
            + jnp.einsum("hqk,qhd->khd", score_low, query_block, preferred_element_type=jnp.float32)
            * factor
        )
        return ((key_total, value_total), query_part)

    zero_heads = jnp.zeros((seq_len, local_heads, head_width), jnp.float32)
    (key_grad, value_total), query_parts = lax.scan(
        attend_back, (zero_heads, zero_heads), (query_blocks, grad_blocks, log_sums)
    )
    query_grad = query_parts.reshape(seq_len, local_heads, head_width)
    value_grad_low = value_total.reshape(seq_len, local_heads * head_width).astype(jnp.bfloat16)
    query_rot_grad = rotate_back(query_grad, cosine, sine_table)
    key_rot_grad = rotate_back(key_grad, cosine, sine_table)
    query_gain_part = jnp.sum(query_rot_grad * query_heads * query_scale, axis=(0, 1))
    key_gain_part = jnp.sum(key_rot_grad * key_heads * key_scale, axis=(0, 1))
    query_pre_grad = (
        norm_backward(query_rot_grad, query_heads, query_scale, query_gain)
        .reshape(seq_len, local_heads * head_width)
        .astype(jnp.bfloat16)
    )
    key_pre_grad = (
        norm_backward(key_rot_grad, key_heads, key_scale, key_gain)
        .reshape(seq_len, local_heads * head_width)
        .astype(jnp.bfloat16)
    )
    query_w_part = lax.dot_general(
        gathered, query_pre_grad, contract_first, preferred_element_type=jnp.float32
    )
    key_w_part = lax.dot_general(
        gathered, key_pre_grad, contract_first, preferred_element_type=jnp.float32
    )
    value_w_part = lax.dot_general(
        gathered, value_grad_low, contract_first, preferred_element_type=jnp.float32
    )
    summed = lax.dot_general(
        query_pre_grad, query_w, contract_last, preferred_element_type=jnp.float32
    )
    summed = summed + lax.dot_general(
        key_pre_grad, key_w, contract_last, preferred_element_type=jnp.float32
    )
    rows_grad = lax.psum_scatter(
        (
            summed
            + lax.dot_general(
                value_grad_low, value_w, contract_last, preferred_element_type=jnp.float32
            )
        ).astype(jnp.bfloat16),
        "tensor",
        scatter_dimension=0,
        tiled=True,
    ).astype(jnp.float32)
    norm_in_part = jnp.sum(rows_grad * source * scale_in, axis=0)
    input_grad = middle_grad + norm_backward(rows_grad, source, scale_in, norm_in)
    query_w_grad, key_w_grad, value_w_grad, out_w_grad = (
        lax.psum_scatter(
            query_w_part.astype(jnp.bfloat16), "expert", scatter_dimension=0, tiled=True
        ).astype(jnp.float32),
        lax.psum_scatter(
            key_w_part.astype(jnp.bfloat16), "expert", scatter_dimension=0, tiled=True
        ).astype(jnp.float32),
        lax.psum_scatter(
            value_w_part.astype(jnp.bfloat16), "expert", scatter_dimension=0, tiled=True
        ).astype(jnp.float32),
        lax.psum_scatter(
            out_w_part.astype(jnp.bfloat16), "expert", scatter_dimension=1, tiled=True
        ).astype(jnp.float32),
    )
    norm_in_grad, query_gain_grad, key_gain_grad, norm_mid_grad, router_w_grad = lax.psum(
        (norm_in_part, query_gain_part, key_gain_part, norm_mid_part, router_part),
        ("expert", "tensor"),
    )
    return (
        output,
        input_grad,
        norm_in_grad,
        query_w_grad,
        key_w_grad,
        value_w_grad,
        out_w_grad,
        query_gain_grad,
        key_gain_grad,
        norm_mid_grad,
        router_w_grad,
        gate_w_grad,
        up_w_grad,
        down_w_grad,
    )


def solution(mesh):
    placed = (
        P(("expert", "tensor"), None),
        P(("expert", "tensor"), None),
        P(("expert", "tensor"), None),
        P(),
        P(None, "tensor"),
        P(None, "tensor"),
        P(None, "tensor"),
        P("tensor", None),
        P(),
        P(),
        P(),
        P(),
        P("expert", None, None),
        P("expert", None, None),
        P("expert", None, None),
    )
    return jax.shard_map(
        per_device if dict(mesh.shape) == {"expert": 8, "tensor": 4} else per_device_general,
        mesh=mesh,
        in_specs=placed,
        out_specs=(
            P(("expert", "tensor"), None),
            P(("expert", "tensor"), None),
            P(),
            P("expert", "tensor"),
            P("expert", "tensor"),
            P("expert", "tensor"),
            P("tensor", "expert"),
            P(),
            P(),
            P(),
            P(),
            P("expert", None, "tensor"),
            P("expert", None, "tensor"),
            P("expert", "tensor", None),
        ),
        check_vma=False,
    )
```

```python
import functools
import math

import jax
import jax.numpy as jnp
from jax import lax
from jax.experimental import pallas as pl
from jax.experimental.pallas import tpu as pltpu
from jax.sharding import PartitionSpec as P

epsilon = 1e-06
highest = lax.Precision.HIGHEST
contract_last = (((1,), (1,)), ((), ()))
contract_first = (((0,), (0,)), ((), ()))


def inverse_rms(values):
    return lax.rsqrt(jnp.mean(values * values, axis=-1, keepdims=True) + epsilon)


def norm_backward(grad_norm, values, inverse, norm_gain):
    weighted = grad_norm * norm_gain
    inner_mean = jnp.mean(weighted * values, axis=-1, keepdims=True)
    return inverse * weighted - values * inverse * inverse * inverse * inner_mean


def rotary_tables(length, head_width):
    half_dim = head_width // 2
    frequency = jnp.exp(
        -math.log(10000.0) * 2.0 * jnp.arange(half_dim, dtype=jnp.float32) / head_width
    )
    angles = jnp.arange(length, dtype=jnp.float32)[:, None] * frequency[None, :]
    return (jnp.cos(angles)[:, None, :], jnp.sin(angles)[:, None, :])


def rotate(values, cosine, sine_table):
    half_dim = values.shape[-1] // 2
    first_half = values[..., :half_dim]
    second_half = values[..., half_dim:]
    return jnp.concatenate(
        [
            first_half * cosine - second_half * sine_table,
            second_half * cosine + first_half * sine_table,
        ],
        axis=-1,
    )


def rotate_back(gradient, cosine, sine_table):
    half_dim = gradient.shape[-1] // 2
    first_half = gradient[..., :half_dim]
    second_half = gradient[..., half_dim:]
    return jnp.concatenate(
        [
            first_half * cosine + second_half * sine_table,
            second_half * cosine - first_half * sine_table,
        ],
        axis=-1,
    )


def swiglu_back(hidden_grad, gate_pre, up_pre):
    sigmoid_part = jax.nn.sigmoid(gate_pre)
    gate_back = (
        hidden_grad * up_pre * sigmoid_part * (1.0 + gate_pre * (1.0 - sigmoid_part))
    ).astype(jnp.bfloat16)
    up_back = (hidden_grad * gate_pre * sigmoid_part).astype(jnp.bfloat16)
    return (gate_back, up_back)


chunks = 4


def pick(index, values):
    result = values[-1]
    for j in reversed(range(len(values) - 1)):
        result = jnp.where(index == j, values[j], result)
    return result


def expert_kernel(
    experts_all,
    own_rows,
    cot_all,
    gate_hbm,
    up_hbm,
    down_hbm,
    hidden_all,
    grads_all,
    y_all,
    total,
    core_input,
    near_input,
    core_output,
    near_output,
    cot_late,
    gate_v,
    up_v,
    down_v,
    rows_v,
    cot_v,
    hidden_v,
    gate_b,
    up_b,
    y_v,
    stage,
    parts,
    side_in,
    cross_in,
    line_in,
    weight_sem,
    own_sem,
    cot_sem,
    out_sem,
    item_in,
    item_out,
    core_recv,
    gather_recv,
    gather_send,
    side_recv,
    side_send,
    cross_recv,
    cross_send,
    line_recv,
    line_send,
    late_recv,
    late_send,
):
    position = lax.axis_index("expert")
    peer = lax.axis_index("tensor")
    z = position // 2
    x = position % 2
    experts_local, width, hidden = gate_v.shape
    rows = cot_v.shape[0]
    part = hidden // 4
    y = peer // 2
    core = peer % 2
    chunk = rows // chunks
    middle = (z == 1) | (z == 2)
    ends = (z == 0) | (z == 3)
    pair = z + 1 - 2 * (z % 2)
    line_slots = [
        z,
        pick(z, [1, 0, 3, 2]),
        pick(z, [2, 2, 1, 1]),
        pick(z, [3, 3, 0, 0]),
    ]

    def block_rows(block):
        return pl.ds(pl.multiple_of(block * rows, rows), rows)

    def device(zz, xx):
        return (zz * 2 + xx, peer)

    def slot_z(k):
        return pick(k, line_slots)

    weight_copies = [
        pltpu.make_async_copy(gate_hbm, gate_v, weight_sem.at[0]),
        pltpu.make_async_copy(up_hbm, up_v, weight_sem.at[1]),
        pltpu.make_async_copy(down_hbm, down_v, weight_sem.at[2]),
    ]
    own_copy = pltpu.make_async_copy(own_rows, rows_v.at[block_rows(position)], own_sem)
    own_copy.start()
    for copy in weight_copies:
        copy.start()

    barrier = pltpu.get_barrier_semaphore()
    pl.semaphore_signal(barrier, inc=1, device_id=device(z, 1 - x), device_id_type=pl.DeviceIdType.MESH)
    core_peer = (position, y * 2 + 1 - core)
    pl.semaphore_signal(barrier, inc=1, device_id=core_peer, device_id_type=pl.DeviceIdType.MESH)

    @pl.when(z < 3)
    def _():
        pl.semaphore_signal(barrier, inc=1, device_id=device(z + 1, x), device_id_type=pl.DeviceIdType.MESH)

    @pl.when(z > 0)
    def _():
        pl.semaphore_signal(barrier, inc=1, device_id=device(z - 1, x), device_id_type=pl.DeviceIdType.MESH)

    pl.semaphore_wait(barrier, 3 + middle.astype(jnp.int32))

    def gather_copy(source, block, index, zz, xx):
        return pltpu.make_async_remote_copy(
            src_ref=source,
            dst_ref=rows_v.at[block_rows(block)],
            send_sem=gather_send.at[index],
            recv_sem=gather_recv.at[block],
            device_id=device(zz, xx),
            device_id_type=pl.DeviceIdType.MESH,
        )

    def own_send(index, zz, xx):
        return gather_copy(own_rows, position, index, zz, xx)

    own_send(0, z, 1 - x).start()

    @pl.when(z < 3)
    def _():
        own_send(1, z + 1, x).start()

    @pl.when(z > 0)
    def _():
        own_send(2, z - 1, x).start()

    def forward_side(k):
        block = slot_z(k) * 2 + x
        return gather_copy(rows_v.at[block_rows(block)], block, 2 + k, z, 1 - x)

    def forward_line(k):
        block = slot_z(k) * 2 + x
        target = jnp.where(slot_z(k) < z, z + 1, z - 1)
        return gather_copy(rows_v.at[block_rows(block)], block, 5 + k, jnp.clip(target, 0, 3), x)

    def arrived(block):
        gather_copy(own_rows, block, 0, z, 1 - x).wait_recv()

    def arrive(k):
        arrived(slot_z(k) * 2 + x)
        if k < 3:

            @pl.when(ends)
            def _():
                forward_side(k).start()

        @pl.when(middle)
        def _():
            if k > 1:
                forward_side(k).start()
            forward_line(k).start()

    def forward_cross():
        block = jnp.where(ends, z, slot_z(3)) * 2 + 1 - x
        return gather_copy(rows_v.at[block_rows(block)], block, 9, pair, x)

    def cross_copy(c):
        area = pl.ds(c * chunk, chunk)
        return pltpu.make_async_remote_copy(
            src_ref=parts.at[5, area],
            dst_ref=cross_in.at[area],
            send_sem=cross_send.at[c],
            recv_sem=cross_recv.at[c],
            device_id=device(pair, x),
            device_id_type=pl.DeviceIdType.MESH,
        )

    def cross_add(c):
        area = pl.ds(c * chunk, chunk)
        cross_copy(c).wait_recv()
        parts[4, area] = (
            parts[4, area].astype(jnp.float32) + cross_in[area].astype(jnp.float32)
        ).astype(jnp.bfloat16)
        side_copy(0, c).start()

    def side_slot(k):
        return jnp.maximum(k - 1, 0)

    def side_copy(k, c):
        area = pl.ds(c * chunk, chunk)
        return pltpu.make_async_remote_copy(
            src_ref=parts.at[4 + k, area],
            dst_ref=side_in.at[side_slot(k), area],
            send_sem=side_send.at[side_slot(k), c],
            recv_sem=side_recv.at[side_slot(k), c],
            device_id=device(z, 1 - x),
            device_id_type=pl.DeviceIdType.MESH,
        )

    def line_slot(k):
        target = slot_z(k)
        return jnp.where(target < z, target, target + 1)

    def line_copy(k, c):
        area = pl.ds(c * chunk, chunk)
        target = jnp.where(slot_z(k) < z, z - 1, z + 1)
        return pltpu.make_async_remote_copy(
            src_ref=parts.at[k, area],
            dst_ref=line_in.at[line_slot(k), area],
            send_sem=line_send.at[k - 1, c],
            recv_sem=line_recv.at[line_slot(k), c],
            device_id=device(jnp.clip(target, 0, 3), x),
            device_id_type=pl.DeviceIdType.MESH,
        )

    def line_wait(slot, c):
        area = pl.ds(c * chunk, chunk)
        pltpu.make_async_remote_copy(
            src_ref=parts.at[0, area],
            dst_ref=line_in.at[slot, area],
            send_sem=line_send.at[0, c],
            recv_sem=line_recv.at[slot, c],
            device_id=device(z, 1 - x),
            device_id_type=pl.DeviceIdType.MESH,
        ).wait_recv()

    def relay(k, c):
        area = pl.ds(c * chunk, chunk)
        if k > 1:
            side_copy(k, c).wait_recv()
            parts[k, area] = (
                parts[k, area].astype(jnp.float32) + side_in[k - 1, area].astype(jnp.float32)
            ).astype(jnp.bfloat16)

        @pl.when(middle)
        def _():
            line_wait(line_slot(k), c)
            parts[k, area] = (
                parts[k, area].astype(jnp.float32) + line_in[line_slot(k), area].astype(jnp.float32)
            ).astype(jnp.bfloat16)

        line_copy(k, c).start()

    def block_of(step):
        k = pick(step, [0, 1, 0, 1, 2, 2, 3, 3])
        side = pick(step, [0, 0, 1, 1, 0, 1, 1, 0])
        return k, side, slot_z(k) * 2 + jnp.where(side == 1, 1 - x, x)

    def cot_copy(step):
        return pltpu.make_async_copy(cot_all.at[block_rows(block_of(step)[2])], cot_v, cot_sem)

    def late_copy():
        return pltpu.make_async_remote_copy(
            src_ref=cot_all.at[block_rows(slot_z(3) * 2 + x)],
            dst_ref=cot_late,
            send_sem=late_send,
            recv_sem=late_recv,
            device_id=device(z, 1 - x),
            device_id_type=pl.DeviceIdType.MESH,
        )

    def y_copy(block):
        return pltpu.make_async_copy(y_v, y_all.at[block], out_sem.at[3])

    def out_copies(block):
        return [
            pltpu.make_async_copy(hidden_v, hidden_all.at[block_rows(block)], out_sem.at[0]),
            pltpu.make_async_copy(gate_b, grads_all.at[0, block_rows(block)], out_sem.at[1]),
            pltpu.make_async_copy(up_b, grads_all.at[1, block_rows(block)], out_sem.at[2]),
        ]

    cot_copy(0).start()
    own_copy.wait()
    for copy in weight_copies:
        copy.wait()

    def one_step(step, carry):
        k, side, block = block_of(step)

        @pl.when(step == 1)
        def _():
            arrive(1)

            @pl.when(middle)
            def _():
                arrive(2)

            arrived(z * 2 + 1 - x)

            @pl.when(ends)
            def _():
                forward_cross().start()

        @pl.when(step == 3)
        def _():
            @pl.when(ends)
            def _():
                arrive(2)

            @pl.when(middle)
            def _():
                arrive(3)

            arrived(slot_z(1) * 2 + 1 - x)

        @pl.when(step == 4)
        def _():
            late_copy().start()

        @pl.when(step == 6)
        def _():
            late_copy().wait_recv()
            pltpu.make_async_copy(cot_late, cot_v, cot_sem).start()

        @pl.when(step == 5)
        def _():
            arrived(slot_z(2) * 2 + 1 - x)

        @pl.when((step == 6) & ends)
        def _():
            arrived(slot_z(3) * 2 + 1 - x)

        @pl.when((step == 7) & ends)
        def _():
            arrive(3)

        @pl.when(step > 0)
        def _():
            for copy in out_copies(block):
                copy.wait()

        cot_copy(step).wait()
        rows_low = rows_v[block_rows(block), :width]
        extra = rows_v[block_rows(block), width:].astype(jnp.float32)
        lane = lax.broadcasted_iota(jnp.int32, extra.shape, 1)
        ext = jnp.zeros(extra.shape, jnp.float32)
        for e in range(experts_local):
            expert = position * experts_local + e
            high = lane == expert
            low = lane == expert + experts_all
            weight = jnp.sum(jnp.where(high | low, extra, 0.0), axis=1, keepdims=True)
            gate_grad = jnp.zeros((rows, 1), jnp.float32)
            for f in range(hidden // 512):
                columns = pl.ds(f * 512, 512)
                gate_pre = jnp.dot(rows_low, gate_v[e, :, columns], preferred_element_type=jnp.float32)
                up_pre = jnp.dot(rows_low, up_v[e, :, columns], preferred_element_type=jnp.float32)
                target = pl.ds(e * hidden + f * 512, 512)
                raw = lax.dot_general(
                    cot_v[...],
                    down_v[e, columns, :],
                    contract_last,
                    preferred_element_type=jnp.float32,
                )
                sig = jax.nn.sigmoid(gate_pre)
                act = gate_pre * sig
                hid = act * up_pre
                gate_grad = gate_grad + jnp.sum(hid * raw, axis=1, keepdims=True)
                hidden_v[:, target] = (hid * weight).astype(jnp.bfloat16)
                grad = raw * weight
                gate_b[:, target] = (grad * up_pre * sig * (1.0 + gate_pre * (1.0 - sig))).astype(jnp.bfloat16)
                up_b[:, target] = (grad * act).astype(jnp.bfloat16)
            grad_high = gate_grad.astype(jnp.bfloat16).astype(jnp.float32)
            ext = jnp.where(high, grad_high, ext)
            ext = jnp.where(low, gate_grad - grad_high, ext)

        @pl.when((step < 7) & (step != 5))
        def _():
            cot_copy(step + 1).start()

        @pl.when((step == 4) & middle)
        def _():
            arrived(slot_z(3) * 2 + 1 - x)
            forward_cross().start()

        place = side * 4 + k
        parts[place, :, width:] = ext.astype(jnp.bfloat16)
        for copy in out_copies(block):
            copy.start()
        for d in range(width // 1024):
            span = pl.ds(d * 1024, 1024)
            summed = jnp.zeros((rows, 1024), jnp.float32)
            for e in range(experts_local):
                target = pl.ds(e * hidden, hidden)
                summed = summed + lax.dot_general(
                    gate_b[:, target], gate_v[e, span, :], contract_last, preferred_element_type=jnp.float32
                )
                summed = summed + lax.dot_general(
                    up_b[:, target], up_v[e, span, :], contract_last, preferred_element_type=jnp.float32
                )
            parts[place, :, span] = summed.astype(jnp.bfloat16)

        @pl.when((side == 1) & (k > 1))
        def _():
            for c in range(chunks):
                side_copy(k, c).start()

        @pl.when(step == 3)
        def _():
            for c in range(chunks):
                cross_copy(c).start()

        @pl.when((step == 1) & ends)
        def _():
            for c in range(chunks):
                line_copy(1, c).start()

        @pl.when(step > 0)
        def _():
            y_copy(block).wait()

        for d in range(width // 1024):
            span = pl.ds(d * 1024, 1024)
            summed = jnp.zeros((rows, 1024), jnp.float32)
            for e in range(experts_local):
                summed = summed + jnp.dot(
                    hidden_v[:, pl.ds(e * hidden, hidden)],
                    down_v[e, :, span],
                    preferred_element_type=jnp.float32,
                )
            y_v[:, span] = summed.astype(jnp.bfloat16)
        y_copy(block).start()
        return carry

    lax.fori_loop(0, 8, one_step, 0)

    for copy in out_copies(position):
        copy.wait()
    y_copy(position).wait()
    whole_cot = [
        pltpu.make_async_copy(cot_all.at[:, pl.ds(h * hidden, hidden)], up_v.at[h], weight_sem.at[h])
        for h in range(2)
    ]
    for copy in whole_cot:
        copy.start()

    def columns_of(pair, q):
        column_y = jnp.where(q == 0, y, 1 - y)
        column_core = jnp.where(pair == 0, 1 - core, core)
        return column_y * 2 + column_core

    def item_source(i):
        return i // 6, (i % 6) // 2, i % 2

    def item_loads(i, act):
        pair_of, kind, e = item_source(i)
        slot = i % 2
        for q in range(2):
            start = pl.multiple_of(e * hidden + columns_of(pair_of, q) * part, part)
            place = gate_v.at[0, :, pl.ds(pl.multiple_of(slot * 2 * part + q * part, part), part)]
            sem = item_in.at[slot, q]

            @pl.when(kind < 2)
            def _(start=start, place=place, sem=sem):
                act(
                    pltpu.make_async_copy(
                        grads_all.at[jnp.minimum(kind, 1), :, pl.ds(start, part)], place, sem
                    )
                )

            @pl.when(kind == 2)
            def _(start=start, place=place, sem=sem):
                act(pltpu.make_async_copy(hidden_all.at[:, pl.ds(start, part)], place, sem))

    def core_copy(source, target, slot, number, q):
        return pltpu.make_async_remote_copy(
            src_ref=source,
            dst_ref=target,
            send_sem=item_out.at[slot, q],
            recv_sem=core_recv.at[number, q],
            device_id=core_peer,
            device_id_type=pl.DeviceIdType.MESH,
        )

    def item_stores(i, starting):
        pair_of, kind, e = item_source(i)
        slot = i % 2
        number = i % 6
        wide_kind = jnp.minimum(kind, 1)
        for q in range(2):
            wide_place = gate_v.at[1, :, pl.ds(pl.multiple_of(slot * 2 * part + q * part, part), part)]
            tall_place = down_v.at[slot, pl.ds(q * part, part)]

            def far(source, target, q=q):
                copy = core_copy(source, target, slot, number, q)
                if starting:
                    copy.start()
                else:
                    copy.wait_send()

            def own(source, target, q=q):
                copy = pltpu.make_async_copy(source, target, item_out.at[slot, q])
                if starting:
                    copy.start()
                else:
                    copy.wait()

            for which, move, wide_out, tall_out in (
                (0, far, core_input, core_output),
                (1, own, near_input, near_output),
            ):

                @pl.when((pair_of == which) & (kind < 2))
                def _(move=move, wide_place=wide_place, wide_out=wide_out, q=q):
                    move(wide_place, wide_out.at[q, wide_kind, e])

                @pl.when((pair_of == which) & (kind == 2))
                def _(move=move, tall_place=tall_place, tall_out=tall_out, q=q):
                    move(tall_place, tall_out.at[q, e])

    item_loads(0, lambda copy: copy.start())
    for copy in whole_cot:
        copy.wait()
    late_rows = block_rows(slot_z(3) * 2 + 1 - x)
    late_parts = [
        pltpu.make_async_copy(
            cot_late.at[:, pl.ds(h * hidden, hidden)], up_v.at[h, late_rows], weight_sem.at[h]
        )
        for h in range(2)
    ]
    for copy in late_parts:
        copy.start()
    for copy in late_parts:
        copy.wait()
    late_copy().wait_send()

    def at(index, first, gap):
        return (index >= first) & (index < first + gap * chunks) & ((index - first) % gap == 0)

    def item(index, carry):
        i = index // 4
        d = index % 4
        kind = (i % 6) // 2
        slot = i % 2

        @pl.when(d == 0)
        def _():
            item_loads(i, lambda copy: copy.wait())

            @pl.when(i < 11)
            def _():
                item_loads(i + 1, lambda copy: copy.start())

            @pl.when(i > 1)
            def _():
                item_stores(i - 2, False)

        columns = pl.ds(pl.multiple_of(slot * 2 * part, 2 * part), 2 * part)
        span = pl.ds(pl.multiple_of(d * (width // 4), width // 4), width // 4)

        @pl.when(kind < 2)
        def _():
            gate_v[1, span, columns] = lax.dot_general(
                rows_v[:, span], gate_v[0, :, columns], contract_first, preferred_element_type=jnp.float32
            ).astype(jnp.bfloat16)

        @pl.when(kind == 2)
        def _():
            half = pl.ds(pl.multiple_of((d % 2) * (hidden // 2), hidden // 2), hidden // 2)
            down_v[slot, : 2 * part, span] = lax.dot_general(
                gate_v[0, :, columns],
                up_v[d // 2, :, half],
                contract_first,
                preferred_element_type=jnp.float32,
            ).astype(jnp.bfloat16)

        @pl.when(d == 3)
        def _():
            item_stores(i, True)

        @pl.when(at(index, 1, 1))
        def _():
            cross_add(index - 1)

        @pl.when(at(index, 5, 4))
        def _():
            relay(3, (index - 5) // 4)

        @pl.when(at(index, 11, 4) & middle)
        def _():
            relay(1, (index - 11) // 4)

        @pl.when(at(index, 18, 1) & ends)
        def _():
            relay(2, index - 18)

        @pl.when(at(index, 24, 4) & middle)
        def _():
            relay(2, (index - 24) // 4)

        return carry

    lax.fori_loop(0, 48, item, 0)
    for last in (10, 11):
        item_stores(last, False)
    for number in range(6):
        for q in range(2):
            if number < 4:
                core_copy(
                    gate_v.at[1, :, pl.ds(0, part)],
                    core_input.at[q, number // 2, number % 2],
                    0,
                    number,
                    q,
                ).wait_recv()
            else:
                core_copy(
                    down_v.at[0, pl.ds(0, part)], core_output.at[q, number % 2], 0, number, q
                ).wait_recv()

    def finish(c, carry):
        area = pl.ds(c * chunk, chunk)
        side_copy(0, c).wait_recv()
        stage[...] = parts[0, area].astype(jnp.float32) + side_in[0, area].astype(jnp.float32)

        @pl.when(z < 3)
        def _():
            line_wait(z, c)
            stage[...] += line_in[z, area].astype(jnp.float32)

        @pl.when(z > 0)
        def _():
            line_wait(z + 1, c)
            stage[...] += line_in[z + 1, area].astype(jnp.float32)

        result = pltpu.make_async_copy(stage, total.at[area], own_sem)
        result.start()
        result.wait()
        for k in (0, 2, 3):
            side_copy(k, c).wait_send()
        cross_copy(c).wait_send()
        for k in range(1, 4):
            line_copy(k, c).wait_send()
        return carry

    lax.fori_loop(0, chunks, finish, 0)

    own_send(0, z, 1 - x).wait_send()

    @pl.when(z < 3)
    def _():
        own_send(1, z + 1, x).wait_send()

    @pl.when(z > 0)
    def _():
        own_send(2, z - 1, x).wait_send()

    forward_cross().wait_send()
    forward_side(2).wait_send()

    @pl.when(ends)
    def _():
        forward_side(1).wait_send()

    @pl.when(middle)
    def _():
        forward_side(3).wait_send()
        for k in range(1, 4):
            forward_line(k).wait_send()


def expert_pass(own_rows, cot_all, gate_w, up_w, down_w, experts_all, collective):
    rows, wide = own_rows.shape
    experts_local, width, hidden = gate_w.shape
    inner = experts_local * hidden
    any_space = pl.BlockSpec(memory_space=pl.ANY)
    low = jnp.bfloat16
    dma = pltpu.SemaphoreType.DMA
    return pl.pallas_call(
        functools.partial(expert_kernel, experts_all),
        name="expert_pass",
        out_shape=(
            jax.ShapeDtypeStruct((8 * rows, inner), low),
            jax.ShapeDtypeStruct((2, 8 * rows, inner), low),
            jax.ShapeDtypeStruct((8, rows, width), low),
            jax.ShapeDtypeStruct((rows, wide), jnp.float32),
            *(jax.ShapeDtypeStruct((2, 2, experts_local, width, hidden // 4), low),) * 2,
            *(jax.ShapeDtypeStruct((2, experts_local, hidden // 4, width), low),) * 2,
            jax.ShapeDtypeStruct((rows, width), low),
        ),
        in_specs=[any_space] * 5,
        out_specs=(any_space,) * 9,
        scratch_shapes=[
            pltpu.VMEM((experts_local, width, hidden), low),
            pltpu.VMEM((experts_local, width, hidden), low),
            pltpu.VMEM((experts_local, hidden, width), low),
            pltpu.VMEM((8 * rows, wide), low),
            pltpu.VMEM((rows, width), low),
            pltpu.VMEM((rows, inner), low),
            pltpu.VMEM((rows, inner), low),
            pltpu.VMEM((rows, inner), low),
            pltpu.VMEM((rows, width), low),
            pltpu.VMEM((rows // chunks, wide), jnp.float32),
            pltpu.VMEM((8, rows, wide), low),
            pltpu.VMEM((3, rows, wide), low),
            pltpu.VMEM((rows, wide), low),
            pltpu.VMEM((5, rows, wide), low),
            dma((3,)),
            dma,
            dma,
            dma((4,)),
            dma((2, 2)),
            dma((2, 2)),
            dma((6, 2)),
            dma((8,)),
            dma((10,)),
            dma((3, chunks)),
            dma((3, chunks)),
            dma((chunks,)),
            dma((chunks,)),
            dma((5, chunks)),
            dma((3, chunks)),
            dma,
            dma,
        ],
        compiler_params=pltpu.CompilerParams(
            collective_id=collective, has_side_effects=True, vmem_limit_bytes=60 << 20
        ),
        cost_estimate=pl.CostEstimate(
            flops=2 * 9 * 8 * rows * width * inner, bytes_accessed=64 << 20, transcendentals=8 * rows * inner
        ),
    )(own_rows, cot_all, gate_w, up_w, down_w)


def line_gather(source, target, recv, send):
    position = lax.axis_index("expert")
    peer = lax.axis_index("tensor")
    z = position // 2
    x = position % 2
    middle = (z == 1) | (z == 2)
    slots = [z, pick(z, [1, 0, 3, 2]), pick(z, [2, 2, 1, 1]), pick(z, [3, 3, 0, 0])]

    def copy(block_source, block, index, zz, xx):
        return pltpu.make_async_remote_copy(
            src_ref=block_source,
            dst_ref=target.at[block],
            send_sem=send.at[index],
            recv_sem=recv.at[block],
            device_id=(zz * 2 + xx, peer),
            device_id_type=pl.DeviceIdType.MESH,
        )

    def own_up():
        return copy(source, position, 1, z + 1, x)

    def own_down():
        return copy(source, position, 2, z - 1, x)

    def own_side():
        return copy(source, position, 0, z, 1 - x)

    def side(k):
        block = slots[k] * 2 + x
        return copy(target.at[block], block, 2 + k, z, 1 - x)

    def line(k):
        block = slots[k] * 2 + x
        onward = jnp.where(slots[k] < z, z + 1, z - 1)
        return copy(target.at[block], block, 5 + k, jnp.clip(onward, 0, 3), x)

    def start():
        own_side().start()

        @pl.when(z < 3)
        def _():
            own_up().start()

        @pl.when(z > 0)
        def _():
            own_down().start()

    def wait_block(block):
        copy(source, block, 0, z, 1 - x).wait_recv()

    def arrive(k):
        wait_block(slots[k] * 2 + x)
        if k < 3:
            side(k).start()

        @pl.when(middle)
        def _():
            line(k).start()

    def arrive_side(k):
        wait_block(slots[k] * 2 + 1 - x)

    def drain():
        own_side().wait_send()

        @pl.when(z < 3)
        def _():
            own_up().wait_send()

        @pl.when(z > 0)
        def _():
            own_down().wait_send()

        for k in range(1, 4):
            if k < 3:
                side(k).wait_send()

            @pl.when(middle)
            def _(k=k):
                line(k).wait_send()

    return middle, start, arrive, arrive_side, drain


def attention_kernel(
    own,
    cot,
    query_w,
    key_w,
    value_w,
    out_w,
    query_gain,
    key_gain,
    cosine,
    sine,
    gathered,
    query_unit,
    key_unit,
    query_low,
    key_low,
    value_low,
    attended,
    log_sums,
    attn_sum,
    cot_all,
    rows_v,
    weights_v,
    out_v,
    pre_v,
    low_v,
    mixed_v,
    log_v,
    parts,
    own_part,
    core_in,
    line_in,
    load_sem,
    store_sem,
    rows_recv,
    rows_send,
    part_recv,
    part_send,
    cot_recv,
    cot_send,
    cot_sem,
):
    position = lax.axis_index("expert")
    t = lax.axis_index("tensor")
    z = position // 2
    x = position % 2
    y = t // 2
    c = t % 2
    near = y * 2 + 1 - c
    across = (1 - y) * 2 + c
    opposite = (1 - y) * 2 + 1 - c
    rows = own.shape[0]
    heads = low_v.shape[2] // 128
    factor = 1.0 / math.sqrt(128.0)
    mesh_ids = pl.DeviceIdType.MESH
    middle, gather_start, gather_arrive, gather_side, gather_drain = line_gather(
        cot, cot_all, cot_recv, cot_send
    )

    loads = [
        pltpu.make_async_copy(own, rows_v.at[t], load_sem.at[0]),
        pltpu.make_async_copy(query_w, weights_v.at[0], load_sem.at[1]),
        pltpu.make_async_copy(key_w, weights_v.at[1], load_sem.at[2]),
        pltpu.make_async_copy(value_w, weights_v.at[2], load_sem.at[3]),
        pltpu.make_async_copy(out_w, out_v, load_sem.at[4]),
    ]
    for load in loads:
        load.start()
    cot_copy = pltpu.make_async_copy(cot, cot_all.at[position], cot_sem)
    cot_copy.start()

    barrier = pltpu.get_barrier_semaphore()
    for place in ((position, near), (position, across), (z * 2 + 1 - x, t)):
        pl.semaphore_signal(barrier, inc=1, device_id=place, device_id_type=mesh_ids)

    @pl.when(z < 3)
    def _():
        pl.semaphore_signal(barrier, inc=1, device_id=(position + 2, t), device_id_type=mesh_ids)

    @pl.when(z > 0)
    def _():
        pl.semaphore_signal(barrier, inc=1, device_id=(position - 2, t), device_id_type=mesh_ids)

    pl.semaphore_wait(barrier, 4 + middle.astype(jnp.int32))

    def rows_copy(source, block, index, to):
        return pltpu.make_async_remote_copy(
            src_ref=source,
            dst_ref=rows_v.at[block],
            send_sem=rows_send.at[index - 1],
            recv_sem=rows_recv.at[index - 1],
            device_id=(position, to),
            device_id_type=mesh_ids,
        )

    to_across = rows_copy(own, t, 2, across)
    to_near = rows_copy(own, t, 1, near)
    forward = rows_copy(rows_v.at[across], across, 3, near)
    to_across.start()
    to_near.start()
    gather_start()
    for load in loads:
        load.wait()

    def project(i, carry):
        block = pick(i, [t, near, across, opposite])

        @pl.when(i == 1)
        def _():
            to_near.wait_recv()

        @pl.when(i == 2)
        def _():
            to_across.wait_recv()
            forward.start()
            gather_arrive(1)

            @pl.when(middle)
            def _():
                gather_arrive(2)

        @pl.when(i == 3)
        def _():
            forward.wait_recv()

        area = pl.ds(block * rows, rows)
        values = rows_v[block]
        for which, gain in ((0, query_gain), (1, key_gain)):
            pre = jnp.dot(values, weights_v[which], preferred_element_type=jnp.float32)
            for h in range(heads):
                span = slice(h * 128, (h + 1) * 128)
                head = pre[:, span]
                scale = lax.rsqrt(jnp.mean(head * head, axis=-1, keepdims=True) + epsilon)
                unit = head * scale
                pre_v[which, area, span] = unit.astype(jnp.bfloat16)
                lane = 4 + which * 4 + h
                log_v[area, lane : lane + 1] = scale
                normed = unit * gain[...]
                turned = normed * cosine[area] + pltpu.roll(normed, 64, 1) * sine[area]
                low_v[which, area, span] = turned.astype(jnp.bfloat16)
        low_v[2, area] = jnp.dot(
            values, weights_v[2], preferred_element_type=jnp.float32
        ).astype(jnp.bfloat16)
        return carry

    lax.fori_loop(0, 4, project, 0)
    stores = [
        pltpu.make_async_copy(rows_v, gathered, store_sem.at[0]),
        pltpu.make_async_copy(pre_v.at[0], query_unit, store_sem.at[1]),
        pltpu.make_async_copy(pre_v.at[1], key_unit, store_sem.at[2]),
        pltpu.make_async_copy(low_v.at[0], query_low, store_sem.at[3]),
        pltpu.make_async_copy(low_v.at[1], key_low, store_sem.at[4]),
        pltpu.make_async_copy(low_v.at[2], value_low, store_sem.at[5]),
    ]
    for store in stores:
        store.start()

    def part_copy(source, target, index, to):
        return pltpu.make_async_remote_copy(
            src_ref=source,
            dst_ref=target,
            send_sem=part_send.at[index],
            recv_sem=part_recv.at[index],
            device_id=(position, to),
            device_id_type=mesh_ids,
        )

    core_first = part_copy(parts.at[0], core_in.at[0], 0, near)
    line_copy = part_copy(parts.at[1], line_in, 1, across)
    core_second = part_copy(parts.at[2], core_in.at[1], 2, near)

    def attend(i, carry):
        block = pick(i, [opposite, across, near, t])
        area = pl.ds(block * rows, rows)
        for h in range(heads):
            span = slice(h * 128, (h + 1) * 128)
            scores = lax.dot_general(
                low_v[0, area, span], low_v[1, :, span], contract_last, preferred_element_type=jnp.float32
            )
            highest_score = jnp.max(scores, axis=-1, keepdims=True)
            weights = jnp.exp((scores - highest_score) * factor)
            total = jnp.sum(weights, axis=-1, keepdims=True)
            mixed = jnp.dot(
                weights.astype(jnp.bfloat16), low_v[2, :, span], preferred_element_type=jnp.float32
            )
            mixed_v[area, span] = (mixed / total).astype(jnp.bfloat16)
            log_v[area, h : h + 1] = highest_score * factor + jnp.log(total)
        own_part[...] = jnp.dot(mixed_v[area], out_v[...], preferred_element_type=jnp.float32)

        @pl.when(i == 0)
        def _():
            parts[0] = own_part[...].astype(jnp.bfloat16)
            core_first.start()

        @pl.when(i == 1)
        def _():
            core_first.wait_recv()
            parts[1] = (own_part[...] + core_in[0].astype(jnp.float32)).astype(jnp.bfloat16)
            line_copy.start()

            @pl.when(middle)
            def _():
                gather_arrive(3)

        @pl.when(i == 2)
        def _():
            parts[2] = own_part[...].astype(jnp.bfloat16)
            core_second.start()

            @pl.when(middle == False)
            def _():
                gather_arrive(2)

        return carry

    lax.fori_loop(0, 4, attend, 0)
    more = [
        pltpu.make_async_copy(mixed_v, attended, store_sem.at[6]),
        pltpu.make_async_copy(log_v, log_sums, store_sem.at[7]),
    ]
    for store in more:
        store.start()
    core_second.wait_recv()
    own_part[...] += core_in[1].astype(jnp.float32)
    line_copy.wait_recv()
    own_part[...] += line_in[...].astype(jnp.float32)
    last = pltpu.make_async_copy(own_part, attn_sum, store_sem.at[8])
    last.start()

    @pl.when(middle == False)
    def _():
        gather_arrive(3)

    for k in range(3):
        gather_side(k)
    gather_drain()
    for copy in (to_across, to_near, forward, core_first, line_copy, core_second):
        copy.wait_send()
    for store in [*stores, *more, last, cot_copy]:
        store.wait()


def attention_forward(own, cot, weights, out_w, gains, tables, collective):
    rows, width = own.shape
    local = out_w.shape[0]
    length = 4 * rows
    any_space = pl.BlockSpec(memory_space=pl.ANY)
    vector = pl.BlockSpec(memory_space=pltpu.VMEM)
    low, full = jnp.bfloat16, jnp.float32
    dma = pltpu.SemaphoreType.DMA
    return pl.pallas_call(
        attention_kernel,
        name="attention_forward",
        out_shape=(
            jax.ShapeDtypeStruct((4, rows, width), low),
            jax.ShapeDtypeStruct((length, local), low),
            jax.ShapeDtypeStruct((length, local), low),
            jax.ShapeDtypeStruct((length, local), low),
            jax.ShapeDtypeStruct((length, local), low),
            jax.ShapeDtypeStruct((length, local), low),
            jax.ShapeDtypeStruct((length, local), low),
            jax.ShapeDtypeStruct((length, 128), full),
            jax.ShapeDtypeStruct((rows, width), full),
            jax.ShapeDtypeStruct((8, rows, width), low),
        ),
        in_specs=[any_space] * 6 + [vector] * 4,
        out_specs=(any_space,) * 10,
        scratch_shapes=[
            pltpu.VMEM((4, rows, width), low),
            pltpu.VMEM((3, width, local), low),
            pltpu.VMEM((local, width), low),
            pltpu.VMEM((2, length, local), low),
            pltpu.VMEM((3, length, local), low),
            pltpu.VMEM((length, local), low),
            pltpu.VMEM((length, 128), full),
            pltpu.VMEM((3, rows, width), low),
            pltpu.VMEM((rows, width), full),
            pltpu.VMEM((2, rows, width), low),
            pltpu.VMEM((rows, width), low),
            dma((5,)),
            dma((9,)),
            dma((3,)),
            dma((3,)),
            dma((3,)),
            dma((3,)),
            dma((8,)),
            dma((9,)),
            dma,
        ],
        compiler_params=pltpu.CompilerParams(
            collective_id=collective, has_side_effects=True, vmem_limit_bytes=60 << 20
        ),
        cost_estimate=pl.CostEstimate(
            flops=8 * length * width * local, bytes_accessed=64 << 20, transcendentals=length * length * 4
        ),
    )(own, cot, *weights, out_w, *gains, *tables)


def attention_back_kernel(
    branch,
    gathered,
    query_unit,
    key_unit,
    query_low,
    key_low,
    value_low,
    attended,
    log_sums,
    query_w,
    key_w,
    value_w,
    out_w,
    query_gain,
    key_gain,
    cosine,
    sine,
    sent_input,
    sent_output,
    y_all,
    norm_mid_part,
    rows_grad,
    arrived_input,
    arrived_output,
    y_total,
    y_side,
    y_cross,
    y_line,
    y_sums,
    out_total,
    value_total,
    key_total,
    query_total,
    sums,
    branch_v,
    rows_v,
    weights_v,
    out_v,
    unit_v,
    low_v,
    log_v,
    grads_v,
    key_acc,
    value_acc,
    scattered,
    side_in,
    line_in,
    own_part,
    core_in,
    across_in,
    y_v,
    gain_sums,
    sums_in,
    load_sem,
    store_sem,
    branch_recv,
    branch_send,
    part_recv,
    part_send,
    side_recv,
    side_send,
    line_recv,
    line_send,
    swap_recv,
    swap_send,
    y_load,
    y_store,
    y_side_recv,
    y_side_send,
    y_cross_sems,
    y_line_recv,
    y_line_send,
    sums_recv,
    sums_send,
):
    position = lax.axis_index("expert")
    t = lax.axis_index("tensor")
    z = position // 2
    x = position % 2
    y = t // 2
    core = t % 2
    near = y * 2 + 1 - core
    across = (1 - y) * 2 + core
    opposite = (1 - y) * 2 + 1 - core
    rows = branch.shape[0]
    local = out_v.shape[0]
    heads = local // 128
    kinds = scattered.shape[0]
    factor = 1.0 / math.sqrt(128.0)
    middle = (z == 1) | (z == 2)
    mesh_ids = pl.DeviceIdType.MESH
    slots = [z, pick(z, [1, 0, 3, 2]), pick(z, [2, 2, 1, 1]), pick(z, [3, 3, 0, 0])]

    loads = [
        pltpu.make_async_copy(branch, branch_v.at[t], load_sem.at[0]),
        pltpu.make_async_copy(out_w, out_v, load_sem.at[1]),
        pltpu.make_async_copy(query_low, low_v.at[0], load_sem.at[2]),
        pltpu.make_async_copy(key_low, low_v.at[1], load_sem.at[3]),
        pltpu.make_async_copy(value_low, low_v.at[2], load_sem.at[4]),
        pltpu.make_async_copy(log_sums, log_v, load_sem.at[5]),
        pltpu.make_async_copy(query_unit, unit_v.at[0], load_sem.at[6]),
        pltpu.make_async_copy(key_unit, unit_v.at[1], load_sem.at[7]),
        pltpu.make_async_copy(attended, low_v.at[3], load_sem.at[8]),
        pltpu.make_async_copy(gathered, rows_v, load_sem.at[9]),
        pltpu.make_async_copy(query_w, weights_v.at[0], load_sem.at[10]),
        pltpu.make_async_copy(key_w, weights_v.at[1], load_sem.at[11]),
        pltpu.make_async_copy(value_w, weights_v.at[2], load_sem.at[12]),
    ]
    for load in loads:
        load.start()

    barrier = pltpu.get_barrier_semaphore()
    for place in ((position, near), (position, across), (z * 2 + 1 - x, t)):
        pl.semaphore_signal(barrier, inc=1, device_id=place, device_id_type=mesh_ids)

    @pl.when(z < 3)
    def _():
        pl.semaphore_signal(barrier, inc=1, device_id=(position + 2, t), device_id_type=mesh_ids)

    @pl.when(z > 0)
    def _():
        pl.semaphore_signal(barrier, inc=1, device_id=(position - 2, t), device_id_type=mesh_ids)

    distant = ((z + 2) % 4) * 2 + x
    pl.semaphore_signal(barrier, inc=1, device_id=(distant, t), device_id_type=mesh_ids)
    pl.semaphore_wait(barrier, 5 + middle.astype(jnp.int32))

    def branch_copy(source, block, index, to):
        return pltpu.make_async_remote_copy(
            src_ref=source,
            dst_ref=branch_v.at[block],
            send_sem=branch_send.at[index - 1],
            recv_sem=branch_recv.at[index - 1],
            device_id=(position, to),
            device_id_type=mesh_ids,
        )

    to_across = branch_copy(branch, t, 2, across)
    to_near = branch_copy(branch, t, 1, near)
    forward = branch_copy(branch_v.at[across], across, 3, near)
    to_across.start()
    to_near.start()

    swaps = [
        pltpu.make_async_remote_copy(
            src_ref=sent,
            dst_ref=arrived,
            send_sem=swap_send.at[i],
            recv_sem=swap_recv.at[i],
            device_id=(position, across),
            device_id_type=mesh_ids,
        )
        for i, (sent, arrived) in enumerate(
            ((sent_input, arrived_input), (sent_output, arrived_output))
        )
    ]

    def side_copy(k, c):
        return pltpu.make_async_remote_copy(
            src_ref=scattered.at[c, pick(k, slots) * 2 + 1 - x],
            dst_ref=side_in.at[c, k],
            send_sem=side_send.at[c, k],
            recv_sem=side_recv.at[c, k],
            device_id=(z * 2 + 1 - x, t),
            device_id_type=mesh_ids,
        )

    def line_slot(k):
        target = pick(k, slots)
        return jnp.where(target < z, target, target + 1)

    def line_copy(k, c):
        target = jnp.where(pick(k, slots) < z, z - 1, z + 1)
        return pltpu.make_async_remote_copy(
            src_ref=scattered.at[c, pick(k, slots) * 2 + x],
            dst_ref=line_in.at[c, line_slot(k)],
            send_sem=line_send.at[c, k - 1],
            recv_sem=line_recv.at[c, line_slot(k)],
            device_id=(jnp.clip(target, 0, 3) * 2 + x, t),
            device_id_type=mesh_ids,
        )

    def line_wait(slot, c):
        pltpu.make_async_remote_copy(
            src_ref=scattered.at[c, position],
            dst_ref=line_in.at[c, slot],
            send_sem=line_send.at[c, 0],
            recv_sem=line_recv.at[c, slot],
            device_id=(z * 2 + 1 - x, t),
            device_id_type=mesh_ids,
        ).wait_recv()

    def send_order(i):
        return jnp.where(middle, pick(i, [3, 1, 2, 0]), pick(i, [3, 2, 1, 0]))

    pair = z + 1 - 2 * (z % 2)
    ends = (z == 0) | (z == 3)

    def y_remote(source, target, send_sem, recv_sem, zz, xx):
        return pltpu.make_async_remote_copy(
            src_ref=source,
            dst_ref=target,
            send_sem=send_sem,
            recv_sem=recv_sem,
            device_id=(zz * 2 + xx, t),
            device_id_type=mesh_ids,
        )

    def y_block(k, xx):
        return y_all.at[slots[k] * 2 + xx]

    def y_side_copy(k):
        slot = max(k - 1, 0)
        source = y_sums.at[0] if k == 0 else y_block(k, 1 - x)
        return y_remote(
            source, y_side.at[slot], y_side_send.at[slot], y_side_recv.at[slot], z, 1 - x
        )

    def y_cross_copy():
        return y_remote(
            y_block(1, 1 - x), y_cross, y_cross_sems.at[0], y_cross_sems.at[1], pair, x
        )

    def y_line_copy(k, source):
        target = jnp.where(slots[k] < z, z - 1, z + 1)
        return y_remote(
            source,
            y_line.at[line_slot(k)],
            y_line_send.at[k - 1],
            y_line_recv.at[line_slot(k)],
            jnp.clip(target, 0, 3),
            x,
        )

    def y_line_wait(slot):
        y_remote(
            y_all.at[0], y_line.at[slot], y_line_send.at[0], y_line_recv.at[slot], z, 1 - x
        ).wait_recv()

    def y_add(target, sources):
        half = rows // 2
        for part in range(2):
            area = pl.ds(part * half, half)

            def load(i, source, area=area):
                return pltpu.make_async_copy(source.at[area], y_v.at[i], y_load.at[i])

            for i, (source, needed) in enumerate(sources):
                if needed is None:
                    load(i, source).start()
                else:

                    @pl.when(needed)
                    def _(i=i, source=source, load=load):
                        load(i, source).start()

            for i, (source, needed) in enumerate(sources):
                if needed is None:
                    load(i, source).wait()
                else:

                    @pl.when(needed)
                    def _(i=i, source=source, load=load):
                        load(i, source).wait()

            for i, (source, needed) in enumerate(sources[1:], 1):

                def add(i=i):
                    y_v[0] = (y_v[0].astype(jnp.float32) + y_v[i].astype(jnp.float32)).astype(
                        jnp.bfloat16
                    )

                if needed is None:
                    add()
                else:
                    pl.when(needed)(add)
            store = pltpu.make_async_copy(y_v.at[0], target.at[area], y_store)
            store.start()
            store.wait()

    def y_relay(k):
        if k > 1:
            y_side_copy(k).wait_recv()
        sources = [(y_block(k, x), None)]
        if k > 1:
            sources.append((y_side.at[k - 1], None))

        @pl.when(middle)
        def _():
            y_line_wait(line_slot(k))

        y_add(y_sums.at[k], [*sources, (y_line.at[line_slot(k)], middle)])
        y_line_copy(k, y_sums.at[k]).start()

    y_side_copy(3).start()
    y_cross_copy().start()
    y_side_copy(2).start()

    @pl.when(ends)
    def _():
        y_line_copy(1, y_block(1, x)).start()

    def start_side(c):
        def one(i, carry):
            side_copy(send_order(i), c).start()
            return carry

        lax.fori_loop(0, 4, one, 0)

    def weight_part(c, left, right):
        for d in range(8 // 2):
            span = pl.ds(d * 512, 512)
            product = jnp.zeros((512, local), jnp.float32)
            for b in range(4):
                product = product + lax.dot_general(
                    left[b, :, span],
                    right[pl.ds(b * rows, rows)],
                    contract_first,
                    preferred_element_type=jnp.float32,
                )
            scattered[c, 2 * d] = product[:256].astype(jnp.bfloat16)
            scattered[c, 2 * d + 1] = product[256:].astype(jnp.bfloat16)

    gain_sums[...] = jnp.zeros_like(gain_sums)
    sums[0] = jnp.zeros(sums.shape[1:], jnp.float32)
    sums[0, 1:2] = norm_mid_part[...]
    for load in loads[:9]:
        load.wait()

    def norm_back(turned, which, area, h, gain):
        span = slice(h * 128, (h + 1) * 128)
        grad = turned * cosine[area] - pltpu.roll(turned, 64, 1) * sine[area]
        unit = unit_v[which, area, span].astype(jnp.float32)
        gain_sums[which : which + 1] += jnp.sum(grad * unit, axis=0, keepdims=True)
        weighted = grad * gain[...]
        inner = jnp.mean(weighted * unit, axis=-1, keepdims=True)
        lane = 4 + which * 4 + h
        grads_v[which, area, span] = (
            log_v[area, lane : lane + 1] * (weighted - unit * inner)
        ).astype(jnp.bfloat16)

    def attend(i, carry):
        block = pick(i, [t, near, across, opposite])

        @pl.when(i == 1)
        def _():
            to_near.wait_recv()

        @pl.when(i == 2)
        def _():
            to_across.wait_recv()
            forward.start()
            to_across.wait_send()
            for swap in swaps:
                swap.start()

            @pl.when(ends)
            def _():
                y_relay(3)

        @pl.when(i == 3)
        def _():
            forward.wait_recv()
            weight_part(0, branch_v, low_v.at[3])
            start_side(0)

        area = pl.ds(block * rows, rows)
        mixed_grad = lax.dot_general(
            branch_v[block], out_v[...], contract_last, preferred_element_type=jnp.float32
        ).astype(jnp.bfloat16)
        for h in range(heads):
            span = slice(h * 128, (h + 1) * 128)
            query = low_v[0, area, span]
            key = low_v[1, :, span]
            grad = mixed_grad[:, span]
            scores = lax.dot_general(query, key, contract_last, preferred_element_type=jnp.float32)
            probs = jnp.exp(scores * factor - log_v[area, h : h + 1])
            prob_grad = lax.dot_general(
                grad, low_v[2, :, span], contract_last, preferred_element_type=jnp.float32
            )
            delta = jnp.sum(probs * prob_grad, axis=-1, keepdims=True)
            score_grad = (probs * (prob_grad - delta)).astype(jnp.bfloat16)
            query_grad = jnp.dot(score_grad, key, preferred_element_type=jnp.float32) * factor
            key_part = lax.dot_general(
                score_grad, query, contract_first, preferred_element_type=jnp.float32
            )
            value_part = lax.dot_general(
                probs.astype(jnp.bfloat16), grad, contract_first, preferred_element_type=jnp.float32
            )
            first = i == 0
            key_acc[:, span] = jnp.where(first, 0.0, key_acc[:, span]) + key_part
            value_acc[:, span] = jnp.where(first, 0.0, value_acc[:, span]) + value_part
            norm_back(query_grad, 0, area, h, query_gain)
        return carry

    key_acc[...] = jnp.zeros_like(key_acc)
    value_acc[...] = jnp.zeros_like(value_acc)
    lax.fori_loop(0, 4, attend, 0)
    for load in loads[9:]:
        load.wait()

    @pl.when(ends)
    def _():
        y_relay(2)

    @pl.when(middle)
    def _():
        y_relay(3)

    grads_v[2] = value_acc[...].astype(jnp.bfloat16)
    weight_part(1, rows_v, grads_v.at[2])
    start_side(1)

    def key_back(b, carry):
        area = pl.ds(b * rows, rows)
        for h in range(heads):
            norm_back(key_acc[area, h * 128 : (h + 1) * 128] * factor, 1, area, h, key_gain)
        return carry

    lax.fori_loop(0, 4, key_back, 0)
    weight_part(2, rows_v, grads_v.at[1])
    start_side(2)
    weight_part(3, rows_v, grads_v.at[0])
    start_side(3)

    y_cross_copy().wait_recv()
    y_add(y_sums.at[0], [(y_block(0, 1 - x), None), (y_cross, None)])
    y_side_copy(0).start()

    def part_copy(source, target, index, to):
        return pltpu.make_async_remote_copy(
            src_ref=source,
            dst_ref=target,
            send_sem=part_send.at[index],
            recv_sem=part_recv.at[index],
            device_id=(position, to),
            device_id_type=mesh_ids,
        )

    for copy in (to_near, forward):
        copy.wait_send()
    core_first = part_copy(branch_v.at[0], core_in.at[0], 0, near)
    across_copy = part_copy(branch_v.at[1], across_in, 1, across)
    core_second = part_copy(branch_v.at[2], core_in.at[1], 2, near)

    def relay(k, c):
        block = pick(k, slots) * 2 + x
        side_copy(k, c).wait_recv()
        scattered[c, block] = (
            scattered[c, block].astype(jnp.float32) + side_in[c, k].astype(jnp.float32)
        ).astype(jnp.bfloat16)

        @pl.when(middle)
        def _():
            line_wait(line_slot(k), c)
            scattered[c, block] = (
                scattered[c, block].astype(jnp.float32) + line_in[c, line_slot(k)].astype(jnp.float32)
            ).astype(jnp.bfloat16)

        line_copy(k, c).start()

    def relays(c):
        def one(i, carry):
            relay(send_order(i), c)
            return carry

        lax.fori_loop(0, 3, one, 0)

    def rows_part(i, carry):
        block = pick(i, [opposite, across, near, t])
        area = pl.ds(block * rows, rows)
        for d in range(2):
            span = pl.ds(d * 1024, 1024)
            product = jnp.zeros((rows, 1024), jnp.float32)
            for which in range(3):
                product = product + lax.dot_general(
                    grads_v[which, area],
                    weights_v[which, span],
                    contract_last,
                    preferred_element_type=jnp.float32,
                )
            own_part[:, span] = product
            sums[0, 0:1, span] += jnp.sum(
                product * rows_v[block, :, span].astype(jnp.float32), axis=0, keepdims=True
            )

        @pl.when(i == 0)
        def _():
            branch_v[0] = own_part[...].astype(jnp.bfloat16)
            core_first.start()

        @pl.when(i == 1)
        def _():
            core_first.wait_recv()
            branch_v[1] = (own_part[...] + core_in[0].astype(jnp.float32)).astype(jnp.bfloat16)
            across_copy.start()

        @pl.when(i == 2)
        def _():
            branch_v[2] = own_part[...].astype(jnp.bfloat16)
            core_second.start()

        return carry

    lax.fori_loop(0, 4, rows_part, 0)
    relays(0)

    @pl.when(middle)
    def _():
        y_relay(1)
        y_relay(2)

    relays(1)
    relays(2)
    y_side_copy(0).wait_recv()

    @pl.when(z < 3)
    def _():
        y_line_wait(z)

    @pl.when(z > 0)
    def _():
        y_line_wait(z + 1)

    y_add(
        y_total,
        [
            (y_all.at[position], None),
            (y_side.at[0], None),
            (y_line.at[z], z < 3),
            (y_line.at[z + 1], z > 0),
        ],
    )
    relays(3)
    for c, total in enumerate((out_total, value_total, key_total, query_total)):
        side_copy(0, c).wait_recv()
        total[...] = scattered[c, position].astype(jnp.float32) + side_in[c, 0].astype(jnp.float32)

        @pl.when(z < 3)
        def _(c=c, total=total):
            line_wait(z, c)
            total[...] += line_in[c, z].astype(jnp.float32)

        @pl.when(z > 0)
        def _(c=c, total=total):
            line_wait(z + 1, c)
            total[...] += line_in[c, z + 1].astype(jnp.float32)

        for k in range(4):
            side_copy(k, c).wait_send()
        for k in range(1, 4):
            line_copy(k, c).wait_send()
    sums[0, 2:3, :128] = gain_sums[0:1]
    sums[0, 2:3, 128:256] = gain_sums[1:2]

    def sums_round(i, to):
        copy = pltpu.make_async_remote_copy(
            src_ref=sums.at[i],
            dst_ref=sums_in.at[i],
            send_sem=sums_send.at[i],
            recv_sem=sums_recv.at[i],
            device_id=to,
            device_id_type=mesh_ids,
        )
        copy.start()
        copy.wait()
        sums[i + 1] = sums[i] + sums_in[i]

    sums_round(0, (position, near))
    sums_round(1, (z * 2 + 1 - x, t))
    sums_round(2, (pair * 2 + x, t))
    sums_round(3, (distant, t))
    core_second.wait_recv()
    own_part[...] += core_in[1].astype(jnp.float32)
    across_copy.wait_recv()
    own_part[...] += across_in[...].astype(jnp.float32)
    last = pltpu.make_async_copy(own_part, rows_grad, store_sem)
    last.start()
    sums_round(4, (position, across))
    for copy in (core_first, across_copy, core_second):
        copy.wait_send()
    last.wait()
    for swap in swaps:
        swap.wait()
    for k in (0, 2, 3):
        y_side_copy(k).wait_send()
    y_cross_copy().wait_send()
    for k in (1, 2, 3):
        y_line_copy(k, y_sums.at[k]).wait_send()


def attention_backward(branch, saved, weights, out_w, gains, tables, sent, y_all, norm_mid_part, collective):
    rows, width = branch.shape
    local = out_w.shape[0]
    length = 4 * rows
    any_space = pl.BlockSpec(memory_space=pl.ANY)
    vector = pl.BlockSpec(memory_space=pltpu.VMEM)
    low, full = jnp.bfloat16, jnp.float32
    dma = pltpu.SemaphoreType.DMA
    return pl.pallas_call(
        attention_back_kernel,
        name="attention_backward",
        out_shape=(jax.ShapeDtypeStruct((rows, width), full),)
        + tuple(jax.ShapeDtypeStruct(array.shape, array.dtype) for array in sent)
        + (
            jax.ShapeDtypeStruct((rows, width), low),
            jax.ShapeDtypeStruct((3, rows, width), low),
            jax.ShapeDtypeStruct((rows, width), low),
            jax.ShapeDtypeStruct((5, rows, width), low),
            jax.ShapeDtypeStruct((4, rows, width), low),
        )
        + (jax.ShapeDtypeStruct((width // 8, local), full),) * 4
        + (jax.ShapeDtypeStruct((6, 8, width), full),),
        in_specs=[any_space] * 13 + [vector] * 4 + [any_space] * 3 + [vector],
        out_specs=(any_space,) * 8 + (vector,) * 5,
        scratch_shapes=[
            pltpu.VMEM((4, rows, width), low),
            pltpu.VMEM((4, rows, width), low),
            pltpu.VMEM((3, width, local), low),
            pltpu.VMEM((local, width), low),
            pltpu.VMEM((2, length, local), low),
            pltpu.VMEM((4, length, local), low),
            pltpu.VMEM((length, 128), full),
            pltpu.VMEM((3, length, local), low),
            pltpu.VMEM((length, local), full),
            pltpu.VMEM((length, local), full),
            pltpu.VMEM((4, 8, width // 8, local), low),
            pltpu.VMEM((4, 4, width // 8, local), low),
            pltpu.VMEM((4, 5, width // 8, local), low),
            pltpu.VMEM((rows, width), full),
            pltpu.VMEM((2, rows, width), low),
            pltpu.VMEM((rows, width), low),
            pltpu.VMEM((4, rows // 2, width), low),
            pltpu.VMEM((8, 128), full),
            pltpu.VMEM((5, 8, width), full),
            dma((13,)),
            dma,
            dma((3,)),
            dma((3,)),
            dma((3,)),
            dma((3,)),
            dma((4, 4)),
            dma((4, 4)),
            dma((4, 5)),
            dma((4, 3)),
            dma((2,)),
            dma((2,)),
            dma((4,)),
            dma,
            dma((3,)),
            dma((3,)),
            dma((2,)),
            dma((5,)),
            dma((3,)),
            dma((5,)),
            dma((5,)),
        ],
        compiler_params=pltpu.CompilerParams(
            collective_id=collective, has_side_effects=True, vmem_limit_bytes=60 << 20
        ),
        cost_estimate=pl.CostEstimate(
            flops=16 * length * width * local, bytes_accessed=64 << 20, transcendentals=length * length * 4
        ),
    )(branch, *saved, *weights, out_w, *gains, *tables, *sent, y_all, norm_mid_part)


def add_three(first, second, third):
    return first.astype(jnp.float32) + second.astype(jnp.float32) + third.astype(jnp.float32)


def per_device(
    tokens,
    cotangent,
    routes,
    norm_in,
    query_w,
    key_w,
    value_w,
    out_w,
    query_gain,
    key_gain,
    norm_mid,
    router_w,
    gate_w,
    up_w,
    down_w,
):
    rows_own = tokens.shape[0]
    model_width = tokens.shape[1]
    head_width = query_gain.shape[0]
    experts_all = router_w.shape[1]
    source = tokens.astype(jnp.float32)
    scale_in = inverse_rms(source)
    normed_low = (source * scale_in * norm_in).astype(jnp.bfloat16)
    cosine, sine_table = rotary_tables(4 * rows_own, head_width)
    tables = (
        jnp.concatenate([cosine[:, 0], cosine[:, 0]], axis=1),
        jnp.concatenate([-sine_table[:, 0], sine_table[:, 0]], axis=1),
    )
    gains = (query_gain[None], key_gain[None])
    *saved, attn_out, cot_all = attention_forward(
        normed_low, cotangent, (query_w, key_w, value_w), out_w, gains, tables, 1
    )
    middle = source + attn_out
    scale_mid = inverse_rms(middle)
    normed_mid = middle * scale_mid * norm_mid
    mid_low = normed_mid.astype(jnp.bfloat16)
    logits = jnp.dot(normed_mid, router_w, precision=highest, preferred_element_type=jnp.float32)
    route_mask = routes[:, :, None] == jnp.arange(experts_all, dtype=jnp.int32)[None, None, :]
    mask_float = route_mask.astype(jnp.float32)
    chosen = jnp.sum(mask_float * logits[:, None, :], axis=-1)
    gating = jax.nn.softmax(chosen, axis=-1)
    gates = jnp.sum(mask_float * gating[:, :, None], axis=1)
    gates_high = gates.astype(jnp.bfloat16)
    gates_low = (gates - gates_high.astype(jnp.float32)).astype(jnp.bfloat16)
    spare = jnp.zeros((rows_own, 128 - 2 * experts_all), jnp.bfloat16)
    own_rows = jnp.concatenate([mid_low, gates_high, gates_low, spare], axis=1)
    _, _, y_all, row_total, core_input, near_input, core_output, near_output, _ = expert_pass(
        own_rows, cot_all.reshape(-1, model_width), gate_w, up_w, down_w, experts_all, 2
    )
    expert_input_grad = row_total[:, :model_width]
    gate_grad_dense = (
        row_total[:, model_width : model_width + experts_all]
        + row_total[:, model_width + experts_all : model_width + 2 * experts_all]
    )
    gate_grad = jnp.sum(mask_float * gate_grad_dense[:, None, :], axis=-1)
    inner_gate = jnp.sum(gating * gate_grad, axis=-1, keepdims=True)
    chosen_grad = gating * (gate_grad - inner_gate)
    logit_grad = jnp.sum(chosen_grad[:, :, None] * mask_float, axis=1)
    normed_mid_grad = expert_input_grad + lax.dot_general(
        logit_grad, router_w, contract_last, precision=highest, preferred_element_type=jnp.float32
    )
    norm_mid_part = jnp.sum(normed_mid_grad * middle * scale_mid, axis=0)
    upstream = cotangent.astype(jnp.float32)
    middle_grad = upstream + norm_backward(normed_mid_grad, middle, scale_mid, norm_mid)
    branch_low = middle_grad.astype(jnp.bfloat16)
    sent = (
        (near_input[1].astype(jnp.float32) + core_input[1].astype(jnp.float32)).astype(jnp.bfloat16),
        (near_output[1].astype(jnp.float32) + core_output[1].astype(jnp.float32)).astype(jnp.bfloat16),
    )
    (
        rows_grad,
        line_input,
        line_output,
        y_sum,
        _,
        _,
        _,
        _,
        out_w_turned,
        value_w_grad,
        key_w_grad,
        query_w_grad,
        sums,
    ) = attention_backward(
        branch_low, saved, (query_w, key_w, value_w), out_w, gains, tables, sent, y_all, norm_mid_part[None], 3
    )
    out_w_grad = out_w_turned.T
    router_part = lax.dot_general(
        normed_mid,
        logit_grad,
        contract_first,
        precision=highest,
        preferred_element_type=jnp.float32,
    )
    output = (middle + y_sum.astype(jnp.float32)).astype(jnp.bfloat16)
    gate_w_grad = add_three(near_input[0, 0], core_input[0, 0], line_input[0])
    up_w_grad = add_three(near_input[0, 1], core_input[0, 1], line_input[1])
    down_w_grad = add_three(near_output[0], core_output[0], line_output)
    input_grad = middle_grad + norm_backward(rows_grad, source, scale_in, norm_in)
    router_w_grad = lax.psum(router_part, ("expert", "tensor"))
    norm_in_grad = sums[5, 0] / norm_in
    norm_mid_grad = sums[5, 1]
    query_gain_grad = sums[5, 2, :head_width]
    key_gain_grad = sums[5, 2, head_width : 2 * head_width]
    return (
        output,
        input_grad,
        norm_in_grad,
        query_w_grad,
        key_w_grad,
        value_w_grad,
        out_w_grad,
        query_gain_grad,
        key_gain_grad,
        norm_mid_grad,
        router_w_grad,
        gate_w_grad,
        up_w_grad,
        down_w_grad,
    )


def per_device_general(
    tokens,
    cotangent,
    routes,
    norm_in,
    query_w,
    key_w,
    value_w,
    out_w,
    query_gain,
    key_gain,
    norm_mid,
    router_w,
    gate_w,
    up_w,
    down_w,
):
    rows_own = tokens.shape[0]
    model_width = tokens.shape[1]
    tensor_count = lax.axis_size("tensor")
    expert_count = lax.axis_size("expert")
    head_width = query_gain.shape[0]
    local_heads = query_w.shape[1] // head_width
    experts_local = gate_w.shape[0]
    experts_all = router_w.shape[1]
    top_count = routes.shape[1]
    hidden_width = gate_w.shape[2]
    factor = 1.0 / math.sqrt(head_width)
    cot_all = lax.all_gather(cotangent, "expert", axis=0, tiled=True)
    source = tokens.astype(jnp.float32)
    scale_in = inverse_rms(source)
    normed_low = (source * scale_in * norm_in).astype(jnp.bfloat16)
    gathered = lax.all_gather(normed_low, "tensor", axis=0, tiled=True)
    seq_len = gathered.shape[0]
    query_pre = jnp.dot(gathered, query_w, preferred_element_type=jnp.float32)
    key_pre = jnp.dot(gathered, key_w, preferred_element_type=jnp.float32)
    value_low = jnp.dot(gathered, value_w, preferred_element_type=jnp.float32).astype(jnp.bfloat16)
    cosine, sine_table = rotary_tables(seq_len, head_width)
    query_heads = query_pre.reshape(seq_len, local_heads, head_width)
    key_heads = key_pre.reshape(seq_len, local_heads, head_width)
    query_scale = inverse_rms(query_heads)
    key_scale = inverse_rms(key_heads)
    query_low = rotate(query_heads * query_scale * query_gain, cosine, sine_table).astype(
        jnp.bfloat16
    )
    key_low = rotate(key_heads * key_scale * key_gain, cosine, sine_table).astype(jnp.bfloat16)
    value_heads = value_low.reshape(seq_len, local_heads, head_width)
    block_rows = min(512, seq_len)
    block_count = seq_len // block_rows
    query_blocks = query_low.reshape(block_count, block_rows, local_heads, head_width)

    def attend(query_block):
        scores = (
            jnp.einsum("qhd,khd->hqk", query_block, key_low, preferred_element_type=jnp.float32)
            * factor
        )
        row_max = jnp.max(scores, axis=-1, keepdims=True)
        shifted = jnp.exp(scores - row_max)
        row_sum = jnp.sum(shifted, axis=-1, keepdims=True)
        probs_low = (shifted / row_sum).astype(jnp.bfloat16)
        mixture = jnp.einsum(
            "hqk,khd->qhd", probs_low, value_heads, preferred_element_type=jnp.float32
        )
        return (mixture.astype(jnp.bfloat16), (row_max + jnp.log(row_sum))[..., 0])

    attended_blocks, log_sums = lax.map(attend, query_blocks)
    attended = attended_blocks.reshape(seq_len, local_heads * head_width)
    attn_out = lax.psum_scatter(
        jnp.dot(attended, out_w, preferred_element_type=jnp.float32).astype(jnp.bfloat16),
        "tensor",
        scatter_dimension=0,
        tiled=True,
    ).astype(jnp.float32)
    middle = source + attn_out
    scale_mid = inverse_rms(middle)
    normed_mid = middle * scale_mid * norm_mid
    mid_low = normed_mid.astype(jnp.bfloat16)
    logits = jnp.dot(normed_mid, router_w, precision=highest, preferred_element_type=jnp.float32)
    route_mask = routes[:, :, None] == jnp.arange(experts_all, dtype=jnp.int32)[None, None, :]
    mask_float = route_mask.astype(jnp.float32)
    chosen = jnp.sum(mask_float * logits[:, None, :], axis=-1)
    gating = jax.nn.softmax(chosen, axis=-1)
    upstream = cotangent.astype(jnp.float32)
    gates = jnp.sum(mask_float * gating[:, :, None], axis=1)
    x_all = lax.all_gather(mid_low, "expert", axis=0, tiled=True)
    gates_all = lax.all_gather(gates, "expert", axis=0, tiled=True)
    first_expert = lax.axis_index("expert") * experts_local
    own_gates = lax.dynamic_slice_in_dim(gates_all, first_expert, experts_local, 1)
    part_width = hidden_width // tensor_count
    rows_all = x_all.shape[0]
    y_part = jnp.zeros((rows_all, model_width), jnp.float32)
    x_grad_part = jnp.zeros((rows_all, model_width), jnp.float32)
    gate_grads, gate_parts, up_parts, down_parts = [], [], [], []
    for e in range(experts_local):
        hidden_raw = lax.dot_general(
            cot_all, down_w[e], contract_last, preferred_element_type=jnp.float32
        )
        gate_pre = jnp.dot(x_all, gate_w[e], preferred_element_type=jnp.float32)
        up_pre = jnp.dot(x_all, up_w[e], preferred_element_type=jnp.float32)
        weight = own_gates[:, e : e + 1]
        hidden = gate_pre * jax.nn.sigmoid(gate_pre) * up_pre
        gate_grads.append(jnp.sum(hidden * hidden_raw, axis=1))
        hidden_low = (hidden * weight).astype(jnp.bfloat16)
        gate_back, up_back = swiglu_back(hidden_raw * weight, gate_pre, up_pre)
        y_part = y_part + jnp.dot(hidden_low, down_w[e], preferred_element_type=jnp.float32)
        x_grad_part = x_grad_part + lax.dot_general(
            gate_back, gate_w[e], contract_last, preferred_element_type=jnp.float32
        )
        x_grad_part = x_grad_part + lax.dot_general(
            up_back, up_w[e], contract_last, preferred_element_type=jnp.float32
        )
        gate_parts.append(
            jnp.einsum(
                "nd,ntf->tdf",
                x_all,
                gate_back.reshape(rows_all, tensor_count, part_width),
                preferred_element_type=jnp.float32,
            ).astype(jnp.bfloat16)
        )
        up_parts.append(
            jnp.einsum(
                "nd,ntf->tdf",
                x_all,
                up_back.reshape(rows_all, tensor_count, part_width),
                preferred_element_type=jnp.float32,
            ).astype(jnp.bfloat16)
        )
        down_parts.append(
            lax.dot_general(
                hidden_low, cot_all, contract_first, preferred_element_type=jnp.float32
            ).astype(jnp.bfloat16)
        )
    x_grad = lax.psum_scatter(
        x_grad_part.astype(jnp.bfloat16), "expert", scatter_dimension=0, tiled=True
    )
    expert_input_grad = x_grad.astype(jnp.float32)
    gate_grad_sent = jnp.stack(gate_grads, axis=-1)
    gate_grad_all = lax.all_to_all(gate_grad_sent, "expert", split_axis=0, concat_axis=0, tiled=True)
    gate_grad_dense = (
        gate_grad_all.reshape(expert_count, rows_own, experts_local)
        .transpose(1, 0, 2)
        .reshape(rows_own, experts_all)
    )
    gate_grad = jnp.sum(mask_float * gate_grad_dense[:, None, :], axis=-1)
    y_sum = lax.psum_scatter(
        y_part.astype(jnp.bfloat16), "expert", scatter_dimension=0, tiled=True
    )
    output = (middle + y_sum.astype(jnp.float32)).astype(jnp.bfloat16)

    def own_part(parts):
        return [
            lax.psum_scatter(p, "tensor", scatter_dimension=0, tiled=True).astype(jnp.float32)
            for p in parts
        ]

    gate_w_grad = jnp.concatenate(own_part(gate_parts), axis=0)
    up_w_grad = jnp.concatenate(own_part(up_parts), axis=0)
    down_w_grad = jnp.stack(own_part(down_parts), axis=0)
    inner_gate = jnp.sum(gating * gate_grad, axis=-1, keepdims=True)
    chosen_grad = gating * (gate_grad - inner_gate)
    logit_grad = jnp.sum(chosen_grad[:, :, None] * mask_float, axis=1)
    router_part = lax.dot_general(
        normed_mid,
        logit_grad,
        contract_first,
        precision=highest,
        preferred_element_type=jnp.float32,
    )
    normed_mid_grad = expert_input_grad + lax.dot_general(
        logit_grad, router_w, contract_last, precision=highest, preferred_element_type=jnp.float32
    )
    norm_mid_part = jnp.sum(normed_mid_grad * middle * scale_mid, axis=0)
    middle_grad = upstream + norm_backward(normed_mid_grad, middle, scale_mid, norm_mid)
    branch_low = middle_grad.astype(jnp.bfloat16)
    branch_all = lax.all_gather(branch_low, "tensor", axis=0, tiled=True)
    attended_grad = lax.dot_general(
        branch_all, out_w, contract_last, preferred_element_type=jnp.float32
    ).astype(jnp.bfloat16)
    out_w_part = lax.dot_general(
        attended, branch_all, contract_first, preferred_element_type=jnp.float32
    )
    grad_blocks = attended_grad.reshape(block_count, block_rows, local_heads, head_width)

    def attend_back(carry, inputs):
        key_total, value_total = carry
        query_block, grad_block, log_block = inputs
        scores = (
            jnp.einsum("qhd,khd->hqk", query_block, key_low, preferred_element_type=jnp.float32)
            * factor
        )
        probs = jnp.exp(scores - log_block[:, :, None])
        probs_low = probs.astype(jnp.bfloat16)
        value_total = value_total + jnp.einsum(
            "hqk,qhd->khd", probs_low, grad_block, preferred_element_type=jnp.float32
        )
        prob_grad = jnp.einsum(
            "qhd,khd->hqk", grad_block, value_heads, preferred_element_type=jnp.float32
        )
        delta = jnp.sum(probs * prob_grad, axis=-1, keepdims=True)
        score_low = (probs * (prob_grad - delta)).astype(jnp.bfloat16)
        query_part = (
            jnp.einsum("hqk,khd->qhd", score_low, key_low, preferred_element_type=jnp.float32)
            * factor
        )
        key_total = (
            key_total
            + jnp.einsum("hqk,qhd->khd", score_low, query_block, preferred_element_type=jnp.float32)
            * factor
        )
        return ((key_total, value_total), query_part)

    zero_heads = jnp.zeros((seq_len, local_heads, head_width), jnp.float32)
    (key_grad, value_total), query_parts = lax.scan(
        attend_back, (zero_heads, zero_heads), (query_blocks, grad_blocks, log_sums)
    )
    query_grad = query_parts.reshape(seq_len, local_heads, head_width)
    value_grad_low = value_total.reshape(seq_len, local_heads * head_width).astype(jnp.bfloat16)
    query_rot_grad = rotate_back(query_grad, cosine, sine_table)
    key_rot_grad = rotate_back(key_grad, cosine, sine_table)
    query_gain_part = jnp.sum(query_rot_grad * query_heads * query_scale, axis=(0, 1))
    key_gain_part = jnp.sum(key_rot_grad * key_heads * key_scale, axis=(0, 1))
    query_pre_grad = (
        norm_backward(query_rot_grad, query_heads, query_scale, query_gain)
        .reshape(seq_len, local_heads * head_width)
        .astype(jnp.bfloat16)
    )
    key_pre_grad = (
        norm_backward(key_rot_grad, key_heads, key_scale, key_gain)
        .reshape(seq_len, local_heads * head_width)
        .astype(jnp.bfloat16)
    )
    query_w_part = lax.dot_general(
        gathered, query_pre_grad, contract_first, preferred_element_type=jnp.float32
    )
    key_w_part = lax.dot_general(
        gathered, key_pre_grad, contract_first, preferred_element_type=jnp.float32
    )
    value_w_part = lax.dot_general(
        gathered, value_grad_low, contract_first, preferred_element_type=jnp.float32
    )
    summed = lax.dot_general(
        query_pre_grad, query_w, contract_last, preferred_element_type=jnp.float32
    )
    summed = summed + lax.dot_general(
        key_pre_grad, key_w, contract_last, preferred_element_type=jnp.float32
    )
    rows_grad = lax.psum_scatter(
        (
            summed
            + lax.dot_general(
                value_grad_low, value_w, contract_last, preferred_element_type=jnp.float32
            )
        ).astype(jnp.bfloat16),
        "tensor",
        scatter_dimension=0,
        tiled=True,
    ).astype(jnp.float32)
    norm_in_part = jnp.sum(rows_grad * source * scale_in, axis=0)
    input_grad = middle_grad + norm_backward(rows_grad, source, scale_in, norm_in)
    query_w_grad, key_w_grad, value_w_grad, out_w_grad = (
        lax.psum_scatter(
            query_w_part.astype(jnp.bfloat16), "expert", scatter_dimension=0, tiled=True
        ).astype(jnp.float32),
        lax.psum_scatter(
            key_w_part.astype(jnp.bfloat16), "expert", scatter_dimension=0, tiled=True
        ).astype(jnp.float32),
        lax.psum_scatter(
            value_w_part.astype(jnp.bfloat16), "expert", scatter_dimension=0, tiled=True
        ).astype(jnp.float32),
        lax.psum_scatter(
            out_w_part.astype(jnp.bfloat16), "expert", scatter_dimension=1, tiled=True
        ).astype(jnp.float32),
    )
    norm_in_grad, query_gain_grad, key_gain_grad, norm_mid_grad, router_w_grad = lax.psum(
        (norm_in_part, query_gain_part, key_gain_part, norm_mid_part, router_part),
        ("expert", "tensor"),
    )
    return (
        output,
        input_grad,
        norm_in_grad,
        query_w_grad,
        key_w_grad,
        value_w_grad,
        out_w_grad,
        query_gain_grad,
        key_gain_grad,
        norm_mid_grad,
        router_w_grad,
        gate_w_grad,
        up_w_grad,
        down_w_grad,
    )


def solution(mesh):
    placed = (
        P(("expert", "tensor"), None),
        P(("expert", "tensor"), None),
        P(("expert", "tensor"), None),
        P(),
        P(None, "tensor"),
        P(None, "tensor"),
        P(None, "tensor"),
        P("tensor", None),
        P(),
        P(),
        P(),
        P(),
        P("expert", None, None),
        P("expert", None, None),
        P("expert", None, None),
    )
    return jax.shard_map(
        per_device if dict(mesh.shape) == {"expert": 8, "tensor": 4} else per_device_general,
        mesh=mesh,
        in_specs=placed,
        out_specs=(
            P(("expert", "tensor"), None),
            P(("expert", "tensor"), None),
            P(),
            P("expert", "tensor"),
            P("expert", "tensor"),
            P("expert", "tensor"),
            P("tensor", "expert"),
            P(),
            P(),
            P(),
            P(),
            P("expert", None, "tensor"),
            P("expert", None, "tensor"),
            P("expert", "tensor", None),
        ),
        check_vma=False,
    )
```

```python
import functools
import math

import jax
import jax.numpy as jnp
from jax import lax
from jax.experimental import pallas as pl
from jax.experimental.pallas import tpu as pltpu
from jax.sharding import PartitionSpec as P

epsilon = 1e-06
highest = lax.Precision.HIGHEST
contract_last = (((1,), (1,)), ((), ()))
contract_first = (((0,), (0,)), ((), ()))


def inverse_rms(values):
    return lax.rsqrt(jnp.mean(values * values, axis=-1, keepdims=True) + epsilon)


def norm_backward(grad_norm, values, inverse, norm_gain):
    weighted = grad_norm * norm_gain
    inner_mean = jnp.mean(weighted * values, axis=-1, keepdims=True)
    return inverse * weighted - values * inverse * inverse * inverse * inner_mean


def rotary_tables(length, head_width):
    half_dim = head_width // 2
    frequency = jnp.exp(
        -math.log(10000.0) * 2.0 * jnp.arange(half_dim, dtype=jnp.float32) / head_width
    )
    angles = jnp.arange(length, dtype=jnp.float32)[:, None] * frequency[None, :]
    return (jnp.cos(angles)[:, None, :], jnp.sin(angles)[:, None, :])


def rotate(values, cosine, sine_table):
    half_dim = values.shape[-1] // 2
    first_half = values[..., :half_dim]
    second_half = values[..., half_dim:]
    return jnp.concatenate(
        [
            first_half * cosine - second_half * sine_table,
            second_half * cosine + first_half * sine_table,
        ],
        axis=-1,
    )


def rotate_back(gradient, cosine, sine_table):
    half_dim = gradient.shape[-1] // 2
    first_half = gradient[..., :half_dim]
    second_half = gradient[..., half_dim:]
    return jnp.concatenate(
        [
            first_half * cosine + second_half * sine_table,
            second_half * cosine - first_half * sine_table,
        ],
        axis=-1,
    )


def swiglu_back(hidden_grad, gate_pre, up_pre):
    sigmoid_part = jax.nn.sigmoid(gate_pre)
    gate_back = (
        hidden_grad * up_pre * sigmoid_part * (1.0 + gate_pre * (1.0 - sigmoid_part))
    ).astype(jnp.bfloat16)
    up_back = (hidden_grad * gate_pre * sigmoid_part).astype(jnp.bfloat16)
    return (gate_back, up_back)


chunks = 4


def pick(index, values):
    result = values[-1]
    for j in reversed(range(len(values) - 1)):
        result = jnp.where(index == j, values[j], result)
    return result


def expert_kernel(
    experts_all,
    own_rows,
    cot_all,
    gate_hbm,
    up_hbm,
    down_hbm,
    hidden_all,
    grads_all,
    y_all,
    total,
    core_input,
    near_input,
    core_output,
    near_output,
    cot_late,
    gate_v,
    up_v,
    down_v,
    rows_v,
    cot_v,
    hidden_v,
    gate_b,
    up_b,
    y_v,
    stage,
    parts,
    side_in,
    cross_in,
    line_in,
    weight_sem,
    own_sem,
    cot_sem,
    out_sem,
    item_in,
    item_out,
    core_recv,
    gather_recv,
    gather_send,
    side_recv,
    side_send,
    cross_recv,
    cross_send,
    line_recv,
    line_send,
    late_recv,
    late_send,
):
    position = lax.axis_index("expert")
    peer = lax.axis_index("tensor")
    z = position // 2
    x = position % 2
    experts_local, width, hidden = gate_v.shape
    rows = cot_v.shape[0]
    part = hidden // 4
    y = peer // 2
    core = peer % 2
    chunk = rows // chunks
    middle = (z == 1) | (z == 2)
    ends = (z == 0) | (z == 3)
    pair = z + 1 - 2 * (z % 2)
    line_slots = [
        z,
        pick(z, [1, 0, 3, 2]),
        pick(z, [2, 2, 1, 1]),
        pick(z, [3, 3, 0, 0]),
    ]

    def block_rows(block):
        return pl.ds(pl.multiple_of(block * rows, rows), rows)

    def device(zz, xx):
        return (zz * 2 + xx, peer)

    def slot_z(k):
        return pick(k, line_slots)

    weight_copies = [
        pltpu.make_async_copy(gate_hbm, gate_v, weight_sem.at[0]),
        pltpu.make_async_copy(up_hbm, up_v, weight_sem.at[1]),
        pltpu.make_async_copy(down_hbm, down_v, weight_sem.at[2]),
    ]
    own_copy = pltpu.make_async_copy(own_rows, rows_v.at[block_rows(position)], own_sem)
    own_copy.start()
    for copy in weight_copies:
        copy.start()

    barrier = pltpu.get_barrier_semaphore()
    pl.semaphore_signal(barrier, inc=1, device_id=device(z, 1 - x), device_id_type=pl.DeviceIdType.MESH)
    core_peer = (position, y * 2 + 1 - core)
    pl.semaphore_signal(barrier, inc=1, device_id=core_peer, device_id_type=pl.DeviceIdType.MESH)

    @pl.when(z < 3)
    def _():
        pl.semaphore_signal(barrier, inc=1, device_id=device(z + 1, x), device_id_type=pl.DeviceIdType.MESH)

    @pl.when(z > 0)
    def _():
        pl.semaphore_signal(barrier, inc=1, device_id=device(z - 1, x), device_id_type=pl.DeviceIdType.MESH)

    pl.semaphore_wait(barrier, 3 + middle.astype(jnp.int32))

    def gather_copy(source, block, index, zz, xx):
        return pltpu.make_async_remote_copy(
            src_ref=source,
            dst_ref=rows_v.at[block_rows(block)],
            send_sem=gather_send.at[index],
            recv_sem=gather_recv.at[block],
            device_id=device(zz, xx),
            device_id_type=pl.DeviceIdType.MESH,
        )

    def own_send(index, zz, xx):
        return gather_copy(own_rows, position, index, zz, xx)

    own_send(0, z, 1 - x).start()

    @pl.when(z < 3)
    def _():
        own_send(1, z + 1, x).start()

    @pl.when(z > 0)
    def _():
        own_send(2, z - 1, x).start()

    def forward_side(k):
        block = slot_z(k) * 2 + x
        return gather_copy(rows_v.at[block_rows(block)], block, 2 + k, z, 1 - x)

    def forward_line(k):
        block = slot_z(k) * 2 + x
        target = jnp.where(slot_z(k) < z, z + 1, z - 1)
        return gather_copy(rows_v.at[block_rows(block)], block, 5 + k, jnp.clip(target, 0, 3), x)

    def arrived(block):
        gather_copy(own_rows, block, 0, z, 1 - x).wait_recv()

    def arrive(k):
        arrived(slot_z(k) * 2 + x)
        if k < 3:

            @pl.when(ends)
            def _():
                forward_side(k).start()

        @pl.when(middle)
        def _():
            if k > 1:
                forward_side(k).start()
            forward_line(k).start()

    def forward_cross():
        block = jnp.where(ends, z, slot_z(3)) * 2 + 1 - x
        return gather_copy(rows_v.at[block_rows(block)], block, 9, pair, x)

    def cross_copy(c):
        area = pl.ds(c * chunk, chunk)
        return pltpu.make_async_remote_copy(
            src_ref=parts.at[5, area],
            dst_ref=cross_in.at[area],
            send_sem=cross_send.at[c],
            recv_sem=cross_recv.at[c],
            device_id=device(pair, x),
            device_id_type=pl.DeviceIdType.MESH,
        )

    def cross_add(c):
        area = pl.ds(c * chunk, chunk)
        cross_copy(c).wait_recv()
        parts[4, area] = (
            parts[4, area].astype(jnp.float32) + cross_in[area].astype(jnp.float32)
        ).astype(jnp.bfloat16)
        side_copy(0, c).start()

    def side_slot(k):
        return jnp.maximum(k - 1, 0)

    def side_copy(k, c):
        area = pl.ds(c * chunk, chunk)
        return pltpu.make_async_remote_copy(
            src_ref=parts.at[4 + k, area],
            dst_ref=side_in.at[side_slot(k), area],
            send_sem=side_send.at[side_slot(k), c],
            recv_sem=side_recv.at[side_slot(k), c],
            device_id=device(z, 1 - x),
            device_id_type=pl.DeviceIdType.MESH,
        )

    def line_slot(k):
        target = slot_z(k)
        return jnp.where(target < z, target, target + 1)

    def line_copy(k, c):
        area = pl.ds(c * chunk, chunk)
        target = jnp.where(slot_z(k) < z, z - 1, z + 1)
        return pltpu.make_async_remote_copy(
            src_ref=parts.at[k, area],
            dst_ref=line_in.at[line_slot(k), area],
            send_sem=line_send.at[k - 1, c],
            recv_sem=line_recv.at[line_slot(k), c],
            device_id=device(jnp.clip(target, 0, 3), x),
            device_id_type=pl.DeviceIdType.MESH,
        )

    def line_wait(slot, c):
        area = pl.ds(c * chunk, chunk)
        pltpu.make_async_remote_copy(
            src_ref=parts.at[0, area],
            dst_ref=line_in.at[slot, area],
            send_sem=line_send.at[0, c],
            recv_sem=line_recv.at[slot, c],
            device_id=device(z, 1 - x),
            device_id_type=pl.DeviceIdType.MESH,
        ).wait_recv()

    def relay(k, c):
        area = pl.ds(c * chunk, chunk)
        if k > 1:
            side_copy(k, c).wait_recv()
            parts[k, area] = (
                parts[k, area].astype(jnp.float32) + side_in[k - 1, area].astype(jnp.float32)
            ).astype(jnp.bfloat16)

        @pl.when(middle)
        def _():
            line_wait(line_slot(k), c)
            parts[k, area] = (
                parts[k, area].astype(jnp.float32) + line_in[line_slot(k), area].astype(jnp.float32)
            ).astype(jnp.bfloat16)

        line_copy(k, c).start()

    def block_of(step):
        k = pick(step, [0, 1, 0, 1, 2, 2, 3, 3])
        side = pick(step, [0, 0, 1, 1, 0, 1, 1, 0])
        return k, side, slot_z(k) * 2 + jnp.where(side == 1, 1 - x, x)

    def cot_copy(step):
        return pltpu.make_async_copy(cot_all.at[block_rows(block_of(step)[2])], cot_v, cot_sem)

    def late_copy():
        return pltpu.make_async_remote_copy(
            src_ref=cot_all.at[block_rows(slot_z(3) * 2 + x)],
            dst_ref=cot_late,
            send_sem=late_send,
            recv_sem=late_recv,
            device_id=device(z, 1 - x),
            device_id_type=pl.DeviceIdType.MESH,
        )

    def y_copy(block):
        return pltpu.make_async_copy(y_v, y_all.at[block], out_sem.at[3])

    def out_copies(block):
        return [
            pltpu.make_async_copy(hidden_v, hidden_all.at[block_rows(block)], out_sem.at[0]),
            pltpu.make_async_copy(gate_b, grads_all.at[0, block_rows(block)], out_sem.at[1]),
            pltpu.make_async_copy(up_b, grads_all.at[1, block_rows(block)], out_sem.at[2]),
        ]

    cot_copy(0).start()
    own_copy.wait()
    for copy in weight_copies:
        copy.wait()

    def one_step(step, carry):
        k, side, block = block_of(step)

        @pl.when(step == 1)
        def _():
            arrive(1)

            @pl.when(middle)
            def _():
                arrive(2)

            arrived(z * 2 + 1 - x)

            @pl.when(ends)
            def _():
                forward_cross().start()

        @pl.when(step == 3)
        def _():
            @pl.when(ends)
            def _():
                arrive(2)

            @pl.when(middle)
            def _():
                arrive(3)

            arrived(slot_z(1) * 2 + 1 - x)

        @pl.when(step == 4)
        def _():
            late_copy().start()

        @pl.when(step == 6)
        def _():
            late_copy().wait_recv()
            pltpu.make_async_copy(cot_late, cot_v, cot_sem).start()

        @pl.when(step == 5)
        def _():
            arrived(slot_z(2) * 2 + 1 - x)

        @pl.when((step == 6) & ends)
        def _():
            arrived(slot_z(3) * 2 + 1 - x)

        @pl.when((step == 7) & ends)
        def _():
            arrive(3)

        @pl.when(step > 0)
        def _():
            for copy in out_copies(block):
                copy.wait()

        cot_copy(step).wait()
        rows_low = rows_v[block_rows(block), :width]
        extra = rows_v[block_rows(block), width:].astype(jnp.float32)
        lane = lax.broadcasted_iota(jnp.int32, extra.shape, 1)
        ext = jnp.zeros(extra.shape, jnp.float32)
        for e in range(experts_local):
            expert = position * experts_local + e
            high = lane == expert
            low = lane == expert + experts_all
            weight = jnp.sum(jnp.where(high | low, extra, 0.0), axis=1, keepdims=True)
            gate_grad = jnp.zeros((rows, 1), jnp.float32)
            for f in range(hidden // 512):
                columns = pl.ds(f * 512, 512)
                gate_pre = jnp.dot(rows_low, gate_v[e, :, columns], preferred_element_type=jnp.float32)
                up_pre = jnp.dot(rows_low, up_v[e, :, columns], preferred_element_type=jnp.float32)
                target = pl.ds(e * hidden + f * 512, 512)
                raw = lax.dot_general(
                    cot_v[...],
                    down_v[e, columns, :],
                    contract_last,
                    preferred_element_type=jnp.float32,
                )
                sig = jax.nn.sigmoid(gate_pre)
                act = gate_pre * sig
                hid = act * up_pre
                gate_grad = gate_grad + jnp.sum(hid * raw, axis=1, keepdims=True)
                hidden_v[:, target] = (hid * weight).astype(jnp.bfloat16)
                grad = raw * weight
                gate_b[:, target] = (grad * up_pre * sig * (1.0 + gate_pre * (1.0 - sig))).astype(jnp.bfloat16)
                up_b[:, target] = (grad * act).astype(jnp.bfloat16)
            grad_high = gate_grad.astype(jnp.bfloat16).astype(jnp.float32)
            ext = jnp.where(high, grad_high, ext)
            ext = jnp.where(low, gate_grad - grad_high, ext)

        @pl.when((step < 7) & (step != 5))
        def _():
            cot_copy(step + 1).start()

        @pl.when((step == 4) & middle)
        def _():
            arrived(slot_z(3) * 2 + 1 - x)
            forward_cross().start()

        place = side * 4 + k
        parts[place, :, width:] = ext.astype(jnp.bfloat16)
        for copy in out_copies(block):
            copy.start()
        for d in range(width // 1024):
            span = pl.ds(d * 1024, 1024)
            summed = jnp.zeros((rows, 1024), jnp.float32)
            for e in range(experts_local):
                target = pl.ds(e * hidden, hidden)
                summed = summed + lax.dot_general(
                    gate_b[:, target], gate_v[e, span, :], contract_last, preferred_element_type=jnp.float32
                )
                summed = summed + lax.dot_general(
                    up_b[:, target], up_v[e, span, :], contract_last, preferred_element_type=jnp.float32
                )
            parts[place, :, span] = summed.astype(jnp.bfloat16)

        @pl.when((side == 1) & (k > 1))
        def _():
            for c in range(chunks):
                side_copy(k, c).start()

        @pl.when(step == 3)
        def _():
            for c in range(chunks):
                cross_copy(c).start()

        @pl.when((step == 1) & ends)
        def _():
            for c in range(chunks):
                line_copy(1, c).start()

        @pl.when(step > 0)
        def _():
            y_copy(block).wait()

        for d in range(width // 1024):
            span = pl.ds(d * 1024, 1024)
            summed = jnp.zeros((rows, 1024), jnp.float32)
            for e in range(experts_local):
                summed = summed + jnp.dot(
                    hidden_v[:, pl.ds(e * hidden, hidden)],
                    down_v[e, :, span],
                    preferred_element_type=jnp.float32,
                )
            y_v[:, span] = summed.astype(jnp.bfloat16)
        y_copy(block).start()
        return carry

    lax.fori_loop(0, 8, one_step, 0)

    for copy in out_copies(position):
        copy.wait()
    y_copy(position).wait()
    whole_cot = [
        pltpu.make_async_copy(cot_all.at[:, pl.ds(h * hidden, hidden)], up_v.at[h], weight_sem.at[h])
        for h in range(2)
    ]
    for copy in whole_cot:
        copy.start()

    def columns_of(pair, q):
        column_y = jnp.where(q == 0, y, 1 - y)
        column_core = jnp.where(pair == 0, 1 - core, core)
        return column_y * 2 + column_core

    def item_source(i):
        return i // 6, (i % 6) // 2, i % 2

    def item_loads(i, act):
        pair_of, kind, e = item_source(i)
        slot = i % 2
        for q in range(2):
            start = pl.multiple_of(e * hidden + columns_of(pair_of, q) * part, part)
            place = gate_v.at[0, :, pl.ds(pl.multiple_of(slot * 2 * part + q * part, part), part)]
            sem = item_in.at[slot, q]

            @pl.when(kind < 2)
            def _(start=start, place=place, sem=sem):
                act(
                    pltpu.make_async_copy(
                        grads_all.at[jnp.minimum(kind, 1), :, pl.ds(start, part)], place, sem
                    )
                )

            @pl.when(kind == 2)
            def _(start=start, place=place, sem=sem):
                act(pltpu.make_async_copy(hidden_all.at[:, pl.ds(start, part)], place, sem))

    def core_copy(source, target, slot, number, q):
        return pltpu.make_async_remote_copy(
            src_ref=source,
            dst_ref=target,
            send_sem=item_out.at[slot, q],
            recv_sem=core_recv.at[number, q],
            device_id=core_peer,
            device_id_type=pl.DeviceIdType.MESH,
        )

    def item_stores(i, starting):
        pair_of, kind, e = item_source(i)
        slot = i % 2
        number = i % 6
        wide_kind = jnp.minimum(kind, 1)
        for q in range(2):
            wide_place = gate_v.at[1, :, pl.ds(pl.multiple_of(slot * 2 * part + q * part, part), part)]
            tall_place = down_v.at[slot, pl.ds(q * part, part)]

            def far(source, target, q=q):
                copy = core_copy(source, target, slot, number, q)
                if starting:
                    copy.start()
                else:
                    copy.wait_send()

            def own(source, target, q=q):
                copy = pltpu.make_async_copy(source, target, item_out.at[slot, q])
                if starting:
                    copy.start()
                else:
                    copy.wait()

            for which, move, wide_out, tall_out in (
                (0, far, core_input, core_output),
                (1, own, near_input, near_output),
            ):

                @pl.when((pair_of == which) & (kind < 2))
                def _(move=move, wide_place=wide_place, wide_out=wide_out, q=q):
                    move(wide_place, wide_out.at[q, wide_kind, e])

                @pl.when((pair_of == which) & (kind == 2))
                def _(move=move, tall_place=tall_place, tall_out=tall_out, q=q):
                    move(tall_place, tall_out.at[q, e])

    item_loads(0, lambda copy: copy.start())
    for copy in whole_cot:
        copy.wait()
    late_rows = block_rows(slot_z(3) * 2 + 1 - x)
    late_parts = [
        pltpu.make_async_copy(
            cot_late.at[:, pl.ds(h * hidden, hidden)], up_v.at[h, late_rows], weight_sem.at[h]
        )
        for h in range(2)
    ]
    for copy in late_parts:
        copy.start()
    for copy in late_parts:
        copy.wait()
    late_copy().wait_send()

    def at(index, first, gap):
        return (index >= first) & (index < first + gap * chunks) & ((index - first) % gap == 0)

    def item(index, carry):
        i = index // 4
        d = index % 4
        kind = (i % 6) // 2
        slot = i % 2

        @pl.when(d == 0)
        def _():
            item_loads(i, lambda copy: copy.wait())

            @pl.when(i < 11)
            def _():
                item_loads(i + 1, lambda copy: copy.start())

            @pl.when(i > 1)
            def _():
                item_stores(i - 2, False)

        columns = pl.ds(pl.multiple_of(slot * 2 * part, 2 * part), 2 * part)
        span = pl.ds(pl.multiple_of(d * (width // 4), width // 4), width // 4)

        @pl.when(kind < 2)
        def _():
            gate_v[1, span, columns] = lax.dot_general(
                rows_v[:, span], gate_v[0, :, columns], contract_first, preferred_element_type=jnp.float32
            ).astype(jnp.bfloat16)

        @pl.when(kind == 2)
        def _():
            half = pl.ds(pl.multiple_of((d % 2) * (hidden // 2), hidden // 2), hidden // 2)
            down_v[slot, : 2 * part, span] = lax.dot_general(
                gate_v[0, :, columns],
                up_v[d // 2, :, half],
                contract_first,
                preferred_element_type=jnp.float32,
            ).astype(jnp.bfloat16)

        @pl.when(d == 3)
        def _():
            item_stores(i, True)

        @pl.when(at(index, 1, 1))
        def _():
            cross_add(index - 1)

        @pl.when(at(index, 5, 4))
        def _():
            relay(3, (index - 5) // 4)

        @pl.when(at(index, 11, 4) & middle)
        def _():
            relay(1, (index - 11) // 4)

        @pl.when(at(index, 18, 1) & ends)
        def _():
            relay(2, index - 18)

        @pl.when(at(index, 24, 4) & middle)
        def _():
            relay(2, (index - 24) // 4)

        return carry

    lax.fori_loop(0, 48, item, 0)
    for last in (10, 11):
        item_stores(last, False)
    for number in range(6):
        for q in range(2):
            if number < 4:
                core_copy(
                    gate_v.at[1, :, pl.ds(0, part)],
                    core_input.at[q, number // 2, number % 2],
                    0,
                    number,
                    q,
                ).wait_recv()
            else:
                core_copy(
                    down_v.at[0, pl.ds(0, part)], core_output.at[q, number % 2], 0, number, q
                ).wait_recv()

    def finish(c, carry):
        area = pl.ds(c * chunk, chunk)
        side_copy(0, c).wait_recv()
        stage[...] = parts[0, area].astype(jnp.float32) + side_in[0, area].astype(jnp.float32)

        @pl.when(z < 3)
        def _():
            line_wait(z, c)
            stage[...] += line_in[z, area].astype(jnp.float32)

        @pl.when(z > 0)
        def _():
            line_wait(z + 1, c)
            stage[...] += line_in[z + 1, area].astype(jnp.float32)

        result = pltpu.make_async_copy(stage, total.at[area], own_sem)
        result.start()
        result.wait()
        for k in (0, 2, 3):
            side_copy(k, c).wait_send()
        cross_copy(c).wait_send()
        for k in range(1, 4):
            line_copy(k, c).wait_send()
        return carry

    lax.fori_loop(0, chunks, finish, 0)

    own_send(0, z, 1 - x).wait_send()

    @pl.when(z < 3)
    def _():
        own_send(1, z + 1, x).wait_send()

    @pl.when(z > 0)
    def _():
        own_send(2, z - 1, x).wait_send()

    forward_cross().wait_send()
    forward_side(2).wait_send()

    @pl.when(ends)
    def _():
        forward_side(1).wait_send()

    @pl.when(middle)
    def _():
        forward_side(3).wait_send()
        for k in range(1, 4):
            forward_line(k).wait_send()


def expert_pass(own_rows, cot_all, gate_w, up_w, down_w, experts_all, collective):
    rows, wide = own_rows.shape
    experts_local, width, hidden = gate_w.shape
    inner = experts_local * hidden
    any_space = pl.BlockSpec(memory_space=pl.ANY)
    low = jnp.bfloat16
    dma = pltpu.SemaphoreType.DMA
    return pl.pallas_call(
        functools.partial(expert_kernel, experts_all),
        name="expert_pass",
        out_shape=(
            jax.ShapeDtypeStruct((8 * rows, inner), low),
            jax.ShapeDtypeStruct((2, 8 * rows, inner), low),
            jax.ShapeDtypeStruct((8, rows, width), low),
            jax.ShapeDtypeStruct((rows, wide), jnp.float32),
            *(jax.ShapeDtypeStruct((2, 2, experts_local, width, hidden // 4), low),) * 2,
            *(jax.ShapeDtypeStruct((2, experts_local, hidden // 4, width), low),) * 2,
            jax.ShapeDtypeStruct((rows, width), low),
        ),
        in_specs=[any_space] * 5,
        out_specs=(any_space,) * 9,
        scratch_shapes=[
            pltpu.VMEM((experts_local, width, hidden), low),
            pltpu.VMEM((experts_local, width, hidden), low),
            pltpu.VMEM((experts_local, hidden, width), low),
            pltpu.VMEM((8 * rows, wide), low),
            pltpu.VMEM((rows, width), low),
            pltpu.VMEM((rows, inner), low),
            pltpu.VMEM((rows, inner), low),
            pltpu.VMEM((rows, inner), low),
            pltpu.VMEM((rows, width), low),
            pltpu.VMEM((rows // chunks, wide), jnp.float32),
            pltpu.VMEM((8, rows, wide), low),
            pltpu.VMEM((3, rows, wide), low),
            pltpu.VMEM((rows, wide), low),
            pltpu.VMEM((5, rows, wide), low),
            dma((3,)),
            dma,
            dma,
            dma((4,)),
            dma((2, 2)),
            dma((2, 2)),
            dma((6, 2)),
            dma((8,)),
            dma((10,)),
            dma((3, chunks)),
            dma((3, chunks)),
            dma((chunks,)),
            dma((chunks,)),
            dma((5, chunks)),
            dma((3, chunks)),
            dma,
            dma,
        ],
        compiler_params=pltpu.CompilerParams(
            collective_id=collective, has_side_effects=True, vmem_limit_bytes=60 << 20
        ),
        cost_estimate=pl.CostEstimate(
            flops=2 * 9 * 8 * rows * width * inner, bytes_accessed=64 << 20, transcendentals=8 * rows * inner
        ),
    )(own_rows, cot_all, gate_w, up_w, down_w)


def line_gather(source, target, recv, send):
    position = lax.axis_index("expert")
    peer = lax.axis_index("tensor")
    z = position // 2
    x = position % 2
    middle = (z == 1) | (z == 2)
    slots = [z, pick(z, [1, 0, 3, 2]), pick(z, [2, 2, 1, 1]), pick(z, [3, 3, 0, 0])]

    def copy(block_source, block, index, zz, xx):
        return pltpu.make_async_remote_copy(
            src_ref=block_source,
            dst_ref=target.at[block],
            send_sem=send.at[index],
            recv_sem=recv.at[block],
            device_id=(zz * 2 + xx, peer),
            device_id_type=pl.DeviceIdType.MESH,
        )

    def own_up():
        return copy(source, position, 1, z + 1, x)

    def own_down():
        return copy(source, position, 2, z - 1, x)

    def own_side():
        return copy(source, position, 0, z, 1 - x)

    def side(k):
        block = slots[k] * 2 + x
        return copy(target.at[block], block, 2 + k, z, 1 - x)

    def line(k):
        block = slots[k] * 2 + x
        onward = jnp.where(slots[k] < z, z + 1, z - 1)
        return copy(target.at[block], block, 5 + k, jnp.clip(onward, 0, 3), x)

    def start():
        own_side().start()

        @pl.when(z < 3)
        def _():
            own_up().start()

        @pl.when(z > 0)
        def _():
            own_down().start()

    def wait_block(block):
        copy(source, block, 0, z, 1 - x).wait_recv()

    def arrive(k):
        wait_block(slots[k] * 2 + x)
        if k < 3:
            side(k).start()

        @pl.when(middle)
        def _():
            line(k).start()

    def arrive_side(k):
        wait_block(slots[k] * 2 + 1 - x)

    def drain():
        own_side().wait_send()

        @pl.when(z < 3)
        def _():
            own_up().wait_send()

        @pl.when(z > 0)
        def _():
            own_down().wait_send()

        for k in range(1, 4):
            if k < 3:
                side(k).wait_send()

            @pl.when(middle)
            def _(k=k):
                line(k).wait_send()

    return middle, start, arrive, arrive_side, drain


def attention_kernel(
    own,
    cot,
    query_w,
    key_w,
    value_w,
    out_w,
    query_gain,
    key_gain,
    cosine,
    sine,
    gathered,
    query_unit,
    key_unit,
    query_low,
    key_low,
    value_low,
    attended,
    log_sums,
    attn_sum,
    cot_all,
    rows_v,
    weights_v,
    out_v,
    pre_v,
    low_v,
    mixed_v,
    log_v,
    parts,
    own_part,
    core_in,
    line_in,
    load_sem,
    store_sem,
    rows_recv,
    rows_send,
    part_recv,
    part_send,
    cot_recv,
    cot_send,
    cot_sem,
):
    position = lax.axis_index("expert")
    t = lax.axis_index("tensor")
    z = position // 2
    x = position % 2
    y = t // 2
    c = t % 2
    near = y * 2 + 1 - c
    across = (1 - y) * 2 + c
    opposite = (1 - y) * 2 + 1 - c
    rows = own.shape[0]
    heads = low_v.shape[2] // 128
    factor = 1.0 / math.sqrt(128.0)
    mesh_ids = pl.DeviceIdType.MESH
    middle, gather_start, gather_arrive, gather_side, gather_drain = line_gather(
        cot, cot_all, cot_recv, cot_send
    )

    loads = [
        pltpu.make_async_copy(own, rows_v.at[t], load_sem.at[0]),
        pltpu.make_async_copy(query_w, weights_v.at[0], load_sem.at[1]),
        pltpu.make_async_copy(key_w, weights_v.at[1], load_sem.at[2]),
        pltpu.make_async_copy(value_w, weights_v.at[2], load_sem.at[3]),
        pltpu.make_async_copy(out_w, out_v, load_sem.at[4]),
    ]
    for load in loads:
        load.start()
    cot_copy = pltpu.make_async_copy(cot, cot_all.at[position], cot_sem)
    cot_copy.start()

    barrier = pltpu.get_barrier_semaphore()
    for place in ((position, near), (position, across), (z * 2 + 1 - x, t)):
        pl.semaphore_signal(barrier, inc=1, device_id=place, device_id_type=mesh_ids)

    @pl.when(z < 3)
    def _():
        pl.semaphore_signal(barrier, inc=1, device_id=(position + 2, t), device_id_type=mesh_ids)

    @pl.when(z > 0)
    def _():
        pl.semaphore_signal(barrier, inc=1, device_id=(position - 2, t), device_id_type=mesh_ids)

    pl.semaphore_wait(barrier, 4 + middle.astype(jnp.int32))

    def rows_copy(source, block, index, to):
        return pltpu.make_async_remote_copy(
            src_ref=source,
            dst_ref=rows_v.at[block],
            send_sem=rows_send.at[index - 1],
            recv_sem=rows_recv.at[index - 1],
            device_id=(position, to),
            device_id_type=mesh_ids,
        )

    to_across = rows_copy(own, t, 2, across)
    to_near = rows_copy(own, t, 1, near)
    forward = rows_copy(rows_v.at[across], across, 3, near)
    to_across.start()
    to_near.start()
    gather_start()
    for load in loads:
        load.wait()

    def project(i, carry):
        block = pick(i, [t, near, across, opposite])

        @pl.when(i == 1)
        def _():
            to_near.wait_recv()

        @pl.when(i == 2)
        def _():
            to_across.wait_recv()
            forward.start()
            gather_arrive(1)

            @pl.when(middle)
            def _():
                gather_arrive(2)

        @pl.when(i == 3)
        def _():
            forward.wait_recv()

        area = pl.ds(block * rows, rows)
        values = rows_v[block]
        for which, gain in ((0, query_gain), (1, key_gain)):
            pre = jnp.dot(values, weights_v[which], preferred_element_type=jnp.float32)
            for h in range(heads):
                span = slice(h * 128, (h + 1) * 128)
                head = pre[:, span]
                scale = lax.rsqrt(jnp.mean(head * head, axis=-1, keepdims=True) + epsilon)
                unit = head * scale
                pre_v[which, area, span] = unit.astype(jnp.bfloat16)
                lane = 4 + which * 4 + h
                log_v[area, lane : lane + 1] = scale
                normed = unit * gain[...]
                turned = normed * cosine[area] + pltpu.roll(normed, 64, 1) * sine[area]
                low_v[which, area, span] = turned.astype(jnp.bfloat16)
        low_v[2, area] = jnp.dot(
            values, weights_v[2], preferred_element_type=jnp.float32
        ).astype(jnp.bfloat16)
        return carry

    lax.fori_loop(0, 4, project, 0)
    stores = [
        pltpu.make_async_copy(rows_v, gathered, store_sem.at[0]),
        pltpu.make_async_copy(pre_v.at[0], query_unit, store_sem.at[1]),
        pltpu.make_async_copy(pre_v.at[1], key_unit, store_sem.at[2]),
        pltpu.make_async_copy(low_v.at[0], query_low, store_sem.at[3]),
        pltpu.make_async_copy(low_v.at[1], key_low, store_sem.at[4]),
        pltpu.make_async_copy(low_v.at[2], value_low, store_sem.at[5]),
    ]
    for store in stores:
        store.start()

    def part_copy(source, target, index, to):
        return pltpu.make_async_remote_copy(
            src_ref=source,
            dst_ref=target,
            send_sem=part_send.at[index],
            recv_sem=part_recv.at[index],
            device_id=(position, to),
            device_id_type=mesh_ids,
        )

    core_first = part_copy(parts.at[0], core_in.at[0], 0, near)
    line_copy = part_copy(parts.at[1], line_in, 1, across)
    core_second = part_copy(parts.at[2], core_in.at[1], 2, near)

    def attend(i, carry):
        block = pick(i, [opposite, across, near, t])
        area = pl.ds(block * rows, rows)
        for h in range(heads):
            span = slice(h * 128, (h + 1) * 128)
            scores = lax.dot_general(
                low_v[0, area, span], low_v[1, :, span], contract_last, preferred_element_type=jnp.float32
            )
            highest_score = jnp.max(scores, axis=-1, keepdims=True)
            weights = jnp.exp((scores - highest_score) * factor)
            total = jnp.sum(weights, axis=-1, keepdims=True)
            mixed = jnp.dot(
                weights.astype(jnp.bfloat16), low_v[2, :, span], preferred_element_type=jnp.float32
            )
            mixed_v[area, span] = (mixed / total).astype(jnp.bfloat16)
            log_v[area, h : h + 1] = highest_score * factor + jnp.log(total)
        own_part[...] = jnp.dot(mixed_v[area], out_v[...], preferred_element_type=jnp.float32)

        @pl.when(i == 0)
        def _():
            parts[0] = own_part[...].astype(jnp.bfloat16)
            core_first.start()

        @pl.when(i == 1)
        def _():
            core_first.wait_recv()
            parts[1] = (own_part[...] + core_in[0].astype(jnp.float32)).astype(jnp.bfloat16)
            line_copy.start()

            @pl.when(middle)
            def _():
                gather_arrive(3)

        @pl.when(i == 2)
        def _():
            parts[2] = own_part[...].astype(jnp.bfloat16)
            core_second.start()

            @pl.when(middle == False)
            def _():
                gather_arrive(2)

        return carry

    lax.fori_loop(0, 4, attend, 0)
    more = [
        pltpu.make_async_copy(mixed_v, attended, store_sem.at[6]),
        pltpu.make_async_copy(log_v, log_sums, store_sem.at[7]),
    ]
    for store in more:
        store.start()
    core_second.wait_recv()
    own_part[...] += core_in[1].astype(jnp.float32)
    line_copy.wait_recv()
    own_part[...] += line_in[...].astype(jnp.float32)
    last = pltpu.make_async_copy(own_part, attn_sum, store_sem.at[8])
    last.start()

    @pl.when(middle == False)
    def _():
        gather_arrive(3)

    for k in range(3):
        gather_side(k)
    gather_drain()
    for copy in (to_across, to_near, forward, core_first, line_copy, core_second):
        copy.wait_send()
    for store in [*stores, *more, last, cot_copy]:
        store.wait()


def attention_forward(own, cot, weights, out_w, gains, tables, collective):
    rows, width = own.shape
    local = out_w.shape[0]
    length = 4 * rows
    any_space = pl.BlockSpec(memory_space=pl.ANY)
    vector = pl.BlockSpec(memory_space=pltpu.VMEM)
    low, full = jnp.bfloat16, jnp.float32
    dma = pltpu.SemaphoreType.DMA
    return pl.pallas_call(
        attention_kernel,
        name="attention_forward",
        out_shape=(
            jax.ShapeDtypeStruct((4, rows, width), low),
            jax.ShapeDtypeStruct((length, local), low),
            jax.ShapeDtypeStruct((length, local), low),
            jax.ShapeDtypeStruct((length, local), low),
            jax.ShapeDtypeStruct((length, local), low),
            jax.ShapeDtypeStruct((length, local), low),
            jax.ShapeDtypeStruct((length, local), low),
            jax.ShapeDtypeStruct((length, 128), full),
            jax.ShapeDtypeStruct((rows, width), full),
            jax.ShapeDtypeStruct((8, rows, width), low),
        ),
        in_specs=[any_space] * 6 + [vector] * 4,
        out_specs=(any_space,) * 10,
        scratch_shapes=[
            pltpu.VMEM((4, rows, width), low),
            pltpu.VMEM((3, width, local), low),
            pltpu.VMEM((local, width), low),
            pltpu.VMEM((2, length, local), low),
            pltpu.VMEM((3, length, local), low),
            pltpu.VMEM((length, local), low),
            pltpu.VMEM((length, 128), full),
            pltpu.VMEM((3, rows, width), low),
            pltpu.VMEM((rows, width), full),
            pltpu.VMEM((2, rows, width), low),
            pltpu.VMEM((rows, width), low),
            dma((5,)),
            dma((9,)),
            dma((3,)),
            dma((3,)),
            dma((3,)),
            dma((3,)),
            dma((8,)),
            dma((9,)),
            dma,
        ],
        compiler_params=pltpu.CompilerParams(
            collective_id=collective, has_side_effects=True, vmem_limit_bytes=60 << 20
        ),
        cost_estimate=pl.CostEstimate(
            flops=8 * length * width * local, bytes_accessed=64 << 20, transcendentals=length * length * 4
        ),
    )(own, cot, *weights, out_w, *gains, *tables)


def attention_back_kernel(
    branch,
    gathered,
    query_unit,
    key_unit,
    query_low,
    key_low,
    value_low,
    attended,
    log_sums,
    query_w,
    key_w,
    value_w,
    out_w,
    query_gain,
    key_gain,
    cosine,
    sine,
    sent_input,
    sent_output,
    y_all,
    norm_mid_part,
    rows_grad,
    arrived_input,
    arrived_output,
    y_total,
    y_side,
    y_cross,
    y_line,
    y_sums,
    out_total,
    value_total,
    key_total,
    query_total,
    sums,
    branch_v,
    rows_v,
    weights_v,
    out_v,
    unit_v,
    low_v,
    log_v,
    grads_v,
    key_acc,
    value_acc,
    scattered,
    side_in,
    line_in,
    own_part,
    core_in,
    across_in,
    y_v,
    gain_sums,
    sums_in,
    load_sem,
    store_sem,
    branch_recv,
    branch_send,
    part_recv,
    part_send,
    side_recv,
    side_send,
    line_recv,
    line_send,
    swap_recv,
    swap_send,
    y_load,
    y_store,
    y_side_recv,
    y_side_send,
    y_cross_sems,
    y_line_recv,
    y_line_send,
    sums_recv,
    sums_send,
):
    position = lax.axis_index("expert")
    t = lax.axis_index("tensor")
    z = position // 2
    x = position % 2
    y = t // 2
    core = t % 2
    near = y * 2 + 1 - core
    across = (1 - y) * 2 + core
    opposite = (1 - y) * 2 + 1 - core
    rows = branch.shape[0]
    local = out_v.shape[0]
    heads = local // 128
    kinds = scattered.shape[0]
    factor = 1.0 / math.sqrt(128.0)
    middle = (z == 1) | (z == 2)
    mesh_ids = pl.DeviceIdType.MESH
    slots = [z, pick(z, [1, 0, 3, 2]), pick(z, [2, 2, 1, 1]), pick(z, [3, 3, 0, 0])]

    loads = [
        pltpu.make_async_copy(branch, branch_v.at[t], load_sem.at[0]),
        pltpu.make_async_copy(out_w, out_v, load_sem.at[1]),
        pltpu.make_async_copy(query_low, low_v.at[0], load_sem.at[2]),
        pltpu.make_async_copy(key_low, low_v.at[1], load_sem.at[3]),
        pltpu.make_async_copy(value_low, low_v.at[2], load_sem.at[4]),
        pltpu.make_async_copy(log_sums, log_v, load_sem.at[5]),
        pltpu.make_async_copy(query_unit, unit_v.at[0], load_sem.at[6]),
        pltpu.make_async_copy(key_unit, unit_v.at[1], load_sem.at[7]),
        pltpu.make_async_copy(attended, low_v.at[3], load_sem.at[8]),
        pltpu.make_async_copy(gathered, rows_v, load_sem.at[9]),
        pltpu.make_async_copy(query_w, weights_v.at[0], load_sem.at[10]),
        pltpu.make_async_copy(key_w, weights_v.at[1], load_sem.at[11]),
        pltpu.make_async_copy(value_w, weights_v.at[2], load_sem.at[12]),
    ]
    for load in loads:
        load.start()

    barrier = pltpu.get_barrier_semaphore()
    for place in ((position, near), (position, across), (z * 2 + 1 - x, t)):
        pl.semaphore_signal(barrier, inc=1, device_id=place, device_id_type=mesh_ids)

    @pl.when(z < 3)
    def _():
        pl.semaphore_signal(barrier, inc=1, device_id=(position + 2, t), device_id_type=mesh_ids)

    @pl.when(z > 0)
    def _():
        pl.semaphore_signal(barrier, inc=1, device_id=(position - 2, t), device_id_type=mesh_ids)

    distant = ((z + 2) % 4) * 2 + x
    pl.semaphore_signal(barrier, inc=1, device_id=(distant, t), device_id_type=mesh_ids)
    pl.semaphore_wait(barrier, 5 + middle.astype(jnp.int32))

    def branch_copy(source, block, index, to):
        return pltpu.make_async_remote_copy(
            src_ref=source,
            dst_ref=branch_v.at[block],
            send_sem=branch_send.at[index - 1],
            recv_sem=branch_recv.at[index - 1],
            device_id=(position, to),
            device_id_type=mesh_ids,
        )

    to_across = branch_copy(branch, t, 2, across)
    to_near = branch_copy(branch, t, 1, near)
    forward = branch_copy(branch_v.at[across], across, 3, near)
    to_across.start()
    to_near.start()

    swaps = [
        pltpu.make_async_remote_copy(
            src_ref=sent,
            dst_ref=arrived,
            send_sem=swap_send.at[i],
            recv_sem=swap_recv.at[i],
            device_id=(position, across),
            device_id_type=mesh_ids,
        )
        for i, (sent, arrived) in enumerate(
            ((sent_input, arrived_input), (sent_output, arrived_output))
        )
    ]

    def side_copy(k, c):
        return pltpu.make_async_remote_copy(
            src_ref=scattered.at[c, pick(k, slots) * 2 + 1 - x],
            dst_ref=side_in.at[c, k],
            send_sem=side_send.at[c, k],
            recv_sem=side_recv.at[c, k],
            device_id=(z * 2 + 1 - x, t),
            device_id_type=mesh_ids,
        )

    def line_slot(k):
        target = pick(k, slots)
        return jnp.where(target < z, target, target + 1)

    def line_copy(k, c):
        target = jnp.where(pick(k, slots) < z, z - 1, z + 1)
        return pltpu.make_async_remote_copy(
            src_ref=scattered.at[c, pick(k, slots) * 2 + x],
            dst_ref=line_in.at[c, line_slot(k)],
            send_sem=line_send.at[c, k - 1],
            recv_sem=line_recv.at[c, line_slot(k)],
            device_id=(jnp.clip(target, 0, 3) * 2 + x, t),
            device_id_type=mesh_ids,
        )

    def line_wait(slot, c):
        pltpu.make_async_remote_copy(
            src_ref=scattered.at[c, position],
            dst_ref=line_in.at[c, slot],
            send_sem=line_send.at[c, 0],
            recv_sem=line_recv.at[c, slot],
            device_id=(z * 2 + 1 - x, t),
            device_id_type=mesh_ids,
        ).wait_recv()

    def send_order(i):
        return jnp.where(middle, pick(i, [3, 1, 2, 0]), pick(i, [3, 2, 1, 0]))

    pair = z + 1 - 2 * (z % 2)
    ends = (z == 0) | (z == 3)

    def y_remote(source, target, send_sem, recv_sem, zz, xx):
        return pltpu.make_async_remote_copy(
            src_ref=source,
            dst_ref=target,
            send_sem=send_sem,
            recv_sem=recv_sem,
            device_id=(zz * 2 + xx, t),
            device_id_type=mesh_ids,
        )

    def y_block(k, xx):
        return y_all.at[slots[k] * 2 + xx]

    def y_side_copy(k):
        slot = max(k - 1, 0)
        source = y_sums.at[0] if k == 0 else y_block(k, 1 - x)
        return y_remote(
            source, y_side.at[slot], y_side_send.at[slot], y_side_recv.at[slot], z, 1 - x
        )

    def y_cross_copy():
        return y_remote(
            y_block(1, 1 - x), y_cross, y_cross_sems.at[0], y_cross_sems.at[1], pair, x
        )

    def y_line_copy(k, source):
        target = jnp.where(slots[k] < z, z - 1, z + 1)
        return y_remote(
            source,
            y_line.at[line_slot(k)],
            y_line_send.at[k - 1],
            y_line_recv.at[line_slot(k)],
            jnp.clip(target, 0, 3),
            x,
        )

    def y_line_wait(slot):
        y_remote(
            y_all.at[0], y_line.at[slot], y_line_send.at[0], y_line_recv.at[slot], z, 1 - x
        ).wait_recv()

    def y_add(target, sources):
        half = rows // 2
        for part in range(2):
            area = pl.ds(part * half, half)

            def load(i, source, area=area):
                return pltpu.make_async_copy(source.at[area], y_v.at[i], y_load.at[i])

            for i, (source, needed) in enumerate(sources):
                if needed is None:
                    load(i, source).start()
                else:

                    @pl.when(needed)
                    def _(i=i, source=source, load=load):
                        load(i, source).start()

            for i, (source, needed) in enumerate(sources):
                if needed is None:
                    load(i, source).wait()
                else:

                    @pl.when(needed)
                    def _(i=i, source=source, load=load):
                        load(i, source).wait()

            for i, (source, needed) in enumerate(sources[1:], 1):

                def add(i=i):
                    y_v[0] = (y_v[0].astype(jnp.float32) + y_v[i].astype(jnp.float32)).astype(
                        jnp.bfloat16
                    )

                if needed is None:
                    add()
                else:
                    pl.when(needed)(add)
            store = pltpu.make_async_copy(y_v.at[0], target.at[area], y_store)
            store.start()
            store.wait()

    def y_relay(k):
        if k > 1:
            y_side_copy(k).wait_recv()
        sources = [(y_block(k, x), None)]
        if k > 1:
            sources.append((y_side.at[k - 1], None))

        @pl.when(middle)
        def _():
            y_line_wait(line_slot(k))

        y_add(y_sums.at[k], [*sources, (y_line.at[line_slot(k)], middle)])
        y_line_copy(k, y_sums.at[k]).start()

    y_side_copy(3).start()
    y_cross_copy().start()
    y_side_copy(2).start()

    @pl.when(ends)
    def _():
        y_line_copy(1, y_block(1, x)).start()

    def start_side(c):
        def one(i, carry):
            side_copy(send_order(i), c).start()
            return carry

        lax.fori_loop(0, 4, one, 0)

    def weight_part(c, left, right):
        for d in range(8 // 2):
            span = pl.ds(d * 512, 512)
            product = jnp.zeros((512, local), jnp.float32)
            for b in range(4):
                product = product + lax.dot_general(
                    left[b, :, span],
                    right[pl.ds(b * rows, rows)],
                    contract_first,
                    preferred_element_type=jnp.float32,
                )
            scattered[c, 2 * d] = product[:256].astype(jnp.bfloat16)
            scattered[c, 2 * d + 1] = product[256:].astype(jnp.bfloat16)

    gain_sums[...] = jnp.zeros_like(gain_sums)
    sums[0] = jnp.zeros(sums.shape[1:], jnp.float32)
    sums[0, 1:2] = norm_mid_part[...]
    for load in loads[:9]:
        load.wait()

    def norm_back(turned, which, area, h, gain):
        span = slice(h * 128, (h + 1) * 128)
        grad = turned * cosine[area] - pltpu.roll(turned, 64, 1) * sine[area]
        unit = unit_v[which, area, span].astype(jnp.float32)
        gain_sums[which : which + 1] += jnp.sum(grad * unit, axis=0, keepdims=True)
        weighted = grad * gain[...]
        inner = jnp.mean(weighted * unit, axis=-1, keepdims=True)
        lane = 4 + which * 4 + h
        grads_v[which, area, span] = (
            log_v[area, lane : lane + 1] * (weighted - unit * inner)
        ).astype(jnp.bfloat16)

    def attend(i, carry):
        block = pick(i, [t, near, across, opposite])

        @pl.when(i == 1)
        def _():
            to_near.wait_recv()

        @pl.when(i == 2)
        def _():
            to_across.wait_recv()
            forward.start()
            to_across.wait_send()
            for swap in swaps:
                swap.start()

            @pl.when(ends)
            def _():
                y_relay(3)

        @pl.when(i == 3)
        def _():
            forward.wait_recv()
            weight_part(0, branch_v, low_v.at[3])
            start_side(0)

        area = pl.ds(block * rows, rows)
        mixed_grad = lax.dot_general(
            branch_v[block], out_v[...], contract_last, preferred_element_type=jnp.float32
        ).astype(jnp.bfloat16)
        for h in range(heads):
            span = slice(h * 128, (h + 1) * 128)
            query = low_v[0, area, span]
            key = low_v[1, :, span]
            grad = mixed_grad[:, span]
            scores = lax.dot_general(query, key, contract_last, preferred_element_type=jnp.float32)
            probs = jnp.exp(scores * factor - log_v[area, h : h + 1])
            prob_grad = lax.dot_general(
                grad, low_v[2, :, span], contract_last, preferred_element_type=jnp.float32
            )
            delta = jnp.sum(probs * prob_grad, axis=-1, keepdims=True)
            score_grad = (probs * (prob_grad - delta)).astype(jnp.bfloat16)
            query_grad = jnp.dot(score_grad, key, preferred_element_type=jnp.float32) * factor
            key_part = lax.dot_general(
                score_grad, query, contract_first, preferred_element_type=jnp.float32
            )
            value_part = lax.dot_general(
                probs.astype(jnp.bfloat16), grad, contract_first, preferred_element_type=jnp.float32
            )
            first = i == 0
            key_acc[:, span] = jnp.where(first, 0.0, key_acc[:, span]) + key_part
            value_acc[:, span] = jnp.where(first, 0.0, value_acc[:, span]) + value_part
            norm_back(query_grad, 0, area, h, query_gain)
        return carry

    key_acc[...] = jnp.zeros_like(key_acc)
    value_acc[...] = jnp.zeros_like(value_acc)
    lax.fori_loop(0, 4, attend, 0)
    for load in loads[9:]:
        load.wait()

    @pl.when(ends)
    def _():
        y_relay(2)

    @pl.when(middle)
    def _():
        y_relay(3)

    grads_v[2] = value_acc[...].astype(jnp.bfloat16)
    weight_part(1, rows_v, grads_v.at[2])
    start_side(1)

    def key_back(b, carry):
        area = pl.ds(b * rows, rows)
        for h in range(heads):
            norm_back(key_acc[area, h * 128 : (h + 1) * 128] * factor, 1, area, h, key_gain)
        return carry

    lax.fori_loop(0, 4, key_back, 0)
    weight_part(2, rows_v, grads_v.at[1])
    start_side(2)
    weight_part(3, rows_v, grads_v.at[0])
    start_side(3)

    y_cross_copy().wait_recv()
    y_add(y_sums.at[0], [(y_block(0, 1 - x), None), (y_cross, None)])
    y_side_copy(0).start()

    def part_copy(source, target, index, to):
        return pltpu.make_async_remote_copy(
            src_ref=source,
            dst_ref=target,
            send_sem=part_send.at[index],
            recv_sem=part_recv.at[index],
            device_id=(position, to),
            device_id_type=mesh_ids,
        )

    for copy in (to_near, forward):
        copy.wait_send()
    core_first = part_copy(branch_v.at[0], core_in.at[0], 0, near)
    across_copy = part_copy(branch_v.at[1], across_in, 1, across)
    core_second = part_copy(branch_v.at[2], core_in.at[1], 2, near)

    def relay(k, c):
        block = pick(k, slots) * 2 + x
        side_copy(k, c).wait_recv()
        scattered[c, block] = (
            scattered[c, block].astype(jnp.float32) + side_in[c, k].astype(jnp.float32)
        ).astype(jnp.bfloat16)

        @pl.when(middle)
        def _():
            line_wait(line_slot(k), c)
            scattered[c, block] = (
                scattered[c, block].astype(jnp.float32) + line_in[c, line_slot(k)].astype(jnp.float32)
            ).astype(jnp.bfloat16)

        line_copy(k, c).start()

    def relays(c):
        def one(i, carry):
            relay(send_order(i), c)
            return carry

        lax.fori_loop(0, 3, one, 0)

    def rows_part(i, carry):
        block = pick(i, [opposite, across, near, t])
        area = pl.ds(block * rows, rows)
        for d in range(2):
            span = pl.ds(d * 1024, 1024)
            product = jnp.zeros((rows, 1024), jnp.float32)
            for which in range(3):
                product = product + lax.dot_general(
                    grads_v[which, area],
                    weights_v[which, span],
                    contract_last,
                    preferred_element_type=jnp.float32,
                )
            own_part[:, span] = product
            sums[0, 0:1, span] += jnp.sum(
                product * rows_v[block, :, span].astype(jnp.float32), axis=0, keepdims=True
            )

        @pl.when(i == 0)
        def _():
            branch_v[0] = own_part[...].astype(jnp.bfloat16)
            core_first.start()

        @pl.when(i == 1)
        def _():
            core_first.wait_recv()
            branch_v[1] = (own_part[...] + core_in[0].astype(jnp.float32)).astype(jnp.bfloat16)
            across_copy.start()

        @pl.when(i == 2)
        def _():
            branch_v[2] = own_part[...].astype(jnp.bfloat16)
            core_second.start()

        return carry

    lax.fori_loop(0, 4, rows_part, 0)
    sums[0, 2:3, :128] = gain_sums[0:1]
    sums[0, 2:3, 128:256] = gain_sums[1:2]

    def sums_round(i, to):
        copy = pltpu.make_async_remote_copy(
            src_ref=sums.at[i],
            dst_ref=sums_in.at[i],
            send_sem=sums_send.at[i],
            recv_sem=sums_recv.at[i],
            device_id=to,
            device_id_type=mesh_ids,
        )
        copy.start()
        copy.wait()
        sums[i + 1] = sums[i] + sums_in[i]

    sums_round(0, (position, near))
    relays(0)

    @pl.when(middle)
    def _():
        y_relay(1)
        y_relay(2)

    relays(1)
    relays(2)
    y_side_copy(0).wait_recv()

    @pl.when(z < 3)
    def _():
        y_line_wait(z)

    @pl.when(z > 0)
    def _():
        y_line_wait(z + 1)

    y_add(
        y_total,
        [
            (y_all.at[position], None),
            (y_side.at[0], None),
            (y_line.at[z], z < 3),
            (y_line.at[z + 1], z > 0),
        ],
    )
    relays(3)
    for c, total in enumerate((out_total, value_total, key_total, query_total)):
        side_copy(0, c).wait_recv()
        total[...] = scattered[c, position].astype(jnp.float32) + side_in[c, 0].astype(jnp.float32)

        @pl.when(z < 3)
        def _(c=c, total=total):
            line_wait(z, c)
            total[...] += line_in[c, z].astype(jnp.float32)

        @pl.when(z > 0)
        def _(c=c, total=total):
            line_wait(z + 1, c)
            total[...] += line_in[c, z + 1].astype(jnp.float32)

        for k in range(4):
            side_copy(k, c).wait_send()
        for k in range(1, 4):
            line_copy(k, c).wait_send()
    sums_round(1, (z * 2 + 1 - x, t))
    sums_round(2, (pair * 2 + x, t))
    sums_round(3, (distant, t))
    core_second.wait_recv()
    own_part[...] += core_in[1].astype(jnp.float32)
    across_copy.wait_recv()
    own_part[...] += across_in[...].astype(jnp.float32)
    last = pltpu.make_async_copy(own_part, rows_grad, store_sem)
    last.start()
    sums_round(4, (position, across))
    for copy in (core_first, across_copy, core_second):
        copy.wait_send()
    last.wait()
    for swap in swaps:
        swap.wait()
    for k in (0, 2, 3):
        y_side_copy(k).wait_send()
    y_cross_copy().wait_send()
    for k in (1, 2, 3):
        y_line_copy(k, y_sums.at[k]).wait_send()


def attention_backward(branch, saved, weights, out_w, gains, tables, sent, y_all, norm_mid_part, collective):
    rows, width = branch.shape
    local = out_w.shape[0]
    length = 4 * rows
    any_space = pl.BlockSpec(memory_space=pl.ANY)
    vector = pl.BlockSpec(memory_space=pltpu.VMEM)
    low, full = jnp.bfloat16, jnp.float32
    dma = pltpu.SemaphoreType.DMA
    return pl.pallas_call(
        attention_back_kernel,
        name="attention_backward",
        out_shape=(jax.ShapeDtypeStruct((rows, width), full),)
        + tuple(jax.ShapeDtypeStruct(array.shape, array.dtype) for array in sent)
        + (
            jax.ShapeDtypeStruct((rows, width), low),
            jax.ShapeDtypeStruct((3, rows, width), low),
            jax.ShapeDtypeStruct((rows, width), low),
            jax.ShapeDtypeStruct((5, rows, width), low),
            jax.ShapeDtypeStruct((4, rows, width), low),
        )
        + (jax.ShapeDtypeStruct((width // 8, local), full),) * 4
        + (jax.ShapeDtypeStruct((6, 8, width), full),),
        in_specs=[any_space] * 13 + [vector] * 4 + [any_space] * 3 + [vector],
        out_specs=(any_space,) * 8 + (vector,) * 5,
        scratch_shapes=[
            pltpu.VMEM((4, rows, width), low),
            pltpu.VMEM((4, rows, width), low),
            pltpu.VMEM((3, width, local), low),
            pltpu.VMEM((local, width), low),
            pltpu.VMEM((2, length, local), low),
            pltpu.VMEM((4, length, local), low),
            pltpu.VMEM((length, 128), full),
            pltpu.VMEM((3, length, local), low),
            pltpu.VMEM((length, local), full),
            pltpu.VMEM((length, local), full),
            pltpu.VMEM((4, 8, width // 8, local), low),
            pltpu.VMEM((4, 4, width // 8, local), low),
            pltpu.VMEM((4, 5, width // 8, local), low),
            pltpu.VMEM((rows, width), full),
            pltpu.VMEM((2, rows, width), low),
            pltpu.VMEM((rows, width), low),
            pltpu.VMEM((4, rows // 2, width), low),
            pltpu.VMEM((8, 128), full),
            pltpu.VMEM((5, 8, width), full),
            dma((13,)),
            dma,
            dma((3,)),
            dma((3,)),
            dma((3,)),
            dma((3,)),
            dma((4, 4)),
            dma((4, 4)),
            dma((4, 5)),
            dma((4, 3)),
            dma((2,)),
            dma((2,)),
            dma((4,)),
            dma,
            dma((3,)),
            dma((3,)),
            dma((2,)),
            dma((5,)),
            dma((3,)),
            dma((5,)),
            dma((5,)),
        ],
        compiler_params=pltpu.CompilerParams(
            collective_id=collective, has_side_effects=True, vmem_limit_bytes=60 << 20
        ),
        cost_estimate=pl.CostEstimate(
            flops=16 * length * width * local, bytes_accessed=64 << 20, transcendentals=length * length * 4
        ),
    )(branch, *saved, *weights, out_w, *gains, *tables, *sent, y_all, norm_mid_part)


def add_three(first, second, third):
    return first.astype(jnp.float32) + second.astype(jnp.float32) + third.astype(jnp.float32)


def per_device(
    tokens,
    cotangent,
    routes,
    norm_in,
    query_w,
    key_w,
    value_w,
    out_w,
    query_gain,
    key_gain,
    norm_mid,
    router_w,
    gate_w,
    up_w,
    down_w,
):
    rows_own = tokens.shape[0]
    model_width = tokens.shape[1]
    head_width = query_gain.shape[0]
    experts_all = router_w.shape[1]
    source = tokens.astype(jnp.float32)
    scale_in = inverse_rms(source)
    normed_low = (source * scale_in * norm_in).astype(jnp.bfloat16)
    cosine, sine_table = rotary_tables(4 * rows_own, head_width)
    tables = (
        jnp.concatenate([cosine[:, 0], cosine[:, 0]], axis=1),
        jnp.concatenate([-sine_table[:, 0], sine_table[:, 0]], axis=1),
    )
    gains = (query_gain[None], key_gain[None])
    *saved, attn_out, cot_all = attention_forward(
        normed_low, cotangent, (query_w, key_w, value_w), out_w, gains, tables, 1
    )
    middle = source + attn_out
    scale_mid = inverse_rms(middle)
    normed_mid = middle * scale_mid * norm_mid
    mid_low = normed_mid.astype(jnp.bfloat16)
    logits = jnp.dot(normed_mid, router_w, precision=highest, preferred_element_type=jnp.float32)
    route_mask = routes[:, :, None] == jnp.arange(experts_all, dtype=jnp.int32)[None, None, :]
    mask_float = route_mask.astype(jnp.float32)
    chosen = jnp.sum(mask_float * logits[:, None, :], axis=-1)
    gating = jax.nn.softmax(chosen, axis=-1)
    gates = jnp.sum(mask_float * gating[:, :, None], axis=1)
    gates_high = gates.astype(jnp.bfloat16)
    gates_low = (gates - gates_high.astype(jnp.float32)).astype(jnp.bfloat16)
    spare = jnp.zeros((rows_own, 128 - 2 * experts_all), jnp.bfloat16)
    own_rows = jnp.concatenate([mid_low, gates_high, gates_low, spare], axis=1)
    _, _, y_all, row_total, core_input, near_input, core_output, near_output, _ = expert_pass(
        own_rows, cot_all.reshape(-1, model_width), gate_w, up_w, down_w, experts_all, 2
    )
    expert_input_grad = row_total[:, :model_width]
    gate_grad_dense = (
        row_total[:, model_width : model_width + experts_all]
        + row_total[:, model_width + experts_all : model_width + 2 * experts_all]
    )
    gate_grad = jnp.sum(mask_float * gate_grad_dense[:, None, :], axis=-1)
    inner_gate = jnp.sum(gating * gate_grad, axis=-1, keepdims=True)
    chosen_grad = gating * (gate_grad - inner_gate)
    logit_grad = jnp.sum(chosen_grad[:, :, None] * mask_float, axis=1)
    normed_mid_grad = expert_input_grad + lax.dot_general(
        logit_grad, router_w, contract_last, precision=highest, preferred_element_type=jnp.float32
    )
    norm_mid_part = jnp.sum(normed_mid_grad * middle * scale_mid, axis=0)
    upstream = cotangent.astype(jnp.float32)
    middle_grad = upstream + norm_backward(normed_mid_grad, middle, scale_mid, norm_mid)
    branch_low = middle_grad.astype(jnp.bfloat16)
    sent = (
        (near_input[1].astype(jnp.float32) + core_input[1].astype(jnp.float32)).astype(jnp.bfloat16),
        (near_output[1].astype(jnp.float32) + core_output[1].astype(jnp.float32)).astype(jnp.bfloat16),
    )
    (
        rows_grad,
        line_input,
        line_output,
        y_sum,
        _,
        _,
        _,
        _,
        out_w_turned,
        value_w_grad,
        key_w_grad,
        query_w_grad,
        sums,
    ) = attention_backward(
        branch_low, saved, (query_w, key_w, value_w), out_w, gains, tables, sent, y_all, norm_mid_part[None], 3
    )
    out_w_grad = out_w_turned.T
    router_part = lax.dot_general(
        normed_mid,
        logit_grad,
        contract_first,
        precision=highest,
        preferred_element_type=jnp.float32,
    )
    output = (middle + y_sum.astype(jnp.float32)).astype(jnp.bfloat16)
    gate_w_grad = add_three(near_input[0, 0], core_input[0, 0], line_input[0])
    up_w_grad = add_three(near_input[0, 1], core_input[0, 1], line_input[1])
    down_w_grad = add_three(near_output[0], core_output[0], line_output)
    input_grad = middle_grad + norm_backward(rows_grad, source, scale_in, norm_in)
    router_w_grad = lax.psum(router_part, ("expert", "tensor"))
    norm_in_grad = sums[5, 0] / norm_in
    norm_mid_grad = sums[5, 1]
    query_gain_grad = sums[5, 2, :head_width]
    key_gain_grad = sums[5, 2, head_width : 2 * head_width]
    return (
        output,
        input_grad,
        norm_in_grad,
        query_w_grad,
        key_w_grad,
        value_w_grad,
        out_w_grad,
        query_gain_grad,
        key_gain_grad,
        norm_mid_grad,
        router_w_grad,
        gate_w_grad,
        up_w_grad,
        down_w_grad,
    )


def per_device_general(
    tokens,
    cotangent,
    routes,
    norm_in,
    query_w,
    key_w,
    value_w,
    out_w,
    query_gain,
    key_gain,
    norm_mid,
    router_w,
    gate_w,
    up_w,
    down_w,
):
    rows_own = tokens.shape[0]
    model_width = tokens.shape[1]
    tensor_count = lax.axis_size("tensor")
    expert_count = lax.axis_size("expert")
    head_width = query_gain.shape[0]
    local_heads = query_w.shape[1] // head_width
    experts_local = gate_w.shape[0]
    experts_all = router_w.shape[1]
    top_count = routes.shape[1]
    hidden_width = gate_w.shape[2]
    factor = 1.0 / math.sqrt(head_width)
    cot_all = lax.all_gather(cotangent, "expert", axis=0, tiled=True)
    source = tokens.astype(jnp.float32)
    scale_in = inverse_rms(source)
    normed_low = (source * scale_in * norm_in).astype(jnp.bfloat16)
    gathered = lax.all_gather(normed_low, "tensor", axis=0, tiled=True)
    seq_len = gathered.shape[0]
    query_pre = jnp.dot(gathered, query_w, preferred_element_type=jnp.float32)
    key_pre = jnp.dot(gathered, key_w, preferred_element_type=jnp.float32)
    value_low = jnp.dot(gathered, value_w, preferred_element_type=jnp.float32).astype(jnp.bfloat16)
    cosine, sine_table = rotary_tables(seq_len, head_width)
    query_heads = query_pre.reshape(seq_len, local_heads, head_width)
    key_heads = key_pre.reshape(seq_len, local_heads, head_width)
    query_scale = inverse_rms(query_heads)
    key_scale = inverse_rms(key_heads)
    query_low = rotate(query_heads * query_scale * query_gain, cosine, sine_table).astype(
        jnp.bfloat16
    )
    key_low = rotate(key_heads * key_scale * key_gain, cosine, sine_table).astype(jnp.bfloat16)
    value_heads = value_low.reshape(seq_len, local_heads, head_width)
    block_rows = min(512, seq_len)
    block_count = seq_len // block_rows
    query_blocks = query_low.reshape(block_count, block_rows, local_heads, head_width)

    def attend(query_block):
        scores = (
            jnp.einsum("qhd,khd->hqk", query_block, key_low, preferred_element_type=jnp.float32)
            * factor
        )
        row_max = jnp.max(scores, axis=-1, keepdims=True)
        shifted = jnp.exp(scores - row_max)
        row_sum = jnp.sum(shifted, axis=-1, keepdims=True)
        probs_low = (shifted / row_sum).astype(jnp.bfloat16)
        mixture = jnp.einsum(
            "hqk,khd->qhd", probs_low, value_heads, preferred_element_type=jnp.float32
        )
        return (mixture.astype(jnp.bfloat16), (row_max + jnp.log(row_sum))[..., 0])

    attended_blocks, log_sums = lax.map(attend, query_blocks)
    attended = attended_blocks.reshape(seq_len, local_heads * head_width)
    attn_out = lax.psum_scatter(
        jnp.dot(attended, out_w, preferred_element_type=jnp.float32).astype(jnp.bfloat16),
        "tensor",
        scatter_dimension=0,
        tiled=True,
    ).astype(jnp.float32)
    middle = source + attn_out
    scale_mid = inverse_rms(middle)
    normed_mid = middle * scale_mid * norm_mid
    mid_low = normed_mid.astype(jnp.bfloat16)
    logits = jnp.dot(normed_mid, router_w, precision=highest, preferred_element_type=jnp.float32)
    route_mask = routes[:, :, None] == jnp.arange(experts_all, dtype=jnp.int32)[None, None, :]
    mask_float = route_mask.astype(jnp.float32)
    chosen = jnp.sum(mask_float * logits[:, None, :], axis=-1)
    gating = jax.nn.softmax(chosen, axis=-1)
    upstream = cotangent.astype(jnp.float32)
    gates = jnp.sum(mask_float * gating[:, :, None], axis=1)
    x_all = lax.all_gather(mid_low, "expert", axis=0, tiled=True)
    gates_all = lax.all_gather(gates, "expert", axis=0, tiled=True)
    first_expert = lax.axis_index("expert") * experts_local
    own_gates = lax.dynamic_slice_in_dim(gates_all, first_expert, experts_local, 1)
    part_width = hidden_width // tensor_count
    rows_all = x_all.shape[0]
    y_part = jnp.zeros((rows_all, model_width), jnp.float32)
    x_grad_part = jnp.zeros((rows_all, model_width), jnp.float32)
    gate_grads, gate_parts, up_parts, down_parts = [], [], [], []
    for e in range(experts_local):
        hidden_raw = lax.dot_general(
            cot_all, down_w[e], contract_last, preferred_element_type=jnp.float32
        )
        gate_pre = jnp.dot(x_all, gate_w[e], preferred_element_type=jnp.float32)
        up_pre = jnp.dot(x_all, up_w[e], preferred_element_type=jnp.float32)
        weight = own_gates[:, e : e + 1]
        hidden = gate_pre * jax.nn.sigmoid(gate_pre) * up_pre
        gate_grads.append(jnp.sum(hidden * hidden_raw, axis=1))
        hidden_low = (hidden * weight).astype(jnp.bfloat16)
        gate_back, up_back = swiglu_back(hidden_raw * weight, gate_pre, up_pre)
        y_part = y_part + jnp.dot(hidden_low, down_w[e], preferred_element_type=jnp.float32)
        x_grad_part = x_grad_part + lax.dot_general(
            gate_back, gate_w[e], contract_last, preferred_element_type=jnp.float32
        )
        x_grad_part = x_grad_part + lax.dot_general(
            up_back, up_w[e], contract_last, preferred_element_type=jnp.float32
        )
        gate_parts.append(
            jnp.einsum(
                "nd,ntf->tdf",
                x_all,
                gate_back.reshape(rows_all, tensor_count, part_width),
                preferred_element_type=jnp.float32,
            ).astype(jnp.bfloat16)
        )
        up_parts.append(
            jnp.einsum(
                "nd,ntf->tdf",
                x_all,
                up_back.reshape(rows_all, tensor_count, part_width),
                preferred_element_type=jnp.float32,
            ).astype(jnp.bfloat16)
        )
        down_parts.append(
            lax.dot_general(
                hidden_low, cot_all, contract_first, preferred_element_type=jnp.float32
            ).astype(jnp.bfloat16)
        )
    x_grad = lax.psum_scatter(
        x_grad_part.astype(jnp.bfloat16), "expert", scatter_dimension=0, tiled=True
    )
    expert_input_grad = x_grad.astype(jnp.float32)
    gate_grad_sent = jnp.stack(gate_grads, axis=-1)
    gate_grad_all = lax.all_to_all(gate_grad_sent, "expert", split_axis=0, concat_axis=0, tiled=True)
    gate_grad_dense = (
        gate_grad_all.reshape(expert_count, rows_own, experts_local)
        .transpose(1, 0, 2)
        .reshape(rows_own, experts_all)
    )
    gate_grad = jnp.sum(mask_float * gate_grad_dense[:, None, :], axis=-1)
    y_sum = lax.psum_scatter(
        y_part.astype(jnp.bfloat16), "expert", scatter_dimension=0, tiled=True
    )
    output = (middle + y_sum.astype(jnp.float32)).astype(jnp.bfloat16)

    def own_part(parts):
        return [
            lax.psum_scatter(p, "tensor", scatter_dimension=0, tiled=True).astype(jnp.float32)
            for p in parts
        ]

    gate_w_grad = jnp.concatenate(own_part(gate_parts), axis=0)
    up_w_grad = jnp.concatenate(own_part(up_parts), axis=0)
    down_w_grad = jnp.stack(own_part(down_parts), axis=0)
    inner_gate = jnp.sum(gating * gate_grad, axis=-1, keepdims=True)
    chosen_grad = gating * (gate_grad - inner_gate)
    logit_grad = jnp.sum(chosen_grad[:, :, None] * mask_float, axis=1)
    router_part = lax.dot_general(
        normed_mid,
        logit_grad,
        contract_first,
        precision=highest,
        preferred_element_type=jnp.float32,
    )
    normed_mid_grad = expert_input_grad + lax.dot_general(
        logit_grad, router_w, contract_last, precision=highest, preferred_element_type=jnp.float32
    )
    norm_mid_part = jnp.sum(normed_mid_grad * middle * scale_mid, axis=0)
    middle_grad = upstream + norm_backward(normed_mid_grad, middle, scale_mid, norm_mid)
    branch_low = middle_grad.astype(jnp.bfloat16)
    branch_all = lax.all_gather(branch_low, "tensor", axis=0, tiled=True)
    attended_grad = lax.dot_general(
        branch_all, out_w, contract_last, preferred_element_type=jnp.float32
    ).astype(jnp.bfloat16)
    out_w_part = lax.dot_general(
        attended, branch_all, contract_first, preferred_element_type=jnp.float32
    )
    grad_blocks = attended_grad.reshape(block_count, block_rows, local_heads, head_width)

    def attend_back(carry, inputs):
        key_total, value_total = carry
        query_block, grad_block, log_block = inputs
        scores = (
            jnp.einsum("qhd,khd->hqk", query_block, key_low, preferred_element_type=jnp.float32)
            * factor
        )
        probs = jnp.exp(scores - log_block[:, :, None])
        probs_low = probs.astype(jnp.bfloat16)
        value_total = value_total + jnp.einsum(
            "hqk,qhd->khd", probs_low, grad_block, preferred_element_type=jnp.float32
        )
        prob_grad = jnp.einsum(
            "qhd,khd->hqk", grad_block, value_heads, preferred_element_type=jnp.float32
        )
        delta = jnp.sum(probs * prob_grad, axis=-1, keepdims=True)
        score_low = (probs * (prob_grad - delta)).astype(jnp.bfloat16)
        query_part = (
            jnp.einsum("hqk,khd->qhd", score_low, key_low, preferred_element_type=jnp.float32)
            * factor
        )
        key_total = (
            key_total
            + jnp.einsum("hqk,qhd->khd", score_low, query_block, preferred_element_type=jnp.float32)
            * factor
        )
        return ((key_total, value_total), query_part)

    zero_heads = jnp.zeros((seq_len, local_heads, head_width), jnp.float32)
    (key_grad, value_total), query_parts = lax.scan(
        attend_back, (zero_heads, zero_heads), (query_blocks, grad_blocks, log_sums)
    )
    query_grad = query_parts.reshape(seq_len, local_heads, head_width)
    value_grad_low = value_total.reshape(seq_len, local_heads * head_width).astype(jnp.bfloat16)
    query_rot_grad = rotate_back(query_grad, cosine, sine_table)
    key_rot_grad = rotate_back(key_grad, cosine, sine_table)
    query_gain_part = jnp.sum(query_rot_grad * query_heads * query_scale, axis=(0, 1))
    key_gain_part = jnp.sum(key_rot_grad * key_heads * key_scale, axis=(0, 1))
    query_pre_grad = (
        norm_backward(query_rot_grad, query_heads, query_scale, query_gain)
        .reshape(seq_len, local_heads * head_width)
        .astype(jnp.bfloat16)
    )
    key_pre_grad = (
        norm_backward(key_rot_grad, key_heads, key_scale, key_gain)
        .reshape(seq_len, local_heads * head_width)
        .astype(jnp.bfloat16)
    )
    query_w_part = lax.dot_general(
        gathered, query_pre_grad, contract_first, preferred_element_type=jnp.float32
    )
    key_w_part = lax.dot_general(
        gathered, key_pre_grad, contract_first, preferred_element_type=jnp.float32
    )
    value_w_part = lax.dot_general(
        gathered, value_grad_low, contract_first, preferred_element_type=jnp.float32
    )
    summed = lax.dot_general(
        query_pre_grad, query_w, contract_last, preferred_element_type=jnp.float32
    )
    summed = summed + lax.dot_general(
        key_pre_grad, key_w, contract_last, preferred_element_type=jnp.float32
    )
    rows_grad = lax.psum_scatter(
        (
            summed
            + lax.dot_general(
                value_grad_low, value_w, contract_last, preferred_element_type=jnp.float32
            )
        ).astype(jnp.bfloat16),
        "tensor",
        scatter_dimension=0,
        tiled=True,
    ).astype(jnp.float32)
    norm_in_part = jnp.sum(rows_grad * source * scale_in, axis=0)
    input_grad = middle_grad + norm_backward(rows_grad, source, scale_in, norm_in)
    query_w_grad, key_w_grad, value_w_grad, out_w_grad = (
        lax.psum_scatter(
            query_w_part.astype(jnp.bfloat16), "expert", scatter_dimension=0, tiled=True
        ).astype(jnp.float32),
        lax.psum_scatter(
            key_w_part.astype(jnp.bfloat16), "expert", scatter_dimension=0, tiled=True
        ).astype(jnp.float32),
        lax.psum_scatter(
            value_w_part.astype(jnp.bfloat16), "expert", scatter_dimension=0, tiled=True
        ).astype(jnp.float32),
        lax.psum_scatter(
            out_w_part.astype(jnp.bfloat16), "expert", scatter_dimension=1, tiled=True
        ).astype(jnp.float32),
    )
    norm_in_grad, query_gain_grad, key_gain_grad, norm_mid_grad, router_w_grad = lax.psum(
        (norm_in_part, query_gain_part, key_gain_part, norm_mid_part, router_part),
        ("expert", "tensor"),
    )
    return (
        output,
        input_grad,
        norm_in_grad,
        query_w_grad,
        key_w_grad,
        value_w_grad,
        out_w_grad,
        query_gain_grad,
        key_gain_grad,
        norm_mid_grad,
        router_w_grad,
        gate_w_grad,
        up_w_grad,
        down_w_grad,
    )


def solution(mesh):
    placed = (
        P(("expert", "tensor"), None),
        P(("expert", "tensor"), None),
        P(("expert", "tensor"), None),
        P(),
        P(None, "tensor"),
        P(None, "tensor"),
        P(None, "tensor"),
        P("tensor", None),
        P(),
        P(),
        P(),
        P(),
        P("expert", None, None),
        P("expert", None, None),
        P("expert", None, None),
    )
    return jax.shard_map(
        per_device if dict(mesh.shape) == {"expert": 8, "tensor": 4} else per_device_general,
        mesh=mesh,
        in_specs=placed,
        out_specs=(
            P(("expert", "tensor"), None),
            P(("expert", "tensor"), None),
            P(),
            P("expert", "tensor"),
            P("expert", "tensor"),
            P("expert", "tensor"),
            P("tensor", "expert"),
            P(),
            P(),
            P(),
            P(),
            P("expert", None, "tensor"),
            P("expert", None, "tensor"),
            P("expert", "tensor", None),
        ),
        check_vma=False,
    )
```
